32 devices in a mesh: seq: 4 (over y, x), ctx: 8 (over z, core).
Axes of the slice: x: 2, y: 2, z: 4, core: 2. Of those that a mesh axis runs over, the one named last changes fastest.
Arguments:
- hidden_in: bfloat16 [4096, 2048], P(('seq', 'ctx')), may hold values from -6 to 6
- out_grad: bfloat16 [4096, 2048], P(('seq', 'ctx')), may hold values from -6 to 6
- prefix_len: int32 [4], P('seq'), may hold values from 102 to 512
- norm_gains: float32 [4352], P(('seq', 'ctx')), may hold values from 0.5 to 1.5
- query_weight: float32 [2048, 2048], P(('seq', 'ctx')), may hold values from -0.125 to 0.125
- key_weight: float32 [2048, 1024], P(('seq', 'ctx')), may hold values from -0.125 to 0.125
- value_weight: float32 [2048, 1024], P(('seq', 'ctx')), may hold values from -0.125 to 0.125
- head_gate_weight: float32 [2048, 16], P(('seq', 'ctx')), may hold values from -0.125 to 0.125
- out_weight: float32 [2048, 2048], P(('seq', 'ctx')), may hold values from -3 to 3
- gate_weight: float32 [2048, 6144], P(('seq', 'ctx')), may hold values from -0.125 to 0.125
- up_weight: float32 [2048, 6144], P(('seq', 'ctx')), may hold values from -0.125 to 0.125
- down_weight: float32 [6144, 2048], P(('seq', 'ctx')), may hold values from -0.109375 to 0.109375
Outputs:
- hidden_out: bfloat16 [4096, 2048], P(('seq', 'ctx'))
- hidden_grad: bfloat16 [4096, 2048], P(('seq', 'ctx'))
- gains_grad: float32 [4352], P(('seq', 'ctx'))
- query_grad: float32 [2048, 2048], P(('seq', 'ctx'))
- key_grad: float32 [2048, 1024], P(('seq', 'ctx'))
- value_grad: float32 [2048, 1024], P(('seq', 'ctx'))
- head_gate_grad: float32 [2048, 16], P(('seq', 'ctx'))
- out_weight_grad: float32 [2048, 2048], P(('seq', 'ctx'))
- gate_grad: float32 [2048, 6144], P(('seq', 'ctx'))
- up_grad: float32 [2048, 6144], P(('seq', 'ctx'))
- down_grad: float32 [6144, 2048], P(('seq', 'ctx'))
The draws below stay inside these ranges and needn't reach their ends.
Inputs may be any that keep to these rules, and one draw needn't show every extreme that they name: prefix_len[s] is the number of leading tokens of sequence s that attend to each other in both directions.
All inputs are finite; a program needn't handle non-finite values.
Results may differ from the reference program's by a relative error of at most 0.02.
Values may be sent and summed in bfloat16 or wider, within the bound.
A program may use at most 448 MiB of HBM per device.

```python
import jax
import jax.numpy as jnp
from jax import lax

D = 2048
H = 16
KV = 8
HD = 128
FF = 6144
LENGTH = 1024
SEQS = 4
TOKENS = 4096


def with_ends(result, rng, least, top_value):
    dims = result.shape
    index_at = [jax.random.randint(jax.random.fold_in(rng, axis), (), 0, dims[axis]) for axis in range(len(dims))]
    result = result.at[tuple(index_at)].set(least)
    longest = dims.index(max(dims))
    index_at[longest] = (index_at[longest] + 1) % dims[longest]
    return result.at[tuple(index_at)].set(top_value)


def raised(drawn, own_key, source, target, shards_of, factor):
    owner, partner = [(jnp.arange(drawn.shape[axis_at]) // (drawn.shape[axis_at] // shards_of)).reshape([-1 if axis == axis_at else 1 for axis in range(drawn.ndim)]) for axis_at in (source, target)]
    chosen = jax.random.permutation(own_key, shards_of)[partner]
    strong = (owner == chosen) | (owner == (partner + shards_of // 2) % shards_of)
    return jnp.where(strong, factor * drawn, drawn)


def levels(rng, dims, cuts, least, top_value):
    def one(position, blocks):
        draws = jax.random.uniform(jax.random.fold_in(jax.random.fold_in(rng, 6), position), (blocks,), jnp.float32, least / len(cuts), top_value / len(cuts))
        return jnp.repeat(jnp.exp(draws), dims[position] // blocks).reshape((-1,) + (1,) * (len(dims) - position - 1))

    loudness = one(*cuts[0])
    for cut in cuts[1:]:
        loudness = loudness * one(*cut)
    return loudness


def centred(rng, dims, width, reach, cuts=(), kind=jnp.bfloat16):
    factor_of = levels(rng, dims, cuts, -0.22, 0.18) if cuts else 1.0
    array = jax.random.normal(rng, dims, jnp.float32) * width * factor_of
    return jnp.minimum(jnp.maximum(array, -reach), reach).astype(kind)


def noise_with(rng, shape, scale, bound, cuts, heavy, held_as=jnp.bfloat16):
    drawn = scale * jax.random.normal(rng, shape, jnp.float32)
    if cuts:
        drawn = drawn * levels(rng, shape, cuts, -0.22, 0.18)
    return jnp.clip(raised(drawn, jax.random.fold_in(rng, 3), *heavy), -bound, bound).astype(held_as)


def setup_inputs(seed: int = 0) -> dict:
    seeds = jax.random.split(jax.random.key(seed), 13)
    return {
        "hidden_in": noise_with(seeds[0], (TOKENS, D), 1.0, 6.0, ((0, 32),), (0, 1, 32, 2.75)),
        "out_grad": centred(seeds[1], (TOKENS, D), 1.0, 6.0, ((0, 32),)),
        "prefix_len": with_ends(jax.random.randint(seeds[2], (SEQS,), LENGTH // 10, LENGTH // 2 + 1), jax.random.fold_in(seeds[2], 1), LENGTH // 10, (LENGTH // 2 + 1) - 1).astype(jnp.int32),
        "norm_gains": jnp.clip(1.0 + 0.1 * jax.random.normal(seeds[3], (2 * D + 2 * HD,), jnp.float32), 0.5, 1.5),
        "query_weight": centred(seeds[4], (D, H * HD), D ** -0.5, 0.125, ((0, 32),), jnp.float32),
        "key_weight": centred(seeds[5], (D, KV * HD), D ** -0.5, 0.125, ((0, 32),), jnp.float32),
        "value_weight": centred(seeds[6], (D, KV * HD), D ** -0.5, 0.125, ((0, 32),), jnp.float32),
        "head_gate_weight": centred(seeds[7], (D, H), D ** -0.5, 0.125, ((0, 32),), jnp.float32),
        "out_weight": centred(seeds[8], (H * HD, D), (max(1, 2 * H * HD // LENGTH)) ** -0.5, 3.0, ((0, 32),), jnp.float32),
        "gate_weight": centred(seeds[9], (D, FF), D ** -0.5, 0.125, ((0, 32),), jnp.float32),
        "up_weight": centred(seeds[10], (D, FF), D ** -0.5, 0.125, ((0, 32),), jnp.float32),
        "down_weight": centred(seeds[11], (FF, D), (FF // 2) ** -0.5, 0.109375, ((0, 32),), jnp.float32),
    }


epsilon = 1e-06
rope_base = 1000000.0
negative = -1e+30

@jax.custom_vjp
def low(v):
    return lax.optimization_barrier(v.astype(jnp.bfloat16)).astype(jnp.float32)

@jax.custom_vjp
def low_back(v):
    return v

def low_keep(v):
    return (low(v), None)

def low_pass(kept, grad):
    return (grad,)

def back_keep(v):
    return (v, None)

def back_low(kept, grad):
    return (low(grad),)
low.defvjp(low_keep, low_pass)
low_back.defvjp(back_keep, back_low)

def matmul(left_side, right_side):
    return jnp.dot(left_side, right_side, precision=lax.Precision.HIGHEST, preferred_element_type=jnp.float32)

def rms_scale(values, gain_vector):
    inverse = lax.rsqrt(lax.optimization_barrier(jnp.mean(values * values, axis=-1, keepdims=True)) + epsilon)
    return values * inverse * gain_vector

def rope_tables(positions, head_width):
    half_width = head_width // 2
    inverse = rope_base ** (-jnp.arange(half_width, dtype=jnp.float32) * 2.0 / head_width)
    angles = positions.astype(jnp.float32)[:, None] * inverse[None, :]
    angles = jnp.concatenate([angles, angles], axis=-1)
    return (jnp.cos(angles)[:, None, :], jnp.sin(angles)[:, None, :])

def rotate(values, cosine_table, sine_table):
    half_width = values.shape[-1] // 2
    turned = jnp.concatenate([-values[..., half_width:], values[..., :half_width]], axis=-1)
    return values * cosine_table + turned * sine_table

def qk_piece(query_raw, key_raw, query_gain, key_gain, cosine_table, sine_table):
    row_count = query_raw.shape[0]
    queries = rms_scale(query_raw.reshape(row_count, H, HD), query_gain)
    keys = rms_scale(key_raw.reshape(row_count, KV, HD), key_gain)
    return (rotate(queries, cosine_table, sine_table), rotate(keys, cosine_table, sine_table))

def attention(queries, keys, values, prefix):
    length = queries.shape[0]
    group_size = H // KV
    block_rows = min(512, length)
    score_scale = HD ** (-0.5)
    key_pos = jnp.arange(length, dtype=jnp.int32)
    blocks = queries.reshape(length // block_rows, block_rows, KV, group_size, HD)
    starts = jnp.arange(length // block_rows, dtype=jnp.int32) * block_rows

    def one_block(block_item):
        query_block, first_row = block_item
        scores = jnp.einsum('tkgd,skd->kgts', query_block, keys, precision=lax.Precision.HIGHEST) * score_scale
        scores = low_back(scores)
        query_pos = first_row + jnp.arange(block_rows, dtype=jnp.int32)
        allowed = key_pos[None, :] <= jnp.maximum(query_pos, prefix - 1)[:, None]
        scores = jnp.where(allowed, scores, negative)
        row_max = lax.optimization_barrier(jnp.max(scores, axis=-1, keepdims=True))
        expanded = jnp.exp(scores - row_max)
        probabilities = low(expanded / lax.optimization_barrier(jnp.sum(expanded, axis=-1, keepdims=True)))
        out_block = jnp.einsum('kgts,skd->tkgd', probabilities, values, precision=lax.Precision.HIGHEST)
        return low_back(out_block)
    outputs = lax.map(jax.checkpoint(one_block), (blocks, starts))
    return outputs.reshape(length, H * HD)

def sequence_forward(hidden, prefix, params):
    norm_gains, query_weight, key_weight, value_weight, head_gate_weight, out_weight, gate_weight, up_weight, down_weight = params
    length = hidden.shape[0]
    gains = low(norm_gains)
    attention_gain = gains[:D]
    swiglu_gain = gains[D:2 * D]
    query_gain = gains[2 * D:2 * D + HD]
    key_gain = gains[2 * D + HD:]
    normed = low(rms_scale(hidden, attention_gain))
    query_raw = low_back(matmul(normed, low(query_weight)))
    key_raw = low_back(matmul(normed, low(key_weight)))
    values = low(low_back(matmul(normed, low(value_weight))))
    gate_raw = low_back(matmul(normed, low(head_gate_weight)))
    cosine_table, sine_table = rope_tables(jnp.arange(length, dtype=jnp.int32), HD)
    queries, keys = qk_piece(query_raw, key_raw, query_gain, key_gain, cosine_table, sine_table)
    attended = attention(low(queries), low(keys), values.reshape(length, KV, HD), prefix)
    gated = (attended.reshape(length, H, HD) * jax.nn.sigmoid(gate_raw)[:, :, None]).reshape(length, H * HD)
    branch = low_back(matmul(low(gated), low(out_weight)))
    middle = hidden + branch
    normed_two = low(rms_scale(middle, swiglu_gain))
    gate_pre = low_back(matmul(normed_two, low(gate_weight)))
    up_pre = low_back(matmul(normed_two, low(up_weight)))
    hidden_ff = low(jax.nn.silu(gate_pre) * up_pre)
    return middle + low_back(matmul(hidden_ff, low(down_weight)))

def reference(hidden_in, out_grad, prefix_len, norm_gains, query_weight, key_weight, value_weight, head_gate_weight, out_weight, gate_weight, up_weight, down_weight):
    weights = (norm_gains, query_weight, key_weight, value_weight, head_gate_weight, out_weight, gate_weight, up_weight, down_weight)
    inputs = hidden_in.astype(jnp.float32).reshape(SEQS, LENGTH, D)
    cotangents = out_grad.astype(jnp.float32).reshape(SEQS, LENGTH, D)

    def one_sequence(totals, seq_entry):
        hidden, cotangent, prefix = seq_entry

        def forward(hidden_value, params):
            return sequence_forward(hidden_value, prefix, params)
        output, pull_back = jax.vjp(forward, hidden, weights)
        grad_hidden, grad_weights = pull_back(cotangent)
        totals = jax.tree.map(lambda first_term, second_term: first_term + second_term, totals, grad_weights)
        return (totals, (output.astype(jnp.bfloat16), grad_hidden.astype(jnp.bfloat16)))
    start_totals = jax.tree.map(jnp.zeros_like, weights)
    totals, (outputs, input_grads) = lax.scan(one_sequence, start_totals, (inputs, cotangents, prefix_len))
    return (outputs.reshape(TOKENS, D), input_grads.reshape(TOKENS, D), totals[0], totals[1], totals[2], totals[3], totals[4], totals[5], totals[6], totals[7], totals[8])
```

```python
from functools import partial

import jax
import jax.numpy as jnp
from jax import lax
from jax.sharding import PartitionSpec as P

H = 16
KV = 8
HD = 128


epsilon = 1e-06
rope_base = 1000000.0
negative = -1e30
low = jnp.bfloat16


def product(left_side, right_side):
    return jnp.dot(left_side, right_side, preferred_element_type=jnp.float32)


def product_nt(left_side, right_side):
    return lax.dot_general(
        left_side, right_side, (((1,), (1,)), ((), ())), preferred_element_type=jnp.float32
    )


def product_tn(left_side, right_side):
    return lax.dot_general(
        left_side, right_side, (((0,), (0,)), ((), ())), preferred_element_type=jnp.float32
    )


def rms_scale(values, gain_vector):
    inverse = lax.rsqrt(jnp.mean(values * values, axis=-1, keepdims=True) + epsilon)
    return values * inverse * gain_vector


def rope_tables(positions, head_width):
    half_width = head_width // 2
    inverse = rope_base ** (-jnp.arange(half_width, dtype=jnp.float32) * 2.0 / head_width)
    angles = positions.astype(jnp.float32)[:, None] * inverse[None, :]
    angles = jnp.concatenate([angles, angles], axis=-1)
    return (jnp.cos(angles)[:, None, :], jnp.sin(angles)[:, None, :])


def rotate(values, cosine_table, sine_table):
    half_width = values.shape[-1] // 2
    turned = jnp.concatenate([-values[..., half_width:], values[..., :half_width]], axis=-1)
    return values * cosine_table + turned * sine_table


def qk_piece(query_raw, key_raw, query_gain, key_gain, cosine_table, sine_table):
    queries = rms_scale(query_raw, query_gain)
    keys = rms_scale(key_raw, key_gain)
    return (rotate(queries, cosine_table, sine_table), rotate(keys, cosine_table, sine_table))


def gate_heads(attended, gate_raw):
    return attended * jax.nn.sigmoid(gate_raw)[:, :, None]


def swiglu(gate_pre, up_pre):
    return jax.nn.silu(gate_pre) * up_pre


def gather_ctx(block):
    return lax.all_gather(block, "ctx", axis=0, tiled=True)


def gather_seq(block):
    return lax.all_gather(block, "seq", axis=0, tiled=True)


def scatter_ctx(block):
    return lax.psum_scatter(block.astype(low), "ctx", scatter_dimension=0, tiled=True).astype(
        jnp.float32
    )


def scatter_seq(block):
    return lax.psum_scatter(block.astype(low), "seq", scatter_dimension=0, tiled=True)


def to_columns(block):
    rows, pieces, width = block.shape
    return lax.all_to_all(block, "ctx", split_axis=1, concat_axis=0, tiled=True).reshape(
        pieces * rows, width
    )


def to_rows(block, pieces):
    rows = block.shape[0] // pieces
    block = block.reshape(pieces * rows, 1, block.shape[1])
    return lax.all_to_all(block, "ctx", split_axis=0, concat_axis=1, tiled=True)


def on_device(
    hidden_in,
    out_grad,
    prefix_len,
    norm_gains,
    query_weight,
    key_weight,
    value_weight,
    head_gate_weight,
    out_weight,
    gate_weight,
    up_weight,
    down_weight,
):
    row_count, model = hidden_in.shape
    groups = lax.axis_size("seq")
    pieces = lax.axis_size("ctx")
    length = row_count * pieces
    weight_rows = query_weight.shape[0]
    heads = H // pieces
    kv_heads = max(1, KV // pieces)
    copies = max(1, pieces // KV)
    per_kv = heads // kv_heads
    ff_block = down_weight.shape[0]
    ff_own = ff_block * groups
    prefix = prefix_len[0]
    q_width, kv_width = heads * HD, kv_heads * HD
    attn_width = -(-(q_width + 2 * kv_width + heads) // 128) * 128

    def kv_columns(weight):
        columns = weight.astype(low).reshape(weight_rows, KV, HD)
        return jnp.repeat(columns, copies, axis=1).reshape(weight_rows, pieces, kv_width)

    def ff_columns(weight):
        columns = weight.astype(low).reshape(weight_rows, groups, pieces, ff_block)
        return columns.transpose(0, 2, 1, 3).reshape(weight_rows, pieces, ff_own)

    attn_rows = jnp.concatenate(
        [
            query_weight.astype(low).reshape(weight_rows, pieces, q_width),
            kv_columns(key_weight),
            kv_columns(value_weight),
            head_gate_weight.astype(low).reshape(weight_rows, pieces, heads),
            jnp.zeros(
                (weight_rows, pieces, attn_width - q_width - 2 * kv_width - heads), low
            ),
        ],
        axis=-1,
    )
    attn_low = gather_seq(to_columns(attn_rows))
    ff_rows = jnp.concatenate([ff_columns(gate_weight), ff_columns(up_weight)], axis=-1)
    ff_low = gather_seq(to_columns(ff_rows))
    down_low = gather_seq(down_weight.astype(low))
    spread = [(i, (i % groups) * pieces + i // groups) for i in range(groups * pieces)]
    collect = [(target, source) for source, target in spread]
    out_low = gather_seq(lax.ppermute(out_weight.astype(low), ("seq", "ctx"), spread))
    gains_full = lax.all_gather(
        norm_gains.astype(low), ("seq", "ctx"), axis=0, tiled=True
    ).astype(jnp.float32)
    attention_gain = gains_full[:model]
    swiglu_gain = gains_full[model : 2 * model]
    query_gain = gains_full[2 * model : 2 * model + HD]
    key_gain = gains_full[2 * model + HD :]

    residual_in = hidden_in.astype(jnp.float32)
    normed_local, pull_norm_one = jax.vjp(rms_scale, residual_in, attention_gain)
    normed = gather_ctx(normed_local.astype(low))
    out_grad_all = gather_ctx(out_grad)
    raw = product(normed, attn_low)
    query_raw = raw[:, :q_width].reshape(length, heads, HD)
    key_raw = raw[:, q_width : q_width + kv_width].reshape(length, kv_heads, HD)
    values = raw[:, q_width + kv_width : q_width + 2 * kv_width].astype(low)
    values = values.reshape(length, kv_heads, HD)
    gate_raw = raw[:, q_width + 2 * kv_width : q_width + 2 * kv_width + heads]
    positions = jnp.arange(length, dtype=jnp.int32)
    cosine_table, sine_table = rope_tables(positions, HD)
    (queries_full, keys_full), pull_rope = jax.vjp(
        partial(qk_piece, cosine_table=cosine_table, sine_table=sine_table),
        query_raw,
        key_raw,
        query_gain,
        key_gain,
    )
    queries = queries_full.astype(low).reshape(length, kv_heads, per_kv, HD)
    keys = keys_full.astype(low)
    limits = jnp.maximum(positions, prefix - 1)
    allowed = positions[None, :] <= limits[:, None]
    score_scale = HD ** (-0.5)
    scores = (
        jnp.einsum("tkgd,skd->kgts", queries, keys, preferred_element_type=jnp.float32)
        * score_scale
    )
    scores = jnp.where(allowed, scores, negative)
    row_max = jnp.max(scores, axis=-1, keepdims=True)
    expanded = jnp.exp(scores - row_max)
    row_sum = jnp.sum(expanded, axis=-1, keepdims=True)
    log_norm = row_max + jnp.log(row_sum)
    attended = (
        jnp.einsum("kgts,skd->kgtd", expanded.astype(low), values, preferred_element_type=jnp.float32)
        / row_sum
    )
    attended_rows = attended.transpose(2, 0, 1, 3).reshape(length, heads, HD)
    gated_full, pull_gate = jax.vjp(gate_heads, attended_rows, gate_raw)
    gated = gated_full.astype(low).reshape(length, q_width)
    middle = residual_in + scatter_ctx(product(gated, out_low))

    normed_two_local, pull_norm_two = jax.vjp(rms_scale, middle, swiglu_gain)
    normed_two = gather_ctx(normed_two_local.astype(low))
    pre = product(normed_two, ff_low)
    gate_pre, up_pre = pre[:, :ff_own], pre[:, ff_own:]
    hidden_ff_full, pull_swiglu = jax.vjp(swiglu, gate_pre, up_pre)
    hidden_ff = hidden_ff_full.astype(low)
    hidden_out = (middle + scatter_ctx(product(hidden_ff, down_low))).astype(low)

    grad_hidden_ff = product_nt(out_grad_all, down_low)
    grad_gate_full, grad_up_full = pull_swiglu(grad_hidden_ff)
    grad_pre = jnp.concatenate([grad_gate_full.astype(low), grad_up_full.astype(low)], axis=-1)
    grad_normed_two = scatter_ctx(product_nt(grad_pre, ff_low))
    down_share = scatter_seq(product_tn(hidden_ff, out_grad_all)).astype(jnp.float32)
    ff_share = to_rows(scatter_seq(product_tn(normed_two, grad_pre)), pieces).astype(jnp.float32)

    def ff_back(columns):
        columns = columns.reshape(weight_rows, pieces, groups, ff_block)
        return columns.transpose(0, 2, 1, 3).reshape(weight_rows, groups * pieces * ff_block)

    gate_share = ff_back(ff_share[:, :, :ff_own])
    up_share = ff_back(ff_share[:, :, ff_own:])

    grad_middle_part, swiglu_gain_grad = pull_norm_two(grad_normed_two)
    grad_middle = out_grad.astype(jnp.float32) + grad_middle_part
    grad_branch = gather_ctx(grad_middle.astype(low))
    grad_gated = product_nt(grad_branch, out_low).reshape(length, heads, HD)
    output_share = lax.ppermute(
        scatter_seq(product_tn(gated, grad_branch)), ("seq", "ctx"), collect
    ).astype(jnp.float32)
    grad_attended_full, grad_gate_raw_full = pull_gate(grad_gated)
    grad_attended = grad_attended_full.astype(low)
    grad_heads = grad_attended.reshape(length, kv_heads, per_kv, HD).transpose(1, 2, 0, 3)
    row_delta = jnp.sum(grad_heads.astype(jnp.float32) * attended, axis=-1, keepdims=True)
    probabilities = jnp.exp(scores - log_norm)
    prob_grad = jnp.einsum(
        "kgtd,skd->kgts", grad_heads, values, preferred_element_type=jnp.float32
    )
    score_grad = (probabilities * (prob_grad - row_delta)).astype(low)
    grad_queries = (
        jnp.einsum("kgts,skd->tkgd", score_grad, keys, preferred_element_type=jnp.float32)
        * score_scale
    )
    grad_keys = (
        jnp.einsum("kgts,tkgd->skd", score_grad, queries, preferred_element_type=jnp.float32)
        * score_scale
    )
    grad_values = jnp.einsum(
        "kgts,kgtd->skd", probabilities.astype(low), grad_heads, preferred_element_type=jnp.float32
    )
    grad_query_full, grad_key_full, query_gain_grad, key_gain_grad = pull_rope(
        (grad_queries.reshape(length, heads, HD), grad_keys)
    )
    grad_raw = jnp.concatenate(
        [
            grad_query_full.reshape(length, q_width).astype(low),
            grad_key_full.reshape(length, kv_width).astype(low),
            grad_values.reshape(length, kv_width).astype(low),
            grad_gate_raw_full.astype(low),
            jnp.zeros((length, attn_width - q_width - 2 * kv_width - heads), low),
        ],
        axis=-1,
    )
    grad_normed = scatter_ctx(product_nt(grad_raw, attn_low))
    attn_share = to_rows(scatter_seq(product_tn(normed, grad_raw)), pieces).astype(jnp.float32)

    def kv_back(columns):
        columns = columns.reshape(weight_rows, KV, copies, HD)
        return columns.sum(axis=2).reshape(weight_rows, KV * HD)

    query_share = attn_share[:, :, :q_width].reshape(weight_rows, H * HD)
    key_share = kv_back(attn_share[:, :, q_width : q_width + kv_width])
    value_share = kv_back(attn_share[:, :, q_width + kv_width : q_width + 2 * kv_width])
    head_share = attn_share[
        :, :, q_width + 2 * kv_width : q_width + 2 * kv_width + heads
    ].reshape(weight_rows, H)
    grad_input_part, attention_gain_grad = pull_norm_one(grad_normed)
    hidden_grad = (grad_middle + grad_input_part).astype(low)
    gains_term = jnp.concatenate(
        [attention_gain_grad, swiglu_gain_grad, query_gain_grad, key_gain_grad]
    )
    gains_share = lax.psum_scatter(gains_term, ("seq", "ctx"), scatter_dimension=0, tiled=True)
    return (
        hidden_out,
        hidden_grad,
        gains_share,
        query_share,
        key_share,
        value_share,
        head_share,
        output_share,
        gate_share,
        up_share,
        down_share,
    )


def solution(mesh):
    rows = P(("seq", "ctx"), None)
    return jax.shard_map(
        on_device,
        mesh=mesh,
        in_specs=(rows, rows, P("seq"), P(("seq", "ctx"))) + (rows,) * 8,
        out_specs=(rows, rows, P(("seq", "ctx"))) + (rows,) * 8,
        check_vma=False,
    )
```

```python
import functools

import jax
import jax.numpy as jnp
from jax import lax
from jax.experimental import pallas as pl
from jax.experimental.pallas import tpu as pltpu
from jax.sharding import PartitionSpec as P

H = 16
KV = 8
HD = 128


epsilon = 1e-06
rope_base = 1000000.0
negative = -1e30
low = jnp.bfloat16
full = jnp.float32
MESH = pl.DeviceIdType.MESH
ANY = pl.BlockSpec(memory_space=pl.ANY)
IN_VMEM = pl.BlockSpec(memory_space=pltpu.VMEM)
DMA = pltpu.SemaphoreType.DMA
GAIN_COLUMNS = 3


def product(left_side, right_side):
    return jnp.dot(left_side, right_side, preferred_element_type=full)


def product_nt(left_side, right_side):
    return lax.dot_general(
        left_side, right_side, (((1,), (1,)), ((), ())), preferred_element_type=full
    )


def product_tn(left_side, right_side):
    return lax.dot_general(
        left_side, right_side, (((0,), (0,)), ((), ())), preferred_element_type=full
    )


def rms_scale(values, gain_vector):
    inverse = lax.rsqrt(jnp.mean(values * values, axis=-1, keepdims=True) + epsilon)
    return values * inverse * gain_vector


def rms_scale_back(values, gain_vector, grad):
    inverse = lax.rsqrt(jnp.mean(values * values, axis=-1, keepdims=True) + epsilon)
    scaled = grad * gain_vector
    return inverse * scaled - values * (
        inverse * inverse * inverse * jnp.mean(scaled * values, axis=-1, keepdims=True)
    )


def rope_tables(positions, head_width):
    half_width = head_width // 2
    inverse = rope_base ** (-jnp.arange(half_width, dtype=full) * 2.0 / head_width)
    angles = positions.astype(full)[:, None] * inverse[None, :]
    angles = jnp.concatenate([angles, angles], axis=-1)
    return (jnp.cos(angles)[:, None, :], jnp.sin(angles)[:, None, :])


def rotate(values, cosine_table, sine_table):
    half_width = values.shape[-1] // 2
    turned = jnp.concatenate([-values[..., half_width:], values[..., :half_width]], axis=-1)
    return values * cosine_table + turned * sine_table


def qk_piece(query_raw, key_raw, query_gain, key_gain, cosine_table, sine_table):
    queries = rms_scale(query_raw, query_gain)
    keys = rms_scale(key_raw, key_gain)
    return (rotate(queries, cosine_table, sine_table), rotate(keys, cosine_table, sine_table))


def gate_heads(attended, gate_raw):
    return attended * jax.nn.sigmoid(gate_raw)[:, :, None]


def swiglu(gate_pre, up_pre):
    return jax.nn.silu(gate_pre) * up_pre


def remote(source, target, send, receive, axis, peer):
    return pltpu.make_async_remote_copy(
        src_ref=source,
        dst_ref=target,
        send_sem=send,
        recv_sem=receive,
        device_id={axis: peer},
        device_id_type=MESH,
    )


def greet(peers):
    barrier = pltpu.get_barrier_semaphore()
    for axis, peer, exists in peers:
        if exists is True:
            pl.semaphore_signal(barrier, inc=1, device_id={axis: peer}, device_id_type=MESH)
        else:

            @pl.when(exists)
            def _():
                pl.semaphore_signal(barrier, inc=1, device_id={axis: peer}, device_id_type=MESH)

    arrivals = sum(1 for _, _, exists in peers if exists is True)
    for _, _, exists in peers:
        if exists is not True:
            arrivals = arrivals + exists.astype(jnp.int32)
    pl.semaphore_wait(barrier, arrivals)


def others(axis, count):
    me = lax.axis_index(axis)
    return [(axis, lax.rem(me + shift, count), True) for shift in range(1, count)]


class Line:
    def __init__(self, pieces):
        self.chips = pieces // 2
        self.me = lax.axis_index("ctx")
        self.chip, self.core = self.me // 2, lax.rem(self.me, 2)
        self.sibling = self.me + 1 - 2 * self.core
        self.right, self.left = self.me + 2, self.me - 2
        self.has_right, self.has_left = self.chip < self.chips - 1, self.chip > 0

    def peers(self):
        return [
            ("ctx", self.sibling, True),
            ("ctx", self.right, self.has_right),
            ("ctx", self.left, self.has_left),
        ]


def gather_scratch(pieces, parts):
    chips = pieces // 2
    return [DMA((chips, 2, parts))] * 2 + [DMA((chips, parts))] * 4


class Gather:
    def __init__(self, line, parts, rows, out_ref, sems):
        self.line, self.parts, self.rows, self.out_ref = line, parts, rows, out_ref
        self.size = rows // parts
        self.sib_send, self.sib_recv, self.r_send, self.r_recv, self.l_send, self.l_recv = sems

    def at(self, position, part):
        start = pl.multiple_of(position * self.rows + part * self.size, self.size)
        return self.out_ref.at[pl.ds(start, self.size)]

    def to_sibling(self, source, hop, side, part, position):
        return remote(
            source,
            self.at(position, part),
            self.sib_send.at[hop, side, part],
            self.sib_recv.at[hop, side, part],
            "ctx",
            self.line.sibling,
        )

    def to_right(self, source, hop, part, position):
        return remote(
            source,
            self.at(position, part),
            self.r_send.at[hop, part],
            self.r_recv.at[hop, part],
            "ctx",
            self.line.right,
        )

    def to_left(self, source, hop, part, position):
        return remote(
            source,
            self.at(position, part),
            self.l_send.at[hop, part],
            self.l_recv.at[hop, part],
            "ctx",
            self.line.left,
        )

    def start(self, x_ref):
        line = self.line
        for part in range(self.parts):
            piece = x_ref.at[pl.ds(part * self.size, self.size)]

            @pl.when(line.has_right)
            def _():
                self.to_right(piece, 0, part, line.me).start()

            @pl.when(line.has_left)
            def _():
                self.to_left(piece, 0, part, line.me).start()

            self.to_sibling(piece, 0, 0, part, line.me).start()

    def forward(self, hop):
        line = self.line
        for part in range(self.parts):
            from_left, from_right = line.me - 2 * hop, line.me + 2 * hop

            @pl.when(line.chip - hop >= 0)
            def _():
                piece = self.at(from_left, part)
                self.to_right(piece, hop - 1, part, from_left).wait_recv()

                @pl.when(line.has_right)
                def _():
                    self.to_right(piece, hop, part, from_left).start()

                self.to_sibling(piece, hop, 0, part, from_left).start()

            @pl.when(line.chip + hop < line.chips)
            def _():
                piece = self.at(from_right, part)
                self.to_left(piece, hop - 1, part, from_right).wait_recv()

                @pl.when(line.has_left)
                def _():
                    self.to_left(piece, hop, part, from_right).start()

                self.to_sibling(piece, hop, 1, part, from_right).start()

    def finish(self):
        line = self.line
        for hop in range(line.chips):
            for part in range(self.parts):
                for side in range(1 if hop == 0 else 2):
                    there = (line.chip - hop >= 0) if side == 0 else (line.chip + hop < line.chips)
                    position = (line.me - 2 * hop) if side == 0 else (line.me + 2 * hop)

                    @pl.when(there)
                    def _():
                        piece = self.at(position, part)
                        copy = self.to_sibling(piece, hop, side, part, position)
                        copy.wait_recv()
                        copy.wait_send()
                        if side == 0:

                            @pl.when(line.has_right)
                            def _():
                                self.to_right(piece, hop, part, position).wait_send()

                        if side == 1 or hop == 0:

                            @pl.when(line.has_left)
                            def _():
                                self.to_left(piece, hop, part, position).wait_send()


def gather_kernel(pieces, parts, x_ref, out_ref, own_sem, *sems):
    line = Line(pieces)
    greet(line.peers())
    rows = x_ref.shape[0]
    gather = Gather(line, parts, rows, out_ref, sems)
    gather.start(x_ref)
    start = pl.multiple_of(line.me * rows, rows)
    own = pltpu.make_async_copy(x_ref, out_ref.at[pl.ds(start, rows)], own_sem)
    own.start()
    for hop in range(1, line.chips):
        gather.forward(hop)
    own.wait()
    gather.finish()


def gather_ctx(x, number, parts=2):
    pieces = lax.axis_size("ctx")
    return pl.pallas_call(
        functools.partial(gather_kernel, pieces, parts),
        out_shape=jax.ShapeDtypeStruct((pieces * x.shape[0],) + x.shape[1:], x.dtype),
        in_specs=[IN_VMEM],
        out_specs=ANY,
        scratch_shapes=[DMA] + gather_scratch(pieces, parts),
        compiler_params=pltpu.CompilerParams(collective_id=number, has_side_effects=True),
        name=f"gather_rows_{number}",
    )(x)


def scatter_scratch(pieces, rows, width):
    chips = pieces // 2
    slots = pltpu.VMEM((chips, rows, width), low)
    return [slots, slots, pltpu.VMEM((2, chips, rows, width), low), slots, slots] + [
        DMA((2, chips))
    ] * 2 + [DMA((chips,))] * 4


class Scatter:
    def __init__(self, line, p_ref, rows, scratch):
        self.line, self.p_ref, self.rows = line, p_ref, rows
        (
            self.stage_r,
            self.stage_l,
            self.sib,
            self.in_r,
            self.in_l,
            self.sib_send,
            self.sib_recv,
            self.r_send,
            self.r_recv,
            self.l_send,
            self.l_recv,
        ) = scratch

    def block(self, chip, core):
        start = pl.multiple_of((chip * 2 + core) * self.rows, self.rows)
        return self.p_ref.at[pl.ds(start, self.rows)]

    def there(self, far, side):
        line = self.line
        return (line.chip + far < line.chips) if side == 0 else (line.chip - far >= 0)

    def target(self, far, side):
        return self.line.chip + far if side == 0 else self.line.chip - far

    def exchange(self, far, side):
        return remote(
            self.block(self.target(far, side), 1 - self.line.core),
            self.sib.at[side, far],
            self.sib_send.at[side, far],
            self.sib_recv.at[side, far],
            "ctx",
            self.line.sibling,
        )

    def send(self, far, side):
        if side == 0:
            return remote(
                self.stage_r.at[far],
                self.in_r.at[far - 1],
                self.r_send.at[far],
                self.r_recv.at[far - 1],
                "ctx",
                self.line.right,
            )
        return remote(
            self.stage_l.at[far],
            self.in_l.at[far - 1],
            self.l_send.at[far],
            self.l_recv.at[far - 1],
            "ctx",
            self.line.left,
        )

    def order(self):
        return [
            (far, side)
            for far in range(self.line.chips - 1, -1, -1)
            for side in range(2 if far else 1)
        ]

    def swap(self, far, side):
        @pl.when(self.there(far, side))
        def _():
            self.exchange(far, side).start()

    def push(self, far, side):
        line = self.line
        stage, arrived = (self.stage_r, self.in_r) if side == 0 else (self.stage_l, self.in_l)
        behind = line.has_left if side == 0 else line.has_right

        @pl.when(self.there(far, side))
        def _():
            self.exchange(far, side).wait_recv()
            own = self.block(self.target(far, side), line.core)
            if far == line.chips - 1:
                stage[far] = (own[...].astype(full) + self.sib[side, far].astype(full)).astype(low)
            else:

                @pl.when(behind)
                def _():
                    self.send(far + 1, side).wait_recv()
                    stage[far] = (
                        own[...].astype(full)
                        + self.sib[side, far].astype(full)
                        + arrived[far].astype(full)
                    ).astype(low)

                @pl.when(jnp.logical_not(behind))
                def _():
                    stage[far] = (
                        own[...].astype(full) + self.sib[side, far].astype(full)
                    ).astype(low)

            self.send(far, side).start()

    def total(self, total_ref):
        line = self.line
        self.exchange(0, 0).wait_recv()
        total_ref[...] = self.block(line.chip, line.core)[...].astype(full) + self.sib[
            0, 0
        ].astype(full)

        @pl.when(line.has_left)
        def _():
            self.send(1, 0).wait_recv()
            total_ref[...] += self.in_r[0].astype(full)

        @pl.when(line.has_right)
        def _():
            self.send(1, 1).wait_recv()
            total_ref[...] += self.in_l[0].astype(full)

    def finish(self):
        for far, side in self.order():

            @pl.when(self.there(far, side))
            def _():
                self.exchange(far, side).wait_send()
                if far > 0:
                    self.send(far, side).wait_send()


def scatter_kernel(pieces, p_ref, out_ref, *scratch):
    line = Line(pieces)
    greet(line.peers())
    scatter = Scatter(line, p_ref, out_ref.shape[0], scratch)
    for far, side in scatter.order():
        scatter.swap(far, side)
    for far, side in scatter.order():
        if far > 0:
            scatter.push(far, side)
    scatter.total(out_ref)
    scatter.finish()


def scatter_ctx(p, number):
    pieces = lax.axis_size("ctx")
    rows, width = p.shape[0] // pieces, p.shape[1]
    return pl.pallas_call(
        functools.partial(scatter_kernel, pieces),
        out_shape=jax.ShapeDtypeStruct((rows, width), full),
        in_specs=[IN_VMEM],
        out_specs=IN_VMEM,
        scratch_shapes=scatter_scratch(pieces, rows, width),
        compiler_params=pltpu.CompilerParams(
            collective_id=number, has_side_effects=True, vmem_limit_bytes=60 << 20
        ),
        name=f"scatter_rows_{number}",
    )(p.astype(low))


class Swap:
    def __init__(self, pieces, send_of, recv_of, send_sem, recv_sem):
        self.pieces, self.me = pieces, lax.axis_index("ctx")
        self.send_of, self.recv_of = send_of, recv_of
        self.send_sem, self.recv_sem = send_sem, recv_sem

    def copy(self, shift):
        peer = lax.rem(self.me + shift, self.pieces)
        return remote(
            self.send_of(peer),
            self.recv_of(self.me),
            self.send_sem.at[shift],
            self.recv_sem.at[shift],
            "ctx",
            peer,
        )

    def start(self):
        for shift in range(1, self.pieces):
            self.copy(shift).start()

    def wait_recv(self, shift):
        source = lax.rem(self.me + self.pieces - shift, self.pieces)
        remote(
            self.send_of(source),
            self.recv_of(source),
            self.send_sem.at[shift],
            self.recv_sem.at[shift],
            "ctx",
            source,
        ).wait_recv()
        return source

    def finish(self):
        for shift in range(1, self.pieces):
            self.copy(shift).wait_send()


def ff_columns_kernel(pieces, groups, block, gate_ref, up_ref, out_ref, send, own_sem, s_sem, r_sem):
    greet(others("ctx", pieces))
    me = lax.axis_index("ctx")
    own_width = groups * block
    for half, weight_ref in enumerate((gate_ref, up_ref)):
        for group in range(groups):
            for piece in range(pieces):
                start = (group * pieces + piece) * block
                send[piece, :, pl.ds(half * own_width + group * block, block)] = weight_ref[
                    :, pl.ds(start, block)
                ].astype(low)
    swap = Swap(pieces, lambda peer: send.at[peer], lambda peer: out_ref.at[peer], s_sem, r_sem)
    swap.start()
    own = pltpu.make_async_copy(send.at[me], out_ref.at[me], own_sem)
    own.start()
    for shift in range(1, pieces):
        swap.wait_recv(shift)
    own.wait()
    swap.finish()


def ff_columns(gate_weight, up_weight, block, number):
    pieces, groups = lax.axis_size("ctx"), lax.axis_size("seq")
    rows = gate_weight.shape[0]
    shape = (pieces, rows, 2 * groups * block)
    return pl.pallas_call(
        functools.partial(ff_columns_kernel, pieces, groups, block),
        out_shape=jax.ShapeDtypeStruct(shape, low),
        in_specs=[IN_VMEM, IN_VMEM],
        out_specs=ANY,
        scratch_shapes=[pltpu.VMEM(shape, low), DMA, DMA((pieces,)), DMA((pieces,))],
        compiler_params=pltpu.CompilerParams(
            collective_id=number, has_side_effects=True, vmem_limit_bytes=60 << 20
        ),
        name=f"ff_columns_{number}",
    )(gate_weight, up_weight)


def ff_rows_kernel(pieces, groups, block, x_ref, gate_ref, up_ref, recv, s_sem, r_sem):
    greet(others("ctx", pieces))
    me = lax.axis_index("ctx")
    swap = Swap(pieces, lambda peer: x_ref.at[peer], lambda peer: recv.at[peer], s_sem, r_sem)
    swap.start()
    recv[me] = x_ref[me]
    for shift in range(1, pieces):
        swap.wait_recv(shift)
    own_width = groups * block
    for half, grad_ref in enumerate((gate_ref, up_ref)):
        for group in range(groups):
            for piece in range(pieces):
                start = (group * pieces + piece) * block
                grad_ref[:, pl.ds(start, block)] = recv[
                    piece, :, pl.ds(half * own_width + group * block, block)
                ].astype(full)
    swap.finish()


def ff_rows(x, block, number):
    pieces, groups = lax.axis_size("ctx"), lax.axis_size("seq")
    rows = x.shape[1]
    grad = jax.ShapeDtypeStruct((rows, pieces * groups * block), full)
    return pl.pallas_call(
        functools.partial(ff_rows_kernel, pieces, groups, block),
        out_shape=(grad, grad),
        in_specs=[IN_VMEM],
        out_specs=(IN_VMEM, IN_VMEM),
        scratch_shapes=[pltpu.VMEM(x.shape, low), DMA((pieces,)), DMA((pieces,))],
        compiler_params=pltpu.CompilerParams(
            collective_id=number, has_side_effects=True, vmem_limit_bytes=60 << 20
        ),
        name=f"ff_rows_{number}",
    )(x)


def attn_rows_kernel(pieces, x_ref, out_ref, s_sem, r_sem):
    greet(others("ctx", pieces))
    me = lax.axis_index("ctx")
    swap = Swap(pieces, lambda peer: x_ref.at[peer], lambda peer: out_ref.at[peer], s_sem, r_sem)
    swap.start()
    out_ref[me] = x_ref[me]
    for shift in range(1, pieces):
        swap.wait_recv(shift)
    swap.finish()


def attn_rows(x, number):
    pieces = lax.axis_size("ctx")
    return pl.pallas_call(
        functools.partial(attn_rows_kernel, pieces),
        out_shape=jax.ShapeDtypeStruct(x.shape, low),
        in_specs=[IN_VMEM],
        out_specs=IN_VMEM,
        scratch_shapes=[DMA((pieces,)), DMA((pieces,))],
        compiler_params=pltpu.CompilerParams(
            collective_id=number, has_side_effects=True, vmem_limit_bytes=60 << 20
        ),
        name=f"attn_rows_{number}",
    )(x)


def opening_kernel(
    pieces,
    groups,
    parts,
    hidden_ref,
    gains_ref,
    attn_ref,
    normed_ref,
    attn_out,
    gains_out,
    gains_row,
    gains_all,
    gain_vector,
    normed,
    own_sem,
    own_attn,
    ga_send,
    ga_recv,
    gs_send,
    gs_recv,
    at_send,
    at_recv,
    as_send,
    as_recv,
    *sems,
):
    line = Line(pieces)
    me, group = line.me, lax.axis_index("seq")
    greet(others("ctx", pieces) + others("seq", groups))
    rows, model = hidden_ref.shape
    gain_count = gains_ref.shape[1]
    gains_row[...] = jnp.zeros(gains_row.shape, full)
    gains_row[0:1, pl.ds(0, gain_count)] = gains_ref[...].astype(low).astype(full)
    gains_all[group, me] = gains_row[...]
    gain_swap = Swap(
        pieces, lambda peer: gains_row, lambda peer: gains_all.at[group, peer], ga_send, ga_recv
    )
    gain_swap.start()
    attn_swap = Swap(
        pieces, lambda peer: attn_ref.at[peer], lambda peer: attn_out.at[group, peer], at_send, at_recv
    )
    attn_swap.start()
    attn_own = pltpu.make_async_copy(attn_ref.at[me], attn_out.at[group, me], own_attn)
    attn_own.start()
    values = hidden_ref[...].astype(full)
    inverse = lax.rsqrt(jnp.mean(values * values, axis=-1, keepdims=True) + epsilon)

    def to_groups(ref, sends, receives, shift):
        peer = lax.rem(group + shift, groups)
        return remote(ref.at[group], ref.at[group], sends.at[shift], receives.at[shift], "seq", peer)

    def from_groups(ref, sends, receives, shift):
        peer = lax.rem(group + groups - shift, groups)
        remote(
            ref.at[peer], ref.at[peer], sends.at[shift], receives.at[shift], "seq", peer
        ).wait_recv()

    for shift in range(1, pieces):
        gain_swap.wait_recv(shift)
    for shift in range(1, groups):
        to_groups(gains_all, gs_send, gs_recv, shift).start()
    for shift in range(1, groups):
        from_groups(gains_all, gs_send, gs_recv, shift)
    for index in range(groups * pieces):
        gain_vector[0:1, pl.ds(index * gain_count, gain_count)] = gains_all[
            index // pieces, index % pieces, 0:1, pl.ds(0, gain_count)
        ]
    gains_out[...] = gain_vector[...]
    normed[...] = (values * inverse * gain_vector[0:1, pl.ds(0, model)]).astype(low)
    gather = Gather(line, parts, rows, normed_ref, sems)
    gather.start(normed)
    start = pl.multiple_of(me * rows, rows)
    own = pltpu.make_async_copy(normed, normed_ref.at[pl.ds(start, rows)], own_sem)
    own.start()
    for shift in range(1, pieces):
        attn_swap.wait_recv(shift)
    attn_own.wait()
    for shift in range(1, groups):
        to_groups(attn_out, as_send, as_recv, shift).start()
    for hop in range(1, line.chips):
        gather.forward(hop)
    own.wait()
    gather.finish()
    for shift in range(1, groups):
        from_groups(attn_out, as_send, as_recv, shift)
    gain_swap.finish()
    attn_swap.finish()
    for shift in range(1, groups):
        to_groups(gains_all, gs_send, gs_recv, shift).wait_send()
        to_groups(attn_out, as_send, as_recv, shift).wait_send()


def opening(hidden_in, norm_gains, attn_blocks, number, parts=2):
    pieces, groups = lax.axis_size("ctx"), lax.axis_size("seq")
    rows, model = hidden_in.shape
    gains = norm_gains.shape[0]
    lanes = -(-gains // 128) * 128
    return pl.pallas_call(
        functools.partial(opening_kernel, pieces, groups, parts),
        out_shape=(
            jax.ShapeDtypeStruct((pieces * rows, model), low),
            jax.ShapeDtypeStruct((groups,) + attn_blocks.shape, low),
            jax.ShapeDtypeStruct((1, groups * pieces * gains), full),
        ),
        in_specs=[IN_VMEM, IN_VMEM, IN_VMEM],
        out_specs=(ANY, ANY, IN_VMEM),
        scratch_shapes=[
            pltpu.VMEM((8, lanes), full),
            pltpu.VMEM((groups, pieces, 8, lanes), full),
            pltpu.VMEM((1, groups * pieces * gains), full),
            pltpu.VMEM((rows, model), low),
            DMA,
            DMA,
            DMA((pieces,)),
            DMA((pieces,)),
            DMA((groups,)),
            DMA((groups,)),
            DMA((pieces,)),
            DMA((pieces,)),
            DMA((groups,)),
            DMA((groups,)),
        ]
        + gather_scratch(pieces, parts),
        compiler_params=pltpu.CompilerParams(
            collective_id=number, has_side_effects=True, vmem_limit_bytes=60 << 20
        ),
        name=f"opening_{number}",
    )(hidden_in, norm_gains.reshape(1, gains), attn_blocks)


def gather_seq(block):
    return lax.all_gather(block, "seq", axis=0, tiled=True)


def scatter_seq(block):
    return lax.psum_scatter(block.astype(low), "seq", scatter_dimension=0, tiled=True)


def on_device(
    hidden_in,
    out_grad,
    prefix_len,
    norm_gains,
    query_weight,
    key_weight,
    value_weight,
    head_gate_weight,
    out_weight,
    gate_weight,
    up_weight,
    down_weight,
):
    row_count, model = hidden_in.shape
    groups = lax.axis_size("seq")
    pieces = lax.axis_size("ctx")
    length = row_count * pieces
    weight_rows = query_weight.shape[0]
    heads = H // pieces
    kv_heads = max(1, KV // pieces)
    copies = max(1, pieces // KV)
    per_kv = heads // kv_heads
    ff_block = down_weight.shape[0]
    ff_own = ff_block * groups
    prefix = prefix_len[0]
    q_width, kv_width = heads * HD, kv_heads * HD
    gain_count = norm_gains.shape[0]
    gain_columns = -(-gain_count // weight_rows)
    used = q_width + 2 * kv_width + heads
    attn_width = -(-(used + gain_columns) // 128) * 128

    def kv_columns(weight):
        columns = weight.astype(low).reshape(weight_rows, KV, HD)
        return jnp.repeat(columns, copies, axis=1).reshape(weight_rows, pieces, kv_width)

    attn_blocks = jnp.concatenate(
        [
            query_weight.astype(low).reshape(weight_rows, pieces, q_width),
            kv_columns(key_weight),
            kv_columns(value_weight),
            head_gate_weight.astype(low).reshape(weight_rows, pieces, heads),
            jnp.zeros((weight_rows, pieces, attn_width - used), low),
        ],
        axis=-1,
    ).transpose(1, 0, 2)
    normed, attn_low, gains_full = opening(hidden_in, norm_gains, attn_blocks, 0)
    attn_low = attn_low.reshape(model, attn_width)
    gains_full = gains_full.reshape(-1)
    ff_low = gather_seq(
        ff_columns(gate_weight, up_weight, ff_block, 1).reshape(pieces * weight_rows, 2 * ff_own)
    )
    down_low = gather_seq(down_weight.astype(low))
    spread = [(i, (i % groups) * pieces + i // groups) for i in range(groups * pieces)]
    collect = [(target, source) for source, target in spread]
    out_low = gather_seq(lax.ppermute(out_weight.astype(low), ("seq", "ctx"), spread))
    attention_gain = gains_full[:model]
    swiglu_gain = gains_full[model : 2 * model]
    query_gain = gains_full[2 * model : 2 * model + HD]
    key_gain = gains_full[2 * model + HD :]

    residual_in = hidden_in.astype(full)
    out_grad_all = gather_ctx(out_grad, 2)
    raw = product(normed, attn_low)
    query_raw = raw[:, :q_width].reshape(length, heads, HD)
    key_raw = raw[:, q_width : q_width + kv_width].reshape(length, kv_heads, HD)
    values = raw[:, q_width + kv_width : q_width + 2 * kv_width].astype(low)
    values = values.reshape(length, kv_heads, HD)
    gate_raw = raw[:, q_width + 2 * kv_width : used]
    positions = jnp.arange(length, dtype=jnp.int32)
    cosine_table, sine_table = rope_tables(positions, HD)
    (queries_full, keys_full), pull_rope = jax.vjp(
        functools.partial(qk_piece, cosine_table=cosine_table, sine_table=sine_table),
        query_raw,
        key_raw,
        query_gain,
        key_gain,
    )
    queries = queries_full.astype(low).reshape(length, kv_heads, per_kv, HD)
    keys = keys_full.astype(low)
    limits = jnp.maximum(positions, prefix - 1)
    allowed = positions[None, :] <= limits[:, None]
    score_scale = HD ** (-0.5)
    scores = (
        jnp.einsum("tkgd,skd->kgts", queries, keys, preferred_element_type=full) * score_scale
    )
    scores = jnp.where(allowed, scores, negative)
    row_max = jnp.max(scores, axis=-1, keepdims=True)
    expanded = jnp.exp(scores - row_max)
    row_sum = jnp.sum(expanded, axis=-1, keepdims=True)
    log_norm = row_max + jnp.log(row_sum)
    attended = (
        jnp.einsum("kgts,skd->kgtd", expanded.astype(low), values, preferred_element_type=full)
        / row_sum
    )
    attended_rows = attended.transpose(2, 0, 1, 3).reshape(length, heads, HD)
    gated_full, pull_gate = jax.vjp(gate_heads, attended_rows, gate_raw)
    gated = gated_full.astype(low).reshape(length, q_width)
    middle = residual_in + scatter_ctx(product(gated, out_low), 3)

    normed_two = gather_ctx(rms_scale(middle, swiglu_gain).astype(low), 4)
    pre = product(normed_two, ff_low)
    gate_pre, up_pre = pre[:, :ff_own], pre[:, ff_own:]
    hidden_ff_full, pull_swiglu = jax.vjp(swiglu, gate_pre, up_pre)
    hidden_ff = hidden_ff_full.astype(low)

    grad_hidden_ff = product_nt(out_grad_all, down_low)
    grad_gate_full, grad_up_full = pull_swiglu(grad_hidden_ff)
    grad_pre = jnp.concatenate([grad_gate_full.astype(low), grad_up_full.astype(low)], axis=-1)
    grad_normed_two = scatter_ctx(product_nt(grad_pre, ff_low), 5)
    ff_term = product_tn(normed_two, grad_pre)
    swiglu_gain_grad = jnp.sum(ff_term * ff_low.astype(full), axis=-1) / swiglu_gain
    ff_share = scatter_seq(ff_term).reshape(pieces, weight_rows, 2 * ff_own)
    down_share = scatter_seq(product_tn(hidden_ff, out_grad_all)).astype(full)

    grad_middle = out_grad.astype(full) + rms_scale_back(middle, swiglu_gain, grad_normed_two)
    grad_branch = gather_ctx(grad_middle.astype(low), 6)
    hidden_out = (middle + scatter_ctx(product(hidden_ff, down_low), 7)).astype(low)
    gate_share, up_share = ff_rows(ff_share, ff_block, 8)
    grad_gated = product_nt(grad_branch, out_low).reshape(length, heads, HD)
    output_share = lax.ppermute(
        scatter_seq(product_tn(gated, grad_branch)), ("seq", "ctx"), collect
    ).astype(full)
    grad_attended_full, grad_gate_raw_full = pull_gate(grad_gated)
    grad_attended = grad_attended_full.astype(low)
    grad_heads = grad_attended.reshape(length, kv_heads, per_kv, HD).transpose(1, 2, 0, 3)
    row_delta = jnp.sum(grad_heads.astype(full) * attended, axis=-1, keepdims=True)
    probabilities = jnp.exp(scores - log_norm)
    prob_grad = jnp.einsum("kgtd,skd->kgts", grad_heads, values, preferred_element_type=full)
    score_grad = (probabilities * (prob_grad - row_delta)).astype(low)
    grad_queries = (
        jnp.einsum("kgts,skd->tkgd", score_grad, keys, preferred_element_type=full) * score_scale
    )
    grad_keys = (
        jnp.einsum("kgts,tkgd->skd", score_grad, queries, preferred_element_type=full)
        * score_scale
    )
    grad_values = jnp.einsum(
        "kgts,kgtd->skd", probabilities.astype(low), grad_heads, preferred_element_type=full
    )
    grad_query_full, grad_key_full, query_gain_grad, key_gain_grad = pull_rope(
        (grad_queries.reshape(length, heads, HD), grad_keys)
    )
    grad_raw = jnp.concatenate(
        [
            grad_query_full.reshape(length, q_width).astype(low),
            grad_key_full.reshape(length, kv_width).astype(low),
            grad_values.reshape(length, kv_width).astype(low),
            grad_gate_raw_full.astype(low),
            jnp.zeros((length, attn_width - used), low),
        ],
        axis=-1,
    )
    attn_term = product_tn(normed, grad_raw)
    attention_gain_grad = jnp.sum(attn_term * attn_low.astype(full), axis=-1) / attention_gain
    gains_term = jnp.concatenate(
        [attention_gain_grad, swiglu_gain_grad, query_gain_grad, key_gain_grad]
    ).reshape(groups * pieces, gain_count)
    gains_term = jnp.pad(gains_term, ((0, 0), (0, gain_columns * weight_rows - gain_count)))
    gains_term = gains_term.reshape(model, gain_columns)
    attn_term = jnp.concatenate(
        [
            attn_term[:, :used].astype(low),
            gains_term.astype(low),
            jnp.zeros((model, attn_width - used - gain_columns), low),
        ],
        axis=-1,
    )
    attn_share = scatter_seq(attn_term).reshape(pieces, weight_rows, attn_width)
    grad_normed = scatter_ctx(product_nt(grad_raw, attn_low), 9)
    hidden_grad = (grad_middle + rms_scale_back(residual_in, attention_gain, grad_normed)).astype(
        low
    )
    attn_share = attn_rows(attn_share, 10).transpose(1, 0, 2).astype(full)

    def kv_back(columns):
        columns = columns.reshape(weight_rows, KV, copies, HD)
        return columns.sum(axis=2).reshape(weight_rows, KV * HD)

    query_share = attn_share[:, :, :q_width].reshape(weight_rows, H * HD)
    key_share = kv_back(attn_share[:, :, q_width : q_width + kv_width])
    value_share = kv_back(attn_share[:, :, q_width + kv_width : q_width + 2 * kv_width])
    head_share = attn_share[:, :, q_width + 2 * kv_width : used].reshape(weight_rows, H)
    gains_share = attn_share[:, :, used : used + gain_columns].sum(axis=1).reshape(-1)[:gain_count]
    return (
        hidden_out,
        hidden_grad,
        gains_share,
        query_share,
        key_share,
        value_share,
        head_share,
        output_share,
        gate_share,
        up_share,
        down_share,
    )


def solution(mesh):
    rows = P(("seq", "ctx"), None)
    return jax.shard_map(
        on_device,
        mesh=mesh,
        in_specs=(rows, rows, P("seq"), P(("seq", "ctx"))) + (rows,) * 8,
        out_specs=(rows, rows, P(("seq", "ctx"))) + (rows,) * 8,
        check_vma=False,
    )
```

```python
import functools

import jax
import jax.numpy as jnp
from jax import lax
from jax.experimental import pallas as pl
from jax.experimental.pallas import tpu as pltpu
from jax.sharding import PartitionSpec as P

H = 16
KV = 8
HD = 128


epsilon = 1e-06
rope_base = 1000000.0
negative = -1e30
low = jnp.bfloat16
full = jnp.float32
MESH = pl.DeviceIdType.MESH
ANY = pl.BlockSpec(memory_space=pl.ANY)
IN_VMEM = pl.BlockSpec(memory_space=pltpu.VMEM)
DMA = pltpu.SemaphoreType.DMA


def product(left_side, right_side):
    return jnp.dot(left_side, right_side, preferred_element_type=full)


def product_nt(left_side, right_side):
    return lax.dot_general(
        left_side, right_side, (((1,), (1,)), ((), ())), preferred_element_type=full
    )


def product_tn(left_side, right_side):
    return lax.dot_general(
        left_side, right_side, (((0,), (0,)), ((), ())), preferred_element_type=full
    )


def remote(source, target, send, receive, axis, peer):
    return pltpu.make_async_remote_copy(
        src_ref=source,
        dst_ref=target,
        send_sem=send,
        recv_sem=receive,
        device_id={axis: peer},
        device_id_type=MESH,
    )


def greet(peers):
    barrier = pltpu.get_barrier_semaphore()
    for axis, peer, exists in peers:
        if exists is True:
            pl.semaphore_signal(barrier, inc=1, device_id={axis: peer}, device_id_type=MESH)
        else:

            @pl.when(exists)
            def _():
                pl.semaphore_signal(barrier, inc=1, device_id={axis: peer}, device_id_type=MESH)

    arrivals = sum(1 for _, _, exists in peers if exists is True)
    for _, _, exists in peers:
        if exists is not True:
            arrivals = arrivals + exists.astype(jnp.int32)
    pl.semaphore_wait(barrier, arrivals)


def others(axis, count):
    me = lax.axis_index(axis)
    return [(axis, lax.rem(me + shift, count), True) for shift in range(1, count)]


class Line:
    def __init__(self, pieces):
        self.chips = pieces // 2
        self.me = lax.axis_index("ctx")
        self.chip, self.core = self.me // 2, lax.rem(self.me, 2)
        self.sibling = self.me + 1 - 2 * self.core
        self.right, self.left = self.me + 2, self.me - 2
        self.has_right, self.has_left = self.chip < self.chips - 1, self.chip > 0

    def peers(self):
        return [
            ("ctx", self.sibling, True),
            ("ctx", self.right, self.has_right),
            ("ctx", self.left, self.has_left),
        ]


def gather_scratch(pieces, parts):
    chips = pieces // 2
    return [DMA((chips, 2, parts))] * 2 + [DMA((chips, parts))] * 4


class Gather:
    def __init__(self, line, parts, rows, out_ref, sems):
        self.line, self.parts, self.rows, self.out_ref = line, parts, rows, out_ref
        self.size = rows // parts
        self.sib_send, self.sib_recv, self.r_send, self.r_recv, self.l_send, self.l_recv = sems

    def at(self, position, part):
        start = pl.multiple_of(position * self.rows + part * self.size, self.size)
        return self.out_ref.at[pl.ds(start, self.size)]

    def to_sibling(self, source, hop, side, part, position):
        return remote(
            source,
            self.at(position, part),
            self.sib_send.at[hop, side, part],
            self.sib_recv.at[hop, side, part],
            "ctx",
            self.line.sibling,
        )

    def to_right(self, source, hop, part, position):
        return remote(
            source,
            self.at(position, part),
            self.r_send.at[hop, part],
            self.r_recv.at[hop, part],
            "ctx",
            self.line.right,
        )

    def to_left(self, source, hop, part, position):
        return remote(
            source,
            self.at(position, part),
            self.l_send.at[hop, part],
            self.l_recv.at[hop, part],
            "ctx",
            self.line.left,
        )

    def start(self, x_ref):
        line = self.line
        for part in range(self.parts):
            piece = x_ref.at[pl.ds(part * self.size, self.size)]

            @pl.when(line.has_right)
            def _():
                self.to_right(piece, 0, part, line.me).start()

            @pl.when(line.has_left)
            def _():
                self.to_left(piece, 0, part, line.me).start()

            self.to_sibling(piece, 0, 0, part, line.me).start()

    def forward(self, hop):
        line = self.line
        for part in range(self.parts):
            from_left, from_right = line.me - 2 * hop, line.me + 2 * hop

            @pl.when(line.chip - hop >= 0)
            def _():
                piece = self.at(from_left, part)
                self.to_right(piece, hop - 1, part, from_left).wait_recv()

                @pl.when(line.has_right)
                def _():
                    self.to_right(piece, hop, part, from_left).start()

                self.to_sibling(piece, hop, 0, part, from_left).start()

            @pl.when(line.chip + hop < line.chips)
            def _():
                piece = self.at(from_right, part)
                self.to_left(piece, hop - 1, part, from_right).wait_recv()

                @pl.when(line.has_left)
                def _():
                    self.to_left(piece, hop, part, from_right).start()

                self.to_sibling(piece, hop, 1, part, from_right).start()

    def legs(self, hop):
        line = self.line
        return [
            (
                side,
                (line.chip - hop >= 0) if side == 0 else (line.chip + hop < line.chips),
                (line.me - 2 * hop) if side == 0 else (line.me + 2 * hop),
            )
            for side in range(1 if hop == 0 else 2)
        ]

    def arrive(self, hop):
        for side, there, position in self.legs(hop):
            for part in range(self.parts):

                @pl.when(there)
                def _():
                    self.to_sibling(
                        self.at(position, part), hop, side, part, position
                    ).wait_recv()

    def finish(self):
        line = self.line
        for hop in range(line.chips):
            for side, there, position in self.legs(hop):
                for part in range(self.parts):

                    @pl.when(there)
                    def _():
                        piece = self.at(position, part)
                        self.to_sibling(piece, hop, side, part, position).wait_send()
                        if side == 0:

                            @pl.when(line.has_right)
                            def _():
                                self.to_right(piece, hop, part, position).wait_send()

                        if side == 1 or hop == 0:

                            @pl.when(line.has_left)
                            def _():
                                self.to_left(piece, hop, part, position).wait_send()

    def complete(self):
        for hop in range(self.line.chips):
            self.arrive(hop)
        self.finish()


def scatter_scratch(pieces, rows, width):
    chips = pieces // 2
    slots = pltpu.VMEM((chips, rows, width), low)
    return [slots] * 3 + [pltpu.VMEM((chips + 1, rows, width), low)] + [DMA((chips,))] * 6


class Scatter:
    def __init__(self, line, rows, scratch):
        self.line, self.rows = line, rows
        (
            self.own,
            self.give,
            self.sib,
            self.arrived,
            self.sib_send,
            self.sib_recv,
            self.r_send,
            self.r_recv,
            self.l_send,
            self.l_recv,
        ) = scratch

    def there(self, far, side):
        line = self.line
        return (line.chip + far < line.chips) if side == 0 else (line.chip - far >= 0)

    def target(self, far, side):
        return self.line.chip + far if side == 0 else self.line.chip - far

    def exchange(self, target):
        return remote(
            self.give.at[target],
            self.sib.at[target],
            self.sib_send.at[target],
            self.sib_recv.at[target],
            "ctx",
            self.line.sibling,
        )

    def send(self, target, side):
        if side == 0:
            return remote(
                self.own.at[target],
                self.arrived.at[target],
                self.r_send.at[target],
                self.r_recv.at[target],
                "ctx",
                self.line.right,
            )
        chips, chip = self.line.chips, self.line.chip
        return remote(
            self.own.at[target],
            self.arrived.at[jnp.where(target == chip - 1, chips, target)],
            self.l_send.at[target],
            self.l_recv.at[target],
            "ctx",
            self.line.left,
        )

    def order(self):
        return [
            (far, side)
            for far in range(self.line.chips - 1, -1, -1)
            for side in range(2 if far else 1)
        ]

    def fill(self, far, side, block):
        @pl.when(self.there(far, side))
        def _():
            target = self.target(far, side)

            def store(columns, value):
                first, second = value[: self.rows], value[self.rows :]
                mine = self.line.core == 0
                self.own[target, :, columns] = jnp.where(mine, first, second).astype(low)
                self.give[target, :, columns] = jnp.where(mine, second, first).astype(low)

            block(target, store)
            self.exchange(target).start()

    def push(self, far, side):
        line = self.line
        behind = line.has_left if side == 0 else line.has_right

        @pl.when(self.there(far, side))
        def _():
            target = self.target(far, side)
            self.exchange(target).wait_recv()
            total = self.own[target].astype(full) + self.sib[target].astype(full)
            if far == line.chips - 1:
                self.own[target] = total.astype(low)
            else:

                @pl.when(behind)
                def _():
                    self.send(target, side).wait_recv()
                    self.own[target] = (total + self.arrived[target].astype(full)).astype(low)

                @pl.when(jnp.logical_not(behind))
                def _():
                    self.own[target] = total.astype(low)

            self.send(target, side).start()

    def total(self, total_ref):
        line = self.line
        chip = line.chip
        self.exchange(chip).wait_recv()
        total_ref[...] = self.own[chip].astype(full) + self.sib[chip].astype(full)

        @pl.when(line.has_left)
        def _():
            self.send(chip, 0).wait_recv()
            total_ref[...] += self.arrived[chip].astype(full)

        @pl.when(line.has_right)
        def _():
            self.send(chip, 1).wait_recv()
            total_ref[...] += self.arrived[line.chips].astype(full)

    def finish(self):
        for far, side in self.order():

            @pl.when(self.there(far, side))
            def _():
                target = self.target(far, side)
                self.exchange(target).wait_send()
                if far > 0:
                    self.send(target, side).wait_send()


def blocks_nn(left_ref, right_ref, rows, tile=512):
    def block(target, store):
        start = pl.multiple_of(target * 2 * rows, 2 * rows)
        left_side = left_ref[pl.ds(start, 2 * rows), :]

        def step(index, unused):
            columns = pl.ds(pl.multiple_of(index * tile, tile), tile)
            store(columns, product(left_side, right_ref[:, columns]))
            return unused

        lax.fori_loop(0, right_ref.shape[1] // tile, step, 0)

    return block


def blocks_nt(left_ref, right_ref, rows, tile=512):
    def block(target, store):
        start = pl.multiple_of(target * 2 * rows, 2 * rows)
        left_side = left_ref[pl.ds(start, 2 * rows), :]

        def step(index, unused):
            columns = pl.ds(pl.multiple_of(index * tile, tile), tile)
            store(columns, product_nt(left_side, right_ref[columns, :]))
            return unused

        lax.fori_loop(0, right_ref.shape[0] // tile, step, 0)

    return block


class Swap:
    def __init__(self, pieces, send_of, recv_of, send_sem, recv_sem):
        self.pieces, self.me = pieces, lax.axis_index("ctx")
        self.send_of, self.recv_of = send_of, recv_of
        self.send_sem, self.recv_sem = send_sem, recv_sem

    def copy(self, shift):
        peer = lax.rem(self.me + shift, self.pieces)
        return remote(
            self.send_of(peer),
            self.recv_of(self.me),
            self.send_sem.at[shift],
            self.recv_sem.at[shift],
            "ctx",
            peer,
        )

    def start(self):
        for shift in range(1, self.pieces):
            self.copy(shift).start()

    def wait_recv(self, shift):
        source = lax.rem(self.me + self.pieces - shift, self.pieces)
        remote(
            self.send_of(source),
            self.recv_of(source),
            self.send_sem.at[shift],
            self.recv_sem.at[shift],
            "ctx",
            source,
        ).wait_recv()
        return source

    def finish(self):
        for shift in range(1, self.pieces):
            self.copy(shift).wait_send()


def opening_kernel(
    pieces,
    groups,
    parts,
    hidden_ref,
    gains_ref,
    attn_ref,
    normed_ref,
    attn_out,
    gains_out,
    gains_row,
    gains_all,
    gain_vector,
    normed,
    own_sem,
    own_attn,
    ga_send,
    ga_recv,
    gs_send,
    gs_recv,
    at_send,
    at_recv,
    as_send,
    as_recv,
    *sems,
):
    line = Line(pieces)
    me, group = line.me, lax.axis_index("seq")
    greet(others("ctx", pieces) + others("seq", groups))
    rows, model = hidden_ref.shape
    gain_count = gains_ref.shape[1]
    gains_row[...] = jnp.zeros(gains_row.shape, full)
    gains_row[0:1, pl.ds(0, gain_count)] = gains_ref[...].astype(low).astype(full)
    gains_all[group, me] = gains_row[...]
    gain_swap = Swap(
        pieces, lambda peer: gains_row, lambda peer: gains_all.at[group, peer], ga_send, ga_recv
    )
    gain_swap.start()
    attn_swap = Swap(
        pieces, lambda peer: attn_ref.at[peer], lambda peer: attn_out.at[group, peer], at_send, at_recv
    )
    attn_swap.start()
    attn_own = pltpu.make_async_copy(attn_ref.at[me], attn_out.at[group, me], own_attn)
    attn_own.start()
    values = hidden_ref[...].astype(full)
    inverse = lax.rsqrt(jnp.mean(values * values, axis=-1, keepdims=True) + epsilon)

    def to_groups(ref, sends, receives, shift):
        peer = lax.rem(group + shift, groups)
        return remote(ref.at[group], ref.at[group], sends.at[shift], receives.at[shift], "seq", peer)

    def from_groups(ref, sends, receives, shift):
        peer = lax.rem(group + groups - shift, groups)
        remote(
            ref.at[peer], ref.at[peer], sends.at[shift], receives.at[shift], "seq", peer
        ).wait_recv()

    for shift in range(1, pieces):
        gain_swap.wait_recv(shift)
    for shift in range(1, groups):
        to_groups(gains_all, gs_send, gs_recv, shift).start()
    for shift in range(1, groups):
        from_groups(gains_all, gs_send, gs_recv, shift)
    for index in range(groups * pieces):
        gain_vector[0:1, pl.ds(index * gain_count, gain_count)] = gains_all[
            index // pieces, index % pieces, 0:1, pl.ds(0, gain_count)
        ]
    gains_out[...] = gain_vector[...]
    normed[...] = (values * inverse * gain_vector[0:1, pl.ds(0, model)]).astype(low)
    gather = Gather(line, parts, rows, normed_ref, sems)
    gather.start(normed)
    start = pl.multiple_of(me * rows, rows)
    own = pltpu.make_async_copy(normed, normed_ref.at[pl.ds(start, rows)], own_sem)
    own.start()
    for shift in range(1, pieces):
        attn_swap.wait_recv(shift)
    attn_own.wait()
    for shift in range(1, groups):
        to_groups(attn_out, as_send, as_recv, shift).start()
    for hop in range(1, line.chips):
        gather.forward(hop)
    own.wait()
    gather.complete()
    for shift in range(1, groups):
        from_groups(attn_out, as_send, as_recv, shift)
    gain_swap.finish()
    attn_swap.finish()
    for shift in range(1, groups):
        to_groups(gains_all, gs_send, gs_recv, shift).wait_send()
        to_groups(attn_out, as_send, as_recv, shift).wait_send()


def opening(hidden_in, norm_gains, attn_blocks, number, parts=2):
    pieces, groups = lax.axis_size("ctx"), lax.axis_size("seq")
    rows, model = hidden_in.shape
    gains = norm_gains.shape[0]
    lanes = -(-gains // 128) * 128
    return pl.pallas_call(
        functools.partial(opening_kernel, pieces, groups, parts),
        out_shape=(
            jax.ShapeDtypeStruct((pieces * rows, model), low),
            jax.ShapeDtypeStruct((groups,) + attn_blocks.shape, low),
            jax.ShapeDtypeStruct((1, groups * pieces * gains), full),
        ),
        in_specs=[IN_VMEM, IN_VMEM, IN_VMEM],
        out_specs=(ANY, ANY, IN_VMEM),
        scratch_shapes=[
            pltpu.VMEM((8, lanes), full),
            pltpu.VMEM((groups, pieces, 8, lanes), full),
            pltpu.VMEM((1, groups * pieces * gains), full),
            pltpu.VMEM((rows, model), low),
            DMA,
            DMA,
            DMA((pieces,)),
            DMA((pieces,)),
            DMA((groups,)),
            DMA((groups,)),
            DMA((pieces,)),
            DMA((pieces,)),
            DMA((groups,)),
            DMA((groups,)),
        ]
        + gather_scratch(pieces, parts),
        compiler_params=pltpu.CompilerParams(
            collective_id=number, has_side_effects=True, vmem_limit_bytes=60 << 20
        ),
        name=f"opening_{number}",
    )(hidden_in, norm_gains.reshape(1, gains), attn_blocks)


class LineSwap:
    def __init__(self, line, send_of, recv_of, s_sem, r_sem):
        self.line, self.send_of, self.recv_of = line, send_of, recv_of
        self.s_sem, self.r_sem = s_sem, r_sem

    def copy(self, far, side, core):
        line = self.line
        if far == 0:
            peer, slot = line.sibling, self.r_sem.at[0, 0, 0]
        else:
            peer = (line.chip + (far if side == 0 else -far)) * 2 + core
            slot = self.r_sem.at[far, side, line.core]
        return remote(
            self.send_of(peer), self.recv_of(line.me), self.s_sem.at[far, side, core], slot, "ctx", peer
        )

    def legs(self, far):
        line = self.line
        if far == 0:
            return [(0, 0, True, True)]
        return [
            (
                side,
                core,
                (line.chip + far < line.chips) if side == 0 else (line.chip - far >= 0),
                (line.chip - far >= 0) if side == 0 else (line.chip + far < line.chips),
            )
            for side in range(2)
            for core in range(2)
        ]

    def start(self):
        for far in range(self.line.chips):
            for side, core, sends, _ in self.legs(far):
                if far == 0:
                    self.copy(far, side, core).start()
                else:

                    @pl.when(sends)
                    def _():
                        self.copy(far, side, core).start()

    def receive(self, far, then):
        line = self.line
        for side, core, _, comes in self.legs(far):
            if far == 0:
                source, slot = line.sibling, self.r_sem.at[0, 0, 0]
            else:
                source = (line.chip + (-far if side == 0 else far)) * 2 + core
                slot = self.r_sem.at[far, side, core]

            def wait():
                remote(
                    self.recv_of(source),
                    self.recv_of(source),
                    self.s_sem.at[far, side, core],
                    slot,
                    "ctx",
                    source,
                ).wait_recv()
                then(source)

            if far == 0:
                wait()
            else:
                pl.when(comes)(wait)

    def finish(self):
        for far in range(self.line.chips):
            for side, core, sends, _ in self.legs(far):
                if far == 0:
                    self.copy(far, side, core).wait_send()
                else:

                    @pl.when(sends)
                    def _():
                        self.copy(far, side, core).wait_send()


def swap_scratch(pieces):
    return [DMA((pieces // 2, 2, 2))] * 2


class Share:
    def __init__(self, groups, place, s_sem, r_sem):
        self.groups, self.place, self.s_sem, self.r_sem = groups, place, s_sem, r_sem
        self.group = lax.axis_index("seq")

    def copy(self, source, shift, origin=None):
        peer = lax.rem(self.group + shift, self.groups)
        target = self.place(self.group, source)
        return remote(
            target if origin is None else origin,
            target,
            self.s_sem.at[source, shift],
            self.r_sem.at[source, shift],
            "seq",
            peer,
        )

    def send(self, source, origin=None):
        for shift in range(1, self.groups):
            self.copy(source, shift, origin).start()

    def finish(self, sources):
        for source in range(sources):
            for shift in range(1, self.groups):
                peer = lax.rem(self.group + self.groups - shift, self.groups)
                remote(
                    self.place(peer, source),
                    self.place(peer, source),
                    self.s_sem.at[source, shift],
                    self.r_sem.at[source, shift],
                    "seq",
                    peer,
                ).wait_recv()
                self.copy(source, shift).wait_send()


def lanes(start, size):
    return pl.ds(pl.multiple_of(start, 128), size)


def turn(values, cosine, sine):
    half = values.shape[0] // 2
    first, second = values[:half], values[half:]
    return jnp.concatenate(
        [first * cosine - second * sine, second * cosine + first * sine], axis=0
    )


def turn_back(values, cosine, sine):
    half = values.shape[0] // 2
    first, second = values[:half], values[half:]
    return jnp.concatenate(
        [first * cosine + second * sine, second * cosine - first * sine], axis=0
    )


def inverse_rms(values):
    return lax.rsqrt(jnp.mean(values * values, axis=0, keepdims=True) + epsilon)


def kept(first_key, keys, first_query, queries, prefix):
    key = first_key + lax.broadcasted_iota(jnp.int32, (keys, queries), 0)
    query = first_query + lax.broadcasted_iota(jnp.int32, (keys, queries), 1)
    return key <= jnp.maximum(query, prefix - 1)


def query_blocks(length, body):
    tile = min(256, length // 2)
    half = length // 2

    def early(index, unused):
        body(index * tile, tile, half)
        return unused

    def late(index, unused):
        body(half + index * tile, tile, length)
        return unused

    lax.fori_loop(0, half // tile, early, 0)
    lax.fori_loop(0, half // tile, late, 0)


def attend_kernel(
    shape,
    raw,
    cosine,
    sine,
    query_gain,
    key_gain,
    prefix_ref,
    out_low,
    hidden,
    swiglu_gain,
    out_grad,
    gate_weight,
    up_weight,
    raw_t,
    gate_t,
    q_ref,
    qt_ref,
    k_ref,
    kt_ref,
    v_ref,
    att_t,
    lse_ref,
    gated_t,
    middle,
    normed_two,
    og_all,
    ff_low,
    vt_ref,
    gated,
    blocks,
    own_sem,
    og_sem,
    swap_s,
    swap_r,
    share_s,
    share_r,
    *sems,
):
    pieces, groups, heads, kv_heads, ff_block = shape
    gather_sems, scatter_refs = sems[:6], sems[6:]
    line = Line(pieces)
    me, group = line.me, lax.axis_index("seq")
    length, rows = raw.shape[0], hidden.shape[0]
    greet(others("ctx", pieces) + others("seq", groups))
    own_width = groups * ff_block
    for half, weight_ref in enumerate((gate_weight, up_weight)):
        for index in range(groups):
            for piece in range(pieces):
                start = (index * pieces + piece) * ff_block
                blocks[piece, :, pl.ds(half * own_width + index * ff_block, ff_block)] = weight_ref[
                    :, pl.ds(start, ff_block)
                ].astype(low)
    swap = LineSwap(
        line, lambda peer: blocks.at[peer], lambda source: ff_low.at[group, source], swap_s, swap_r
    )
    swap.start()
    share = Share(groups, lambda index, source: ff_low.at[index, source], share_s, share_r)
    share.send(me, blocks.at[me])
    own = pltpu.make_async_copy(blocks.at[me], ff_low.at[group, me], own_sem)
    own.start()

    prefix = prefix_ref[0, 0]
    scale = HD ** (-0.5)
    for head in range(heads + kv_heads):
        part = pl.ds(head * HD, HD)
        values = raw[:, part].T
        raw_t[part, :] = values
        gain = query_gain[...] if head < heads else key_gain[...]
        turned = turn(values * inverse_rms(values) * gain, cosine[...], sine[...])
        if head < heads:
            qt_ref[part, :] = turned.astype(low)
            q_ref[:, part] = turned.T.astype(low)
        else:
            part = pl.ds((head - heads) * HD, HD)
            kt_ref[part, :] = turned.astype(low)
            k_ref[:, part] = turned.T.astype(low)
    for head in range(kv_heads):
        part = pl.ds(head * HD, HD)
        values = raw[:, pl.ds((heads + kv_heads + head) * HD, HD)]
        v_ref[:, part] = values.astype(low)
        vt_ref[part, :] = values.T.astype(low)
    gate_t[...] = raw[:, pl.ds((heads + 2 * kv_heads) * HD, HD)].T[: gate_t.shape[0]]
    swap.receive(0, share.send)
    for head in range(heads):
        part = pl.ds(head * HD, HD)
        kv_part = pl.ds(head * kv_heads // heads * HD, HD)

        def block(first, tile, keys):
            columns = lanes(first, tile)
            scores = product(k_ref[pl.ds(0, keys), kv_part], qt_ref[part, columns]) * scale
            scores = jnp.where(kept(0, keys, first, tile, prefix), scores, negative)
            top = jnp.max(scores, axis=0, keepdims=True)
            expanded = jnp.exp(scores - top)
            total = jnp.sum(expanded, axis=0, keepdims=True)
            lse_ref[head : head + 1, columns] = top + jnp.log(total)
            att_t[part, columns] = (
                product(vt_ref[kv_part, pl.ds(0, keys)], expanded.astype(low)) / total
            )

        query_blocks(length, block)
        scaled = att_t[part, :] * jax.nn.sigmoid(gate_t[head : head + 1, :])
        gated_t[part, :] = scaled.astype(low)
        gated[:, part] = scaled.T.astype(low)
        if head == 0:
            swap.receive(1, share.send)

    gather = Gather(line, 2, rows, og_all, gather_sems)
    scatter = Scatter(line, rows, scatter_refs)
    block = blocks_nn(gated, out_low, rows)
    last = line.chips - 1
    for far, side in scatter.order():
        if far == last:
            scatter.fill(far, side, block)
    gather.start(out_grad)
    start = pl.multiple_of(me * rows, rows)
    og_own = pltpu.make_async_copy(out_grad, og_all.at[pl.ds(start, rows)], og_sem)
    og_own.start()
    for far, side in scatter.order():
        if far == last:
            scatter.push(far, side)
    for far, side in scatter.order():
        if far < last:
            scatter.fill(far, side, block)
    for far in range(2, line.chips):
        swap.receive(far, share.send)
    for hop in range(1, line.chips):
        for far, side in scatter.order():
            if far == last - hop and far > 0:
                scatter.push(far, side)
        gather.forward(hop)
    scatter.total(middle)
    values = hidden[...].astype(full) + middle[...]
    middle[...] = values
    inverse = lax.rsqrt(jnp.mean(values * values, axis=-1, keepdims=True) + epsilon)
    normed_two[...] = (values * inverse * swiglu_gain[...]).astype(low)
    og_own.wait()
    own.wait()
    gather.complete()
    scatter.finish()
    swap.finish()
    share.finish(pieces)


def attend(raw, tables, gains, prefix, out_low, hidden, swiglu_gain, out_grad, weights, shape, number):
    pieces, groups, heads, kv_heads, ff_block = shape
    length, rows, model = raw.shape[0], hidden.shape[0], hidden.shape[1]
    q_width, kv_width = heads * HD, kv_heads * HD
    weight_rows = weights[0].shape[0]
    struct = jax.ShapeDtypeStruct
    return pl.pallas_call(
        functools.partial(attend_kernel, shape),
        out_shape=(
            struct((q_width + kv_width, length), full),
            struct((8, length), full),
            struct((length, q_width), low),
            struct((q_width, length), low),
            struct((length, kv_width), low),
            struct((kv_width, length), low),
            struct((length, kv_width), low),
            struct((q_width, length), full),
            struct((8, length), full),
            struct((q_width, length), low),
            struct((rows, model), full),
            struct((rows, model), low),
            struct((length, model), low),
            struct((groups, pieces, weight_rows, 2 * groups * ff_block), low),
        ),
        in_specs=[IN_VMEM] * 5 + [pl.BlockSpec(memory_space=pltpu.SMEM)] + [IN_VMEM] * 6,
        out_specs=(IN_VMEM,) * 12 + (ANY, ANY),
        scratch_shapes=[
            pltpu.VMEM((kv_width, length), low),
            pltpu.VMEM((length, q_width), low),
            pltpu.VMEM((pieces, weight_rows, 2 * groups * ff_block), low),
            DMA,
            DMA,
        ]
        + swap_scratch(pieces)
        + [DMA((pieces, groups))] * 2
        + gather_scratch(pieces, 2)
        + scatter_scratch(pieces, rows, model),
        compiler_params=pltpu.CompilerParams(
            collective_id=number, has_side_effects=True, vmem_limit_bytes=60 << 20
        ),
        name=f"attend_{number}",
    )(raw, *tables, *gains, prefix, out_low, hidden, swiglu_gain, out_grad, *weights)


def attend_back_kernel(
    shape,
    grad_branch,
    out_low,
    raw_t,
    gate_t,
    q_ref,
    qt_ref,
    k_ref,
    kt_ref,
    v_ref,
    att_t,
    lse_ref,
    cosine,
    sine,
    query_gain,
    key_gain,
    prefix_ref,
    normed,
    attn_low,
    hidden,
    grad_middle,
    attention_gain,
    swiglu_gain_grad,
    ff_share,
    hidden_grad,
    gains_grad,
    query_grad,
    key_grad,
    value_grad,
    head_grad,
    gate_grad,
    up_grad,
    gg_t,
    ga_t,
    ga,
    gqt,
    dk,
    dv,
    grad_t,
    grad,
    total_ref,
    ff_recv,
    normed_part,
    part_sem,
    term,
    term_in,
    attn_send,
    attn_recv,
    gains_vector,
    gain_give,
    gain_sib,
    gain_row,
    gain_last,
    ffs_s,
    ffs_r,
    at_s,
    at_r,
    gc_s,
    gc_r,
    ts_s,
    ts_r,
    gs_s,
    gs_r,
    *scatter_refs,
):
    pieces, groups, heads, kv_heads, ff_block = shape
    line = Line(pieces)
    me, group = line.me, lax.axis_index("seq")
    length, rows = grad_branch.shape[0], hidden.shape[0]
    width, model = attn_low.shape[1], attn_low.shape[0]
    weight_rows = ff_share.shape[1]
    q_width, kv_width = heads * HD, kv_heads * HD
    greet(others("ctx", pieces) + others("seq", groups))
    ff_swap = LineSwap(
        line, lambda peer: ff_share.at[peer], lambda source: ff_recv.at[source], ffs_s, ffs_r
    )
    ff_swap.start()

    prefix = prefix_ref[0, 0]
    scale = HD ** (-0.5)

    def branch(index, unused):
        columns = lanes(index * 256, 256)
        gg_t[:, columns] = product_nt(out_low[...], grad_branch[columns, :])
        return unused

    lax.fori_loop(0, length // 256, branch, 0)
    dk[...] = jnp.zeros(dk.shape, full)
    dv[...] = jnp.zeros(dv.shape, full)
    gate_rows = []
    for head in range(heads):
        part = pl.ds(head * HD, HD)
        kv_part = pl.ds(head * kv_heads // heads * HD, HD)
        sigmoid = jax.nn.sigmoid(gate_t[head : head + 1, :])
        grads = gg_t[part, :]
        rounded = (grads * sigmoid).astype(low)
        ga_t[...] = rounded
        ga[...] = rounded.astype(full).T.astype(low)
        gate_rows.append(
            jnp.sum(grads * att_t[part, :], axis=0, keepdims=True) * sigmoid * (1.0 - sigmoid)
        )

        def block(first, tile, keys):
            columns, across = lanes(first, tile), pl.ds(0, keys)
            scores = product(k_ref[across, kv_part], qt_ref[part, columns]) * scale
            chance = jnp.where(
                kept(0, keys, first, tile, prefix),
                jnp.exp(scores - lse_ref[head : head + 1, columns]),
                0.0,
            )
            taken = ga_t[:, columns]
            delta = jnp.sum(taken.astype(full) * att_t[part, columns], axis=0, keepdims=True)
            change = product(v_ref[across, kv_part], taken)
            score_grad = (chance * (change - delta)).astype(low)
            gqt[part, columns] = product(kt_ref[kv_part, across], score_grad) * scale
            dk[across, kv_part] += product(score_grad, q_ref[columns, part])
            dv[across, kv_part] += product(chance.astype(low), ga[columns, :])

        query_blocks(length, block)

    gain_columns = [jnp.zeros((HD, 1), full), jnp.zeros((HD, 1), full)]
    for head in range(heads + kv_heads):
        part = pl.ds(head * HD, HD)
        if head < heads:
            turned = gqt[part, :]
            gain = query_gain[...]
        else:
            turned = dk[:, pl.ds((head - heads) * HD, HD)].T * scale
            gain = key_gain[...]
        grads = turn_back(turned, cosine[...], sine[...])
        values = raw_t[part, :]
        inverse = inverse_rms(values)
        kind = 0 if head < heads else 1
        gain_columns[kind] = gain_columns[kind] + jnp.sum(
            grads * values * inverse, axis=1, keepdims=True
        )
        scaled = grads * gain
        result = inverse * scaled - values * (
            inverse * inverse * inverse * jnp.mean(scaled * values, axis=0, keepdims=True)
        )
        grad_t[part, :] = result.astype(low)
        grad[:, part] = result.T.astype(low)
    for head in range(kv_heads):
        part = pl.ds((heads + kv_heads + head) * HD, HD)
        values = dv[:, pl.ds(head * HD, HD)]
        grad[:, part] = values.astype(low)
        grad_t[part, :] = values.T.astype(low)
    part = pl.ds((heads + 2 * kv_heads) * HD, HD)
    gate_block = jnp.concatenate(
        gate_rows + [jnp.zeros((HD - heads, length), full)], axis=0
    )
    grad_t[part, :] = gate_block.astype(low)
    grad[:, part] = gate_block.T.astype(low)

    scatter = Scatter(line, rows, scatter_refs)
    block = blocks_nt(grad, attn_low, rows)
    last = line.chips - 1
    for far, side in scatter.order():
        if far == last:
            scatter.fill(far, side, block)
    for far, side in scatter.order():
        if far == last:
            scatter.push(far, side)
    for far, side in scatter.order():
        if far == last - 1:
            scatter.fill(far, side, block)

    share = model // groups

    def to_group(shift):
        peer = lax.rem(group + shift, groups)
        return remote(term.at[peer], term_in.at[shift], ts_s.at[shift], ts_r.at[shift], "seq", peer)

    shifts = list(range(1, groups)) + [0]

    def load(job):
        index = lax.rem(group + shifts[job], groups)
        return pltpu.make_async_copy(
            normed.at[:, lanes(index * share, share)], normed_part.at[job % 2], part_sem.at[job % 2]
        )

    def weight_grad(job, index):
        load(job).wait()
        if job + 1 < groups:
            load(job + 1).start()

        def step(tile, unused):
            value = product(grad_t[...], normed_part[job % 2, :, lanes(tile * 128, 128)])
            term[index, pl.ds(pl.multiple_of(tile * 128, 128), 128), :] = value.T.astype(low)
            return unused

        lax.fori_loop(0, share // 128, step, 0)

    load(0).start()
    for job, shift in enumerate(shifts):
        weight_grad(job, lax.rem(group + shift, groups))
        if shift:
            to_group(shift).start()
    for far, side in scatter.order():
        if far < last - 1:
            scatter.fill(far, side, block)
    for hop in range(1, line.chips):
        for far, side in scatter.order():
            if far == last - hop and far > 0:
                scatter.push(far, side)

    for far in range(line.chips):
        ff_swap.receive(far, lambda source: None)
    ff_recv[me] = ff_share[me]
    own_width = groups * ff_block
    for half, grad_ref in enumerate((gate_grad, up_grad)):
        for index in range(groups):
            for piece in range(pieces):
                start = (index * pieces + piece) * ff_block
                grad_ref[:, pl.ds(start, ff_block)] = ff_recv[
                    piece, :, pl.ds(half * own_width + index * ff_block, ff_block)
                ]

    for shift in range(1, groups):
        peer = lax.rem(group + groups - shift, groups)
        remote(
            term.at[peer], term_in.at[shift], ts_s.at[shift], ts_r.at[shift], "seq", peer
        ).wait_recv()
    for piece in range(pieces):
        across = pl.ds(piece * weight_rows, weight_rows)
        summed = term[group, across, :].astype(full)
        for shift in range(1, groups):
            summed = summed + term_in[shift, across, :].astype(full)
        attn_send[piece] = summed.astype(low)
    attn_swap = LineSwap(
        line, lambda peer: attn_send.at[peer], lambda source: attn_recv.at[source], at_s, at_r
    )
    attn_swap.start()

    scatter.total(total_ref)
    values = hidden[...].astype(full)
    inverse = lax.rsqrt(jnp.mean(values * values, axis=-1, keepdims=True) + epsilon)
    grads = total_ref[...]
    scaled = grads * attention_gain[...]
    hidden_grad[...] = (
        grad_middle[...]
        + inverse * scaled
        - values
        * (inverse * inverse * inverse * jnp.mean(scaled * values, axis=-1, keepdims=True))
    ).astype(low)

    gain_count = gains_grad.shape[1]
    gains_vector[:, pl.ds(0, model)] = jnp.sum(grads * values * inverse, axis=0, keepdims=True)
    gains_vector[:, pl.ds(model, model)] = swiglu_gain_grad[...]
    for kind in range(2):
        wide = jnp.broadcast_to(gain_columns[kind], (HD, HD)).T
        gains_vector[:, pl.ds(2 * model + kind * HD, HD)] = wide[0:1, :]
    gain_give[...] = jnp.zeros(gain_give.shape, full)
    for index in range(groups * pieces):
        gain_give[index % pieces, index // pieces, 0:1, pl.ds(0, gain_count)] = gains_vector[
            :, pl.ds(index * gain_count, gain_count)
        ]
    gain_swap = LineSwap(
        line, lambda peer: gain_give.at[peer], lambda source: gain_sib.at[source], gc_s, gc_r
    )
    gain_swap.start()
    gain_sib[me] = gain_give[me]
    for far in range(line.chips):
        gain_swap.receive(far, lambda source: None)
    gain_row[...] = jnp.sum(gain_sib[...], axis=0)

    def gain_to(shift):
        peer = lax.rem(group + shift, groups)
        return remote(
            gain_row.at[peer], gain_last.at[shift], gs_s.at[shift], gs_r.at[shift], "seq", peer
        )

    for shift in range(1, groups):
        gain_to(shift).start()
    gain_last[0] = gain_row[group]
    for shift in range(1, groups):
        peer = lax.rem(group + groups - shift, groups)
        remote(
            gain_row.at[peer], gain_last.at[shift], gs_s.at[shift], gs_r.at[shift], "seq", peer
        ).wait_recv()
    gains_grad[...] = jnp.sum(gain_last[...], axis=0)[0:1, pl.ds(0, gain_count)]

    for far in range(line.chips):
        attn_swap.receive(far, lambda source: None)
    attn_recv[me] = attn_send[me]
    copies = max(1, pieces // KV)
    for piece in range(pieces):
        query_grad[:, pl.ds(piece * q_width, q_width)] = attn_recv[piece, :, pl.ds(0, q_width)]
        head_grad[:, pl.ds(piece * heads, heads)] = attn_recv[
            piece, :, pl.ds(q_width + 2 * kv_width, heads)
        ].astype(full)
    for place in range(pieces // copies):
        for kind, grad_ref in enumerate((key_grad, value_grad)):
            columns = pl.ds(q_width + kind * kv_width, kv_width)
            summed = attn_recv[place * copies, :, columns].astype(full)
            for copy in range(1, copies):
                summed = summed + attn_recv[place * copies + copy, :, columns].astype(full)
            grad_ref[:, pl.ds(place * kv_width, kv_width)] = summed
    scatter.finish()
    ff_swap.finish()
    attn_swap.finish()
    gain_swap.finish()
    for shift in range(1, groups):
        to_group(shift).wait_send()
        gain_to(shift).wait_send()


def attend_back(
    grad_branch, out_low, saved, tables, gains, prefix, normed, attn_low, hidden, grad_middle,
    attention_gain, swiglu_gain_grad, ff_share, gain_count, shape, number,
):
    pieces, groups, heads, kv_heads, ff_block = shape
    length, (rows, model) = grad_branch.shape[0], hidden.shape
    width = attn_low.shape[1]
    weight_rows = ff_share.shape[1]
    q_width, kv_width = heads * HD, kv_heads * HD
    struct, vmem = jax.ShapeDtypeStruct, pltpu.VMEM
    padded = -(-gain_count // 128) * 128
    return pl.pallas_call(
        functools.partial(attend_back_kernel, shape),
        out_shape=(
            struct((rows, model), low),
            struct((1, gain_count), full),
            struct((weight_rows, H * HD), low),
            struct((weight_rows, KV * HD), full),
            struct((weight_rows, KV * HD), full),
            struct((weight_rows, H), full),
            struct((weight_rows, pieces * groups * ff_block), low),
            struct((weight_rows, pieces * groups * ff_block), low),
        ),
        in_specs=[IN_VMEM] * 15 + [pl.BlockSpec(memory_space=pltpu.SMEM), ANY] + [IN_VMEM] * 6,
        out_specs=(IN_VMEM,) * 8,
        scratch_shapes=[
            vmem((q_width, length), full),
            vmem((HD, length), low),
            vmem((length, HD), low),
            vmem((q_width, length), full),
            vmem((length, kv_width), full),
            vmem((length, kv_width), full),
            vmem((width, length), low),
            vmem((length, width), low),
            vmem((rows, model), full),
            vmem(ff_share.shape, low),
            vmem((2, length, model // groups), low),
            DMA((2,)),
            vmem((groups, model // groups, width), low),
            vmem((groups, model // groups, width), low),
            vmem((pieces, weight_rows, width), low),
            vmem((pieces, weight_rows, width), low),
            vmem((1, 2 * model + 2 * HD), full),
            vmem((pieces, groups, 8, padded), full),
            vmem((pieces, groups, 8, padded), full),
            vmem((groups, 8, padded), full),
            vmem((groups, 8, padded), full),
        ]
        + swap_scratch(pieces) * 3
        + [DMA((groups,))] * 4
        + scatter_scratch(pieces, rows, model),
        compiler_params=pltpu.CompilerParams(
            collective_id=number, has_side_effects=True, vmem_limit_bytes=63 << 20
        ),
        name=f"attend_back_{number}",
    )(
        grad_branch, out_low, *saved, *tables, *gains, prefix, normed, attn_low, hidden, grad_middle,
        attention_gain, swiglu_gain_grad, ff_share,
    )


def feed_kernel(
    shape,
    normed_two,
    ff_low,
    down_low,
    og_all,
    n2_all,
    hidden_ff,
    grad_pre,
    grad_hidden,
    *gather_sems,
):
    pieces = shape[0]
    line = Line(pieces)
    rows, length = normed_two.shape[0], og_all.shape[0]
    own_width = down_low.shape[0]
    tile = own_width // 3 if own_width % 384 == 0 else 128
    greet(line.peers())
    gather = Gather(line, 2, rows, n2_all, gather_sems)
    gather.start(normed_two)
    n2_all[pl.ds(pl.multiple_of(line.me * rows, rows), rows), :] = normed_two[...]

    def backward(index, unused):
        across = pl.ds(pl.multiple_of(index * 256, 256), 256)
        grad_hidden[across, :] = product_nt(og_all[across, :], down_low[...])
        return unused

    lax.fori_loop(0, length // 256, backward, 0)

    def chip_rows(chip):
        across = pl.ds(pl.multiple_of(chip * 2 * rows, 2 * rows), 2 * rows)

        def step(index, unused):
            start = index * tile
            first, second = lanes(start, tile), lanes(own_width + start, tile)
            gate = product(n2_all[across, :], ff_low[:, first])
            up = product(n2_all[across, :], ff_low[:, second])
            grads = grad_hidden[across, first]
            sigmoid = jax.nn.sigmoid(gate)
            silu = gate * sigmoid
            hidden_ff[across, first] = (silu * up).astype(low)
            grad_pre[across, first] = (
                grads * up * (sigmoid * (1.0 + gate * (1.0 - sigmoid)))
            ).astype(low)
            grad_pre[across, second] = (grads * silu).astype(low)
            return unused

        lax.fori_loop(0, own_width // tile, step, 0)

    def compute(far):
        gather.arrive(far)
        if far == 0:
            chip_rows(line.chip)
            return

        @pl.when(line.chip - far >= 0)
        def _():
            chip_rows(line.chip - far)

        @pl.when(line.chip + far < line.chips)
        def _():
            chip_rows(line.chip + far)

    for hop in range(1, line.chips - 1):
        gather.forward(hop)
        compute(hop - 1)
    if line.chips > 1:
        compute(line.chips - 2)
        gather.forward(line.chips - 1)
    compute(line.chips - 1)
    gather.finish()


def feed(normed_two, ff_low, down_low, og_all, shape, number):
    pieces = shape[0]
    length, model = og_all.shape
    own_width = down_low.shape[0]
    struct = jax.ShapeDtypeStruct
    return pl.pallas_call(
        functools.partial(feed_kernel, shape),
        out_shape=(
            struct((length, model), low),
            struct((length, own_width), low),
            struct((length, 2 * own_width), low),
        ),
        in_specs=[IN_VMEM] * 4,
        out_specs=(IN_VMEM,) * 3,
        scratch_shapes=[pltpu.VMEM((length, own_width), full)] + gather_scratch(pieces, 2),
        compiler_params=pltpu.CompilerParams(
            collective_id=number, has_side_effects=True, vmem_limit_bytes=60 << 20
        ),
        name=f"feed_{number}",
    )(normed_two, ff_low, down_low, og_all)


def feed_back_kernel(
    shape,
    grad_pre,
    ff_low,
    hidden_ff,
    down_low,
    og_all,
    n2_all,
    middle,
    out_grad,
    swiglu_gain,
    gb_all,
    grad_middle,
    gain_grad,
    hidden_out,
    ff_share,
    down_term,
    total_ref,
    branch,
    n2_part,
    term,
    term_in,
    part_sem,
    own_sem,
    ts_s,
    ts_r,
    *sems,
):
    pieces, groups = shape[:2]
    buffers, sems = sems[:2], sems[2:]
    gather_sems, sems = sems[:6], sems[6:]
    line = Line(pieces)
    me, group = line.me, lax.axis_index("seq")
    length, rows, model = og_all.shape[0], middle.shape[0], og_all.shape[1]
    weight_rows = ff_share.shape[1]
    greet(line.peers() + others("seq", groups))
    half = len(sems) // 2
    inner = Scatter(line, rows, buffers + sems[:half])
    outer = Scatter(line, rows, buffers + sems[half:])
    block = blocks_nt(grad_pre, ff_low, rows)
    last = line.chips - 1

    def fills(scatter, far, block):
        for distance, side in scatter.order():
            if distance == far:
                scatter.fill(far, side, block)

    def pushes(scatter, far):
        for distance, side in scatter.order():
            if distance == far and far > 0:
                scatter.push(far, side)

    share = model // groups

    def to_group(shift):
        peer = lax.rem(group + shift, groups)
        return remote(
            term.at[peer], term_in.at[shift - 1], ts_s.at[shift], ts_r.at[shift], "seq", peer
        )

    shifts = list(range(1, groups)) + [0]

    def load(job):
        index = lax.rem(group + shifts[job], groups)
        return pltpu.make_async_copy(
            n2_all.at[:, lanes(index * share, share)], n2_part.at[job % 2], part_sem.at[job % 2]
        )

    def ff_grad(job, index):
        load(job).wait()
        if job + 1 < groups:
            load(job + 1).start()

        def step(tile, unused):
            value = product_tn(n2_part[job % 2, :, lanes(tile * 128, 128)], grad_pre[...])
            term[index, pl.ds(pl.multiple_of(tile * 128, 128), 128), :] = value.astype(low)
            return unused

        lax.fori_loop(0, share // 128, step, 0)

    jobs = list(range(groups))

    def some_grads(count):
        for _ in range(min(count, len(jobs))):
            job = jobs.pop(0)
            shift = shifts[job]
            ff_grad(job, lax.rem(group + shift, groups))
            if shift:
                to_group(shift).start()

    load(0).start()
    fills(inner, last, block)
    pushes(inner, last)
    fills(inner, last - 1, block)
    some_grads(1)
    each = -(-(groups - 1) // max(1, last - 1))
    for hop in range(1, line.chips):
        pushes(inner, last - hop)
        if hop < last:
            fills(inner, last - 1 - hop, block)
        some_grads(each)
    some_grads(groups)

    def down_grad(index, unused):
        across = pl.ds(pl.multiple_of(index * 128, 128), 128)
        down_term[across, :] = product_tn(hidden_ff[:, lanes(index * 128, 128)], og_all[...]).astype(
            low
        )
        return unused

    lax.fori_loop(0, down_low.shape[0] // 128, down_grad, 0)
    inner.total(total_ref)
    inner.finish()
    values, grads = middle[...], total_ref[...]
    inverse = lax.rsqrt(jnp.mean(values * values, axis=-1, keepdims=True) + epsilon)
    gain_grad[...] = jnp.sum(grads * values * inverse, axis=0, keepdims=True)
    scaled = grads * swiglu_gain[...]
    result = (
        out_grad[...].astype(full)
        + inverse * scaled
        - values
        * (inverse * inverse * inverse * jnp.mean(scaled * values, axis=-1, keepdims=True))
    )
    grad_middle[...] = result
    branch[...] = result.astype(low)

    gather = Gather(line, 2, rows, gb_all, gather_sems)
    gather.start(branch)
    start = pl.multiple_of(me * rows, rows)
    own = pltpu.make_async_copy(branch, gb_all.at[pl.ds(start, rows)], own_sem)
    own.start()
    block = blocks_nn(hidden_ff, down_low, rows)
    fills(outer, last, block)
    pushes(outer, last)
    fills(outer, last - 1, block)
    for hop in range(1, line.chips):
        gather.forward(hop)
        pushes(outer, last - hop)
        if hop < last:
            fills(outer, last - 1 - hop, block)
    for shift in range(1, groups):
        peer = lax.rem(group + groups - shift, groups)
        remote(
            term.at[peer], term_in.at[shift - 1], ts_s.at[shift], ts_r.at[shift], "seq", peer
        ).wait_recv()
    for piece in range(pieces):
        across = pl.ds(piece * weight_rows, weight_rows)
        summed = term[group, across, :].astype(full)
        for shift in range(1, groups):
            summed = summed + term_in[shift - 1, across, :].astype(full)
        ff_share[piece] = summed.astype(low)
    outer.total(total_ref)
    hidden_out[...] = (middle[...] + total_ref[...]).astype(low)
    own.wait()
    for hop in range(line.chips):
        gather.arrive(hop)
    gather.finish()
    outer.finish()
    for shift in range(1, groups):
        to_group(shift).wait_send()


def feed_back(
    grad_pre, ff_low, hidden_ff, down_low, og_all, n2_all, middle, out_grad, swiglu_gain, shape, number
):
    pieces, groups = shape[:2]
    length, (rows, model) = og_all.shape[0], middle.shape
    own_width, width = hidden_ff.shape[1], grad_pre.shape[1]
    weight_rows = model // (groups * pieces)
    struct, vmem = jax.ShapeDtypeStruct, pltpu.VMEM
    scatter = scatter_scratch(pieces, rows, model)
    return pl.pallas_call(
        functools.partial(feed_back_kernel, shape),
        out_shape=(
            struct((length, model), low),
            struct((rows, model), full),
            struct((1, model), full),
            struct((rows, model), low),
            struct((pieces, weight_rows, width), low),
            struct((own_width, model), low),
        ),
        in_specs=[IN_VMEM] * 5 + [ANY] + [IN_VMEM] * 3,
        out_specs=(ANY,) + (IN_VMEM,) * 5,
        scratch_shapes=[
            vmem((rows, model), full),
            vmem((rows, model), low),
            vmem((2, length, model // groups), low),
            vmem((groups, model // groups, width), low),
            vmem((groups - 1, model // groups, width), low),
            DMA((2,)),
            DMA,
            DMA((groups,)),
            DMA((groups,)),
        ]
        + scatter[:2]
        + gather_scratch(pieces, 2)
        + scatter[2:] * 2,
        compiler_params=pltpu.CompilerParams(
            collective_id=number, has_side_effects=True, vmem_limit_bytes=63 << 20
        ),
        name=f"feed_back_{number}",
    )(grad_pre, ff_low, hidden_ff, down_low, og_all, n2_all, middle, out_grad, swiglu_gain)


def gather_seq(block):
    return lax.all_gather(block, "seq", axis=0, tiled=True)


def scatter_seq(block):
    return lax.psum_scatter(block.astype(low), "seq", scatter_dimension=0, tiled=True)


def on_device(
    hidden_in,
    out_grad,
    prefix_len,
    norm_gains,
    query_weight,
    key_weight,
    value_weight,
    head_gate_weight,
    out_weight,
    gate_weight,
    up_weight,
    down_weight,
):
    row_count, model = hidden_in.shape
    groups = lax.axis_size("seq")
    pieces = lax.axis_size("ctx")
    length = row_count * pieces
    weight_rows = query_weight.shape[0]
    heads = H // pieces
    kv_heads = max(1, KV // pieces)
    copies = max(1, pieces // KV)
    ff_block = down_weight.shape[0]
    ff_own = ff_block * groups
    q_width, kv_width = heads * HD, kv_heads * HD
    gain_count = norm_gains.shape[0]
    attn_width = q_width + 2 * kv_width + HD
    shape = (pieces, groups, heads, kv_heads, ff_block)

    def kv_columns(weight):
        columns = weight.astype(low).reshape(weight_rows, KV, HD)
        return jnp.repeat(columns, copies, axis=1).reshape(weight_rows, pieces, kv_width)

    attn_blocks = jnp.concatenate(
        [
            query_weight.astype(low).reshape(weight_rows, pieces, q_width),
            kv_columns(key_weight),
            kv_columns(value_weight),
            head_gate_weight.astype(low).reshape(weight_rows, pieces, heads),
            jnp.zeros((weight_rows, pieces, HD - heads), low),
        ],
        axis=-1,
    ).transpose(1, 0, 2)
    normed, attn_low, gains_full = opening(hidden_in, norm_gains, attn_blocks, 0)
    attn_low = attn_low.reshape(model, attn_width)
    down_low = gather_seq(down_weight.astype(low))
    spread = [(i, (i % groups) * pieces + i // groups) for i in range(groups * pieces)]
    collect = [(target, source) for source, target in spread]
    out_low = gather_seq(lax.ppermute(out_weight.astype(low), ("seq", "ctx"), spread))
    attention_gain = gains_full[:, :model]
    swiglu_gain = gains_full[:, model : 2 * model]
    head_gains = (
        gains_full[0, 2 * model : 2 * model + HD, None],
        gains_full[0, 2 * model + HD :, None],
    )
    inverse = rope_base ** (-jnp.arange(HD // 2, dtype=full) * 2.0 / HD)
    angles = inverse[:, None] * jnp.arange(length, dtype=jnp.int32).astype(full)[None, :]
    tables = (jnp.cos(angles), jnp.sin(angles))
    prefix = prefix_len.reshape(1, 1)

    raw = product(normed, attn_low)
    *saved, gated_t, middle, normed_two, out_grad_all, ff_low = attend(
        raw,
        tables,
        head_gains,
        prefix,
        out_low,
        hidden_in,
        swiglu_gain,
        out_grad,
        (gate_weight, up_weight),
        shape,
        1,
    )
    ff_low = ff_low.reshape(model, 2 * ff_own)
    n2_all, hidden_ff, grad_pre = feed(normed_two, ff_low, down_low, out_grad_all, shape, 2)
    grad_branch, grad_middle, swiglu_gain_grad, hidden_out, ff_share, down_term = feed_back(
        grad_pre, ff_low, hidden_ff, down_low, out_grad_all, n2_all, middle, out_grad, swiglu_gain, shape, 3
    )
    down_share = scatter_seq(down_term).astype(full)
    output_share = lax.ppermute(
        scatter_seq(product(gated_t, grad_branch)), ("seq", "ctx"), collect
    ).astype(full)
    hidden_grad, gains_share, query_share, key_share, value_share, head_share, gate_share, up_share = (
        attend_back(
            grad_branch,
            out_low,
            saved,
            tables,
            head_gains,
            prefix,
            normed,
            attn_low,
            hidden_in,
            grad_middle,
            attention_gain,
            swiglu_gain_grad,
            ff_share,
            gain_count,
            shape,
            4,
        )
    )
    return (
        hidden_out,
        hidden_grad,
        gains_share.reshape(gain_count),
        query_share.astype(full),
        key_share,
        value_share,
        head_share,
        output_share,
        gate_share.astype(full),
        up_share.astype(full),
        down_share,
    )


def solution(mesh):
    rows = P(("seq", "ctx"), None)
    return jax.shard_map(
        on_device,
        mesh=mesh,
        in_specs=(rows, rows, P("seq"), P(("seq", "ctx"))) + (rows,) * 8,
        out_specs=(rows, rows, P(("seq", "ctx"))) + (rows,) * 8,
        check_vma=False,
    )
```

```python
import functools
import math

import jax
import jax.numpy as jnp
from jax import lax
from jax.experimental import pallas as pl
from jax.experimental.pallas import tpu as pltpu
from jax.sharding import PartitionSpec as P

H = 16
KV = 8
HD = 128


epsilon = 1e-06
rope_base = 1000000.0
negative = -1e30
low = jnp.bfloat16
full = jnp.float32
MESH = pl.DeviceIdType.MESH
ANY = pl.BlockSpec(memory_space=pl.ANY)
IN_VMEM = pl.BlockSpec(memory_space=pltpu.VMEM)
DMA = pltpu.SemaphoreType.DMA


def product(left_side, right_side):
    return jnp.dot(left_side, right_side, preferred_element_type=full)


def product_nt(left_side, right_side):
    return lax.dot_general(
        left_side, right_side, (((1,), (1,)), ((), ())), preferred_element_type=full
    )


def product_tn(left_side, right_side):
    return lax.dot_general(
        left_side, right_side, (((0,), (0,)), ((), ())), preferred_element_type=full
    )


def remote(source, target, send, receive, axis, peer):
    return pltpu.make_async_remote_copy(
        src_ref=source,
        dst_ref=target,
        send_sem=send,
        recv_sem=receive,
        device_id={axis: peer},
        device_id_type=MESH,
    )


def greet(peers):
    barrier = pltpu.get_barrier_semaphore()
    for axis, peer, exists in peers:
        place = {"seq": peer[0], "ctx": peer[1]} if axis is None else {axis: peer}

        def signal():
            pl.semaphore_signal(barrier, inc=1, device_id=place, device_id_type=MESH)

        if exists is True:
            signal()
        else:
            pl.when(exists)(signal)

    arrivals = sum(1 for _, _, exists in peers if exists is True)
    for _, _, exists in peers:
        if exists is not True:
            arrivals = arrivals + exists.astype(jnp.int32)
    pl.semaphore_wait(barrier, arrivals)


def others(axis, count):
    me = lax.axis_index(axis)
    return [(axis, lax.rem(me + shift, count), True) for shift in range(1, count)]


class Line:
    def __init__(self, pieces):
        self.chips = pieces // 2
        self.me = lax.axis_index("ctx")
        self.chip, self.core = self.me // 2, lax.rem(self.me, 2)
        self.sibling = self.me + 1 - 2 * self.core
        self.right, self.left = self.me + 2, self.me - 2
        self.has_right, self.has_left = self.chip < self.chips - 1, self.chip > 0

    def peers(self):
        return [
            ("ctx", self.sibling, True),
            ("ctx", self.right, self.has_right),
            ("ctx", self.left, self.has_left),
        ]


def gather_scratch(pieces, parts):
    chips = pieces // 2
    return [DMA((chips, 2, parts))] * 2 + [DMA((chips, parts))] * 4


class Gather:
    def __init__(self, line, parts, rows, out_ref, sems):
        self.line, self.parts, self.rows, self.out_ref = line, parts, rows, out_ref
        self.size = rows // parts
        self.sib_send, self.sib_recv, self.r_send, self.r_recv, self.l_send, self.l_recv = sems

    def at(self, position, part):
        start = pl.multiple_of(position * self.rows + part * self.size, self.size)
        return self.out_ref.at[pl.ds(start, self.size)]

    def to_sibling(self, source, hop, side, part, position):
        return remote(
            source,
            self.at(position, part),
            self.sib_send.at[hop, side, part],
            self.sib_recv.at[hop, side, part],
            "ctx",
            self.line.sibling,
        )

    def to_right(self, source, hop, part, position):
        return remote(
            source,
            self.at(position, part),
            self.r_send.at[hop, part],
            self.r_recv.at[hop, part],
            "ctx",
            self.line.right,
        )

    def to_left(self, source, hop, part, position):
        return remote(
            source,
            self.at(position, part),
            self.l_send.at[hop, part],
            self.l_recv.at[hop, part],
            "ctx",
            self.line.left,
        )

    def start(self, x_ref):
        line = self.line
        for part in range(self.parts):
            piece = x_ref.at[pl.ds(part * self.size, self.size)]

            @pl.when(line.has_right)
            def _():
                self.to_right(piece, 0, part, line.me).start()

            @pl.when(line.has_left)
            def _():
                self.to_left(piece, 0, part, line.me).start()

            self.to_sibling(piece, 0, 0, part, line.me).start()

    def forward(self, hop):
        line = self.line
        for part in range(self.parts):
            from_left, from_right = line.me - 2 * hop, line.me + 2 * hop

            @pl.when(line.chip - hop >= 0)
            def _():
                piece = self.at(from_left, part)
                self.to_right(piece, hop - 1, part, from_left).wait_recv()

                @pl.when(line.has_right)
                def _():
                    self.to_right(piece, hop, part, from_left).start()

                self.to_sibling(piece, hop, 0, part, from_left).start()

            @pl.when(line.chip + hop < line.chips)
            def _():
                piece = self.at(from_right, part)
                self.to_left(piece, hop - 1, part, from_right).wait_recv()

                @pl.when(line.has_left)
                def _():
                    self.to_left(piece, hop, part, from_right).start()

                self.to_sibling(piece, hop, 1, part, from_right).start()

    def legs(self, hop):
        line = self.line
        return [
            (
                side,
                (line.chip - hop >= 0) if side == 0 else (line.chip + hop < line.chips),
                (line.me - 2 * hop) if side == 0 else (line.me + 2 * hop),
            )
            for side in range(1 if hop == 0 else 2)
        ]

    def arrive(self, hop):
        for side, there, position in self.legs(hop):
            for part in range(self.parts):

                @pl.when(there)
                def _():
                    self.to_sibling(
                        self.at(position, part), hop, side, part, position
                    ).wait_recv()

    def finish(self):
        line = self.line
        for hop in range(line.chips):
            for side, there, position in self.legs(hop):
                for part in range(self.parts):

                    @pl.when(there)
                    def _():
                        piece = self.at(position, part)
                        self.to_sibling(piece, hop, side, part, position).wait_send()
                        if side == 0:

                            @pl.when(line.has_right)
                            def _():
                                self.to_right(piece, hop, part, position).wait_send()

                        if side == 1 or hop == 0:

                            @pl.when(line.has_left)
                            def _():
                                self.to_left(piece, hop, part, position).wait_send()

    def complete(self):
        for hop in range(self.line.chips):
            self.arrive(hop)
        self.finish()


def scatter_scratch(pieces, rows, width):
    chips = pieces // 2
    slots = pltpu.VMEM((chips, rows, width), low)
    return [slots] * 3 + [pltpu.VMEM((chips + 1, rows, width), low)] + [DMA((chips,))] * 6


class Scatter:
    def __init__(self, line, rows, scratch):
        self.line, self.rows = line, rows
        (
            self.own,
            self.give,
            self.sib,
            self.arrived,
            self.sib_send,
            self.sib_recv,
            self.r_send,
            self.r_recv,
            self.l_send,
            self.l_recv,
        ) = scratch

    def there(self, far, side):
        line = self.line
        return (line.chip + far < line.chips) if side == 0 else (line.chip - far >= 0)

    def target(self, far, side):
        return self.line.chip + far if side == 0 else self.line.chip - far

    def exchange(self, target):
        return remote(
            self.give.at[target],
            self.sib.at[target],
            self.sib_send.at[target],
            self.sib_recv.at[target],
            "ctx",
            self.line.sibling,
        )

    def send(self, target, side):
        if side == 0:
            return remote(
                self.own.at[target],
                self.arrived.at[target],
                self.r_send.at[target],
                self.r_recv.at[target],
                "ctx",
                self.line.right,
            )
        chips, chip = self.line.chips, self.line.chip
        return remote(
            self.own.at[target],
            self.arrived.at[jnp.where(target == chip - 1, chips, target)],
            self.l_send.at[target],
            self.l_recv.at[target],
            "ctx",
            self.line.left,
        )

    def order(self):
        return [
            (far, side)
            for far in range(self.line.chips - 1, -1, -1)
            for side in range(2 if far else 1)
        ]

    def fill(self, far, side, block):
        @pl.when(self.there(far, side))
        def _():
            target = self.target(far, side)

            def store(columns, value):
                first, second = value[: self.rows], value[self.rows :]
                mine = self.line.core == 0
                self.own[target, :, columns] = jnp.where(mine, first, second).astype(low)
                self.give[target, :, columns] = jnp.where(mine, second, first).astype(low)

            block(target, store)
            self.exchange(target).start()

    def push(self, far, side):
        line = self.line
        behind = line.has_left if side == 0 else line.has_right

        @pl.when(self.there(far, side))
        def _():
            target = self.target(far, side)
            self.exchange(target).wait_recv()
            total = self.own[target].astype(full) + self.sib[target].astype(full)
            if far == line.chips - 1:
                self.own[target] = total.astype(low)
            else:

                @pl.when(behind)
                def _():
                    self.send(target, side).wait_recv()
                    self.own[target] = (total + self.arrived[target].astype(full)).astype(low)

                @pl.when(jnp.logical_not(behind))
                def _():
                    self.own[target] = total.astype(low)

            self.send(target, side).start()

    def total(self, total_ref):
        line = self.line
        chip = line.chip
        self.exchange(chip).wait_recv()
        total_ref[...] = self.own[chip].astype(full) + self.sib[chip].astype(full)

        @pl.when(line.has_left)
        def _():
            self.send(chip, 0).wait_recv()
            total_ref[...] += self.arrived[chip].astype(full)

        @pl.when(line.has_right)
        def _():
            self.send(chip, 1).wait_recv()
            total_ref[...] += self.arrived[line.chips].astype(full)

    def finish(self):
        for far, side in self.order():

            @pl.when(self.there(far, side))
            def _():
                target = self.target(far, side)
                self.exchange(target).wait_send()
                if far > 0:
                    self.send(target, side).wait_send()


def blocks_nn(left_ref, right_ref, rows, tile=512):
    def block(target, store):
        start = pl.multiple_of(target * 2 * rows, 2 * rows)
        left_side = left_ref[pl.ds(start, 2 * rows), :]

        def step(index, unused):
            columns = pl.ds(pl.multiple_of(index * tile, tile), tile)
            store(columns, product(left_side, right_ref[:, columns]))
            return unused

        lax.fori_loop(0, right_ref.shape[1] // tile, step, 0)

    return block


def blocks_nt(left_ref, right_ref, rows, tile=512):
    def block(target, store):
        start = pl.multiple_of(target * 2 * rows, 2 * rows)
        left_side = left_ref[pl.ds(start, 2 * rows), :]

        def step(index, unused):
            columns = pl.ds(pl.multiple_of(index * tile, tile), tile)
            store(columns, product_nt(left_side, right_ref[columns, :]))
            return unused

        lax.fori_loop(0, right_ref.shape[0] // tile, step, 0)

    return block


class LineSwap:
    def __init__(self, line, send_of, recv_of, s_sem, r_sem):
        self.line, self.send_of, self.recv_of = line, send_of, recv_of
        self.s_sem, self.r_sem = s_sem, r_sem

    def copy(self, far, side, core):
        line = self.line
        if far == 0:
            peer, slot = line.sibling, self.r_sem.at[0, 0, 0]
        else:
            peer = (line.chip + (far if side == 0 else -far)) * 2 + core
            slot = self.r_sem.at[far, side, line.core]
        return remote(
            self.send_of(peer), self.recv_of(line.me), self.s_sem.at[far, side, core], slot, "ctx", peer
        )

    def legs(self, far):
        line = self.line
        if far == 0:
            return [(0, 0, True, True)]
        return [
            (
                side,
                core,
                (line.chip + far < line.chips) if side == 0 else (line.chip - far >= 0),
                (line.chip - far >= 0) if side == 0 else (line.chip + far < line.chips),
            )
            for side in range(2)
            for core in range(2)
        ]

    def start(self):
        for far in range(self.line.chips):
            for side, core, sends, _ in self.legs(far):
                if far == 0:
                    self.copy(far, side, core).start()
                else:

                    @pl.when(sends)
                    def _():
                        self.copy(far, side, core).start()

    def receive(self, far, then):
        line = self.line
        for side, core, _, comes in self.legs(far):
            if far == 0:
                source, slot = line.sibling, self.r_sem.at[0, 0, 0]
            else:
                source = (line.chip + (-far if side == 0 else far)) * 2 + core
                slot = self.r_sem.at[far, side, core]

            def wait():
                remote(
                    self.recv_of(source),
                    self.recv_of(source),
                    self.s_sem.at[far, side, core],
                    slot,
                    "ctx",
                    source,
                ).wait_recv()
                then(source)

            if far == 0:
                wait()
            else:
                pl.when(comes)(wait)

    def again(self, far, then):
        line = self.line
        for side, core, _, comes in self.legs(far):
            if far == 0:
                then(line.sibling)
            else:
                source = (line.chip + (-far if side == 0 else far)) * 2 + core

                @pl.when(comes)
                def _():
                    then(source)

    def finish(self):
        for far in range(self.line.chips):
            for side, core, sends, _ in self.legs(far):
                if far == 0:
                    self.copy(far, side, core).wait_send()
                else:

                    @pl.when(sends)
                    def _():
                        self.copy(far, side, core).wait_send()


def swap_scratch(pieces):
    return [DMA((pieces // 2, 2, 2))] * 2


class Share:
    def __init__(self, groups, place, s_sem, r_sem):
        self.groups, self.place, self.s_sem, self.r_sem = groups, place, s_sem, r_sem
        self.group = lax.axis_index("seq")
        self.square = groups == 4
        self.across = self.group + 1 - 2 * lax.rem(self.group, 2)
        self.along = lax.rem(self.group + 2, groups)
        self.corner = groups - 1 - self.group

    def copy(self, source, slot, peer, origin, target):
        return remote(
            origin, target, self.s_sem.at[source, slot], self.r_sem.at[source, slot], "seq", peer
        )

    def half(self, index, source, which):
        ref = self.place(index, source)
        rows = ref.shape[0] // 2
        return ref.at[pl.ds(which * rows, rows)]

    def first(self, source, origin=None):
        target = self.place(self.group, source)
        origin = target if origin is None else origin
        if self.square:
            peers = [(1, self.across), (2, self.along)]
        else:
            peers = [
                (shift, lax.rem(self.group + shift, self.groups)) for shift in range(1, self.groups)
            ]
        return [self.copy(source, slot, peer, origin, target) for slot, peer in peers]

    def second(self, source):
        one, two = self.half(self.across, source, 0), self.half(self.along, source, 1)
        return [
            self.copy(source, 3, self.along, one, one),
            self.copy(source, 0, self.across, two, two),
        ]

    def send(self, source, origin=None):
        for copy in self.first(source, origin):
            copy.start()

    def relay(self, source):
        if not self.square:
            return
        for slot, index, copy in zip((1, 2), (self.across, self.along), self.second(source)):
            block = self.place(index, source)
            self.copy(source, slot, index, block, block).wait_recv()
            copy.start()

    def finish(self, sources):
        for source in range(sources):
            if self.square:
                for slot, which in ((3, 0), (0, 1)):
                    half = self.half(self.corner, source, which)
                    self.copy(source, slot, self.corner, half, half).wait_recv()
                for copy in self.second(source):
                    copy.wait_send()
            else:
                for shift in range(1, self.groups):
                    index = lax.rem(self.group + self.groups - shift, self.groups)
                    block = self.place(index, source)
                    self.copy(source, shift, index, block, block).wait_recv()
            for copy in self.first(source):
                copy.wait_send()


class Fold:
    def __init__(self, groups, term_ref, inbox, s_sem, r_sem):
        self.groups, self.term, self.inbox = groups, term_ref, inbox
        self.s_sem, self.r_sem = s_sem, r_sem
        self.group = group = lax.axis_index("seq")
        self.square = groups == 4
        self.rows = term_ref.shape[1]
        if self.square:
            self.across = group + 1 - 2 * lax.rem(group, 2)
            self.along = lax.rem(group + 2, groups)
            self.order = [groups - 1 - group, self.across, self.along, group]
        else:
            self.order = [lax.rem(group + shift, groups) for shift in range(1, groups)] + [group]

    def part(self, which):
        return pl.ds(which * (self.rows // 2), self.rows // 2)

    def copies(self, job):
        index = self.order[job]
        block = self.term.at[index]
        if not self.square:
            return [self.copy(job, block, self.inbox.at[job], index)]
        if job == 0:
            return [
                self.copy(0, block.at[self.part(0)], self.inbox.at[0, self.part(0)], self.across),
                self.copy(3, block.at[self.part(1)], self.inbox.at[0, self.part(1)], self.along),
            ]
        return [self.copy(job, block, self.inbox.at[job], index)]

    def copy(self, slot, source, target, peer):
        return remote(source, target, self.s_sem.at[slot], self.r_sem.at[slot], "seq", peer)

    def ready(self, job):
        if job < self.groups - 1 and (job == 0 or not self.square):
            for copy in self.copies(job):
                copy.start()

    def mix(self):
        if not self.square:
            return
        to_across, to_along = self.copies(0)
        to_across.wait_recv()
        mine, half = self.along, self.part(0)
        self.term[mine, half, :] = (
            self.term[mine, half, :].astype(full) + self.inbox[0, half, :].astype(full)
        ).astype(low)
        self.copies(2)[0].start()
        to_along.wait_recv()
        mine, half = self.across, self.part(1)
        self.term[mine, half, :] = (
            self.term[mine, half, :].astype(full) + self.inbox[0, half, :].astype(full)
        ).astype(low)
        self.copies(1)[0].start()

    def arrive(self):
        for job in range(1 if self.square else 0, self.groups - 1):
            self.copies(job)[0].wait_recv()

    def sum(self, across):
        total = self.term[self.group, across, :].astype(full)
        for job in range(1 if self.square else 0, self.groups - 1):
            total = total + self.inbox[job, across, :].astype(full)
        return total

    def finish(self):
        for job in range(self.groups - 1):
            for copy in self.copies(job):
                copy.wait_send()


class Spread:
    def __init__(self, groups, pieces):
        group, me = lax.axis_index("seq"), lax.axis_index("ctx")
        flat = group * pieces + me
        self.use = (lax.rem(flat, groups), flat // groups)
        held = me * groups + group
        self.rest = (held // pieces, lax.rem(held, pieces))
        self.moves = jnp.logical_or(self.use[0] != group, self.use[1] != me)

    def peers(self):
        return [(None, self.use, self.moves), (None, self.rest, self.moves)]

    def copy(self, source, target, send, receive, back):
        place = self.rest if back else self.use
        return pltpu.make_async_remote_copy(
            src_ref=source,
            dst_ref=target,
            send_sem=send,
            recv_sem=receive,
            device_id={"seq": place[0], "ctx": place[1]},
            device_id_type=MESH,
        )


def opening_kernel(
    shape,
    parts,
    hidden,
    gains_ref,
    query_weight,
    key_weight,
    value_weight,
    gate_weight,
    out_weight,
    normed,
    raw,
    attn_low,
    gains_out,
    out_low,
    hidden_all,
    blocks,
    out_block,
    gains_row,
    gains_all,
    own_attn,
    own_out,
    out_s,
    out_r,
    ga_s,
    ga_r,
    gs_s,
    gs_r,
    at_s,
    at_r,
    as_s,
    as_r,
    os_s,
    os_r,
    *gather_sems,
):
    pieces, groups, heads, kv_heads, _ = shape
    line = Line(pieces)
    me, group = line.me, lax.axis_index("seq")
    rows, model = hidden.shape
    weight_rows = out_weight.shape[0]
    q_width, kv_width = heads * HD, kv_heads * HD
    copies = max(1, pieces // KV)
    spread = Spread(groups, pieces)
    greet(others("ctx", pieces) + others("seq", groups) + spread.peers())
    gain_count = gains_ref.shape[1]
    gains_row[...] = jnp.zeros(gains_row.shape, full)
    gains_row[0:1, pl.ds(0, gain_count)] = gains_ref[...].astype(low).astype(full)
    gains_all[group, me] = gains_row[...]
    gain_swap = LineSwap(
        line, lambda peer: gains_row, lambda source: gains_all.at[group, source], ga_s, ga_r
    )
    gain_swap.start()

    blocks[:, :, pl.ds(q_width + 2 * kv_width, HD)] = jnp.zeros((pieces, weight_rows, HD), low)
    for piece in range(pieces):
        blocks[piece, :, pl.ds(0, q_width)] = query_weight[
            :, pl.ds(piece * q_width, q_width)
        ].astype(low)
        start = piece // copies * kv_width
        blocks[piece, :, pl.ds(q_width, kv_width)] = key_weight[:, pl.ds(start, kv_width)].astype(low)
        blocks[piece, :, pl.ds(q_width + kv_width, kv_width)] = value_weight[
            :, pl.ds(start, kv_width)
        ].astype(low)
        blocks[piece, :, pl.ds(q_width + 2 * kv_width, heads)] = gate_weight[
            :, pl.ds(piece * heads, heads)
        ].astype(low)

    def place(index, source):
        start = pl.multiple_of((index * pieces + source) * weight_rows, weight_rows)
        return attn_low.at[pl.ds(start, weight_rows)]

    attn_swap = LineSwap(
        line, lambda peer: blocks.at[peer], lambda source: place(group, source), at_s, at_r
    )
    attn_swap.start()
    share = Share(groups, place, as_s, as_r)
    share.send(me, blocks.at[me])
    attn_own = pltpu.make_async_copy(blocks.at[me], place(group, me), own_attn)
    attn_own.start()
    gather = Gather(line, parts, rows, hidden_all, gather_sems)
    gather.start(hidden)
    hidden_all[pl.ds(pl.multiple_of(me * rows, rows), rows), :] = hidden[...]
    out_block[...] = out_weight[...].astype(low)

    def out_place(index):
        return out_low.at[pl.ds(pl.multiple_of(index * weight_rows, weight_rows), weight_rows)]

    out_move = spread.copy(out_block, out_place(spread.use[0]), out_s, out_r, False)
    out_stay = pltpu.make_async_copy(out_block, out_place(group), own_out)

    @pl.when(spread.moves)
    def _():
        out_move.start()

    @pl.when(jnp.logical_not(spread.moves))
    def _():
        out_stay.start()

    def to_groups(shift):
        peer = lax.rem(group + shift, groups)
        return remote(
            gains_all.at[group], gains_all.at[group], gs_s.at[shift], gs_r.at[shift], "seq", peer
        )

    def from_groups(shift):
        peer = lax.rem(group + groups - shift, groups)
        return remote(
            gains_all.at[peer], gains_all.at[peer], gs_s.at[shift], gs_r.at[shift], "seq", peer
        )

    attn_swap.receive(0, share.send)
    for far in range(line.chips):
        gain_swap.receive(far, lambda source: None)
    for shift in range(1, groups):
        to_groups(shift).start()
    if line.chips > 1:
        attn_swap.receive(1, share.send)
    for shift in range(1, groups):
        from_groups(shift).wait_recv()
    for index in range(groups * pieces):
        gains_out[0:1, pl.ds(index * gain_count, gain_count)] = gains_all[
            index // pieces, index % pieces, 0:1, pl.ds(0, gain_count)
        ]

    def chip_rows(chip):
        return pl.ds(pl.multiple_of(chip * 2 * rows, 2 * rows), 2 * rows)

    def both(far, body):
        if far == 0:
            body(chip_rows(line.chip))
            return

        @pl.when(line.chip - far >= 0)
        def _():
            body(chip_rows(line.chip - far))

        @pl.when(line.chip + far < line.chips)
        def _():
            body(chip_rows(line.chip + far))

    def normalise(across):
        values = hidden_all[across, :].astype(full)
        inverse = lax.rsqrt(jnp.mean(values * values, axis=-1, keepdims=True) + epsilon)
        normed[across, :] = (values * inverse * gains_out[0:1, pl.ds(0, model)]).astype(low)

    def project(across):
        raw[across, :] = product(normed[across, :], attn_low[...])

    share.relay(me)
    attn_swap.again(0, share.relay)
    for far in range(2, line.chips):
        attn_swap.receive(far, share.send)
        attn_swap.again(far - 1, share.relay)
    out_share = Share(groups, lambda index, source: out_place(index), os_s, os_r)

    @pl.when(spread.moves)
    def _():
        spread.copy(out_place(group), out_place(group), out_s, out_r, False).wait_recv()

    @pl.when(jnp.logical_not(spread.moves))
    def _():
        out_stay.wait()

    out_share.send(0)
    if line.chips > 1:
        attn_swap.again(line.chips - 1, share.relay)
    for hop in range(1, line.chips - 1):
        gather.forward(hop)
        gather.arrive(hop - 1)
        both(hop - 1, normalise)
    gather.arrive(line.chips - 2)
    both(line.chips - 2, normalise)
    attn_own.wait()
    out_share.relay(0)
    share.finish(pieces)
    for far in range(line.chips - 1):
        both(far, project)
    gather.forward(line.chips - 1)
    gather.arrive(line.chips - 1)
    both(line.chips - 1, normalise)
    both(line.chips - 1, project)
    out_share.finish(1)
    gather.finish()
    gain_swap.finish()
    attn_swap.finish()
    for shift in range(1, groups):
        to_groups(shift).wait_send()

    @pl.when(spread.moves)
    def _():
        out_move.wait_send()


def opening(hidden, norm_gains, weights, shape, number, parts=2):
    pieces, groups, heads, kv_heads, _ = shape
    rows, model = hidden.shape
    weight_rows = weights[0].shape[0]
    gains = norm_gains.shape[0]
    padded = -(-gains // 128) * 128
    width = (heads + 2 * kv_heads + 1) * HD
    struct, vmem = jax.ShapeDtypeStruct, pltpu.VMEM
    return pl.pallas_call(
        functools.partial(opening_kernel, shape, parts),
        out_shape=(
            struct((pieces * rows, model), low),
            struct((pieces * rows, width), full),
            struct((model, width), low),
            struct((1, groups * pieces * gains), full),
            struct((groups * weight_rows, model), low),
        ),
        in_specs=[IN_VMEM] * 7,
        out_specs=(IN_VMEM,) * 5,
        scratch_shapes=[
            vmem((pieces * rows, model), low),
            vmem((pieces, weight_rows, width), low),
            vmem((weight_rows, model), low),
            vmem((8, padded), full),
            vmem((groups, pieces, 8, padded), full),
        ]
        + [DMA] * 4
        + swap_scratch(pieces)
        + [DMA((groups,))] * 2
        + swap_scratch(pieces)
        + [DMA((pieces, groups))] * 2
        + [DMA((1, groups))] * 2
        + gather_scratch(pieces, parts),
        compiler_params=pltpu.CompilerParams(
            collective_id=number, has_side_effects=True, vmem_limit_bytes=60 << 20
        ),
        name=f"opening_{number}",
    )(hidden, norm_gains.reshape(1, gains), *weights)


def lanes(start, size):
    return pl.ds(pl.multiple_of(start, 128), size)


def turn(values, cosine, sine):
    half = values.shape[0] // 2
    first, second = values[:half], values[half:]
    return jnp.concatenate(
        [first * cosine - second * sine, second * cosine + first * sine], axis=0
    )


def turn_back(values, cosine, sine):
    half = values.shape[0] // 2
    first, second = values[:half], values[half:]
    return jnp.concatenate(
        [first * cosine + second * sine, second * cosine - first * sine], axis=0
    )


def inverse_rms(values):
    return lax.rsqrt(jnp.mean(values * values, axis=0, keepdims=True) + epsilon)


def kept(first_key, keys, first_query, queries, prefix):
    key = first_key + lax.broadcasted_iota(jnp.int32, (keys, queries), 0)
    query = first_query + lax.broadcasted_iota(jnp.int32, (keys, queries), 1)
    return key <= jnp.maximum(query, prefix - 1)


def query_blocks(length, body):
    tile = min(256, length // 2)
    half = length // 2

    def early(index, unused):
        body(index * tile, tile, half)
        return unused

    def late(index, unused):
        body(half + index * tile, tile, length)
        return unused

    lax.fori_loop(0, half // tile, early, 0)
    lax.fori_loop(0, half // tile, late, 0)


def attend_kernel(
    shape,
    raw,
    cosine,
    sine,
    query_gain,
    key_gain,
    prefix_ref,
    out_low,
    hidden,
    swiglu_gain,
    out_grad,
    gate_weight,
    up_weight,
    down_weight,
    raw_t,
    gate_t,
    q_ref,
    qt_ref,
    k_ref,
    kt_ref,
    v_ref,
    att_t,
    lse_ref,
    gated_t,
    middle,
    normed_two,
    og_all,
    ff_low,
    down_low,
    vt_ref,
    gated,
    blocks,
    down_block,
    down_sem,
    own_sem,
    og_sem,
    swap_s,
    swap_r,
    share_s,
    share_r,
    down_s,
    down_r,
    *sems,
):
    pieces, groups, heads, kv_heads, ff_block = shape
    gather_sems, scatter_refs = sems[:6], sems[6:]
    line = Line(pieces)
    me, group = line.me, lax.axis_index("seq")
    length, rows = raw.shape[0], hidden.shape[0]
    greet(others("ctx", pieces) + others("seq", groups))
    own_width = groups * ff_block
    for half, weight_ref in enumerate((gate_weight, up_weight)):
        for index in range(groups):
            for piece in range(pieces):
                start = (index * pieces + piece) * ff_block
                blocks[piece, :, pl.ds(half * own_width + index * ff_block, ff_block)] = weight_ref[
                    :, pl.ds(start, ff_block)
                ].astype(low)
    swap = LineSwap(
        line, lambda peer: blocks.at[peer], lambda source: ff_low.at[group, source], swap_s, swap_r
    )
    swap.start()
    share = Share(groups, lambda index, source: ff_low.at[index, source], share_s, share_r)
    share.send(me, blocks.at[me])
    own = pltpu.make_async_copy(blocks.at[me], ff_low.at[group, me], own_sem)
    own.start()
    down_block[...] = down_weight[...].astype(low)

    def down_place(index, source):
        start = pl.multiple_of(index * ff_block, ff_block)
        return down_low.at[pl.ds(start, ff_block)]

    down_share = Share(groups, down_place, down_s, down_r)
    down_own = pltpu.make_async_copy(down_block, down_place(group, 0), down_sem)
    down_own.start()

    prefix = prefix_ref[0, 0]
    scale = HD ** (-0.5)
    for head in range(heads + kv_heads):
        part = pl.ds(head * HD, HD)
        values = raw[:, part].T
        raw_t[part, :] = values
        gain = query_gain[...] if head < heads else key_gain[...]
        turned = turn(values * inverse_rms(values) * gain, cosine[...], sine[...])
        if head < heads:
            qt_ref[part, :] = turned.astype(low)
            q_ref[:, part] = turned.T.astype(low)
        else:
            part = pl.ds((head - heads) * HD, HD)
            kt_ref[part, :] = turned.astype(low)
            k_ref[:, part] = turned.T.astype(low)
    for head in range(kv_heads):
        part = pl.ds(head * HD, HD)
        values = raw[:, pl.ds((heads + kv_heads + head) * HD, HD)]
        v_ref[:, part] = values.astype(low)
        vt_ref[part, :] = values.T.astype(low)
    gate_t[...] = raw[:, pl.ds((heads + 2 * kv_heads) * HD, HD)].T[: gate_t.shape[0]]
    swap.receive(0, share.send)
    for head in range(heads):
        part = pl.ds(head * HD, HD)
        kv_part = pl.ds(head * kv_heads // heads * HD, HD)

        def block(first, tile, keys):
            columns = lanes(first, tile)
            scores = product(k_ref[pl.ds(0, keys), kv_part], qt_ref[part, columns]) * scale
            scores = jnp.where(kept(0, keys, first, tile, prefix), scores, negative)
            top = jnp.max(scores, axis=0, keepdims=True)
            expanded = jnp.exp(scores - top)
            total = jnp.sum(expanded, axis=0, keepdims=True)
            lse_ref[head : head + 1, columns] = top + jnp.log(total)
            att_t[part, columns] = (
                product(vt_ref[kv_part, pl.ds(0, keys)], expanded.astype(low)) / total
            )

        query_blocks(length, block)
        scaled = att_t[part, :] * jax.nn.sigmoid(gate_t[head : head + 1, :])
        gated_t[part, :] = scaled.astype(low)
        gated[:, part] = scaled.T.astype(low)
        if head == 0:
            share.relay(me)
            swap.again(0, share.relay)
            if line.chips > 1:
                swap.receive(1, share.send)

    gather = Gather(line, 2, rows, og_all, gather_sems)
    scatter = Scatter(line, rows, scatter_refs)
    block = blocks_nn(gated, out_low, rows)
    last = line.chips - 1
    for far, side in scatter.order():
        if far == last:
            scatter.fill(far, side, block)
    gather.start(out_grad)
    start = pl.multiple_of(me * rows, rows)
    og_own = pltpu.make_async_copy(out_grad, og_all.at[pl.ds(start, rows)], og_sem)
    og_own.start()
    for far, side in scatter.order():
        if far == last:
            scatter.push(far, side)
    for far, side in scatter.order():
        if far < last:
            scatter.fill(far, side, block)
    for far in range(2, line.chips):
        swap.receive(far, share.send)
        swap.again(far - 1, share.relay)
    down_share.send(0, down_block)
    for hop in range(1, line.chips):
        for far, side in scatter.order():
            if far == last - hop and far > 0:
                scatter.push(far, side)
        gather.forward(hop)
        if hop == 1:
            swap.again(last, share.relay)
        if hop == last:
            down_share.relay(0)
    scatter.total(middle)
    values = hidden[...].astype(full) + middle[...]
    middle[...] = values
    inverse = lax.rsqrt(jnp.mean(values * values, axis=-1, keepdims=True) + epsilon)
    normed_two[...] = (values * inverse * swiglu_gain[...]).astype(low)
    og_own.wait()
    own.wait()
    gather.complete()
    scatter.finish()
    swap.finish()
    share.finish(pieces)
    down_own.wait()
    down_share.finish(1)


def attend(raw, tables, gains, prefix, out_low, hidden, swiglu_gain, out_grad, weights, shape, number):
    pieces, groups, heads, kv_heads, ff_block = shape
    length, rows, model = raw.shape[0], hidden.shape[0], hidden.shape[1]
    q_width, kv_width = heads * HD, kv_heads * HD
    weight_rows = weights[0].shape[0]
    struct = jax.ShapeDtypeStruct
    return pl.pallas_call(
        functools.partial(attend_kernel, shape),
        out_shape=(
            struct((q_width + kv_width, length), full),
            struct((8, length), full),
            struct((length, q_width), low),
            struct((q_width, length), low),
            struct((length, kv_width), low),
            struct((kv_width, length), low),
            struct((length, kv_width), low),
            struct((q_width, length), full),
            struct((8, length), full),
            struct((q_width, length), low),
            struct((rows, model), full),
            struct((rows, model), low),
            struct((length, model), low),
            struct((groups, pieces, weight_rows, 2 * groups * ff_block), low),
            struct((groups * ff_block, model), low),
        ),
        in_specs=[IN_VMEM] * 5 + [pl.BlockSpec(memory_space=pltpu.SMEM)] + [IN_VMEM] * 7,
        out_specs=(IN_VMEM,) * 12 + (ANY, ANY, ANY),
        scratch_shapes=[
            pltpu.VMEM((kv_width, length), low),
            pltpu.VMEM((length, q_width), low),
            pltpu.VMEM((pieces, weight_rows, 2 * groups * ff_block), low),
            pltpu.VMEM((ff_block, model), low),
            DMA,
            DMA,
            DMA,
        ]
        + swap_scratch(pieces)
        + [DMA((pieces, groups))] * 2
        + [DMA((1, groups))] * 2
        + gather_scratch(pieces, 2)
        + scatter_scratch(pieces, rows, model),
        compiler_params=pltpu.CompilerParams(
            collective_id=number, has_side_effects=True, vmem_limit_bytes=60 << 20
        ),
        name=f"attend_{number}",
    )(raw, *tables, *gains, prefix, out_low, hidden, swiglu_gain, out_grad, *weights)


def attend_back_kernel(
    shape,
    grad_branch,
    out_low,
    raw_t,
    gate_t,
    q_ref,
    qt_ref,
    k_ref,
    kt_ref,
    v_ref,
    att_t,
    lse_ref,
    gated_t,
    cosine,
    sine,
    query_gain,
    key_gain,
    prefix_ref,
    normed,
    attn_low,
    hidden,
    grad_middle,
    attention_gain,
    swiglu_gain_grad,
    ff_share,
    hidden_grad,
    gains_grad,
    query_grad,
    key_grad,
    value_grad,
    head_grad,
    gate_grad,
    up_grad,
    out_grad,
    out_term,
    out_in,
    out_send,
    gg_t,
    ga_t,
    ga,
    gqt,
    dk,
    dv,
    grad_t,
    grad,
    total_ref,
    ff_recv,
    normed_part,
    part_sem,
    term,
    term_in,
    attn_send,
    attn_recv,
    gains_vector,
    gain_give,
    gain_sib,
    gain_row,
    gain_last,
    ffs_s,
    ffs_r,
    at_s,
    at_r,
    gc_s,
    gc_r,
    ts_s,
    ts_r,
    gs_s,
    gs_r,
    ot_s,
    ot_r,
    om_s,
    om_r,
    *scatter_refs,
):
    pieces, groups, heads, kv_heads, ff_block = shape
    line = Line(pieces)
    me, group = line.me, lax.axis_index("seq")
    length, rows = grad_branch.shape[0], hidden.shape[0]
    width, model = attn_low.shape[1], attn_low.shape[0]
    weight_rows = ff_share.shape[1]
    q_width, kv_width = heads * HD, kv_heads * HD
    spread = Spread(groups, pieces)
    greet(others("ctx", pieces) + others("seq", groups) + spread.peers())
    share = model // groups
    fold = Fold(groups, term, term_in, ts_s, ts_r)
    out_fold = Fold(groups, out_term, out_in, ot_s, ot_r)

    def load(job):
        index = fold.order[job]
        return pltpu.make_async_copy(
            normed.at[:, lanes(index * share, share)], normed_part.at[job % 2], part_sem.at[job % 2]
        )

    load(0).start()
    ff_swap = LineSwap(
        line, lambda peer: ff_share.at[peer], lambda source: ff_recv.at[source], ffs_s, ffs_r
    )
    ff_swap.start()

    prefix = prefix_ref[0, 0]
    scale = HD ** (-0.5)

    def branch(index, unused):
        columns = lanes(index * 256, 256)
        gg_t[:, columns] = product_nt(out_low[...], grad_branch[columns, :])
        return unused

    lax.fori_loop(0, length // 256, branch, 0)

    def out_grads(index, unused):
        columns = lanes(index * 256, 256)
        value = product(gated_t[...], grad_branch[:, columns]).astype(low)
        for place in range(groups):
            out_term[place, :, columns] = value[place * weight_rows : (place + 1) * weight_rows]
        return unused

    lax.fori_loop(0, model // 256, out_grads, 0)

    for job in range(groups):
        out_fold.ready(job)
    dk[...] = jnp.zeros(dk.shape, full)
    dv[...] = jnp.zeros(dv.shape, full)
    gate_rows = []
    for head in range(heads):
        part = pl.ds(head * HD, HD)
        kv_part = pl.ds(head * kv_heads // heads * HD, HD)
        sigmoid = jax.nn.sigmoid(gate_t[head : head + 1, :])
        grads = gg_t[part, :]
        rounded = (grads * sigmoid).astype(low)
        ga_t[...] = rounded
        ga[...] = rounded.astype(full).T.astype(low)
        gate_rows.append(
            jnp.sum(grads * att_t[part, :], axis=0, keepdims=True) * sigmoid * (1.0 - sigmoid)
        )

        def block(first, tile, keys):
            columns, across = lanes(first, tile), pl.ds(0, keys)
            scores = product(k_ref[across, kv_part], qt_ref[part, columns]) * scale
            chance = jnp.where(
                kept(0, keys, first, tile, prefix),
                jnp.exp(scores - lse_ref[head : head + 1, columns]),
                0.0,
            )
            taken = ga_t[:, columns]
            delta = jnp.sum(taken.astype(full) * att_t[part, columns], axis=0, keepdims=True)
            change = product(v_ref[across, kv_part], taken)
            score_grad = (chance * (change - delta)).astype(low)
            gqt[part, columns] = product(kt_ref[kv_part, across], score_grad) * scale
            dk[across, kv_part] += product(score_grad, q_ref[columns, part])
            dv[across, kv_part] += product(chance.astype(low), ga[columns, :])

        query_blocks(length, block)
        if head == heads - 1:
            out_fold.mix()

    gain_columns = [jnp.zeros((HD, 1), full), jnp.zeros((HD, 1), full)]
    for head in range(heads + kv_heads):
        part = pl.ds(head * HD, HD)
        if head < heads:
            turned = gqt[part, :]
            gain = query_gain[...]
        else:
            turned = dk[:, pl.ds((head - heads) * HD, HD)].T * scale
            gain = key_gain[...]
        grads = turn_back(turned, cosine[...], sine[...])
        values = raw_t[part, :]
        inverse = inverse_rms(values)
        kind = 0 if head < heads else 1
        gain_columns[kind] = gain_columns[kind] + jnp.sum(
            grads * values * inverse, axis=1, keepdims=True
        )
        scaled = grads * gain
        result = inverse * scaled - values * (
            inverse * inverse * inverse * jnp.mean(scaled * values, axis=0, keepdims=True)
        )
        grad_t[part, :] = result.astype(low)
        grad[:, part] = result.T.astype(low)
    for head in range(kv_heads):
        part = pl.ds((heads + kv_heads + head) * HD, HD)
        values = dv[:, pl.ds(head * HD, HD)]
        grad[:, part] = values.astype(low)
        grad_t[part, :] = values.T.astype(low)
    part = pl.ds((heads + 2 * kv_heads) * HD, HD)
    gate_block = jnp.concatenate(
        gate_rows + [jnp.zeros((HD - heads, length), full)], axis=0
    )
    grad_t[part, :] = gate_block.astype(low)
    grad[:, part] = gate_block.T.astype(low)

    scatter = Scatter(line, rows, scatter_refs)
    block = blocks_nt(grad, attn_low, rows)
    last = line.chips - 1

    def fills(far):
        for distance, side in scatter.order():
            if distance == far:
                scatter.fill(far, side, block)

    def pushes(far):
        for distance, side in scatter.order():
            if distance == far and far > 0:
                scatter.push(far, side)

    def weight_grad(job):
        index = fold.order[job]
        load(job).wait()
        if job + 1 < groups:
            load(job + 1).start()

        def step(tile, unused):
            start = index * share + tile * 128
            value = product(grad_t[...], normed_part[job % 2, :, lanes(tile * 128, 128)])
            turned = value.T
            term[index, pl.ds(pl.multiple_of(tile * 128, 128), 128), :] = turned.astype(low)
            weighted = jnp.sum(
                turned * attn_low[pl.ds(pl.multiple_of(start, 128), 128), :].astype(full),
                axis=1,
                keepdims=True,
            )
            wide = jnp.broadcast_to(weighted, (128, 128)).T
            gains_vector[:, lanes(start, 128)] = wide[0:1, :] / attention_gain[:, lanes(start, 128)]
            return unused

        lax.fori_loop(0, share // 128, step, 0)
        fold.ready(job)

    weight_grad(0)
    fills(last)
    pushes(last)
    for job in range(1, groups):
        weight_grad(job)
        if last - job >= 0:
            fills(last - job)
    fold.mix()
    for far in range(last - groups, -1, -1):
        fills(far)

    gain_count = gains_grad.shape[1]
    gains_vector[:, pl.ds(model, model)] = swiglu_gain_grad[...]
    for kind in range(2):
        wide = jnp.broadcast_to(gain_columns[kind], (HD, HD)).T
        gains_vector[:, pl.ds(2 * model + kind * HD, HD)] = wide[0:1, :]
    gain_give[...] = jnp.zeros(gain_give.shape, full)
    for index in range(groups * pieces):
        gain_give[index % pieces, index // pieces, 0:1, pl.ds(0, gain_count)] = gains_vector[
            :, pl.ds(index * gain_count, gain_count)
        ]
    gain_swap = LineSwap(
        line, lambda peer: gain_give.at[peer], lambda source: gain_sib.at[source], gc_s, gc_r
    )
    gain_swap.start()
    gain_sib[me] = gain_give[me]
    pushes(last - 1)

    out_fold.arrive()
    out_send[...] = out_fold.sum(pl.ds(0, weight_rows)).astype(low)
    out_move = spread.copy(out_send, out_grad, om_s, om_r, True)

    @pl.when(spread.moves)
    def _():
        out_move.start()

    @pl.when(jnp.logical_not(spread.moves))
    def _():
        out_grad[...] = out_send[...]

    for far in range(line.chips):
        gain_swap.receive(far, lambda source: None)
    gain_row[...] = jnp.sum(gain_sib[...], axis=0)

    def gain_to(shift):
        peer = lax.rem(group + shift, groups)
        return remote(
            gain_row.at[peer], gain_last.at[shift], gs_s.at[shift], gs_r.at[shift], "seq", peer
        )

    for shift in range(1, groups):
        gain_to(shift).start()
    gain_last[0] = gain_row[group]

    for far in range(line.chips):
        ff_swap.receive(far, lambda source: None)
    ff_recv[me] = ff_share[me]
    own_width = groups * ff_block
    for half, grad_ref in enumerate((gate_grad, up_grad)):
        for index in range(groups):
            for piece in range(pieces):
                start = (index * pieces + piece) * ff_block
                grad_ref[:, pl.ds(start, ff_block)] = ff_recv[
                    piece, :, pl.ds(half * own_width + index * ff_block, ff_block)
                ]

    for far in range(last - 2, 0, -1):
        pushes(far)

    fold.arrive()
    for piece in range(pieces):
        attn_send[piece] = fold.sum(pl.ds(piece * weight_rows, weight_rows)).astype(low)
    attn_swap = LineSwap(
        line, lambda peer: attn_send.at[peer], lambda source: attn_recv.at[source], at_s, at_r
    )
    attn_swap.start()

    scatter.total(total_ref)
    values = hidden[...].astype(full)
    inverse = lax.rsqrt(jnp.mean(values * values, axis=-1, keepdims=True) + epsilon)
    grads = total_ref[...]
    scaled = grads * attention_gain[...]
    hidden_grad[...] = (
        grad_middle[...]
        + inverse * scaled
        - values
        * (inverse * inverse * inverse * jnp.mean(scaled * values, axis=-1, keepdims=True))
    ).astype(low)

    for shift in range(1, groups):
        peer = lax.rem(group + groups - shift, groups)
        remote(
            gain_row.at[peer], gain_last.at[shift], gs_s.at[shift], gs_r.at[shift], "seq", peer
        ).wait_recv()
    gains_grad[...] = jnp.sum(gain_last[...], axis=0)[0:1, pl.ds(0, gain_count)]

    for far in range(line.chips):
        attn_swap.receive(far, lambda source: None)
    attn_recv[me] = attn_send[me]
    copies = max(1, pieces // KV)
    for piece in range(pieces):
        query_grad[:, pl.ds(piece * q_width, q_width)] = attn_recv[piece, :, pl.ds(0, q_width)]
        head_grad[:, pl.ds(piece * heads, heads)] = attn_recv[
            piece, :, pl.ds(q_width + 2 * kv_width, heads)
        ].astype(full)
    for place in range(pieces // copies):
        for kind, grad_ref in enumerate((key_grad, value_grad)):
            columns = pl.ds(q_width + kind * kv_width, kv_width)
            summed = attn_recv[place * copies, :, columns].astype(full)
            for copy in range(1, copies):
                summed = summed + attn_recv[place * copies + copy, :, columns].astype(full)
            grad_ref[:, pl.ds(place * kv_width, kv_width)] = summed

    @pl.when(spread.moves)
    def _():
        spread.copy(out_grad, out_grad, om_s, om_r, True).wait_recv()
        out_move.wait_send()

    scatter.finish()
    ff_swap.finish()
    attn_swap.finish()
    gain_swap.finish()
    for shift in range(1, groups):
        gain_to(shift).wait_send()
    fold.finish()
    out_fold.finish()


def attend_back(
    grad_branch, out_low, saved, gated_t, tables, gains, prefix, normed, attn_low, hidden, grad_middle,
    attention_gain, swiglu_gain_grad, ff_share, gain_count, shape, number,
):
    pieces, groups, heads, kv_heads, ff_block = shape
    length, (rows, model) = grad_branch.shape[0], hidden.shape
    width = attn_low.shape[1]
    weight_rows = ff_share.shape[1]
    q_width, kv_width = heads * HD, kv_heads * HD
    struct, vmem = jax.ShapeDtypeStruct, pltpu.VMEM
    padded = -(-gain_count // 128) * 128
    return pl.pallas_call(
        functools.partial(attend_back_kernel, shape),
        out_shape=(
            struct((rows, model), low),
            struct((1, gain_count), full),
            struct((weight_rows, H * HD), low),
            struct((weight_rows, KV * HD), full),
            struct((weight_rows, KV * HD), full),
            struct((weight_rows, H), full),
            struct((weight_rows, pieces * groups * ff_block), low),
            struct((weight_rows, pieces * groups * ff_block), low),
            struct((weight_rows, model), low),
        ),
        in_specs=[IN_VMEM] * 16 + [pl.BlockSpec(memory_space=pltpu.SMEM), ANY] + [IN_VMEM] * 6,
        out_specs=(IN_VMEM,) * 9,
        scratch_shapes=[
            vmem((groups, weight_rows, model), low),
            vmem((groups - 1, weight_rows, model), low),
            vmem((weight_rows, model), low),
            vmem((q_width, length), full),
            vmem((HD, length), low),
            vmem((length, HD), low),
            vmem((q_width, length), full),
            vmem((length, kv_width), full),
            vmem((length, kv_width), full),
            vmem((width, length), low),
            vmem((length, width), low),
            vmem((rows, model), full),
            vmem(ff_share.shape, low),
            vmem((2, length, model // groups), low),
            DMA((2,)),
            vmem((groups, model // groups, width), low),
            vmem((groups - 1, model // groups, width), low),
            vmem((pieces, weight_rows, width), low),
            vmem((pieces, weight_rows, width), low),
            vmem((1, 2 * model + 2 * HD), full),
            vmem((pieces, groups, 8, padded), full),
            vmem((pieces, groups, 8, padded), full),
            vmem((groups, 8, padded), full),
            vmem((groups, 8, padded), full),
        ]
        + swap_scratch(pieces) * 3
        + [DMA((groups,))] * 6
        + [DMA] * 2
        + scatter_scratch(pieces, rows, model),
        compiler_params=pltpu.CompilerParams(
            collective_id=number, has_side_effects=True, vmem_limit_bytes=63 << 20
        ),
        name=f"attend_back_{number}",
    )(
        grad_branch, out_low, *saved, gated_t, *tables, *gains, prefix, normed, attn_low, hidden, grad_middle,
        attention_gain, swiglu_gain_grad, ff_share,
    )


def feed_kernel(
    shape,
    normed_two,
    ff_low,
    down_low,
    og_all,
    n2_all,
    hidden_ff,
    grad_pre,
    grad_hidden,
    *gather_sems,
):
    pieces = shape[0]
    line = Line(pieces)
    rows, length = normed_two.shape[0], og_all.shape[0]
    own_width = down_low.shape[0]
    tile = own_width // 3 if own_width % 384 == 0 else 128
    greet(line.peers())
    gather = Gather(line, 2, rows, n2_all, gather_sems)
    gather.start(normed_two)
    n2_all[pl.ds(pl.multiple_of(line.me * rows, rows), rows), :] = normed_two[...]

    def backward(index, unused):
        across = pl.ds(pl.multiple_of(index * 256, 256), 256)
        grad_hidden[across, :] = product_nt(og_all[across, :], down_low[...])
        return unused

    lax.fori_loop(0, length // 256, backward, 0)

    def chip_rows(chip):
        across = pl.ds(pl.multiple_of(chip * 2 * rows, 2 * rows), 2 * rows)

        def step(index, unused):
            start = index * tile
            first, second = lanes(start, tile), lanes(own_width + start, tile)
            gate = product(n2_all[across, :], ff_low[:, first])
            up = product(n2_all[across, :], ff_low[:, second])
            grads = grad_hidden[across, first]
            sigmoid = jax.nn.sigmoid(gate)
            silu = gate * sigmoid
            hidden_ff[across, first] = (silu * up).astype(low)
            grad_pre[across, first] = (
                grads * up * (sigmoid * (1.0 + gate * (1.0 - sigmoid)))
            ).astype(low)
            grad_pre[across, second] = (grads * silu).astype(low)
            return unused

        lax.fori_loop(0, own_width // tile, step, 0)

    def compute(far):
        gather.arrive(far)
        if far == 0:
            chip_rows(line.chip)
            return

        @pl.when(line.chip - far >= 0)
        def _():
            chip_rows(line.chip - far)

        @pl.when(line.chip + far < line.chips)
        def _():
            chip_rows(line.chip + far)

    for hop in range(1, line.chips - 1):
        gather.forward(hop)
        compute(hop - 1)
    if line.chips > 1:
        compute(line.chips - 2)
        gather.forward(line.chips - 1)
    compute(line.chips - 1)
    gather.finish()


def feed(normed_two, ff_low, down_low, og_all, shape, number):
    pieces = shape[0]
    length, model = og_all.shape
    own_width = down_low.shape[0]
    struct = jax.ShapeDtypeStruct
    return pl.pallas_call(
        functools.partial(feed_kernel, shape),
        out_shape=(
            struct((length, model), low),
            struct((length, own_width), low),
            struct((length, 2 * own_width), low),
        ),
        in_specs=[IN_VMEM] * 4,
        out_specs=(IN_VMEM,) * 3,
        scratch_shapes=[pltpu.VMEM((length, own_width), full)] + gather_scratch(pieces, 2),
        compiler_params=pltpu.CompilerParams(
            collective_id=number, has_side_effects=True, vmem_limit_bytes=60 << 20
        ),
        name=f"feed_{number}",
    )(normed_two, ff_low, down_low, og_all)


def feed_back_kernel(
    shape,
    grad_pre,
    ff_low,
    hidden_ff,
    down_low,
    og_all,
    n2_all,
    middle,
    out_grad,
    swiglu_gain,
    gb_all,
    grad_middle,
    gain_grad,
    hidden_out,
    ff_share,
    down_share,
    down_term,
    down_in,
    total_ref,
    branch,
    n2_part,
    term,
    term_in,
    part_sem,
    own_sem,
    ts_s,
    ts_r,
    ds_s,
    ds_r,
    *sems,
):
    pieces, groups = shape[:2]
    buffers, sems = sems[:2], sems[2:]
    gather_sems, sems = sems[:6], sems[6:]
    line = Line(pieces)
    me, group = line.me, lax.axis_index("seq")
    length, rows, model = og_all.shape[0], middle.shape[0], og_all.shape[1]
    weight_rows = ff_share.shape[1]
    greet(line.peers() + others("seq", groups))
    half = len(sems) // 2
    inner = Scatter(line, rows, buffers + sems[:half])
    outer = Scatter(line, rows, buffers + sems[half:])
    block = blocks_nt(grad_pre, ff_low, rows)
    last = line.chips - 1

    def fills(scatter, far, block):
        for distance, side in scatter.order():
            if distance == far:
                scatter.fill(far, side, block)

    def pushes(scatter, far):
        for distance, side in scatter.order():
            if distance == far and far > 0:
                scatter.push(far, side)

    share = model // groups

    fold = Fold(groups, term, term_in, ts_s, ts_r)
    down_fold = Fold(groups, down_term, down_in, ds_s, ds_r)

    def load(job):
        index = fold.order[job]
        return pltpu.make_async_copy(
            n2_all.at[:, lanes(index * share, share)], n2_part.at[job % 2], part_sem.at[job % 2]
        )

    def ff_grad(job, index):
        load(job).wait()
        if job + 1 < groups:
            load(job + 1).start()

        def step(tile, unused):
            value = product_tn(n2_part[job % 2, :, lanes(tile * 128, 128)], grad_pre[...])
            term[index, pl.ds(pl.multiple_of(tile * 128, 128), 128), :] = value.astype(low)
            return unused

        lax.fori_loop(0, share // 128, step, 0)

    jobs = list(range(groups))

    def some_grads(count):
        for _ in range(min(count, len(jobs))):
            job = jobs.pop(0)
            ff_grad(job, fold.order[job])
            fold.ready(job)
            if not jobs:
                fold.mix()

    load(0).start()
    fills(inner, last, block)
    pushes(inner, last)
    fills(inner, last - 1, block)
    some_grads(1)
    each = -(-(groups - 1) // max(1, last - 1))
    for hop in range(1, line.chips):
        pushes(inner, last - hop)
        if hop < last:
            fills(inner, last - 1 - hop, block)
        some_grads(each)
    some_grads(groups)

    down_rows = down_term.shape[1]
    piece_rows = math.gcd(down_rows, 128)

    def down_grads(index, unused):
        value = product_tn(hidden_ff[:, lanes(index * 128, 128)], og_all[...]).astype(low)
        for part in range(128 // piece_rows):
            row = index * 128 + part * piece_rows
            down_term[row // down_rows, pl.ds(pl.multiple_of(lax.rem(row, down_rows), piece_rows), piece_rows), :] = (
                value[part * piece_rows : (part + 1) * piece_rows]
            )
        return unused

    lax.fori_loop(0, down_low.shape[0] // 128, down_grads, 0)
    for job in range(groups):
        down_fold.ready(job)
    inner.total(total_ref)
    inner.finish()
    values, grads = middle[...], total_ref[...]
    inverse = lax.rsqrt(jnp.mean(values * values, axis=-1, keepdims=True) + epsilon)
    gain_grad[...] = jnp.sum(grads * values * inverse, axis=0, keepdims=True)
    scaled = grads * swiglu_gain[...]
    result = (
        out_grad[...].astype(full)
        + inverse * scaled
        - values
        * (inverse * inverse * inverse * jnp.mean(scaled * values, axis=-1, keepdims=True))
    )
    grad_middle[...] = result
    branch[...] = result.astype(low)

    gather = Gather(line, 2, rows, gb_all, gather_sems)
    gather.start(branch)
    start = pl.multiple_of(me * rows, rows)
    own = pltpu.make_async_copy(branch, gb_all.at[pl.ds(start, rows)], own_sem)
    own.start()
    block = blocks_nn(hidden_ff, down_low, rows)
    fills(outer, last, block)
    pushes(outer, last)
    fills(outer, last - 1, block)
    for hop in range(1, line.chips):
        gather.forward(hop)
        pushes(outer, last - hop)
        if hop < last:
            fills(outer, last - 1 - hop, block)
        if hop == 1:
            down_fold.mix()
    fold.arrive()
    for piece in range(pieces):
        ff_share[piece] = fold.sum(pl.ds(piece * weight_rows, weight_rows)).astype(low)
    down_fold.arrive()
    down_share[...] = down_fold.sum(pl.ds(0, down_rows)).astype(low)
    outer.total(total_ref)
    hidden_out[...] = (middle[...] + total_ref[...]).astype(low)
    own.wait()
    for hop in range(line.chips):
        gather.arrive(hop)
    gather.finish()
    outer.finish()
    fold.finish()
    down_fold.finish()


def feed_back(
    grad_pre, ff_low, hidden_ff, down_low, og_all, n2_all, middle, out_grad, swiglu_gain, shape, number
):
    pieces, groups = shape[:2]
    length, (rows, model) = og_all.shape[0], middle.shape
    own_width, width = hidden_ff.shape[1], grad_pre.shape[1]
    weight_rows = model // (groups * pieces)
    struct, vmem = jax.ShapeDtypeStruct, pltpu.VMEM
    scatter = scatter_scratch(pieces, rows, model)
    return pl.pallas_call(
        functools.partial(feed_back_kernel, shape),
        out_shape=(
            struct((length, model), low),
            struct((rows, model), full),
            struct((1, model), full),
            struct((rows, model), low),
            struct((pieces, weight_rows, width), low),
            struct((own_width // groups, model), low),
        ),
        in_specs=[IN_VMEM] * 5 + [ANY] + [IN_VMEM] * 3,
        out_specs=(ANY,) + (IN_VMEM,) * 5,
        scratch_shapes=[
            vmem((groups, own_width // groups, model), low),
            vmem((groups - 1, own_width // groups, model), low),
            vmem((rows, model), full),
            vmem((rows, model), low),
            vmem((2, length, model // groups), low),
            vmem((groups, model // groups, width), low),
            vmem((groups - 1, model // groups, width), low),
            DMA((2,)),
            DMA,
            DMA((groups,)),
            DMA((groups,)),
            DMA((groups,)),
            DMA((groups,)),
        ]
        + scatter[:2]
        + gather_scratch(pieces, 2)
        + scatter[2:] * 2,
        compiler_params=pltpu.CompilerParams(
            collective_id=number, has_side_effects=True, vmem_limit_bytes=63 << 20
        ),
        name=f"feed_back_{number}",
    )(grad_pre, ff_low, hidden_ff, down_low, og_all, n2_all, middle, out_grad, swiglu_gain)


def widen_kernel(*refs):
    for source, target in zip(refs[: len(refs) // 2], refs[len(refs) // 2 :]):
        target[...] = source[...].astype(full)


def widen(arrays):
    steps = max(1, arrays[0].shape[0] // 16)
    specs = [
        pl.BlockSpec((array.shape[0] // steps, array.shape[1]), lambda step: (step, 0))
        for array in arrays
    ]
    return pl.pallas_call(
        widen_kernel,
        grid=(steps,),
        out_shape=[jax.ShapeDtypeStruct(array.shape, full) for array in arrays],
        in_specs=specs,
        out_specs=specs,
        name="widen",
    )(*arrays)


def on_device(
    hidden_in,
    out_grad,
    prefix_len,
    norm_gains,
    query_weight,
    key_weight,
    value_weight,
    head_gate_weight,
    out_weight,
    gate_weight,
    up_weight,
    down_weight,
):
    row_count, model = hidden_in.shape
    groups = lax.axis_size("seq")
    pieces = lax.axis_size("ctx")
    length = row_count * pieces
    weight_rows = query_weight.shape[0]
    heads = H // pieces
    kv_heads = max(1, KV // pieces)
    ff_block = down_weight.shape[0]
    ff_own = ff_block * groups
    gain_count = norm_gains.shape[0]
    shape = (pieces, groups, heads, kv_heads, ff_block)
    normed, raw, attn_low, gains_full, out_low = opening(
        hidden_in,
        norm_gains,
        (query_weight, key_weight, value_weight, head_gate_weight, out_weight),
        shape,
        0,
    )
    attention_gain = gains_full[:, :model]
    swiglu_gain = gains_full[:, model : 2 * model]
    head_gains = (
        gains_full[0, 2 * model : 2 * model + HD, None],
        gains_full[0, 2 * model + HD :, None],
    )
    inverse = rope_base ** (-jnp.arange(HD // 2, dtype=full) * 2.0 / HD)
    angles = inverse[:, None] * jnp.arange(length, dtype=jnp.int32).astype(full)[None, :]
    tables = (jnp.cos(angles), jnp.sin(angles))
    prefix = prefix_len.reshape(1, 1)

    *saved, gated_t, middle, normed_two, out_grad_all, ff_low, down_low = attend(
        raw,
        tables,
        head_gains,
        prefix,
        out_low,
        hidden_in,
        swiglu_gain,
        out_grad,
        (gate_weight, up_weight, down_weight),
        shape,
        1,
    )
    ff_low = ff_low.reshape(model, 2 * ff_own)
    n2_all, hidden_ff, grad_pre = feed(normed_two, ff_low, down_low, out_grad_all, shape, 2)
    grad_branch, grad_middle, swiglu_gain_grad, hidden_out, ff_share, down_share = feed_back(
        grad_pre, ff_low, hidden_ff, down_low, out_grad_all, n2_all, middle, out_grad, swiglu_gain, shape, 3
    )
    hidden_grad, gains_share, query_share, key_share, value_share, head_share, gate_share, up_share, output_share = (
        attend_back(
            grad_branch,
            out_low,
            saved,
            gated_t,
            tables,
            head_gains,
            prefix,
            normed,
            attn_low,
            hidden_in,
            grad_middle,
            attention_gain,
            swiglu_gain_grad,
            ff_share,
            gain_count,
            shape,
            4,
        )
    )
    query_share, output_share, gate_share, up_share, down_share = widen(
        (query_share, output_share, gate_share, up_share, down_share)
    )
    return (
        hidden_out,
        hidden_grad,
        gains_share.reshape(gain_count),
        query_share,
        key_share,
        value_share,
        head_share,
        output_share,
        gate_share,
        up_share,
        down_share,
    )


def solution(mesh):
    rows = P(("seq", "ctx"), None)
    return jax.shard_map(
        on_device,
        mesh=mesh,
        in_specs=(rows, rows, P("seq"), P(("seq", "ctx"))) + (rows,) * 8,
        out_specs=(rows, rows, P(("seq", "ctx"))) + (rows,) * 8,
        check_vma=False,
    )
```

```python
import functools
import math

import jax
import jax.numpy as jnp
from jax import lax
from jax.experimental import pallas as pl
from jax.experimental.pallas import tpu as pltpu
from jax.sharding import PartitionSpec as P

H = 16
KV = 8
HD = 128


epsilon = 1e-06
rope_base = 1000000.0
negative = -1e30
low = jnp.bfloat16
full = jnp.float32
MESH = pl.DeviceIdType.MESH
ANY = pl.BlockSpec(memory_space=pl.ANY)
IN_VMEM = pl.BlockSpec(memory_space=pltpu.VMEM)
DMA = pltpu.SemaphoreType.DMA


def product(left_side, right_side):
    return jnp.dot(left_side, right_side, preferred_element_type=full)


def product_nt(left_side, right_side):
    return lax.dot_general(
        left_side, right_side, (((1,), (1,)), ((), ())), preferred_element_type=full
    )


def product_tn(left_side, right_side):
    return lax.dot_general(
        left_side, right_side, (((0,), (0,)), ((), ())), preferred_element_type=full
    )


def by_rows(rows, body, tile=32):
    tile = min(tile, rows)

    def step(index, unused):
        body(pl.ds(pl.multiple_of(index * tile, tile), tile))
        return unused

    lax.fori_loop(0, rows // tile, step, 0)


def remote(source, target, send, receive, axis, peer):
    return pltpu.make_async_remote_copy(
        src_ref=source,
        dst_ref=target,
        send_sem=send,
        recv_sem=receive,
        device_id={axis: peer},
        device_id_type=MESH,
    )


def greet(peers):
    barrier = pltpu.get_barrier_semaphore()
    for axis, peer, exists in peers:
        place = {"seq": peer[0], "ctx": peer[1]} if axis is None else {axis: peer}

        def signal():
            pl.semaphore_signal(barrier, inc=1, device_id=place, device_id_type=MESH)

        if exists is True:
            signal()
        else:
            pl.when(exists)(signal)

    arrivals = sum(1 for _, _, exists in peers if exists is True)
    for _, _, exists in peers:
        if exists is not True:
            arrivals = arrivals + exists.astype(jnp.int32)
    pl.semaphore_wait(barrier, arrivals)


def others(axis, count):
    me = lax.axis_index(axis)
    return [(axis, lax.rem(me + shift, count), True) for shift in range(1, count)]


class Line:
    def __init__(self, pieces):
        self.chips = pieces // 2
        self.me = lax.axis_index("ctx")
        self.chip, self.core = self.me // 2, lax.rem(self.me, 2)
        self.sibling = self.me + 1 - 2 * self.core
        self.right, self.left = self.me + 2, self.me - 2
        self.has_right, self.has_left = self.chip < self.chips - 1, self.chip > 0

    def peers(self):
        return [
            ("ctx", self.sibling, True),
            ("ctx", self.right, self.has_right),
            ("ctx", self.left, self.has_left),
        ]


def gather_scratch(pieces, parts):
    chips = pieces // 2
    return [DMA((chips, 2, parts))] * 2 + [DMA((chips, parts))] * 4


class Gather:
    def __init__(self, line, parts, rows, out_ref, sems):
        self.line, self.parts, self.rows, self.out_ref = line, parts, rows, out_ref
        self.size = rows // parts
        self.sib_send, self.sib_recv, self.r_send, self.r_recv, self.l_send, self.l_recv = sems

    def at(self, position, part):
        start = pl.multiple_of(position * self.rows + part * self.size, self.size)
        return self.out_ref.at[pl.ds(start, self.size)]

    def to_sibling(self, source, hop, side, part, position):
        return remote(
            source,
            self.at(position, part),
            self.sib_send.at[hop, side, part],
            self.sib_recv.at[hop, side, part],
            "ctx",
            self.line.sibling,
        )

    def to_right(self, source, hop, part, position):
        return remote(
            source,
            self.at(position, part),
            self.r_send.at[hop, part],
            self.r_recv.at[hop, part],
            "ctx",
            self.line.right,
        )

    def to_left(self, source, hop, part, position):
        return remote(
            source,
            self.at(position, part),
            self.l_send.at[hop, part],
            self.l_recv.at[hop, part],
            "ctx",
            self.line.left,
        )

    def start(self, x_ref):
        line = self.line
        for part in range(self.parts):
            piece = x_ref.at[pl.ds(part * self.size, self.size)]

            @pl.when(line.has_right)
            def _():
                self.to_right(piece, 0, part, line.me).start()

            @pl.when(line.has_left)
            def _():
                self.to_left(piece, 0, part, line.me).start()

            self.to_sibling(piece, 0, 0, part, line.me).start()

    def forward(self, hop):
        line = self.line
        for part in range(self.parts):
            from_left, from_right = line.me - 2 * hop, line.me + 2 * hop

            @pl.when(line.chip - hop >= 0)
            def _():
                piece = self.at(from_left, part)
                self.to_right(piece, hop - 1, part, from_left).wait_recv()

                @pl.when(line.has_right)
                def _():
                    self.to_right(piece, hop, part, from_left).start()

                self.to_sibling(piece, hop, 0, part, from_left).start()

            @pl.when(line.chip + hop < line.chips)
            def _():
                piece = self.at(from_right, part)
                self.to_left(piece, hop - 1, part, from_right).wait_recv()

                @pl.when(line.has_left)
                def _():
                    self.to_left(piece, hop, part, from_right).start()

                self.to_sibling(piece, hop, 1, part, from_right).start()

    def legs(self, hop):
        line = self.line
        return [
            (
                side,
                (line.chip - hop >= 0) if side == 0 else (line.chip + hop < line.chips),
                (line.me - 2 * hop) if side == 0 else (line.me + 2 * hop),
            )
            for side in range(1 if hop == 0 else 2)
        ]

    def arrive(self, hop):
        for side, there, position in self.legs(hop):
            for part in range(self.parts):

                @pl.when(there)
                def _():
                    self.to_sibling(
                        self.at(position, part), hop, side, part, position
                    ).wait_recv()

    def finish(self):
        line = self.line
        for hop in range(line.chips):
            for side, there, position in self.legs(hop):
                for part in range(self.parts):

                    @pl.when(there)
                    def _():
                        piece = self.at(position, part)
                        self.to_sibling(piece, hop, side, part, position).wait_send()
                        if side == 0:

                            @pl.when(line.has_right)
                            def _():
                                self.to_right(piece, hop, part, position).wait_send()

                        if side == 1 or hop == 0:

                            @pl.when(line.has_left)
                            def _():
                                self.to_left(piece, hop, part, position).wait_send()

    def complete(self):
        for hop in range(self.line.chips):
            self.arrive(hop)
        self.finish()


def scatter_scratch(pieces, rows, width):
    chips = pieces // 2
    slots = pltpu.VMEM((chips, rows, width), low)
    return [slots] * 3 + [pltpu.VMEM((chips + 1, rows, width), low)] + [DMA((chips,))] * 6


class Scatter:
    def __init__(self, line, rows, scratch):
        self.line, self.rows = line, rows
        (
            self.own,
            self.give,
            self.sib,
            self.arrived,
            self.sib_send,
            self.sib_recv,
            self.r_send,
            self.r_recv,
            self.l_send,
            self.l_recv,
        ) = scratch

    def clear(self):
        line = self.line

        @pl.when(jnp.logical_not(line.has_left))
        def _():
            self.arrived[line.chip] = jnp.zeros(self.arrived.shape[1:], low)

        @pl.when(jnp.logical_not(line.has_right))
        def _():
            self.arrived[line.chips] = jnp.zeros(self.arrived.shape[1:], low)

    def there(self, far, side):
        line = self.line
        return (line.chip + far < line.chips) if side == 0 else (line.chip - far >= 0)

    def target(self, far, side):
        return self.line.chip + far if side == 0 else self.line.chip - far

    def exchange(self, target):
        return remote(
            self.give.at[target],
            self.sib.at[target],
            self.sib_send.at[target],
            self.sib_recv.at[target],
            "ctx",
            self.line.sibling,
        )

    def send(self, target, side):
        if side == 0:
            return remote(
                self.own.at[target],
                self.arrived.at[target],
                self.r_send.at[target],
                self.r_recv.at[target],
                "ctx",
                self.line.right,
            )
        chips, chip = self.line.chips, self.line.chip
        return remote(
            self.own.at[target],
            self.arrived.at[jnp.where(target == chip - 1, chips, target)],
            self.l_send.at[target],
            self.l_recv.at[target],
            "ctx",
            self.line.left,
        )

    def order(self):
        return [
            (far, side)
            for far in range(self.line.chips - 1, -1, -1)
            for side in range(2 if far else 1)
        ]

    def fill(self, far, side, block):
        @pl.when(self.there(far, side))
        def _():
            target = self.target(far, side)

            def store(columns, value):
                first, second = value[: self.rows], value[self.rows :]
                mine = self.line.core == 0
                self.own[target, :, columns] = jnp.where(mine, first, second).astype(low)
                self.give[target, :, columns] = jnp.where(mine, second, first).astype(low)

            block(target, store)
            self.exchange(target).start()

    def push(self, far, side):
        line = self.line
        behind = line.has_left if side == 0 else line.has_right

        @pl.when(self.there(far, side))
        def _():
            target = self.target(far, side)
            self.exchange(target).wait_recv()

            def add(across):
                self.own[target, across, :] = (
                    self.own[target, across, :].astype(full) + self.sib[target, across, :].astype(full)
                ).astype(low)

            def add_all(across):
                self.own[target, across, :] = (
                    self.own[target, across, :].astype(full)
                    + self.sib[target, across, :].astype(full)
                    + self.arrived[target, across, :].astype(full)
                ).astype(low)

            if far == line.chips - 1:
                by_rows(self.rows, add)
            else:

                @pl.when(behind)
                def _():
                    self.send(target, side).wait_recv()
                    by_rows(self.rows, add_all)

                @pl.when(jnp.logical_not(behind))
                def _():
                    by_rows(self.rows, add)

            self.send(target, side).start()

    def total(self, total_ref):
        line = self.line
        chip = line.chip
        self.exchange(chip).wait_recv()

        @pl.when(line.has_left)
        def _():
            self.send(chip, 0).wait_recv()

        @pl.when(line.has_right)
        def _():
            self.send(chip, 1).wait_recv()

        def add(across):
            total = self.own[chip, across, :].astype(full) + self.sib[chip, across, :].astype(full)
            total = total + jnp.where(
                line.has_left, self.arrived[chip, across, :].astype(full), 0.0
            )
            total_ref[across, :] = total + jnp.where(
                line.has_right, self.arrived[line.chips, across, :].astype(full), 0.0
            )

        by_rows(self.rows, add)

    def finish(self):
        for far, side in self.order():

            @pl.when(self.there(far, side))
            def _():
                target = self.target(far, side)
                self.exchange(target).wait_send()
                if far > 0:
                    self.send(target, side).wait_send()


def blocks_nn(left_ref, right_ref, rows, tile=512):
    def block(target, store):
        start = pl.multiple_of(target * 2 * rows, 2 * rows)
        left_side = left_ref[pl.ds(start, 2 * rows), :]

        def step(index, unused):
            columns = pl.ds(pl.multiple_of(index * tile, tile), tile)
            store(columns, product(left_side, right_ref[:, columns]))
            return unused

        lax.fori_loop(0, right_ref.shape[1] // tile, step, 0)

    return block


def blocks_nt(left_ref, right_ref, rows, tile=512):
    def block(target, store):
        start = pl.multiple_of(target * 2 * rows, 2 * rows)
        left_side = left_ref[pl.ds(start, 2 * rows), :]

        def step(index, unused):
            columns = pl.ds(pl.multiple_of(index * tile, tile), tile)
            store(columns, product_nt(left_side, right_ref[columns, :]))
            return unused

        lax.fori_loop(0, right_ref.shape[0] // tile, step, 0)

    return block


class LineSwap:
    def __init__(self, line, send_of, recv_of, s_sem, r_sem):
        self.line, self.send_of, self.recv_of = line, send_of, recv_of
        self.s_sem, self.r_sem = s_sem, r_sem

    def copy(self, far, side, core):
        line = self.line
        if far == 0:
            peer, slot = line.sibling, self.r_sem.at[0, 0, 0]
        else:
            peer = (line.chip + (far if side == 0 else -far)) * 2 + core
            slot = self.r_sem.at[far, side, line.core]
        return remote(
            self.send_of(peer), self.recv_of(line.me), self.s_sem.at[far, side, core], slot, "ctx", peer
        )

    def legs(self, far):
        line = self.line
        if far == 0:
            return [(0, 0, True, True)]
        return [
            (
                side,
                core,
                (line.chip + far < line.chips) if side == 0 else (line.chip - far >= 0),
                (line.chip - far >= 0) if side == 0 else (line.chip + far < line.chips),
            )
            for side in range(2)
            for core in range(2)
        ]

    def start(self):
        for far in range(self.line.chips):
            for side, core, sends, _ in self.legs(far):
                if far == 0:
                    self.copy(far, side, core).start()
                else:

                    @pl.when(sends)
                    def _():
                        self.copy(far, side, core).start()

    def receive(self, far, then):
        line = self.line
        for side, core, _, comes in self.legs(far):
            if far == 0:
                source, slot = line.sibling, self.r_sem.at[0, 0, 0]
            else:
                source = (line.chip + (-far if side == 0 else far)) * 2 + core
                slot = self.r_sem.at[far, side, core]

            def wait():
                remote(
                    self.recv_of(source),
                    self.recv_of(source),
                    self.s_sem.at[far, side, core],
                    slot,
                    "ctx",
                    source,
                ).wait_recv()
                then(source)

            if far == 0:
                wait()
            else:
                pl.when(comes)(wait)

    def again(self, far, then):
        line = self.line
        for side, core, _, comes in self.legs(far):
            if far == 0:
                then(line.sibling)
            else:
                source = (line.chip + (-far if side == 0 else far)) * 2 + core

                @pl.when(comes)
                def _():
                    then(source)

    def finish(self):
        for far in range(self.line.chips):
            for side, core, sends, _ in self.legs(far):
                if far == 0:
                    self.copy(far, side, core).wait_send()
                else:

                    @pl.when(sends)
                    def _():
                        self.copy(far, side, core).wait_send()


def swap_scratch(pieces):
    return [DMA((pieces // 2, 2, 2))] * 2


class Share:
    def __init__(self, groups, place, s_sem, r_sem, relays=True):
        self.groups, self.place, self.s_sem, self.r_sem = groups, place, s_sem, r_sem
        self.group = lax.axis_index("seq")
        self.square = groups == 4 and relays
        self.across = self.group + 1 - 2 * lax.rem(self.group, 2)
        self.along = lax.rem(self.group + 2, groups)
        self.corner = groups - 1 - self.group

    def copy(self, source, slot, peer, origin, target):
        return remote(
            origin, target, self.s_sem.at[source, slot], self.r_sem.at[source, slot], "seq", peer
        )

    def half(self, index, source, which):
        ref = self.place(index, source)
        rows = ref.shape[0] // 2
        return ref.at[pl.ds(which * rows, rows)]

    def first(self, source, origin=None):
        target = self.place(self.group, source)
        origin = target if origin is None else origin
        if self.square:
            peers = [(1, self.across), (2, self.along)]
        else:
            peers = [
                (shift, lax.rem(self.group + shift, self.groups)) for shift in range(1, self.groups)
            ]
        return [self.copy(source, slot, peer, origin, target) for slot, peer in peers]

    def second(self, source):
        one, two = self.half(self.across, source, 0), self.half(self.along, source, 1)
        return [
            self.copy(source, 3, self.along, one, one),
            self.copy(source, 0, self.across, two, two),
        ]

    def send(self, source, origin=None):
        for copy in self.first(source, origin):
            copy.start()

    def relay(self, source):
        if not self.square:
            return
        for slot, index, copy in zip((1, 2), (self.across, self.along), self.second(source)):
            block = self.place(index, source)
            self.copy(source, slot, index, block, block).wait_recv()
            copy.start()

    def finish(self, sources):
        for source in range(sources):
            if self.square:
                for slot, which in ((3, 0), (0, 1)):
                    half = self.half(self.corner, source, which)
                    self.copy(source, slot, self.corner, half, half).wait_recv()
                for copy in self.second(source):
                    copy.wait_send()
            else:
                for shift in range(1, self.groups):
                    index = lax.rem(self.group + self.groups - shift, self.groups)
                    block = self.place(index, source)
                    self.copy(source, shift, index, block, block).wait_recv()
            for copy in self.first(source):
                copy.wait_send()


class Fold:
    def __init__(self, groups, term_ref, inbox, s_sem, r_sem):
        self.groups, self.term, self.inbox = groups, term_ref, inbox
        self.s_sem, self.r_sem = s_sem, r_sem
        self.group = lax.axis_index("seq")
        self.order = [lax.rem(self.group + shift, groups) for shift in range(1, groups)] + [
            self.group
        ]

    def copy(self, job):
        return remote(
            self.term.at[self.order[job]],
            self.inbox.at[job],
            self.s_sem.at[job],
            self.r_sem.at[job],
            "seq",
            self.order[job],
        )

    def ready(self, job):
        if job < self.groups - 1:
            self.copy(job).start()

    def arrive(self):
        for job in range(self.groups - 1):
            self.copy(job).wait_recv()

    def sum(self, across, own=None):
        total = (self.term[self.group, across, :] if own is None else own[across, :]).astype(full)
        for job in range(self.groups - 1):
            total = total + self.inbox[job, across, :].astype(full)
        return total

    def finish(self):
        for job in range(self.groups - 1):
            self.copy(job).wait_send()


class Spread:
    def __init__(self, groups, pieces):
        group, me = lax.axis_index("seq"), lax.axis_index("ctx")
        flat = group * pieces + me
        self.use = (lax.rem(flat, groups), flat // groups)
        held = me * groups + group
        self.rest = (held // pieces, lax.rem(held, pieces))
        self.moves = jnp.logical_or(self.use[0] != group, self.use[1] != me)

    def peers(self):
        return [(None, self.use, self.moves), (None, self.rest, self.moves)]

    def copy(self, source, target, send, receive, back):
        place = self.rest if back else self.use
        return pltpu.make_async_remote_copy(
            src_ref=source,
            dst_ref=target,
            send_sem=send,
            recv_sem=receive,
            device_id={"seq": place[0], "ctx": place[1]},
            device_id_type=MESH,
        )


def opening_kernel(
    shape,
    parts,
    hidden,
    gains_ref,
    query_weight,
    key_weight,
    value_weight,
    gate_weight,
    out_weight,
    normed,
    raw,
    attn_low,
    gains_out,
    out_low,
    hidden_all,
    blocks,
    out_block,
    gains_row,
    gains_all,
    corner,
    own_attn,
    own_out,
    out_s,
    out_r,
    ga_s,
    ga_r,
    gs_s,
    gs_r,
    at_s,
    at_r,
    as_s,
    as_r,
    os_s,
    os_r,
    *gather_sems,
):
    pieces, groups, heads, kv_heads, _ = shape
    line = Line(pieces)
    me, group = line.me, lax.axis_index("seq")
    rows, model = hidden.shape
    weight_rows = out_weight.shape[0]
    q_width, kv_width = heads * HD, kv_heads * HD
    copies = max(1, pieces // KV)
    spread = Spread(groups, pieces)
    greet(others("ctx", pieces) + others("seq", groups) + spread.peers())
    gain_count = gains_ref.shape[1]
    gains_row[...] = jnp.zeros(gains_row.shape, full)
    gains_row[0:1, pl.ds(0, gain_count)] = gains_ref[...].astype(low).astype(full)
    gains_all[group, me] = gains_row[...]
    gain_swap = LineSwap(
        line, lambda peer: gains_row, lambda source: gains_all.at[group, source], ga_s, ga_r
    )
    gain_swap.start()

    blocks[:, :, pl.ds(q_width + 2 * kv_width, HD)] = jnp.zeros((pieces, weight_rows, HD), low)
    corner[...] = jnp.zeros(corner.shape, full)
    corner[pl.ds(0, gate_weight.shape[0]), pl.ds(0, weight_rows)] = gate_weight[...]
    gate_rows = corner[...].T
    for piece in range(pieces):
        blocks[piece, :, pl.ds(0, q_width)] = query_weight[
            :, pl.ds(piece * q_width, q_width)
        ].astype(low)
        start = piece // copies * kv_width
        blocks[piece, :, pl.ds(q_width, kv_width)] = key_weight[:, pl.ds(start, kv_width)].astype(low)
        blocks[piece, :, pl.ds(q_width + kv_width, kv_width)] = value_weight[
            :, pl.ds(start, kv_width)
        ].astype(low)
        blocks[piece, :, pl.ds(q_width + 2 * kv_width, heads)] = gate_rows[
            :weight_rows, piece * heads : (piece + 1) * heads
        ].astype(low)

    def place(index, source):
        start = pl.multiple_of((index * pieces + source) * weight_rows, weight_rows)
        return attn_low.at[pl.ds(start, weight_rows)]

    attn_swap = LineSwap(
        line, lambda peer: blocks.at[peer], lambda source: place(group, source), at_s, at_r
    )
    attn_swap.start()
    share = Share(groups, place, as_s, as_r, False)
    share.send(me, blocks.at[me])
    attn_own = pltpu.make_async_copy(blocks.at[me], place(group, me), own_attn)
    attn_own.start()
    gather = Gather(line, parts, rows, hidden_all, gather_sems)
    gather.start(hidden)
    hidden_all[pl.ds(pl.multiple_of(me * rows, rows), rows), :] = hidden[...]
    out_block[...] = out_weight[...].astype(low)

    def out_place(index):
        return out_low.at[pl.ds(pl.multiple_of(index * weight_rows, weight_rows), weight_rows)]

    out_move = spread.copy(out_block, out_place(spread.use[0]), out_s, out_r, False)
    out_stay = pltpu.make_async_copy(out_block, out_place(group), own_out)

    @pl.when(spread.moves)
    def _():
        out_move.start()

    @pl.when(jnp.logical_not(spread.moves))
    def _():
        out_stay.start()

    def to_groups(shift):
        peer = lax.rem(group + shift, groups)
        return remote(
            gains_all.at[group], gains_all.at[group], gs_s.at[shift], gs_r.at[shift], "seq", peer
        )

    def from_groups(shift):
        peer = lax.rem(group + groups - shift, groups)
        return remote(
            gains_all.at[peer], gains_all.at[peer], gs_s.at[shift], gs_r.at[shift], "seq", peer
        )

    attn_swap.receive(0, share.send)
    for far in range(line.chips):
        gain_swap.receive(far, lambda source: None)
    for shift in range(1, groups):
        to_groups(shift).start()
    if line.chips > 1:
        attn_swap.receive(1, share.send)
    for shift in range(1, groups):
        from_groups(shift).wait_recv()
    for index in range(groups * pieces):
        gains_out[0:1, pl.ds(index * gain_count, gain_count)] = gains_all[
            index // pieces, index % pieces, 0:1, pl.ds(0, gain_count)
        ]

    def chip_rows(chip):
        return chip * 2 * rows

    def both(far, body):
        if far == 0:
            body(chip_rows(line.chip))
            return

        @pl.when(line.chip - far >= 0)
        def _():
            body(chip_rows(line.chip - far))

        @pl.when(line.chip + far < line.chips)
        def _():
            body(chip_rows(line.chip + far))

    def normalise(start):
        def some(part):
            across = pl.ds(pl.multiple_of(start + part.start, part.size), part.size)
            values = hidden_all[across, :].astype(full)
            inverse = lax.rsqrt(jnp.mean(values * values, axis=-1, keepdims=True) + epsilon)
            normed[across, :] = (values * inverse * gains_out[0:1, pl.ds(0, model)]).astype(low)

        by_rows(2 * rows, some)

    def project(start):
        across = pl.ds(pl.multiple_of(start, 2 * rows), 2 * rows)
        raw[across, :] = product(normed[across, :], attn_low[...])

    for far in range(2, line.chips):
        attn_swap.receive(far, share.send)
    out_share = Share(groups, lambda index, source: out_place(index), os_s, os_r)

    @pl.when(spread.moves)
    def _():
        spread.copy(out_place(group), out_place(group), out_s, out_r, False).wait_recv()

    @pl.when(jnp.logical_not(spread.moves))
    def _():
        out_stay.wait()

    out_share.send(0)
    for hop in range(1, line.chips - 1):
        gather.forward(hop)
        gather.arrive(hop - 1)
        both(hop - 1, normalise)
    gather.arrive(line.chips - 2)
    both(line.chips - 2, normalise)
    attn_own.wait()
    out_share.relay(0)
    share.finish(pieces)
    for far in range(line.chips - 1):
        both(far, project)
    gather.forward(line.chips - 1)
    gather.arrive(line.chips - 1)
    both(line.chips - 1, normalise)
    both(line.chips - 1, project)
    out_share.finish(1)
    gather.finish()
    gain_swap.finish()
    attn_swap.finish()
    for shift in range(1, groups):
        to_groups(shift).wait_send()

    @pl.when(spread.moves)
    def _():
        out_move.wait_send()


def opening(hidden, norm_gains, weights, shape, number, parts=2):
    pieces, groups, heads, kv_heads, _ = shape
    rows, model = hidden.shape
    weight_rows = weights[0].shape[0]
    gains = norm_gains.shape[0]
    padded = -(-gains // 128) * 128
    width = (heads + 2 * kv_heads + 1) * HD
    struct, vmem = jax.ShapeDtypeStruct, pltpu.VMEM
    return pl.pallas_call(
        functools.partial(opening_kernel, shape, parts),
        out_shape=(
            struct((pieces * rows, model), low),
            struct((pieces * rows, width), full),
            struct((model, width), low),
            struct((1, groups * pieces * gains), full),
            struct((groups * weight_rows, model), low),
        ),
        in_specs=[IN_VMEM] * 7,
        out_specs=(IN_VMEM,) * 5,
        scratch_shapes=[
            vmem((pieces * rows, model), low),
            vmem((pieces, weight_rows, width), low),
            vmem((weight_rows, model), low),
            vmem((8, padded), full),
            vmem((groups, pieces, 8, padded), full),
            vmem((HD, HD), full),
        ]
        + [DMA] * 4
        + swap_scratch(pieces)
        + [DMA((groups,))] * 2
        + swap_scratch(pieces)
        + [DMA((pieces, groups))] * 2
        + [DMA((1, groups))] * 2
        + gather_scratch(pieces, parts),
        compiler_params=pltpu.CompilerParams(
            collective_id=number, has_side_effects=True, vmem_limit_bytes=60 << 20
        ),
        name=f"opening_{number}",
    )(hidden, norm_gains.reshape(1, gains), *weights)


def lanes(start, size):
    return pl.ds(pl.multiple_of(start, 128), size)


def turn(values, cosine, sine):
    half = values.shape[0] // 2
    first, second = values[:half], values[half:]
    return jnp.concatenate(
        [first * cosine - second * sine, second * cosine + first * sine], axis=0
    )


def turn_back(values, cosine, sine):
    half = values.shape[0] // 2
    first, second = values[:half], values[half:]
    return jnp.concatenate(
        [first * cosine + second * sine, second * cosine - first * sine], axis=0
    )


def column(gains, start):
    return jnp.broadcast_to(gains[:, pl.ds(start, HD)], (HD, HD)).T[:, 0:1]


def inverse_rms(values):
    return lax.rsqrt(jnp.mean(values * values, axis=0, keepdims=True) + epsilon)


def kept(first_key, keys, first_query, queries, prefix):
    key = first_key + lax.broadcasted_iota(jnp.int32, (keys, queries), 0)
    query = first_query + lax.broadcasted_iota(jnp.int32, (keys, queries), 1)
    return key <= jnp.maximum(query, prefix - 1)


def query_blocks(length, body):
    tile = min(256, length // 2)
    half = length // 2

    def early(index, unused):
        body(index * tile, tile, half)
        return unused

    def late(index, unused):
        body(half + index * tile, tile, length)
        return unused

    lax.fori_loop(0, half // tile, early, 0)
    lax.fori_loop(0, half // tile, late, 0)


def attend_kernel(
    shape,
    raw,
    cosine,
    sine,
    gains,
    prefix_ref,
    out_low,
    hidden,
    out_grad,
    gate_weight,
    up_weight,
    raw_t,
    gate_t,
    q_ref,
    qt_ref,
    k_ref,
    kt_ref,
    v_ref,
    att_t,
    lse_ref,
    gated_t,
    middle,
    normed_two,
    og_all,
    ff_low,
    vt_ref,
    gated,
    blocks,
    own_sem,
    og_sem,
    swap_s,
    swap_r,
    share_s,
    share_r,
    *sems,
):
    pieces, groups, heads, kv_heads, ff_block = shape
    gather_sems, scatter_refs = sems[:6], sems[6:]
    line = Line(pieces)
    me, group = line.me, lax.axis_index("seq")
    length, rows = raw.shape[0], hidden.shape[0]
    greet(others("ctx", pieces) + others("seq", groups))
    own_width = groups * ff_block

    def prepare(across):
        for half, weight_ref in enumerate((gate_weight, up_weight)):
            for index in range(groups):
                for piece in range(pieces):
                    start = (index * pieces + piece) * ff_block
                    blocks[piece, across, pl.ds(half * own_width + index * ff_block, ff_block)] = (
                        weight_ref[across, pl.ds(start, ff_block)].astype(low)
                    )

    by_rows(gate_weight.shape[0], prepare, 16)
    swap = LineSwap(
        line, lambda peer: blocks.at[peer], lambda source: ff_low.at[group, source], swap_s, swap_r
    )
    swap.start()
    share = Share(groups, lambda index, source: ff_low.at[index, source], share_s, share_r, False)
    share.send(me, blocks.at[me])
    own = pltpu.make_async_copy(blocks.at[me], ff_low.at[group, me], own_sem)
    own.start()
    prefix = prefix_ref[0, 0]
    model = hidden.shape[1]
    query_gain, key_gain = column(gains, 2 * model), column(gains, 2 * model + HD)
    scale = HD ** (-0.5)
    for head in range(heads + kv_heads):
        part = pl.ds(head * HD, HD)
        values = raw[:, part].T
        raw_t[part, :] = values
        gain = query_gain if head < heads else key_gain
        turned = turn(values * inverse_rms(values) * gain, cosine[...], sine[...])
        if head < heads:
            qt_ref[part, :] = turned.astype(low)
            q_ref[:, part] = turned.T.astype(low)
        else:
            part = pl.ds((head - heads) * HD, HD)
            kt_ref[part, :] = turned.astype(low)
            k_ref[:, part] = turned.T.astype(low)
    for head in range(kv_heads):
        part = pl.ds(head * HD, HD)
        values = raw[:, pl.ds((heads + kv_heads + head) * HD, HD)]
        v_ref[:, part] = values.astype(low)
        vt_ref[part, :] = values.T.astype(low)
    gate_t[...] = raw[:, pl.ds((heads + 2 * kv_heads) * HD, HD)].T[: gate_t.shape[0]]
    swap.receive(0, share.send)
    for head in range(heads):
        part = pl.ds(head * HD, HD)
        kv_part = pl.ds(head * kv_heads // heads * HD, HD)

        def block(first, tile, keys):
            columns = lanes(first, tile)
            scores = product(k_ref[pl.ds(0, keys), kv_part], qt_ref[part, columns]) * scale
            scores = jnp.where(kept(0, keys, first, tile, prefix), scores, negative)
            top = jnp.max(scores, axis=0, keepdims=True)
            expanded = jnp.exp(scores - top)
            total = jnp.sum(expanded, axis=0, keepdims=True)
            lse_ref[head : head + 1, columns] = top + jnp.log(total)
            att_t[part, columns] = (
                product(vt_ref[kv_part, pl.ds(0, keys)], expanded.astype(low)) / total
            )

        query_blocks(length, block)
        scaled = att_t[part, :] * jax.nn.sigmoid(gate_t[head : head + 1, :])
        gated_t[part, :] = scaled.astype(low)
        gated[:, part] = scaled.T.astype(low)
        if head == 0 and line.chips > 1:
            swap.receive(1, share.send)

    gather = Gather(line, 2, rows, og_all, gather_sems)
    scatter = Scatter(line, rows, scatter_refs)
    scatter.clear()
    block = blocks_nn(gated, out_low, rows)
    last = line.chips - 1
    for far, side in scatter.order():
        if far == last:
            scatter.fill(far, side, block)
    gather.start(out_grad)
    start = pl.multiple_of(me * rows, rows)
    og_own = pltpu.make_async_copy(out_grad, og_all.at[pl.ds(start, rows)], og_sem)
    og_own.start()
    for far, side in scatter.order():
        if far == last:
            scatter.push(far, side)
    for far, side in scatter.order():
        if far < last:
            scatter.fill(far, side, block)
    for far in range(2, line.chips):
        swap.receive(far, share.send)
    for hop in range(1, line.chips):
        for far, side in scatter.order():
            if far == last - hop and far > 0:
                scatter.push(far, side)
        gather.forward(hop)
    scatter.total(middle)

    def normalise(across):
        values = hidden[across, :].astype(full) + middle[across, :]
        middle[across, :] = values
        inverse = lax.rsqrt(jnp.mean(values * values, axis=-1, keepdims=True) + epsilon)
        normed_two[across, :] = (values * inverse * gains[:, pl.ds(model, model)]).astype(low)

    by_rows(rows, normalise)
    og_own.wait()
    own.wait()
    gather.complete()
    scatter.finish()
    swap.finish()
    share.finish(pieces)


def attend(raw, tables, gains, prefix, out_low, hidden, out_grad, weights, shape, number):
    pieces, groups, heads, kv_heads, ff_block = shape
    length, rows, model = raw.shape[0], hidden.shape[0], hidden.shape[1]
    q_width, kv_width = heads * HD, kv_heads * HD
    weight_rows = weights[0].shape[0]
    struct = jax.ShapeDtypeStruct
    return pl.pallas_call(
        functools.partial(attend_kernel, shape),
        out_shape=(
            struct((q_width + kv_width, length), full),
            struct((8, length), full),
            struct((length, q_width), low),
            struct((q_width, length), low),
            struct((length, kv_width), low),
            struct((kv_width, length), low),
            struct((length, kv_width), low),
            struct((q_width, length), full),
            struct((8, length), full),
            struct((q_width, length), low),
            struct((rows, model), full),
            struct((rows, model), low),
            struct((length, model), low),
            struct((groups, pieces, weight_rows, 2 * groups * ff_block), low),
        ),
        in_specs=[IN_VMEM] * 4 + [pl.BlockSpec(memory_space=pltpu.SMEM)] + [IN_VMEM] * 5,
        out_specs=(IN_VMEM,) * 12 + (ANY, ANY),
        scratch_shapes=[
            pltpu.VMEM((kv_width, length), low),
            pltpu.VMEM((length, q_width), low),
            pltpu.VMEM((pieces, weight_rows, 2 * groups * ff_block), low),
            DMA,
            DMA,
        ]
        + swap_scratch(pieces)
        + [DMA((pieces, groups))] * 2
        + gather_scratch(pieces, 2)
        + scatter_scratch(pieces, rows, model),
        compiler_params=pltpu.CompilerParams(
            collective_id=number, has_side_effects=True, vmem_limit_bytes=60 << 20
        ),
        name=f"attend_{number}",
    )(raw, *tables, gains, prefix, out_low, hidden, out_grad, *weights)


def attend_back_kernel(
    shape,
    grad_branch,
    out_low,
    raw_t,
    gate_t,
    q_ref,
    qt_ref,
    k_ref,
    kt_ref,
    v_ref,
    att_t,
    lse_ref,
    gated_t,
    cosine,
    sine,
    gains,
    prefix_ref,
    normed,
    attn_low,
    hidden,
    grad_middle,
    swiglu_gain_grad,
    ff_share,
    down_term,
    hidden_grad,
    gains_grad,
    query_grad,
    key_grad,
    value_grad,
    head_grad,
    gate_grad,
    up_grad,
    out_grad,
    down_grad,
    down_in,
    down_mine,
    down_sem,
    ff_sem,
    corner,
    out_term,
    out_in,
    out_send,
    gg_t,
    ga_t,
    ga,
    gqt,
    dk,
    dv,
    grad_t,
    grad,
    total_ref,
    ff_recv,
    normed_part,
    part_sem,
    term,
    term_in,
    attn_send,
    attn_recv,
    gains_vector,
    gain_give,
    gain_sib,
    gain_row,
    gain_last,
    ffs_s,
    ffs_r,
    at_s,
    at_r,
    gc_s,
    gc_r,
    ts_s,
    ts_r,
    gs_s,
    gs_r,
    ot_s,
    ot_r,
    om_s,
    om_r,
    de_s,
    de_r,
    dl_s,
    dl_r,
    *scatter_refs,
):
    pieces, groups, heads, kv_heads, ff_block = shape
    line = Line(pieces)
    me, group = line.me, lax.axis_index("seq")
    length, rows = grad_branch.shape[0], hidden.shape[0]
    width, model = attn_low.shape[1], attn_low.shape[0]
    weight_rows = ff_share.shape[1]
    q_width, kv_width = heads * HD, kv_heads * HD
    spread = Spread(groups, pieces)
    greet(others("ctx", pieces) + others("seq", groups) + spread.peers())
    share = model // groups
    fold = Fold(groups, term, term_in, ts_s, ts_r)
    out_fold = Fold(groups, out_term, out_in, ot_s, ot_r)

    def load(job):
        index = fold.order[job]
        return pltpu.make_async_copy(
            normed.at[:, lanes(index * share, share)], normed_part.at[job % 2], part_sem.at[job % 2]
        )

    load(0).start()
    down_rows = down_in.shape[1]
    half = down_rows // 32 * 16
    early, late = pl.ds(0, half), pl.ds(half, down_rows - half)
    down_early = Fold(groups, down_term.at[:, early], down_in.at[:, early], de_s, de_r)
    down_late = Fold(groups, down_term.at[:, late], down_in.at[:, late], dl_s, dl_r)
    for job in range(groups):
        down_early.ready(job)
    down_own = pltpu.make_async_copy(down_term.at[group], down_mine, down_sem)
    down_own.start()
    ff_own = pltpu.make_async_copy(ff_share.at[me], ff_recv.at[me], ff_sem)
    ff_own.start()
    ff_swap = LineSwap(
        line, lambda peer: ff_share.at[peer], lambda source: ff_recv.at[source], ffs_s, ffs_r
    )
    ff_swap.start()

    prefix = prefix_ref[0, 0]
    query_gain, key_gain = column(gains, 2 * model), column(gains, 2 * model + HD)
    scale = HD ** (-0.5)

    def branch(index, unused):
        columns = lanes(index * 256, 256)
        gg_t[:, columns] = product_nt(out_low[...], grad_branch[columns, :])
        return unused

    lax.fori_loop(0, length // 256, branch, 0)

    def out_grads(index, unused):
        columns = lanes(index * 256, 256)
        value = product(gated_t[...], grad_branch[:, columns]).astype(low)
        for place in range(groups):
            out_term[place, :, columns] = value[place * weight_rows : (place + 1) * weight_rows]
        return unused

    lax.fori_loop(0, model // 256, out_grads, 0)

    for job in range(groups):
        out_fold.ready(job)
    dk[...] = jnp.zeros(dk.shape, full)
    dv[...] = jnp.zeros(dv.shape, full)
    gate_rows = []
    for head in range(heads):
        part = pl.ds(head * HD, HD)
        kv_part = pl.ds(head * kv_heads // heads * HD, HD)
        sigmoid = jax.nn.sigmoid(gate_t[head : head + 1, :])
        grads = gg_t[part, :]
        rounded = (grads * sigmoid).astype(low)
        ga_t[...] = rounded
        ga[...] = rounded.astype(full).T.astype(low)
        gate_rows.append(
            jnp.sum(grads * att_t[part, :], axis=0, keepdims=True) * sigmoid * (1.0 - sigmoid)
        )

        def block(first, tile, keys):
            columns, across = lanes(first, tile), pl.ds(0, keys)
            scores = product(k_ref[across, kv_part], qt_ref[part, columns]) * scale
            chance = jnp.where(
                kept(0, keys, first, tile, prefix),
                jnp.exp(scores - lse_ref[head : head + 1, columns]),
                0.0,
            )
            taken = ga_t[:, columns]
            delta = jnp.sum(taken.astype(full) * att_t[part, columns], axis=0, keepdims=True)
            change = product(v_ref[across, kv_part], taken)
            score_grad = (chance * (change - delta)).astype(low)
            gqt[part, columns] = product(kt_ref[kv_part, across], score_grad) * scale
            dk[across, kv_part] += product(score_grad, q_ref[columns, part])
            dv[across, kv_part] += product(chance.astype(low), ga[columns, :])

        query_blocks(length, block)

    gain_columns = [jnp.zeros((HD, 1), full), jnp.zeros((HD, 1), full)]
    for head in range(heads + kv_heads):
        part = pl.ds(head * HD, HD)
        if head < heads:
            turned = gqt[part, :]
            gain = query_gain
        else:
            turned = dk[:, pl.ds((head - heads) * HD, HD)].T * scale
            gain = key_gain
        grads = turn_back(turned, cosine[...], sine[...])
        values = raw_t[part, :]
        inverse = inverse_rms(values)
        kind = 0 if head < heads else 1
        gain_columns[kind] = gain_columns[kind] + jnp.sum(
            grads * values * inverse, axis=1, keepdims=True
        )
        scaled = grads * gain
        result = inverse * scaled - values * (
            inverse * inverse * inverse * jnp.mean(scaled * values, axis=0, keepdims=True)
        )
        grad_t[part, :] = result.astype(low)
        grad[:, part] = result.T.astype(low)
    for head in range(kv_heads):
        part = pl.ds((heads + kv_heads + head) * HD, HD)
        values = dv[:, pl.ds(head * HD, HD)]
        grad[:, part] = values.astype(low)
        grad_t[part, :] = values.T.astype(low)
    part = pl.ds((heads + 2 * kv_heads) * HD, HD)
    gate_block = jnp.concatenate(
        gate_rows + [jnp.zeros((HD - heads, length), full)], axis=0
    )
    grad_t[part, :] = gate_block.astype(low)
    grad[:, part] = gate_block.T.astype(low)

    scatter = Scatter(line, rows, scatter_refs)
    scatter.clear()
    block = blocks_nt(grad, attn_low, rows)
    last = line.chips - 1

    def fills(far):
        for distance, side in scatter.order():
            if distance == far:
                scatter.fill(far, side, block)

    def pushes(far):
        for distance, side in scatter.order():
            if distance == far and far > 0:
                scatter.push(far, side)

    def weight_grad(job):
        index = fold.order[job]
        load(job).wait()
        if job + 1 < groups:
            load(job + 1).start()

        def step(tile, unused):
            start = index * share + tile * 128
            value = product(grad_t[...], normed_part[job % 2, :, lanes(tile * 128, 128)])
            turned = value.T
            term[index, pl.ds(pl.multiple_of(tile * 128, 128), 128), :] = turned.astype(low)
            weighted = jnp.sum(
                turned * attn_low[pl.ds(pl.multiple_of(start, 128), 128), :].astype(full),
                axis=1,
                keepdims=True,
            )
            wide = jnp.broadcast_to(weighted, (128, 128)).T
            gains_vector[:, lanes(start, 128)] = wide[0:1, :] / gains[:, lanes(start, 128)]
            return unused

        lax.fori_loop(0, share // 128, step, 0)
        fold.ready(job)

    weight_grad(0)
    fills(last)
    pushes(last)
    for job in range(1, groups):
        weight_grad(job)
        if job <= last:
            fills(last - job)
    for far in range(last - groups, -1, -1):
        fills(far)

    for job in range(groups):
        down_late.ready(job)

    gain_count = gains_grad.shape[1]
    gains_vector[:, pl.ds(model, model)] = swiglu_gain_grad[...]
    for kind in range(2):
        wide = jnp.broadcast_to(gain_columns[kind], (HD, HD)).T
        gains_vector[:, pl.ds(2 * model + kind * HD, HD)] = wide[0:1, :]
    gain_give[...] = jnp.zeros(gain_give.shape, full)
    for index in range(groups * pieces):
        gain_give[index % pieces, index // pieces, 0:1, pl.ds(0, gain_count)] = gains_vector[
            :, pl.ds(index * gain_count, gain_count)
        ]
    gain_swap = LineSwap(
        line, lambda peer: gain_give.at[peer], lambda source: gain_sib.at[source], gc_s, gc_r
    )
    gain_swap.start()
    gain_sib[me] = gain_give[me]
    pushes(last - 1)

    out_fold.arrive()

    def total_out(across):
        out_send[across, :] = out_fold.sum(across).astype(low)

    by_rows(weight_rows, total_out, 16)
    out_move = spread.copy(out_send, out_grad, om_s, om_r, True)

    @pl.when(spread.moves)
    def _():
        out_move.start()

    @pl.when(jnp.logical_not(spread.moves))
    def _():
        out_grad[...] = out_send[...]

    for far in range(line.chips):
        gain_swap.receive(far, lambda source: None)
    gain_row[...] = jnp.sum(gain_sib[...], axis=0)

    def gain_to(shift):
        peer = lax.rem(group + shift, groups)
        return remote(
            gain_row.at[peer], gain_last.at[shift], gs_s.at[shift], gs_r.at[shift], "seq", peer
        )

    for shift in range(1, groups):
        gain_to(shift).start()
    gain_last[0] = gain_row[group]

    for far in range(line.chips):
        ff_swap.receive(far, lambda source: None)
    ff_own.wait()
    own_width = groups * ff_block

    def restore(across):
        for part, grad_ref in enumerate((gate_grad, up_grad)):
            for index in range(groups):
                for piece in range(pieces):
                    start = (index * pieces + piece) * ff_block
                    grad_ref[across, pl.ds(start, ff_block)] = ff_recv[
                        piece, across, pl.ds(part * own_width + index * ff_block, ff_block)
                    ]

    by_rows(weight_rows, restore, 16)

    for far in range(last - 2, 0, -1):
        pushes(far)

    fold.arrive()

    def total_term(piece, unused):
        across = pl.ds(pl.multiple_of(piece * weight_rows, weight_rows), weight_rows)
        attn_send[piece] = fold.sum(across).astype(low)
        return unused

    lax.fori_loop(0, pieces, total_term, 0)
    attn_swap = LineSwap(
        line, lambda peer: attn_send.at[peer], lambda source: attn_recv.at[source], at_s, at_r
    )
    attn_swap.start()

    scatter.total(total_ref)

    def rest(across):
        values = hidden[across, :].astype(full)
        inverse = lax.rsqrt(jnp.mean(values * values, axis=-1, keepdims=True) + epsilon)
        scaled = total_ref[across, :] * gains[:, pl.ds(0, model)]
        hidden_grad[across, :] = (
            grad_middle[across, :]
            + inverse * scaled
            - values
            * (inverse * inverse * inverse * jnp.mean(scaled * values, axis=-1, keepdims=True))
        ).astype(low)

    by_rows(rows, rest)
    down_early.arrive()
    down_late.arrive()
    down_own.wait()
    whole_fold = Fold(groups, down_term, down_in, de_s, de_r)

    def total_down(across):
        down_grad[across, :] = whole_fold.sum(across, down_mine).astype(low)

    by_rows(down_grad.shape[0], total_down, 16)
    for shift in range(1, groups):
        peer = lax.rem(group + groups - shift, groups)
        remote(
            gain_row.at[peer], gain_last.at[shift], gs_s.at[shift], gs_r.at[shift], "seq", peer
        ).wait_recv()
    gains_grad[...] = jnp.sum(gain_last[...], axis=0)[0:1, pl.ds(0, gain_count)]

    for far in range(line.chips):
        attn_swap.receive(far, lambda source: None)
    attn_recv[me] = attn_send[me]
    copies = max(1, pieces // KV)
    corner[...] = jnp.zeros(corner.shape, full)
    for piece in range(pieces):
        query_grad[:, pl.ds(piece * q_width, q_width)] = attn_recv[piece, :, pl.ds(0, q_width)]
        corner[pl.ds(0, weight_rows), pl.ds(piece * heads, heads)] = attn_recv[
            piece, :, pl.ds(q_width + 2 * kv_width, heads)
        ].astype(full)
    head_grad[...] = corner[...].T[: head_grad.shape[0], :weight_rows]
    for place in range(pieces // copies):
        for kind, grad_ref in enumerate((key_grad, value_grad)):
            columns = pl.ds(q_width + kind * kv_width, kv_width)
            summed = attn_recv[place * copies, :, columns].astype(full)
            for copy in range(1, copies):
                summed = summed + attn_recv[place * copies + copy, :, columns].astype(full)
            grad_ref[:, pl.ds(place * kv_width, kv_width)] = summed

    @pl.when(spread.moves)
    def _():
        spread.copy(out_grad, out_grad, om_s, om_r, True).wait_recv()
        out_move.wait_send()

    scatter.finish()
    ff_swap.finish()
    attn_swap.finish()
    gain_swap.finish()
    for shift in range(1, groups):
        gain_to(shift).wait_send()
    fold.finish()
    out_fold.finish()
    down_early.finish()
    down_late.finish()


def attend_back(
    grad_branch, out_low, saved, gated_t, tables, gains, prefix, normed, attn_low, hidden, grad_middle,
    swiglu_gain_grad, ff_share, down_term, gain_count, shape, number,
):
    pieces, groups, heads, kv_heads, ff_block = shape
    length, (rows, model) = grad_branch.shape[0], hidden.shape
    width = attn_low.shape[1]
    weight_rows = ff_share.shape[1]
    q_width, kv_width = heads * HD, kv_heads * HD
    struct, vmem = jax.ShapeDtypeStruct, pltpu.VMEM
    padded = -(-gain_count // 128) * 128
    return pl.pallas_call(
        functools.partial(attend_back_kernel, shape),
        out_shape=(
            struct((rows, model), low),
            struct((1, gain_count), full),
            struct((weight_rows, H * HD), low),
            struct((weight_rows, KV * HD), full),
            struct((weight_rows, KV * HD), full),
            struct((H, weight_rows), full),
            struct((weight_rows, pieces * groups * ff_block), low),
            struct((weight_rows, pieces * groups * ff_block), low),
            struct((weight_rows, model), low),
            struct(down_term.shape[1:], low),
        ),
        in_specs=[IN_VMEM] * 15 + [pl.BlockSpec(memory_space=pltpu.SMEM), ANY] + [IN_VMEM] * 4 + [ANY, ANY],
        out_specs=(IN_VMEM,) * 10,
        scratch_shapes=[
            vmem((groups - 1,) + down_term.shape[1:], low),
            vmem(down_term.shape[1:], low),
            DMA,
            DMA,
            vmem((HD, HD), full),
            vmem((groups, weight_rows, model), low),
            vmem((groups - 1, weight_rows, model), low),
            vmem((weight_rows, model), low),
            vmem((q_width, length), full),
            vmem((HD, length), low),
            vmem((length, HD), low),
            vmem((q_width, length), full),
            vmem((length, kv_width), full),
            vmem((length, kv_width), full),
            vmem((width, length), low),
            vmem((length, width), low),
            vmem((rows, model), full),
            vmem(ff_share.shape, low),
            vmem((2, length, model // groups), low),
            DMA((2,)),
            vmem((groups, model // groups, width), low),
            vmem((groups - 1, model // groups, width), low),
            vmem((pieces, weight_rows, width), low),
            vmem((pieces, weight_rows, width), low),
            vmem((1, 2 * model + 2 * HD), full),
            vmem((pieces, groups, 8, padded), full),
            vmem((pieces, groups, 8, padded), full),
            vmem((groups, 8, padded), full),
            vmem((groups, 8, padded), full),
        ]
        + swap_scratch(pieces) * 3
        + [DMA((groups,))] * 6
        + [DMA] * 2
        + [DMA((groups,))] * 4
        + scatter_scratch(pieces, rows, model),
        compiler_params=pltpu.CompilerParams(
            collective_id=number, has_side_effects=True, vmem_limit_bytes=67043328
        ),
        name=f"attend_back_{number}",
    )(
        grad_branch, out_low, *saved, gated_t, *tables, gains, prefix, normed, attn_low, hidden, grad_middle,
        swiglu_gain_grad, ff_share, down_term,
    )


def feed_kernel(
    shape,
    normed_two,
    ff_low,
    down_weight,
    og_all,
    n2_all,
    hidden_ff,
    grad_pre,
    down_low,
    down_block,
    before,
    share_s,
    share_r,
    *gather_sems,
):
    pieces, groups = shape[:2]
    line = Line(pieces)
    rows, length = normed_two.shape[0], og_all.shape[0]
    own_width = ff_low.shape[1] // 2
    tile = own_width // 3 if own_width % 384 == 0 else 128
    greet(line.peers() + others("seq", groups))
    group = lax.axis_index("seq")
    block_rows = down_weight.shape[0]

    def place(index, source):
        start = pl.multiple_of(index * block_rows, block_rows)
        return down_low.at[pl.ds(start, block_rows)]

    gather = Gather(line, 2, rows, n2_all, gather_sems)
    gather.start(normed_two)
    n2_all[pl.ds(pl.multiple_of(line.me * rows, rows), rows), :] = normed_two[...]

    def narrow(across):
        down_block[across, :] = down_weight[across, :].astype(low)

    by_rows(block_rows, narrow, 16)
    share = Share(groups, place, share_s, share_r, False)
    share.send(0, down_block)
    down_low[pl.ds(pl.multiple_of(group * block_rows, block_rows), block_rows), :] = down_block[...]

    def chip_rows(chip):
        across = pl.ds(pl.multiple_of(chip * 2 * rows, 2 * rows), 2 * rows)

        def step(index, unused):
            start = index * tile
            first, second = lanes(start, tile), lanes(own_width + start, tile)
            before[across, first] = product(n2_all[across, :], ff_low[:, first])
            before[across, second] = product(n2_all[across, :], ff_low[:, second])
            return unused

        lax.fori_loop(0, own_width // tile, step, 0)

    def compute(far):
        gather.arrive(far)
        if far == 0:
            chip_rows(line.chip)
            return

        @pl.when(line.chip - far >= 0)
        def _():
            chip_rows(line.chip - far)

        @pl.when(line.chip + far < line.chips)
        def _():
            chip_rows(line.chip + far)

    for hop in range(1, line.chips - 1):
        gather.forward(hop)
        compute(hop - 1)
    if line.chips > 1:
        compute(line.chips - 2)
        gather.forward(line.chips - 1)
    compute(line.chips - 1)
    share.finish(1)

    def swiglu(index, unused):
        across = pl.ds(pl.multiple_of(index * 256, 256), 256)

        def step(column, unused):
            first, second = lanes(column * tile, tile), lanes(own_width + column * tile, tile)
            grads = product_nt(og_all[across, :], down_low[lanes(column * tile, tile), :])
            gate, up = before[across, first], before[across, second]
            sigmoid = jax.nn.sigmoid(gate)
            silu = gate * sigmoid
            hidden_ff[across, first] = (silu * up).astype(low)
            grad_pre[across, first] = (
                grads * up * (sigmoid * (1.0 + gate * (1.0 - sigmoid)))
            ).astype(low)
            grad_pre[across, second] = (grads * silu).astype(low)
            return unused

        return lax.fori_loop(0, own_width // tile, step, unused)

    lax.fori_loop(0, length // 256, swiglu, 0)
    gather.finish()


def feed(normed_two, ff_low, down_weight, og_all, shape, number):
    pieces, groups = shape[:2]
    length, model = og_all.shape
    own_width = ff_low.shape[1] // 2
    struct = jax.ShapeDtypeStruct
    return pl.pallas_call(
        functools.partial(feed_kernel, shape),
        out_shape=(
            struct((length, model), low),
            struct((length, own_width), low),
            struct((length, 2 * own_width), low),
            struct((own_width, model), low),
        ),
        in_specs=[IN_VMEM] * 4,
        out_specs=(IN_VMEM,) * 4,
        scratch_shapes=[
            pltpu.VMEM(down_weight.shape, low),
            pltpu.VMEM((length, 2 * own_width), full),
            DMA((1, groups)),
            DMA((1, groups)),
        ]
        + gather_scratch(pieces, 2),
        compiler_params=pltpu.CompilerParams(
            collective_id=number, has_side_effects=True, vmem_limit_bytes=60 << 20
        ),
        name=f"feed_{number}",
    )(normed_two, ff_low, down_weight, og_all)


def feed_back_kernel(
    shape,
    grad_pre,
    ff_low,
    hidden_ff,
    down_low,
    og_all,
    n2_all,
    middle,
    out_grad,
    gains,
    gb_all,
    grad_middle,
    gain_grad,
    hidden_out,
    ff_share,
    down_term,
    total_ref,
    branch,
    n2_part,
    term,
    term_in,
    part_sem,
    own_sem,
    ts_s,
    ts_r,
    *sems,
):
    pieces, groups = shape[:2]
    buffers, sems = sems[:2], sems[2:]
    gather_sems, sems = sems[:6], sems[6:]
    line = Line(pieces)
    me, group = line.me, lax.axis_index("seq")
    length, rows, model = og_all.shape[0], middle.shape[0], og_all.shape[1]
    weight_rows = ff_share.shape[1]
    greet(line.peers() + others("seq", groups))
    half = len(sems) // 2
    inner = Scatter(line, rows, buffers + sems[:half])
    outer = Scatter(line, rows, buffers + sems[half:])
    inner.clear()
    outer.clear()
    block = blocks_nt(grad_pre, ff_low, rows)
    last = line.chips - 1

    def fills(scatter, far, block):
        for distance, side in scatter.order():
            if distance == far:
                scatter.fill(far, side, block)

    def pushes(scatter, far):
        for distance, side in scatter.order():
            if distance == far and far > 0:
                scatter.push(far, side)

    share = model // groups

    fold = Fold(groups, term, term_in, ts_s, ts_r)

    def load(job):
        index = fold.order[job]
        return pltpu.make_async_copy(
            n2_all.at[:, lanes(index * share, share)], n2_part.at[job % 2], part_sem.at[job % 2]
        )

    def ff_grad(job, index):
        load(job).wait()
        if job + 1 < groups:
            load(job + 1).start()

        def step(tile, unused):
            value = product_tn(n2_part[job % 2, :, lanes(tile * 128, 128)], grad_pre[...])
            term[index, pl.ds(pl.multiple_of(tile * 128, 128), 128), :] = value.astype(low)
            return unused

        lax.fori_loop(0, share // 128, step, 0)

    jobs = list(range(groups))

    def some_grads(count):
        for _ in range(min(count, len(jobs))):
            job = jobs.pop(0)
            ff_grad(job, fold.order[job])
            fold.ready(job)

    load(0).start()
    fills(inner, last, block)
    pushes(inner, last)
    fills(inner, last - 1, block)
    some_grads(1)
    each = -(-(groups - 1) // max(1, last - 1))
    for hop in range(1, line.chips):
        pushes(inner, last - hop)
        if hop < last:
            fills(inner, last - 1 - hop, block)
        some_grads(each)
    some_grads(groups)

    down_rows = down_term.shape[1]
    piece_rows = math.gcd(down_rows, 128)

    def down_grads(index, unused):
        value = product_tn(hidden_ff[:, lanes(index * 128, 128)], og_all[...]).astype(low)
        for part in range(128 // piece_rows):
            row = index * 128 + part * piece_rows
            down_term[row // down_rows, pl.ds(pl.multiple_of(lax.rem(row, down_rows), piece_rows), piece_rows), :] = (
                value[part * piece_rows : (part + 1) * piece_rows]
            )
        return unused

    lax.fori_loop(0, down_low.shape[0] // 128, down_grads, 0)
    inner.total(total_ref)
    inner.finish()
    gain_grad[...] = jnp.zeros(gain_grad.shape, full)

    def rest(across):
        values, grads = middle[across, :], total_ref[across, :]
        inverse = lax.rsqrt(jnp.mean(values * values, axis=-1, keepdims=True) + epsilon)
        gain_grad[...] += jnp.sum(grads * values * inverse, axis=0, keepdims=True)
        scaled = grads * gains[:, pl.ds(model, model)]
        result = (
            out_grad[across, :].astype(full)
            + inverse * scaled
            - values
            * (inverse * inverse * inverse * jnp.mean(scaled * values, axis=-1, keepdims=True))
        )
        grad_middle[across, :] = result
        branch[across, :] = result.astype(low)

    by_rows(rows, rest)

    gather = Gather(line, 2, rows, gb_all, gather_sems)
    gather.start(branch)
    start = pl.multiple_of(me * rows, rows)
    own = pltpu.make_async_copy(branch, gb_all.at[pl.ds(start, rows)], own_sem)
    own.start()
    block = blocks_nn(hidden_ff, down_low, rows)
    fills(outer, last, block)
    pushes(outer, last)
    fills(outer, last - 1, block)
    for hop in range(1, line.chips):
        gather.forward(hop)
        pushes(outer, last - hop)
        if hop < last:
            fills(outer, last - 1 - hop, block)
    fold.arrive()

    def total_term(piece, unused):
        across = pl.ds(pl.multiple_of(piece * weight_rows, weight_rows), weight_rows)
        ff_share[piece] = fold.sum(across).astype(low)
        return unused

    lax.fori_loop(0, pieces, total_term, 0)
    outer.total(total_ref)

    def output(across):
        hidden_out[across, :] = (middle[across, :] + total_ref[across, :]).astype(low)

    by_rows(rows, output)
    own.wait()
    for hop in range(line.chips):
        gather.arrive(hop)
    gather.finish()
    outer.finish()
    fold.finish()


def feed_back(
    grad_pre, ff_low, hidden_ff, down_low, og_all, n2_all, middle, out_grad, gains, shape, number
):
    pieces, groups = shape[:2]
    length, (rows, model) = og_all.shape[0], middle.shape
    own_width, width = hidden_ff.shape[1], grad_pre.shape[1]
    weight_rows = model // (groups * pieces)
    struct, vmem = jax.ShapeDtypeStruct, pltpu.VMEM
    scatter = scatter_scratch(pieces, rows, model)
    return pl.pallas_call(
        functools.partial(feed_back_kernel, shape),
        out_shape=(
            struct((length, model), low),
            struct((rows, model), full),
            struct((1, model), full),
            struct((rows, model), low),
            struct((pieces, weight_rows, width), low),
            struct((groups, own_width // groups, model), low),
        ),
        in_specs=[IN_VMEM] * 5 + [ANY] + [IN_VMEM] * 3,
        out_specs=(ANY,) + (IN_VMEM,) * 5,
        scratch_shapes=[
            vmem((rows, model), full),
            vmem((rows, model), low),
            vmem((2, length, model // groups), low),
            vmem((groups, model // groups, width), low),
            vmem((groups - 1, model // groups, width), low),
            DMA((2,)),
            DMA,
            DMA((groups,)),
            DMA((groups,)),
        ]
        + scatter[:2]
        + gather_scratch(pieces, 2)
        + scatter[2:] * 2,
        compiler_params=pltpu.CompilerParams(
            collective_id=number, has_side_effects=True, vmem_limit_bytes=63 << 20
        ),
        name=f"feed_back_{number}",
    )(grad_pre, ff_low, hidden_ff, down_low, og_all, n2_all, middle, out_grad, gains)


def widen_kernel(*refs):
    for source, target in zip(refs[: len(refs) // 2], refs[len(refs) // 2 :]):
        target[...] = source[...].astype(target.dtype)


def widen(arrays, kinds):
    steps = math.gcd(*(array.shape[0] for array in arrays[:-2])) // 16
    specs = [
        pl.BlockSpec((array.shape[0] // steps, array.shape[1]), lambda step: (step, 0))
        for array in arrays[:-2]
    ] + [pl.BlockSpec(array.shape, lambda step: (0, 0)) for array in arrays[-2:]]
    return pl.pallas_call(
        widen_kernel,
        grid=(steps,),
        out_shape=[
            jax.ShapeDtypeStruct(array.shape, kind) for array, kind in zip(arrays, kinds)
        ],
        in_specs=specs,
        out_specs=specs,
        name="widen",
    )(*arrays)


def on_device(
    hidden_in,
    out_grad,
    prefix_len,
    norm_gains,
    query_weight,
    key_weight,
    value_weight,
    head_gate_weight,
    out_weight,
    gate_weight,
    up_weight,
    down_weight,
):
    row_count, model = hidden_in.shape
    groups = lax.axis_size("seq")
    pieces = lax.axis_size("ctx")
    length = row_count * pieces
    weight_rows = query_weight.shape[0]
    heads = H // pieces
    kv_heads = max(1, KV // pieces)
    ff_block = down_weight.shape[0]
    ff_own = ff_block * groups
    gain_count = norm_gains.shape[0]
    shape = (pieces, groups, heads, kv_heads, ff_block)
    normed, raw, attn_low, gains_full, out_low = opening(
        hidden_in,
        norm_gains,
        (query_weight, key_weight, value_weight, head_gate_weight.T, out_weight),
        shape,
        0,
    )
    inverse = rope_base ** (-jnp.arange(HD // 2, dtype=full) * 2.0 / HD)
    angles = inverse[:, None] * jnp.arange(length, dtype=jnp.int32).astype(full)[None, :]
    tables = (jnp.cos(angles), jnp.sin(angles))
    prefix = prefix_len.reshape(1, 1)

    *saved, gated_t, middle, normed_two, out_grad_all, ff_low = attend(
        raw,
        tables,
        gains_full,
        prefix,
        out_low,
        hidden_in,
        out_grad,
        (gate_weight, up_weight),
        shape,
        1,
    )
    ff_low = ff_low.reshape(model, 2 * ff_own)
    n2_all, hidden_ff, grad_pre, down_low = feed(
        normed_two, ff_low, down_weight, out_grad_all, shape, 2
    )
    grad_branch, grad_middle, swiglu_gain_grad, hidden_out, ff_share, down_term = feed_back(
        grad_pre, ff_low, hidden_ff, down_low, out_grad_all, n2_all, middle, out_grad, gains_full, shape, 3
    )
    hidden_grad, gains_share, query_share, key_share, value_share, head_share, gate_share, up_share, output_share, down_share = (
        attend_back(
            grad_branch,
            out_low,
            saved,
            gated_t,
            tables,
            gains_full,
            prefix,
            normed,
            attn_low,
            hidden_in,
            grad_middle,
            swiglu_gain_grad,
            ff_share,
            down_term,
            gain_count,
            shape,
            4,
        )
    )
    (
        hidden_out,
        hidden_grad,
        query_share,
        key_share,
        value_share,
        output_share,
        gate_share,
        up_share,
        down_share,
        head_share,
        gains_share,
    ) = widen(
        (
            hidden_out,
            hidden_grad,
            query_share,
            key_share,
            value_share,
            output_share,
            gate_share,
            up_share,
            down_share,
            head_share,
            gains_share,
        ),
        (low, low) + (full,) * 9,
    )
    return (
        hidden_out,
        hidden_grad,
        gains_share.reshape(gain_count),
        query_share,
        key_share,
        value_share,
        head_share.T,
        output_share,
        gate_share,
        up_share,
        down_share,
    )


def solution(mesh):
    rows = P(("seq", "ctx"), None)
    return jax.shard_map(
        on_device,
        mesh=mesh,
        in_specs=(rows, rows, P("seq"), P(("seq", "ctx"))) + (rows,) * 8,
        out_specs=(rows, rows, P(("seq", "ctx"))) + (rows,) * 8,
        check_vma=False,
    )
```

```python
import functools
import math

import jax
import jax.numpy as jnp
from jax import lax
from jax.experimental import pallas as pl
from jax.experimental.pallas import tpu as pltpu
from jax.sharding import PartitionSpec as P

H = 16
KV = 8
HD = 128


epsilon = 1e-06
rope_base = 1000000.0
negative = -1e30
low = jnp.bfloat16
full = jnp.float32
MESH = pl.DeviceIdType.MESH
ANY = pl.BlockSpec(memory_space=pl.ANY)
IN_VMEM = pl.BlockSpec(memory_space=pltpu.VMEM)
DMA = pltpu.SemaphoreType.DMA


def product(left_side, right_side):
    return jnp.dot(left_side, right_side, preferred_element_type=full)


def product_nt(left_side, right_side):
    return lax.dot_general(
        left_side, right_side, (((1,), (1,)), ((), ())), preferred_element_type=full
    )


def product_tn(left_side, right_side):
    return lax.dot_general(
        left_side, right_side, (((0,), (0,)), ((), ())), preferred_element_type=full
    )


def by_rows(rows, body, tile=32):
    tile = min(tile, rows)

    def step(index, unused):
        body(pl.ds(pl.multiple_of(index * tile, tile), tile))
        return unused

    lax.fori_loop(0, rows // tile, step, 0)


def remote(source, target, send, receive, axis, peer):
    return pltpu.make_async_remote_copy(
        src_ref=source,
        dst_ref=target,
        send_sem=send,
        recv_sem=receive,
        device_id={axis: peer},
        device_id_type=MESH,
    )


def greet(peers):
    barrier = pltpu.get_barrier_semaphore()
    for axis, peer, exists in peers:
        place = {"seq": peer[0], "ctx": peer[1]} if axis is None else {axis: peer}

        def signal():
            pl.semaphore_signal(barrier, inc=1, device_id=place, device_id_type=MESH)

        if exists is True:
            signal()
        else:
            pl.when(exists)(signal)

    arrivals = sum(1 for _, _, exists in peers if exists is True)
    for _, _, exists in peers:
        if exists is not True:
            arrivals = arrivals + exists.astype(jnp.int32)
    pl.semaphore_wait(barrier, arrivals)


def others(axis, count):
    me = lax.axis_index(axis)
    return [(axis, lax.rem(me + shift, count), True) for shift in range(1, count)]


class Line:
    def __init__(self, pieces):
        self.chips = pieces // 2
        self.me = lax.axis_index("ctx")
        self.chip, self.core = self.me // 2, lax.rem(self.me, 2)
        self.sibling = self.me + 1 - 2 * self.core
        self.right, self.left = self.me + 2, self.me - 2
        self.has_right, self.has_left = self.chip < self.chips - 1, self.chip > 0

    def peers(self):
        return [
            ("ctx", self.sibling, True),
            ("ctx", self.right, self.has_right),
            ("ctx", self.left, self.has_left),
        ]


def gather_scratch(pieces, parts):
    chips = pieces // 2
    return [DMA((chips, 2, parts))] * 2 + [DMA((chips, parts))] * 4


class Gather:
    def __init__(self, line, parts, rows, out_ref, sems):
        self.line, self.parts, self.rows, self.out_ref = line, parts, rows, out_ref
        self.size = rows // parts
        self.sib_send, self.sib_recv, self.r_send, self.r_recv, self.l_send, self.l_recv = sems

    def at(self, position, part):
        start = pl.multiple_of(position * self.rows + part * self.size, self.size)
        return self.out_ref.at[pl.ds(start, self.size)]

    def to_sibling(self, source, hop, side, part, position):
        return remote(
            source,
            self.at(position, part),
            self.sib_send.at[hop, side, part],
            self.sib_recv.at[hop, side, part],
            "ctx",
            self.line.sibling,
        )

    def to_right(self, source, hop, part, position):
        return remote(
            source,
            self.at(position, part),
            self.r_send.at[hop, part],
            self.r_recv.at[hop, part],
            "ctx",
            self.line.right,
        )

    def to_left(self, source, hop, part, position):
        return remote(
            source,
            self.at(position, part),
            self.l_send.at[hop, part],
            self.l_recv.at[hop, part],
            "ctx",
            self.line.left,
        )

    def start(self, x_ref):
        line = self.line
        for part in range(self.parts):
            piece = x_ref.at[pl.ds(part * self.size, self.size)]

            @pl.when(line.has_right)
            def _():
                self.to_right(piece, 0, part, line.me).start()

            @pl.when(line.has_left)
            def _():
                self.to_left(piece, 0, part, line.me).start()

            self.to_sibling(piece, 0, 0, part, line.me).start()

    def forward(self, hop):
        line = self.line
        for part in range(self.parts):
            from_left, from_right = line.me - 2 * hop, line.me + 2 * hop

            @pl.when(line.chip - hop >= 0)
            def _():
                piece = self.at(from_left, part)
                self.to_right(piece, hop - 1, part, from_left).wait_recv()

                @pl.when(line.has_right)
                def _():
                    self.to_right(piece, hop, part, from_left).start()

                self.to_sibling(piece, hop, 0, part, from_left).start()

            @pl.when(line.chip + hop < line.chips)
            def _():
                piece = self.at(from_right, part)
                self.to_left(piece, hop - 1, part, from_right).wait_recv()

                @pl.when(line.has_left)
                def _():
                    self.to_left(piece, hop, part, from_right).start()

                self.to_sibling(piece, hop, 1, part, from_right).start()

    def legs(self, hop):
        line = self.line
        return [
            (
                side,
                (line.chip - hop >= 0) if side == 0 else (line.chip + hop < line.chips),
                (line.me - 2 * hop) if side == 0 else (line.me + 2 * hop),
            )
            for side in range(1 if hop == 0 else 2)
        ]

    def arrive(self, hop):
        for side, there, position in self.legs(hop):
            for part in range(self.parts):

                @pl.when(there)
                def _():
                    self.to_sibling(
                        self.at(position, part), hop, side, part, position
                    ).wait_recv()

    def finish(self):
        line = self.line
        for hop in range(line.chips):
            for side, there, position in self.legs(hop):
                for part in range(self.parts):

                    @pl.when(there)
                    def _():
                        piece = self.at(position, part)
                        self.to_sibling(piece, hop, side, part, position).wait_send()
                        if side == 0:

                            @pl.when(line.has_right)
                            def _():
                                self.to_right(piece, hop, part, position).wait_send()

                        if side == 1 or hop == 0:

                            @pl.when(line.has_left)
                            def _():
                                self.to_left(piece, hop, part, position).wait_send()

    def complete(self):
        for hop in range(self.line.chips):
            self.arrive(hop)
        self.finish()


def scatter_scratch(pieces, rows, width):
    chips = pieces // 2
    slots = pltpu.VMEM((chips, rows, width), low)
    return [slots] * 3 + [pltpu.VMEM((chips + 1, rows, width), low)] + [DMA((chips,))] * 6


class Scatter:
    def __init__(self, line, rows, scratch):
        self.line, self.rows = line, rows
        (
            self.own,
            self.give,
            self.sib,
            self.arrived,
            self.sib_send,
            self.sib_recv,
            self.r_send,
            self.r_recv,
            self.l_send,
            self.l_recv,
        ) = scratch

    def clear(self):
        line = self.line

        @pl.when(jnp.logical_not(line.has_left))
        def _():
            self.arrived[line.chip] = jnp.zeros(self.arrived.shape[1:], low)

        @pl.when(jnp.logical_not(line.has_right))
        def _():
            self.arrived[line.chips] = jnp.zeros(self.arrived.shape[1:], low)

    def there(self, far, side):
        line = self.line
        return (line.chip + far < line.chips) if side == 0 else (line.chip - far >= 0)

    def target(self, far, side):
        return self.line.chip + far if side == 0 else self.line.chip - far

    def exchange(self, target):
        return remote(
            self.give.at[target],
            self.sib.at[target],
            self.sib_send.at[target],
            self.sib_recv.at[target],
            "ctx",
            self.line.sibling,
        )

    def send(self, target, side):
        if side == 0:
            return remote(
                self.own.at[target],
                self.arrived.at[target],
                self.r_send.at[target],
                self.r_recv.at[target],
                "ctx",
                self.line.right,
            )
        chips, chip = self.line.chips, self.line.chip
        return remote(
            self.own.at[target],
            self.arrived.at[jnp.where(target == chip - 1, chips, target)],
            self.l_send.at[target],
            self.l_recv.at[target],
            "ctx",
            self.line.left,
        )

    def order(self):
        return [
            (far, side)
            for far in range(self.line.chips - 1, -1, -1)
            for side in range(2 if far else 1)
        ]

    def fill(self, far, side, block):
        @pl.when(self.there(far, side))
        def _():
            target = self.target(far, side)

            def store(columns, value):
                first, second = value[: self.rows], value[self.rows :]
                mine = self.line.core == 0
                self.own[target, :, columns] = jnp.where(mine, first, second).astype(low)
                self.give[target, :, columns] = jnp.where(mine, second, first).astype(low)

            block(target, store)
            self.exchange(target).start()

    def push(self, far, side):
        line = self.line
        behind = line.has_left if side == 0 else line.has_right

        @pl.when(self.there(far, side))
        def _():
            target = self.target(far, side)
            self.exchange(target).wait_recv()

            def add(across):
                self.own[target, across, :] = (
                    self.own[target, across, :].astype(full) + self.sib[target, across, :].astype(full)
                ).astype(low)

            def add_all(across):
                self.own[target, across, :] = (
                    self.own[target, across, :].astype(full)
                    + self.sib[target, across, :].astype(full)
                    + self.arrived[target, across, :].astype(full)
                ).astype(low)

            if far == line.chips - 1:
                by_rows(self.rows, add)
            else:

                @pl.when(behind)
                def _():
                    self.send(target, side).wait_recv()
                    by_rows(self.rows, add_all)

                @pl.when(jnp.logical_not(behind))
                def _():
                    by_rows(self.rows, add)

            self.send(target, side).start()

    def total(self, total_ref):
        line = self.line
        chip = line.chip
        self.exchange(chip).wait_recv()

        @pl.when(line.has_left)
        def _():
            self.send(chip, 0).wait_recv()

        @pl.when(line.has_right)
        def _():
            self.send(chip, 1).wait_recv()

        def add(across):
            total = self.own[chip, across, :].astype(full) + self.sib[chip, across, :].astype(full)
            total = total + jnp.where(
                line.has_left, self.arrived[chip, across, :].astype(full), 0.0
            )
            total_ref[across, :] = total + jnp.where(
                line.has_right, self.arrived[line.chips, across, :].astype(full), 0.0
            )

        by_rows(self.rows, add)

    def finish(self):
        for far, side in self.order():

            @pl.when(self.there(far, side))
            def _():
                target = self.target(far, side)
                self.exchange(target).wait_send()
                if far > 0:
                    self.send(target, side).wait_send()


def blocks_nn(left_ref, right_ref, rows, tile=512):
    def block(target, store):
        start = pl.multiple_of(target * 2 * rows, 2 * rows)
        left_side = left_ref[pl.ds(start, 2 * rows), :]

        def step(index, unused):
            columns = pl.ds(pl.multiple_of(index * tile, tile), tile)
            store(columns, product(left_side, right_ref[:, columns]))
            return unused

        lax.fori_loop(0, right_ref.shape[1] // tile, step, 0)

    return block


def blocks_nt(left_ref, right_ref, rows, tile=512):
    def block(target, store):
        start = pl.multiple_of(target * 2 * rows, 2 * rows)
        left_side = left_ref[pl.ds(start, 2 * rows), :]

        def step(index, unused):
            columns = pl.ds(pl.multiple_of(index * tile, tile), tile)
            store(columns, product_nt(left_side, right_ref[columns, :]))
            return unused

        lax.fori_loop(0, right_ref.shape[0] // tile, step, 0)

    return block


class LineSwap:
    def __init__(self, line, send_of, recv_of, s_sem, r_sem):
        self.line, self.send_of, self.recv_of = line, send_of, recv_of
        self.s_sem, self.r_sem = s_sem, r_sem

    def copy(self, far, side, core):
        line = self.line
        if far == 0:
            peer, slot = line.sibling, self.r_sem.at[0, 0, 0]
        else:
            peer = (line.chip + (far if side == 0 else -far)) * 2 + core
            slot = self.r_sem.at[far, side, line.core]
        return remote(
            self.send_of(peer), self.recv_of(line.me), self.s_sem.at[far, side, core], slot, "ctx", peer
        )

    def legs(self, far):
        line = self.line
        if far == 0:
            return [(0, 0, True, True)]
        return [
            (
                side,
                core,
                (line.chip + far < line.chips) if side == 0 else (line.chip - far >= 0),
                (line.chip - far >= 0) if side == 0 else (line.chip + far < line.chips),
            )
            for side in range(2)
            for core in range(2)
        ]

    def start(self):
        for far in range(self.line.chips):
            for side, core, sends, _ in self.legs(far):
                if far == 0:
                    self.copy(far, side, core).start()
                else:

                    @pl.when(sends)
                    def _():
                        self.copy(far, side, core).start()

    def receive(self, far, then):
        line = self.line
        for side, core, _, comes in self.legs(far):
            if far == 0:
                source, slot = line.sibling, self.r_sem.at[0, 0, 0]
            else:
                source = (line.chip + (-far if side == 0 else far)) * 2 + core
                slot = self.r_sem.at[far, side, core]

            def wait():
                remote(
                    self.recv_of(source),
                    self.recv_of(source),
                    self.s_sem.at[far, side, core],
                    slot,
                    "ctx",
                    source,
                ).wait_recv()
                then(source)

            if far == 0:
                wait()
            else:
                pl.when(comes)(wait)

    def again(self, far, then):
        line = self.line
        for side, core, _, comes in self.legs(far):
            if far == 0:
                then(line.sibling)
            else:
                source = (line.chip + (-far if side == 0 else far)) * 2 + core

                @pl.when(comes)
                def _():
                    then(source)

    def finish(self):
        for far in range(self.line.chips):
            for side, core, sends, _ in self.legs(far):
                if far == 0:
                    self.copy(far, side, core).wait_send()
                else:

                    @pl.when(sends)
                    def _():
                        self.copy(far, side, core).wait_send()


def swap_scratch(pieces):
    return [DMA((pieces // 2, 2, 2))] * 2


class Share:
    def __init__(self, groups, place, s_sem, r_sem, relays=True):
        self.groups, self.place, self.s_sem, self.r_sem = groups, place, s_sem, r_sem
        self.group = lax.axis_index("seq")
        self.square = groups == 4 and relays
        self.across = self.group + 1 - 2 * lax.rem(self.group, 2)
        self.along = lax.rem(self.group + 2, groups)
        self.corner = groups - 1 - self.group

    def copy(self, source, slot, peer, origin, target):
        return remote(
            origin, target, self.s_sem.at[source, slot], self.r_sem.at[source, slot], "seq", peer
        )

    def half(self, index, source, which):
        ref = self.place(index, source)
        rows = ref.shape[0] // 2
        return ref.at[pl.ds(which * rows, rows)]

    def first(self, source, origin=None):
        target = self.place(self.group, source)
        origin = target if origin is None else origin
        if self.square:
            peers = [(1, self.across), (2, self.along)]
        else:
            peers = [
                (shift, lax.rem(self.group + shift, self.groups)) for shift in range(1, self.groups)
            ]
        return [self.copy(source, slot, peer, origin, target) for slot, peer in peers]

    def second(self, source):
        one, two = self.half(self.across, source, 0), self.half(self.along, source, 1)
        return [
            self.copy(source, 3, self.along, one, one),
            self.copy(source, 0, self.across, two, two),
        ]

    def send(self, source, origin=None):
        for copy in self.first(source, origin):
            copy.start()

    def relay(self, source):
        if not self.square:
            return
        for slot, index, copy in zip((1, 2), (self.across, self.along), self.second(source)):
            block = self.place(index, source)
            self.copy(source, slot, index, block, block).wait_recv()
            copy.start()

    def finish(self, sources):
        for source in range(sources):
            if self.square:
                for slot, which in ((3, 0), (0, 1)):
                    half = self.half(self.corner, source, which)
                    self.copy(source, slot, self.corner, half, half).wait_recv()
                for copy in self.second(source):
                    copy.wait_send()
            else:
                for shift in range(1, self.groups):
                    index = lax.rem(self.group + self.groups - shift, self.groups)
                    block = self.place(index, source)
                    self.copy(source, shift, index, block, block).wait_recv()
            for copy in self.first(source):
                copy.wait_send()


class Fold:
    def __init__(self, groups, term_ref, inbox, s_sem, r_sem):
        self.groups, self.term, self.inbox = groups, term_ref, inbox
        self.s_sem, self.r_sem = s_sem, r_sem
        self.group = lax.axis_index("seq")
        self.order = [lax.rem(self.group + shift, groups) for shift in range(1, groups)] + [
            self.group
        ]

    def copy(self, job):
        return remote(
            self.term.at[self.order[job]],
            self.inbox.at[job],
            self.s_sem.at[job],
            self.r_sem.at[job],
            "seq",
            self.order[job],
        )

    def ready(self, job):
        if job < self.groups - 1:
            self.copy(job).start()

    def arrive(self):
        for job in range(self.groups - 1):
            self.copy(job).wait_recv()

    def sum(self, across, own=None):
        total = (self.term[self.group, across, :] if own is None else own[across, :]).astype(full)
        for job in range(self.groups - 1):
            total = total + self.inbox[job, across, :].astype(full)
        return total

    def finish(self):
        for job in range(self.groups - 1):
            self.copy(job).wait_send()


class Spread:
    def __init__(self, groups, pieces):
        group, me = lax.axis_index("seq"), lax.axis_index("ctx")
        flat = group * pieces + me
        self.use = (lax.rem(flat, groups), flat // groups)
        held = me * groups + group
        self.rest = (held // pieces, lax.rem(held, pieces))
        self.moves = jnp.logical_or(self.use[0] != group, self.use[1] != me)

    def peers(self):
        return [(None, self.use, self.moves), (None, self.rest, self.moves)]

    def copy(self, source, target, send, receive, back):
        place = self.rest if back else self.use
        return pltpu.make_async_remote_copy(
            src_ref=source,
            dst_ref=target,
            send_sem=send,
            recv_sem=receive,
            device_id={"seq": place[0], "ctx": place[1]},
            device_id_type=MESH,
        )


def lanes(start, size):
    return pl.ds(pl.multiple_of(start, 128), size)


def turn(values, cosine, sine):
    half = values.shape[0] // 2
    first, second = values[:half], values[half:]
    return jnp.concatenate(
        [first * cosine - second * sine, second * cosine + first * sine], axis=0
    )


def turn_back(values, cosine, sine):
    half = values.shape[0] // 2
    first, second = values[:half], values[half:]
    return jnp.concatenate(
        [first * cosine + second * sine, second * cosine - first * sine], axis=0
    )


def column(gains, start):
    return jnp.broadcast_to(gains[:, pl.ds(start, HD)], (HD, HD)).T[:, 0:1]


def inverse_rms(values):
    return lax.rsqrt(jnp.mean(values * values, axis=0, keepdims=True) + epsilon)


def kept(first_key, keys, first_query, queries, prefix):
    key = first_key + lax.broadcasted_iota(jnp.int32, (keys, queries), 0)
    query = first_query + lax.broadcasted_iota(jnp.int32, (keys, queries), 1)
    return key <= jnp.maximum(query, prefix - 1)


def query_blocks(length, body):
    tile = min(256, length // 2)
    half = length // 2

    def early(index, unused):
        body(index * tile, tile, half)
        return unused

    def late(index, unused):
        body(half + index * tile, tile, length)
        return unused

    lax.fori_loop(0, half // tile, early, 0)
    lax.fori_loop(0, half // tile, late, 0)


def forward_kernel(
    shape,
    hidden,
    gains_ref,
    query_weight,
    key_weight,
    value_weight,
    gate_weight_t,
    out_weight,
    cosine,
    sine,
    prefix_ref,
    out_grad,
    gate_weight,
    up_weight,
    normed,
    attn_low,
    gains_out,
    out_low,
    raw_t,
    gate_t,
    q_ref,
    qt_ref,
    k_ref,
    kt_ref,
    v_ref,
    att_t,
    lse_ref,
    gated_t,
    middle,
    normed_two,
    og_all,
    ff_low,
    raw,
    hidden_all,
    blocks,
    out_block,
    gains_row,
    gains_all,
    corner,
    vt_ref,
    gated,
    ff_blocks,
    own_attn,
    own_out,
    out_s,
    out_r,
    ff_sem,
    og_sem,
    ga_s,
    ga_r,
    gs_s,
    gs_r,
    at_s,
    at_r,
    as_s,
    as_r,
    os_s,
    os_r,
    fs_s,
    fs_r,
    fh_s,
    fh_r,
    *sems,
):
    pieces, groups, heads, kv_heads, ff_block = shape
    rows_sems, og_sems, scatter_refs = sems[:6], sems[6:12], sems[12:]
    line = Line(pieces)
    me, group = line.me, lax.axis_index("seq")
    rows, model = hidden.shape
    length = pieces * rows
    weight_rows = out_weight.shape[0]
    q_width, kv_width = heads * HD, kv_heads * HD
    copies = max(1, pieces // KV)
    spread = Spread(groups, pieces)
    greet(others("ctx", pieces) + others("seq", groups) + spread.peers())
    gain_count = gains_ref.shape[1]
    gains_row[...] = jnp.zeros(gains_row.shape, full)
    gains_row[0:1, pl.ds(0, gain_count)] = gains_ref[...].astype(low).astype(full)
    gains_all[group, me] = gains_row[...]
    gain_swap = LineSwap(
        line, lambda peer: gains_row, lambda source: gains_all.at[group, source], ga_s, ga_r
    )
    gain_swap.start()

    blocks[:, :, pl.ds(q_width + 2 * kv_width, HD)] = jnp.zeros((pieces, weight_rows, HD), low)
    corner[...] = jnp.zeros(corner.shape, full)
    corner[pl.ds(0, gate_weight_t.shape[0]), pl.ds(0, weight_rows)] = gate_weight_t[...]
    gate_rows = corner[...].T
    for piece in range(pieces):
        blocks[piece, :, pl.ds(0, q_width)] = query_weight[
            :, pl.ds(piece * q_width, q_width)
        ].astype(low)
        start = piece // copies * kv_width
        blocks[piece, :, pl.ds(q_width, kv_width)] = key_weight[:, pl.ds(start, kv_width)].astype(low)
        blocks[piece, :, pl.ds(q_width + kv_width, kv_width)] = value_weight[
            :, pl.ds(start, kv_width)
        ].astype(low)
        blocks[piece, :, pl.ds(q_width + 2 * kv_width, heads)] = gate_rows[
            :weight_rows, piece * heads : (piece + 1) * heads
        ].astype(low)

    def place(index, source):
        start = pl.multiple_of((index * pieces + source) * weight_rows, weight_rows)
        return attn_low.at[pl.ds(start, weight_rows)]

    attn_swap = LineSwap(
        line, lambda peer: blocks.at[peer], lambda source: place(group, source), at_s, at_r
    )
    attn_swap.start()
    share = Share(groups, place, as_s, as_r, False)
    share.send(me, blocks.at[me])
    attn_own = pltpu.make_async_copy(blocks.at[me], place(group, me), own_attn)
    attn_own.start()
    gather = Gather(line, 2, rows, hidden_all, rows_sems)
    gather.start(hidden)
    hidden_all[pl.ds(pl.multiple_of(me * rows, rows), rows), :] = hidden[...]
    out_block[...] = out_weight[...].astype(low)

    def out_place(index):
        return out_low.at[pl.ds(pl.multiple_of(index * weight_rows, weight_rows), weight_rows)]

    out_move = spread.copy(out_block, out_place(spread.use[0]), out_s, out_r, False)
    out_stay = pltpu.make_async_copy(out_block, out_place(group), own_out)

    @pl.when(spread.moves)
    def _():
        out_move.start()

    @pl.when(jnp.logical_not(spread.moves))
    def _():
        out_stay.start()

    def to_groups(shift):
        peer = lax.rem(group + shift, groups)
        return remote(
            gains_all.at[group], gains_all.at[group], gs_s.at[shift], gs_r.at[shift], "seq", peer
        )

    def from_groups(shift):
        peer = lax.rem(group + groups - shift, groups)
        return remote(
            gains_all.at[peer], gains_all.at[peer], gs_s.at[shift], gs_r.at[shift], "seq", peer
        )

    attn_swap.receive(0, share.send)
    for far in range(line.chips):
        gain_swap.receive(far, lambda source: None)
    for shift in range(1, groups):
        to_groups(shift).start()
    if line.chips > 1:
        attn_swap.receive(1, share.send)

    def chip_rows(chip):
        return chip * 2 * rows

    def both(far, body):
        if far == 0:
            body(chip_rows(line.chip))
            return

        @pl.when(line.chip - far >= 0)
        def _():
            body(chip_rows(line.chip - far))

        @pl.when(line.chip + far < line.chips)
        def _():
            body(chip_rows(line.chip + far))

    def normalise(start):
        def some(part):
            across = pl.ds(pl.multiple_of(start + part.start, part.size), part.size)
            values = hidden_all[across, :].astype(full)
            inverse = lax.rsqrt(jnp.mean(values * values, axis=-1, keepdims=True) + epsilon)
            normed[across, :] = (values * inverse * gains_out[0:1, pl.ds(0, model)]).astype(low)

        by_rows(2 * rows, some)

    def project(start):
        across = pl.ds(pl.multiple_of(start, 2 * rows), 2 * rows)
        raw[across, :] = product(normed[across, :], attn_low[...])

    for far in range(2, line.chips):
        attn_swap.receive(far, share.send)
    out_share = Share(groups, lambda index, source: out_place(index), os_s, os_r)

    @pl.when(spread.moves)
    def _():
        spread.copy(out_place(group), out_place(group), out_s, out_r, False).wait_recv()

    @pl.when(jnp.logical_not(spread.moves))
    def _():
        out_stay.wait()

    out_share.send(0)
    for shift in range(1, groups):
        from_groups(shift).wait_recv()
    for index in range(groups * pieces):
        gains_out[0:1, pl.ds(index * gain_count, gain_count)] = gains_all[
            index // pieces, index % pieces, 0:1, pl.ds(0, gain_count)
        ]
    own_width = groups * ff_block

    def prepare(across):
        for half, weight_ref in enumerate((gate_weight, up_weight)):
            for index in range(groups):
                for piece in range(pieces):
                    start = (index * pieces + piece) * ff_block
                    ff_blocks[piece, across, pl.ds(half * own_width + index * ff_block, ff_block)] = (
                        weight_ref[across, pl.ds(start, ff_block)].astype(low)
                    )

    by_rows(gate_weight.shape[0], prepare, 16)
    for hop in range(1, line.chips - 1):
        gather.forward(hop)
        gather.arrive(hop - 1)
        both(hop - 1, normalise)
    ff_swap = LineSwap(
        line, lambda peer: ff_blocks.at[peer], lambda source: ff_low.at[group, source], fs_s, fs_r
    )
    ff_swap.start()
    ff_share = Share(groups, lambda index, source: ff_low.at[index, source], fh_s, fh_r, False)
    ff_share.send(me, ff_blocks.at[me])
    ff_own = pltpu.make_async_copy(ff_blocks.at[me], ff_low.at[group, me], ff_sem)
    ff_own.start()
    gather.arrive(line.chips - 2)
    both(line.chips - 2, normalise)
    attn_own.wait()
    out_share.relay(0)
    share.finish(pieces)
    for far in range(line.chips - 1):
        both(far, project)
    gather.forward(line.chips - 1)
    gather.arrive(line.chips - 1)
    both(line.chips - 1, normalise)
    both(line.chips - 1, project)
    og_gather = Gather(line, 2, rows, og_all, og_sems)
    og_gather.start(out_grad)
    start = pl.multiple_of(me * rows, rows)
    og_own = pltpu.make_async_copy(out_grad, og_all.at[pl.ds(start, rows)], og_sem)
    og_own.start()
    prefix = prefix_ref[0, 0]
    query_gain, key_gain = column(gains_out, 2 * model), column(gains_out, 2 * model + HD)
    scale = HD ** (-0.5)
    for head in range(heads + kv_heads):
        part = pl.ds(head * HD, HD)
        values = raw[:, part].T
        raw_t[part, :] = values
        gain = query_gain if head < heads else key_gain
        turned = turn(values * inverse_rms(values) * gain, cosine[...], sine[...])
        if head < heads:
            qt_ref[part, :] = turned.astype(low)
            q_ref[:, part] = turned.T.astype(low)
        else:
            part = pl.ds((head - heads) * HD, HD)
            kt_ref[part, :] = turned.astype(low)
            k_ref[:, part] = turned.T.astype(low)
    for head in range(kv_heads):
        part = pl.ds(head * HD, HD)
        values = raw[:, pl.ds((heads + kv_heads + head) * HD, HD)]
        v_ref[:, part] = values.astype(low)
        vt_ref[part, :] = values.T.astype(low)
    gate_t[...] = raw[:, pl.ds((heads + 2 * kv_heads) * HD, HD)].T[: gate_t.shape[0]]
    ff_swap.receive(0, ff_share.send)
    for head in range(heads):
        part = pl.ds(head * HD, HD)
        kv_part = pl.ds(head * kv_heads // heads * HD, HD)

        def block(first, tile, keys):
            columns = lanes(first, tile)
            scores = product(k_ref[pl.ds(0, keys), kv_part], qt_ref[part, columns]) * scale
            scores = jnp.where(kept(0, keys, first, tile, prefix), scores, negative)
            top = jnp.max(scores, axis=0, keepdims=True)
            expanded = jnp.exp(scores - top)
            total = jnp.sum(expanded, axis=0, keepdims=True)
            lse_ref[head : head + 1, columns] = top + jnp.log(total)
            att_t[part, columns] = (
                product(vt_ref[kv_part, pl.ds(0, keys)], expanded.astype(low)) / total
            )

        query_blocks(length, block)
        scaled = att_t[part, :] * jax.nn.sigmoid(gate_t[head : head + 1, :])
        gated_t[part, :] = scaled.astype(low)
        gated[:, part] = scaled.T.astype(low)
        if head == 0 and line.chips > 1:
            ff_swap.receive(1, ff_share.send)

    out_share.finish(1)
    scatter = Scatter(line, rows, scatter_refs)
    scatter.clear()
    block = blocks_nn(gated, out_low, rows)
    last = line.chips - 1
    for far, side in scatter.order():
        if far == last:
            scatter.fill(far, side, block)
    for far, side in scatter.order():
        if far == last:
            scatter.push(far, side)
    for far, side in scatter.order():
        if far < last:
            scatter.fill(far, side, block)
    for far in range(2, line.chips):
        ff_swap.receive(far, ff_share.send)
    for hop in range(1, line.chips):
        og_gather.forward(hop)
        for far, side in scatter.order():
            if far == last - hop and far > 0:
                scatter.push(far, side)
    scatter.total(middle)

    def normalise_two(across):
        values = hidden[across, :].astype(full) + middle[across, :]
        middle[across, :] = values
        inverse = lax.rsqrt(jnp.mean(values * values, axis=-1, keepdims=True) + epsilon)
        normed_two[across, :] = (values * inverse * gains_out[:, pl.ds(model, model)]).astype(low)

    by_rows(rows, normalise_two)
    og_own.wait()
    ff_own.wait()
    og_gather.complete()
    scatter.finish()
    ff_swap.finish()
    ff_share.finish(pieces)
    gather.finish()
    gain_swap.finish()
    attn_swap.finish()
    for shift in range(1, groups):
        to_groups(shift).wait_send()

    @pl.when(spread.moves)
    def _():
        out_move.wait_send()


def forward(hidden, norm_gains, weights, tables, prefix, out_grad, ff_weights, shape, number):
    pieces, groups, heads, kv_heads, ff_block = shape
    rows, model = hidden.shape
    length = pieces * rows
    weight_rows = weights[0].shape[0]
    gains = norm_gains.shape[0]
    padded = -(-gains // 128) * 128
    q_width, kv_width = heads * HD, kv_heads * HD
    width = (heads + 2 * kv_heads + 1) * HD
    ff_shape = (pieces, weight_rows, 2 * groups * ff_block)
    struct, vmem = jax.ShapeDtypeStruct, pltpu.VMEM
    return pl.pallas_call(
        functools.partial(forward_kernel, shape),
        out_shape=(
            struct((length, model), low),
            struct((model, width), low),
            struct((1, groups * pieces * gains), full),
            struct((groups * weight_rows, model), low),
            struct((q_width + kv_width, length), full),
            struct((8, length), full),
            struct((length, q_width), low),
            struct((q_width, length), low),
            struct((length, kv_width), low),
            struct((kv_width, length), low),
            struct((length, kv_width), low),
            struct((q_width, length), full),
            struct((8, length), full),
            struct((q_width, length), low),
            struct((rows, model), full),
            struct((rows, model), low),
            struct((length, model), low),
            struct((groups,) + ff_shape, low),
        ),
        in_specs=[IN_VMEM] * 9 + [pl.BlockSpec(memory_space=pltpu.SMEM)] + [IN_VMEM] * 3,
        out_specs=(IN_VMEM,) * 16 + (ANY, ANY),
        scratch_shapes=[
            vmem((length, width), full),
            vmem((length, model), low),
            vmem((pieces, weight_rows, width), low),
            vmem((weight_rows, model), low),
            vmem((8, padded), full),
            vmem((groups, pieces, 8, padded), full),
            vmem((HD, HD), full),
            vmem((kv_width, length), low),
            vmem((length, q_width), low),
            vmem(ff_shape, low),
        ]
        + [DMA] * 6
        + swap_scratch(pieces)
        + [DMA((groups,))] * 2
        + swap_scratch(pieces)
        + [DMA((pieces, groups))] * 2
        + [DMA((1, groups))] * 2
        + swap_scratch(pieces)
        + [DMA((pieces, groups))] * 2
        + gather_scratch(pieces, 2) * 2
        + scatter_scratch(pieces, rows, model),
        compiler_params=pltpu.CompilerParams(
            collective_id=number, has_side_effects=True, vmem_limit_bytes=67043328
        ),
        name=f"forward_{number}",
    )(
        hidden, norm_gains.reshape(1, gains), *weights, *tables, prefix, out_grad, *ff_weights,
    )


def attend_back_kernel(
    shape,
    grad_branch,
    out_low,
    raw_t,
    gate_t,
    q_ref,
    qt_ref,
    k_ref,
    kt_ref,
    v_ref,
    att_t,
    lse_ref,
    gated_t,
    cosine,
    sine,
    gains,
    prefix_ref,
    normed,
    attn_low,
    hidden,
    grad_middle,
    swiglu_gain_grad,
    ff_share,
    down_term,
    hidden_grad,
    gains_grad,
    query_grad,
    key_grad,
    value_grad,
    head_grad,
    gate_grad,
    up_grad,
    out_grad,
    down_grad,
    down_in,
    down_mine,
    down_sem,
    ff_sem,
    corner,
    out_term,
    out_in,
    out_send,
    gg_t,
    ga_t,
    ga,
    gqt,
    dk,
    dv,
    grad_t,
    grad,
    total_ref,
    ff_recv,
    normed_part,
    part_sem,
    term,
    term_in,
    attn_send,
    attn_recv,
    gains_vector,
    gain_give,
    gain_sib,
    gain_row,
    gain_last,
    ffs_s,
    ffs_r,
    at_s,
    at_r,
    gc_s,
    gc_r,
    ts_s,
    ts_r,
    gs_s,
    gs_r,
    ot_s,
    ot_r,
    om_s,
    om_r,
    de_s,
    de_r,
    dl_s,
    dl_r,
    *scatter_refs,
):
    pieces, groups, heads, kv_heads, ff_block = shape
    line = Line(pieces)
    me, group = line.me, lax.axis_index("seq")
    length, rows = grad_branch.shape[0], hidden.shape[0]
    width, model = attn_low.shape[1], attn_low.shape[0]
    weight_rows = ff_share.shape[1]
    q_width, kv_width = heads * HD, kv_heads * HD
    spread = Spread(groups, pieces)
    greet(others("ctx", pieces) + others("seq", groups) + spread.peers())
    share = model // groups
    fold = Fold(groups, term, term_in, ts_s, ts_r)
    out_fold = Fold(groups, out_term, out_in, ot_s, ot_r)

    def load(job):
        index = fold.order[job]
        return pltpu.make_async_copy(
            normed.at[:, lanes(index * share, share)], normed_part.at[job % 2], part_sem.at[job % 2]
        )

    load(0).start()
    down_rows = down_in.shape[1]
    half = down_rows // 32 * 16
    early, late = pl.ds(0, half), pl.ds(half, down_rows - half)
    down_early = Fold(groups, down_term.at[:, early], down_in.at[:, early], de_s, de_r)
    down_late = Fold(groups, down_term.at[:, late], down_in.at[:, late], dl_s, dl_r)
    for job in range(groups):
        down_early.ready(job)
    down_own = pltpu.make_async_copy(down_term.at[group], down_mine, down_sem)
    down_own.start()
    ff_own = pltpu.make_async_copy(ff_share.at[me], ff_recv.at[me], ff_sem)
    ff_own.start()
    ff_swap = LineSwap(
        line, lambda peer: ff_share.at[peer], lambda source: ff_recv.at[source], ffs_s, ffs_r
    )
    ff_swap.start()

    prefix = prefix_ref[0, 0]
    query_gain, key_gain = column(gains, 2 * model), column(gains, 2 * model + HD)
    scale = HD ** (-0.5)

    def branch(index, unused):
        columns = lanes(index * 256, 256)
        gg_t[:, columns] = product_nt(out_low[...], grad_branch[columns, :])
        return unused

    lax.fori_loop(0, length // 256, branch, 0)

    def out_grads(index, unused):
        columns = lanes(index * 256, 256)
        value = product(gated_t[...], grad_branch[:, columns]).astype(low)
        for place in range(groups):
            out_term[place, :, columns] = value[place * weight_rows : (place + 1) * weight_rows]
        return unused

    lax.fori_loop(0, model // 256, out_grads, 0)

    for job in range(groups):
        out_fold.ready(job)
    dk[...] = jnp.zeros(dk.shape, full)
    dv[...] = jnp.zeros(dv.shape, full)
    gate_rows = []
    for head in range(heads):
        part = pl.ds(head * HD, HD)
        kv_part = pl.ds(head * kv_heads // heads * HD, HD)
        sigmoid = jax.nn.sigmoid(gate_t[head : head + 1, :])
        grads = gg_t[part, :]
        rounded = (grads * sigmoid).astype(low)
        ga_t[...] = rounded
        ga[...] = rounded.astype(full).T.astype(low)
        gate_rows.append(
            jnp.sum(grads * att_t[part, :], axis=0, keepdims=True) * sigmoid * (1.0 - sigmoid)
        )

        def block(first, tile, keys):
            columns, across = lanes(first, tile), pl.ds(0, keys)
            scores = product(k_ref[across, kv_part], qt_ref[part, columns]) * scale
            chance = jnp.where(
                kept(0, keys, first, tile, prefix),
                jnp.exp(scores - lse_ref[head : head + 1, columns]),
                0.0,
            )
            taken = ga_t[:, columns]
            delta = jnp.sum(taken.astype(full) * att_t[part, columns], axis=0, keepdims=True)
            change = product(v_ref[across, kv_part], taken)
            score_grad = (chance * (change - delta)).astype(low)
            gqt[part, columns] = product(kt_ref[kv_part, across], score_grad) * scale
            dk[across, kv_part] += product(score_grad, q_ref[columns, part])
            dv[across, kv_part] += product(chance.astype(low), ga[columns, :])

        query_blocks(length, block)

    gain_columns = [jnp.zeros((HD, 1), full), jnp.zeros((HD, 1), full)]
    for head in range(heads + kv_heads):
        part = pl.ds(head * HD, HD)
        if head < heads:
            turned = gqt[part, :]
            gain = query_gain
        else:
            turned = dk[:, pl.ds((head - heads) * HD, HD)].T * scale
            gain = key_gain
        grads = turn_back(turned, cosine[...], sine[...])
        values = raw_t[part, :]
        inverse = inverse_rms(values)
        kind = 0 if head < heads else 1
        gain_columns[kind] = gain_columns[kind] + jnp.sum(
            grads * values * inverse, axis=1, keepdims=True
        )
        scaled = grads * gain
        result = inverse * scaled - values * (
            inverse * inverse * inverse * jnp.mean(scaled * values, axis=0, keepdims=True)
        )
        grad_t[part, :] = result.astype(low)
        grad[:, part] = result.T.astype(low)
    for head in range(kv_heads):
        part = pl.ds((heads + kv_heads + head) * HD, HD)
        values = dv[:, pl.ds(head * HD, HD)]
        grad[:, part] = values.astype(low)
        grad_t[part, :] = values.T.astype(low)
    part = pl.ds((heads + 2 * kv_heads) * HD, HD)
    gate_block = jnp.concatenate(
        gate_rows + [jnp.zeros((HD - heads, length), full)], axis=0
    )
    grad_t[part, :] = gate_block.astype(low)
    grad[:, part] = gate_block.T.astype(low)

    scatter = Scatter(line, rows, scatter_refs)
    scatter.clear()
    block = blocks_nt(grad, attn_low, rows)
    last = line.chips - 1

    def fills(far):
        for distance, side in scatter.order():
            if distance == far:
                scatter.fill(far, side, block)

    def pushes(far):
        for distance, side in scatter.order():
            if distance == far and far > 0:
                scatter.push(far, side)

    def weight_grad(job):
        index = fold.order[job]
        load(job).wait()
        if job + 1 < groups:
            load(job + 1).start()

        def step(tile, unused):
            start = index * share + tile * 128
            value = product(grad_t[...], normed_part[job % 2, :, lanes(tile * 128, 128)])
            turned = value.T
            term[index, pl.ds(pl.multiple_of(tile * 128, 128), 128), :] = turned.astype(low)
            weighted = jnp.sum(
                turned * attn_low[pl.ds(pl.multiple_of(start, 128), 128), :].astype(full),
                axis=1,
                keepdims=True,
            )
            wide = jnp.broadcast_to(weighted, (128, 128)).T
            gains_vector[:, lanes(start, 128)] = wide[0:1, :] / gains[:, lanes(start, 128)]
            return unused

        lax.fori_loop(0, share // 128, step, 0)
        fold.ready(job)

    weight_grad(0)
    fills(last)
    pushes(last)
    for job in range(1, groups):
        weight_grad(job)
        if job <= last:
            fills(last - job)
    for far in range(last - groups, -1, -1):
        fills(far)

    for job in range(groups):
        down_late.ready(job)

    gain_count = gains_grad.shape[1]
    gains_vector[:, pl.ds(model, model)] = swiglu_gain_grad[...]
    for kind in range(2):
        wide = jnp.broadcast_to(gain_columns[kind], (HD, HD)).T
        gains_vector[:, pl.ds(2 * model + kind * HD, HD)] = wide[0:1, :]
    gain_give[...] = jnp.zeros(gain_give.shape, full)
    for index in range(groups * pieces):
        gain_give[index % pieces, index // pieces, 0:1, pl.ds(0, gain_count)] = gains_vector[
            :, pl.ds(index * gain_count, gain_count)
        ]
    gain_swap = LineSwap(
        line, lambda peer: gain_give.at[peer], lambda source: gain_sib.at[source], gc_s, gc_r
    )
    gain_swap.start()
    gain_sib[me] = gain_give[me]
    pushes(last - 1)

    out_fold.arrive()

    def total_out(across):
        out_send[across, :] = out_fold.sum(across).astype(low)

    by_rows(weight_rows, total_out, 16)
    out_move = spread.copy(out_send, out_grad, om_s, om_r, True)

    @pl.when(spread.moves)
    def _():
        out_move.start()

    @pl.when(jnp.logical_not(spread.moves))
    def _():
        out_grad[...] = out_send[...]

    for far in range(line.chips):
        gain_swap.receive(far, lambda source: None)
    gain_row[...] = jnp.sum(gain_sib[...], axis=0)

    def gain_to(shift):
        peer = lax.rem(group + shift, groups)
        return remote(
            gain_row.at[peer], gain_last.at[shift], gs_s.at[shift], gs_r.at[shift], "seq", peer
        )

    for shift in range(1, groups):
        gain_to(shift).start()
    gain_last[0] = gain_row[group]

    for far in range(line.chips):
        ff_swap.receive(far, lambda source: None)
    ff_own.wait()
    own_width = groups * ff_block

    def restore(across):
        for part, grad_ref in enumerate((gate_grad, up_grad)):
            for index in range(groups):
                for piece in range(pieces):
                    start = (index * pieces + piece) * ff_block
                    grad_ref[across, pl.ds(start, ff_block)] = ff_recv[
                        piece, across, pl.ds(part * own_width + index * ff_block, ff_block)
                    ]

    by_rows(weight_rows, restore, 16)

    for far in range(last - 2, 0, -1):
        pushes(far)

    fold.arrive()

    def total_term(piece, unused):
        across = pl.ds(pl.multiple_of(piece * weight_rows, weight_rows), weight_rows)
        attn_send[piece] = fold.sum(across).astype(low)
        return unused

    lax.fori_loop(0, pieces, total_term, 0)
    attn_swap = LineSwap(
        line, lambda peer: attn_send.at[peer], lambda source: attn_recv.at[source], at_s, at_r
    )
    attn_swap.start()

    scatter.total(total_ref)

    def rest(across):
        values = hidden[across, :].astype(full)
        inverse = lax.rsqrt(jnp.mean(values * values, axis=-1, keepdims=True) + epsilon)
        scaled = total_ref[across, :] * gains[:, pl.ds(0, model)]
        hidden_grad[across, :] = (
            grad_middle[across, :]
            + inverse * scaled
            - values
            * (inverse * inverse * inverse * jnp.mean(scaled * values, axis=-1, keepdims=True))
        ).astype(low)

    by_rows(rows, rest)
    down_early.arrive()
    down_late.arrive()
    down_own.wait()
    whole_fold = Fold(groups, down_term, down_in, de_s, de_r)

    def total_down(across):
        down_grad[across, :] = whole_fold.sum(across, down_mine).astype(low)

    by_rows(down_grad.shape[0], total_down, 16)
    for shift in range(1, groups):
        peer = lax.rem(group + groups - shift, groups)
        remote(
            gain_row.at[peer], gain_last.at[shift], gs_s.at[shift], gs_r.at[shift], "seq", peer
        ).wait_recv()
    gains_grad[...] = jnp.sum(gain_last[...], axis=0)[0:1, pl.ds(0, gain_count)]

    for far in range(line.chips):
        attn_swap.receive(far, lambda source: None)
    attn_recv[me] = attn_send[me]
    copies = max(1, pieces // KV)
    corner[...] = jnp.zeros(corner.shape, full)
    for piece in range(pieces):
        query_grad[:, pl.ds(piece * q_width, q_width)] = attn_recv[piece, :, pl.ds(0, q_width)]
        corner[pl.ds(0, weight_rows), pl.ds(piece * heads, heads)] = attn_recv[
            piece, :, pl.ds(q_width + 2 * kv_width, heads)
        ].astype(full)
    head_grad[...] = corner[...].T[: head_grad.shape[0], :weight_rows]
    for place in range(pieces // copies):
        for kind, grad_ref in enumerate((key_grad, value_grad)):
            columns = pl.ds(q_width + kind * kv_width, kv_width)
            summed = attn_recv[place * copies, :, columns].astype(full)
            for copy in range(1, copies):
                summed = summed + attn_recv[place * copies + copy, :, columns].astype(full)
            grad_ref[:, pl.ds(place * kv_width, kv_width)] = summed

    @pl.when(spread.moves)
    def _():
        spread.copy(out_grad, out_grad, om_s, om_r, True).wait_recv()
        out_move.wait_send()

    scatter.finish()
    ff_swap.finish()
    attn_swap.finish()
    gain_swap.finish()
    for shift in range(1, groups):
        gain_to(shift).wait_send()
    fold.finish()
    out_fold.finish()
    down_early.finish()
    down_late.finish()


def attend_back(
    grad_branch, out_low, saved, gated_t, tables, gains, prefix, normed, attn_low, hidden, grad_middle,
    swiglu_gain_grad, ff_share, down_term, gain_count, shape, number,
):
    pieces, groups, heads, kv_heads, ff_block = shape
    length, (rows, model) = grad_branch.shape[0], hidden.shape
    width = attn_low.shape[1]
    weight_rows = ff_share.shape[1]
    q_width, kv_width = heads * HD, kv_heads * HD
    struct, vmem = jax.ShapeDtypeStruct, pltpu.VMEM
    padded = -(-gain_count // 128) * 128
    return pl.pallas_call(
        functools.partial(attend_back_kernel, shape),
        out_shape=(
            struct((rows, model), low),
            struct((1, gain_count), full),
            struct((weight_rows, H * HD), low),
            struct((weight_rows, KV * HD), full),
            struct((weight_rows, KV * HD), full),
            struct((H, weight_rows), full),
            struct((weight_rows, pieces * groups * ff_block), low),
            struct((weight_rows, pieces * groups * ff_block), low),
            struct((weight_rows, model), low),
            struct(down_term.shape[1:], low),
        ),
        in_specs=[IN_VMEM] * 15 + [pl.BlockSpec(memory_space=pltpu.SMEM), ANY] + [IN_VMEM] * 4 + [ANY, ANY],
        out_specs=(IN_VMEM,) * 10,
        scratch_shapes=[
            vmem((groups - 1,) + down_term.shape[1:], low),
            vmem(down_term.shape[1:], low),
            DMA,
            DMA,
            vmem((HD, HD), full),
            vmem((groups, weight_rows, model), low),
            vmem((groups - 1, weight_rows, model), low),
            vmem((weight_rows, model), low),
            vmem((q_width, length), full),
            vmem((HD, length), low),
            vmem((length, HD), low),
            vmem((q_width, length), full),
            vmem((length, kv_width), full),
            vmem((length, kv_width), full),
            vmem((width, length), low),
            vmem((length, width), low),
            vmem((rows, model), full),
            vmem(ff_share.shape, low),
            vmem((2, length, model // groups), low),
            DMA((2,)),
            vmem((groups, model // groups, width), low),
            vmem((groups - 1, model // groups, width), low),
            vmem((pieces, weight_rows, width), low),
            vmem((pieces, weight_rows, width), low),
            vmem((1, 2 * model + 2 * HD), full),
            vmem((pieces, groups, 8, padded), full),
            vmem((pieces, groups, 8, padded), full),
            vmem((groups, 8, padded), full),
            vmem((groups, 8, padded), full),
        ]
        + swap_scratch(pieces) * 3
        + [DMA((groups,))] * 6
        + [DMA] * 2
        + [DMA((groups,))] * 4
        + scatter_scratch(pieces, rows, model),
        compiler_params=pltpu.CompilerParams(
            collective_id=number, has_side_effects=True, vmem_limit_bytes=67043328
        ),
        name=f"attend_back_{number}",
    )(
        grad_branch, out_low, *saved, gated_t, *tables, gains, prefix, normed, attn_low, hidden, grad_middle,
        swiglu_gain_grad, ff_share, down_term,
    )


def feed_kernel(
    shape,
    normed_two,
    ff_low,
    down_weight,
    og_all,
    n2_all,
    hidden_ff,
    grad_pre,
    down_low,
    down_block,
    before,
    share_s,
    share_r,
    *gather_sems,
):
    pieces, groups = shape[:2]
    line = Line(pieces)
    rows, length = normed_two.shape[0], og_all.shape[0]
    own_width = ff_low.shape[1] // 2
    tile = own_width // 3 if own_width % 384 == 0 else 128
    greet(line.peers() + others("seq", groups))
    group = lax.axis_index("seq")
    block_rows = down_weight.shape[0]

    def place(index, source):
        start = pl.multiple_of(index * block_rows, block_rows)
        return down_low.at[pl.ds(start, block_rows)]

    gather = Gather(line, 2, rows, n2_all, gather_sems)
    gather.start(normed_two)
    n2_all[pl.ds(pl.multiple_of(line.me * rows, rows), rows), :] = normed_two[...]

    def narrow(across):
        down_block[across, :] = down_weight[across, :].astype(low)

    by_rows(block_rows, narrow, 16)
    share = Share(groups, place, share_s, share_r, False)
    share.send(0, down_block)
    down_low[pl.ds(pl.multiple_of(group * block_rows, block_rows), block_rows), :] = down_block[...]

    def chip_rows(chip):
        across = pl.ds(pl.multiple_of(chip * 2 * rows, 2 * rows), 2 * rows)

        def step(index, unused):
            start = index * tile
            first, second = lanes(start, tile), lanes(own_width + start, tile)
            before[across, first] = product(n2_all[across, :], ff_low[:, first])
            before[across, second] = product(n2_all[across, :], ff_low[:, second])
            return unused

        lax.fori_loop(0, own_width // tile, step, 0)

    def compute(far):
        gather.arrive(far)
        if far == 0:
            chip_rows(line.chip)
            return

        @pl.when(line.chip - far >= 0)
        def _():
            chip_rows(line.chip - far)

        @pl.when(line.chip + far < line.chips)
        def _():
            chip_rows(line.chip + far)

    for hop in range(1, line.chips - 1):
        gather.forward(hop)
        compute(hop - 1)
    if line.chips > 1:
        compute(line.chips - 2)
        gather.forward(line.chips - 1)
    compute(line.chips - 1)
    share.finish(1)

    def swiglu(index, unused):
        across = pl.ds(pl.multiple_of(index * 256, 256), 256)

        def step(column, unused):
            first, second = lanes(column * tile, tile), lanes(own_width + column * tile, tile)
            grads = product_nt(og_all[across, :], down_low[lanes(column * tile, tile), :])
            gate, up = before[across, first], before[across, second]
            sigmoid = jax.nn.sigmoid(gate)
            silu = gate * sigmoid
            hidden_ff[across, first] = (silu * up).astype(low)
            grad_pre[across, first] = (
                grads * up * (sigmoid * (1.0 + gate * (1.0 - sigmoid)))
            ).astype(low)
            grad_pre[across, second] = (grads * silu).astype(low)
            return unused

        return lax.fori_loop(0, own_width // tile, step, unused)

    lax.fori_loop(0, length // 256, swiglu, 0)
    gather.finish()


def feed(normed_two, ff_low, down_weight, og_all, shape, number):
    pieces, groups = shape[:2]
    length, model = og_all.shape
    own_width = ff_low.shape[1] // 2
    struct = jax.ShapeDtypeStruct
    return pl.pallas_call(
        functools.partial(feed_kernel, shape),
        out_shape=(
            struct((length, model), low),
            struct((length, own_width), low),
            struct((length, 2 * own_width), low),
            struct((own_width, model), low),
        ),
        in_specs=[IN_VMEM] * 4,
        out_specs=(IN_VMEM,) * 4,
        scratch_shapes=[
            pltpu.VMEM(down_weight.shape, low),
            pltpu.VMEM((length, 2 * own_width), full),
            DMA((1, groups)),
            DMA((1, groups)),
        ]
        + gather_scratch(pieces, 2),
        compiler_params=pltpu.CompilerParams(
            collective_id=number, has_side_effects=True, vmem_limit_bytes=60 << 20
        ),
        name=f"feed_{number}",
    )(normed_two, ff_low, down_weight, og_all)


def feed_back_kernel(
    shape,
    grad_pre,
    ff_low,
    hidden_ff,
    down_low,
    og_all,
    n2_all,
    middle,
    out_grad,
    gains,
    gb_all,
    grad_middle,
    gain_grad,
    hidden_out,
    ff_share,
    down_term,
    total_ref,
    branch,
    n2_part,
    term,
    term_in,
    part_sem,
    own_sem,
    ts_s,
    ts_r,
    *sems,
):
    pieces, groups = shape[:2]
    buffers, sems = sems[:2], sems[2:]
    gather_sems, sems = sems[:6], sems[6:]
    line = Line(pieces)
    me, group = line.me, lax.axis_index("seq")
    length, rows, model = og_all.shape[0], middle.shape[0], og_all.shape[1]
    weight_rows = ff_share.shape[1]
    greet(line.peers() + others("seq", groups))
    half = len(sems) // 2
    inner = Scatter(line, rows, buffers + sems[:half])
    outer = Scatter(line, rows, buffers + sems[half:])
    inner.clear()
    outer.clear()
    block = blocks_nt(grad_pre, ff_low, rows)
    last = line.chips - 1

    def fills(scatter, far, block):
        for distance, side in scatter.order():
            if distance == far:
                scatter.fill(far, side, block)

    def pushes(scatter, far):
        for distance, side in scatter.order():
            if distance == far and far > 0:
                scatter.push(far, side)

    share = model // groups

    fold = Fold(groups, term, term_in, ts_s, ts_r)

    def load(job):
        index = fold.order[job]
        return pltpu.make_async_copy(
            n2_all.at[:, lanes(index * share, share)], n2_part.at[job % 2], part_sem.at[job % 2]
        )

    def ff_grad(job, index):
        load(job).wait()
        if job + 1 < groups:
            load(job + 1).start()

        def step(tile, unused):
            value = product_tn(n2_part[job % 2, :, lanes(tile * 128, 128)], grad_pre[...])
            term[index, pl.ds(pl.multiple_of(tile * 128, 128), 128), :] = value.astype(low)
            return unused

        lax.fori_loop(0, share // 128, step, 0)

    jobs = list(range(groups))

    def some_grads(count):
        for _ in range(min(count, len(jobs))):
            job = jobs.pop(0)
            ff_grad(job, fold.order[job])
            fold.ready(job)

    load(0).start()
    fills(inner, last, block)
    pushes(inner, last)
    fills(inner, last - 1, block)
    some_grads(1)
    each = -(-(groups - 1) // max(1, last - 1))
    for hop in range(1, line.chips):
        pushes(inner, last - hop)
        if hop < last:
            fills(inner, last - 1 - hop, block)
        some_grads(each)
    some_grads(groups)

    down_rows = down_term.shape[1]
    piece_rows = math.gcd(down_rows, 128)

    def down_grads(index, unused):
        value = product_tn(hidden_ff[:, lanes(index * 128, 128)], og_all[...]).astype(low)
        for part in range(128 // piece_rows):
            row = index * 128 + part * piece_rows
            down_term[row // down_rows, pl.ds(pl.multiple_of(lax.rem(row, down_rows), piece_rows), piece_rows), :] = (
                value[part * piece_rows : (part + 1) * piece_rows]
            )
        return unused

    lax.fori_loop(0, down_low.shape[0] // 128, down_grads, 0)
    inner.total(total_ref)
    inner.finish()
    gain_grad[...] = jnp.zeros(gain_grad.shape, full)

    def rest(across):
        values, grads = middle[across, :], total_ref[across, :]
        inverse = lax.rsqrt(jnp.mean(values * values, axis=-1, keepdims=True) + epsilon)
        gain_grad[...] += jnp.sum(grads * values * inverse, axis=0, keepdims=True)
        scaled = grads * gains[:, pl.ds(model, model)]
        result = (
            out_grad[across, :].astype(full)
            + inverse * scaled
            - values
            * (inverse * inverse * inverse * jnp.mean(scaled * values, axis=-1, keepdims=True))
        )
        grad_middle[across, :] = result
        branch[across, :] = result.astype(low)

    by_rows(rows, rest)

    gather = Gather(line, 2, rows, gb_all, gather_sems)
    gather.start(branch)
    start = pl.multiple_of(me * rows, rows)
    own = pltpu.make_async_copy(branch, gb_all.at[pl.ds(start, rows)], own_sem)
    own.start()
    block = blocks_nn(hidden_ff, down_low, rows)
    fills(outer, last, block)
    pushes(outer, last)
    fills(outer, last - 1, block)
    for hop in range(1, line.chips):
        gather.forward(hop)
        pushes(outer, last - hop)
        if hop < last:
            fills(outer, last - 1 - hop, block)
    fold.arrive()

    def total_term(piece, unused):
        across = pl.ds(pl.multiple_of(piece * weight_rows, weight_rows), weight_rows)
        ff_share[piece] = fold.sum(across).astype(low)
        return unused

    lax.fori_loop(0, pieces, total_term, 0)
    outer.total(total_ref)

    def output(across):
        hidden_out[across, :] = (middle[across, :] + total_ref[across, :]).astype(low)

    by_rows(rows, output)
    own.wait()
    for hop in range(line.chips):
        gather.arrive(hop)
    gather.finish()
    outer.finish()
    fold.finish()


def feed_back(
    grad_pre, ff_low, hidden_ff, down_low, og_all, n2_all, middle, out_grad, gains, shape, number
):
    pieces, groups = shape[:2]
    length, (rows, model) = og_all.shape[0], middle.shape
    own_width, width = hidden_ff.shape[1], grad_pre.shape[1]
    weight_rows = model // (groups * pieces)
    struct, vmem = jax.ShapeDtypeStruct, pltpu.VMEM
    scatter = scatter_scratch(pieces, rows, model)
    return pl.pallas_call(
        functools.partial(feed_back_kernel, shape),
        out_shape=(
            struct((length, model), low),
            struct((rows, model), full),
            struct((1, model), full),
            struct((rows, model), low),
            struct((pieces, weight_rows, width), low),
            struct((groups, own_width // groups, model), low),
        ),
        in_specs=[IN_VMEM] * 5 + [ANY] + [IN_VMEM] * 3,
        out_specs=(ANY,) + (IN_VMEM,) * 5,
        scratch_shapes=[
            vmem((rows, model), full),
            vmem((rows, model), low),
            vmem((2, length, model // groups), low),
            vmem((groups, model // groups, width), low),
            vmem((groups - 1, model // groups, width), low),
            DMA((2,)),
            DMA,
            DMA((groups,)),
            DMA((groups,)),
        ]
        + scatter[:2]
        + gather_scratch(pieces, 2)
        + scatter[2:] * 2,
        compiler_params=pltpu.CompilerParams(
            collective_id=number, has_side_effects=True, vmem_limit_bytes=63 << 20
        ),
        name=f"feed_back_{number}",
    )(grad_pre, ff_low, hidden_ff, down_low, og_all, n2_all, middle, out_grad, gains)


def widen_kernel(*refs):
    for source, target in zip(refs[: len(refs) // 2], refs[len(refs) // 2 :]):
        target[...] = source[...].astype(target.dtype)


def widen(arrays, kinds):
    steps = math.gcd(*(array.shape[0] for array in arrays[:-2])) // 16
    specs = [
        pl.BlockSpec((array.shape[0] // steps, array.shape[1]), lambda step: (step, 0))
        for array in arrays[:-2]
    ] + [pl.BlockSpec(array.shape, lambda step: (0, 0)) for array in arrays[-2:]]
    return pl.pallas_call(
        widen_kernel,
        grid=(steps,),
        out_shape=[
            jax.ShapeDtypeStruct(array.shape, kind) for array, kind in zip(arrays, kinds)
        ],
        in_specs=specs,
        out_specs=specs,
        name="widen",
    )(*arrays)


def on_device(
    hidden_in,
    out_grad,
    prefix_len,
    norm_gains,
    query_weight,
    key_weight,
    value_weight,
    head_gate_weight,
    out_weight,
    gate_weight,
    up_weight,
    down_weight,
):
    row_count, model = hidden_in.shape
    groups = lax.axis_size("seq")
    pieces = lax.axis_size("ctx")
    length = row_count * pieces
    weight_rows = query_weight.shape[0]
    heads = H // pieces
    kv_heads = max(1, KV // pieces)
    ff_block = down_weight.shape[0]
    ff_own = ff_block * groups
    gain_count = norm_gains.shape[0]
    shape = (pieces, groups, heads, kv_heads, ff_block)
    inverse = rope_base ** (-jnp.arange(HD // 2, dtype=full) * 2.0 / HD)
    angles = inverse[:, None] * jnp.arange(length, dtype=jnp.int32).astype(full)[None, :]
    tables = (jnp.cos(angles), jnp.sin(angles))
    prefix = prefix_len.reshape(1, 1)

    (
        normed, attn_low, gains_full, out_low, *saved, gated_t, middle, normed_two, out_grad_all, ff_low
    ) = forward(
        hidden_in,
        norm_gains,
        (query_weight, key_weight, value_weight, head_gate_weight.T, out_weight),
        tables,
        prefix,
        out_grad,
        (gate_weight, up_weight),
        shape,
        0,
    )
    ff_low = ff_low.reshape(model, 2 * ff_own)
    n2_all, hidden_ff, grad_pre, down_low = feed(
        normed_two, ff_low, down_weight, out_grad_all, shape, 2
    )
    grad_branch, grad_middle, swiglu_gain_grad, hidden_out, ff_share, down_term = feed_back(
        grad_pre, ff_low, hidden_ff, down_low, out_grad_all, n2_all, middle, out_grad, gains_full, shape, 3
    )
    hidden_grad, gains_share, query_share, key_share, value_share, head_share, gate_share, up_share, output_share, down_share = (
        attend_back(
            grad_branch,
            out_low,
            saved,
            gated_t,
            tables,
            gains_full,
            prefix,
            normed,
            attn_low,
            hidden_in,
            grad_middle,
            swiglu_gain_grad,
            ff_share,
            down_term,
            gain_count,
            shape,
            4,
        )
    )
    (
        hidden_out,
        hidden_grad,
        query_share,
        key_share,
        value_share,
        output_share,
        gate_share,
        up_share,
        down_share,
        head_share,
        gains_share,
    ) = widen(
        (
            hidden_out,
            hidden_grad,
            query_share,
            key_share,
            value_share,
            output_share,
            gate_share,
            up_share,
            down_share,
            head_share,
            gains_share,
        ),
        (low, low) + (full,) * 9,
    )
    return (
        hidden_out,
        hidden_grad,
        gains_share.reshape(gain_count),
        query_share,
        key_share,
        value_share,
        head_share.T,
        output_share,
        gate_share,
        up_share,
        down_share,
    )


def solution(mesh):
    rows = P(("seq", "ctx"), None)
    return jax.shard_map(
        on_device,
        mesh=mesh,
        in_specs=(rows, rows, P("seq"), P(("seq", "ctx"))) + (rows,) * 8,
        out_specs=(rows, rows, P(("seq", "ctx"))) + (rows,) * 8,
        check_vma=False,
    )
```

```python
import functools
import math

import jax
import jax.numpy as jnp
from jax import lax
from jax.experimental import pallas as pl
from jax.experimental.pallas import tpu as pltpu
from jax.sharding import PartitionSpec as P

H = 16
KV = 8
HD = 128


epsilon = 1e-06
rope_base = 1000000.0
negative = -1e30
low = jnp.bfloat16
full = jnp.float32
MESH = pl.DeviceIdType.MESH
ANY = pl.BlockSpec(memory_space=pl.ANY)
IN_VMEM = pl.BlockSpec(memory_space=pltpu.VMEM)
DMA = pltpu.SemaphoreType.DMA


def product(left_side, right_side):
    return jnp.dot(left_side, right_side, preferred_element_type=full)


def product_nt(left_side, right_side):
    return lax.dot_general(
        left_side, right_side, (((1,), (1,)), ((), ())), preferred_element_type=full
    )


def product_tn(left_side, right_side):
    return lax.dot_general(
        left_side, right_side, (((0,), (0,)), ((), ())), preferred_element_type=full
    )


def by_rows(rows, body, tile=32):
    tile = min(tile, rows)

    def step(index, unused):
        body(pl.ds(pl.multiple_of(index * tile, tile), tile))
        return unused

    lax.fori_loop(0, rows // tile, step, 0)


def remote(source, target, send, receive, axis, peer):
    return pltpu.make_async_remote_copy(
        src_ref=source,
        dst_ref=target,
        send_sem=send,
        recv_sem=receive,
        device_id={axis: peer},
        device_id_type=MESH,
    )


def greet(peers):
    barrier = pltpu.get_barrier_semaphore()
    for axis, peer, exists in peers:
        place = {"seq": peer[0], "ctx": peer[1]} if axis is None else {axis: peer}

        def signal():
            pl.semaphore_signal(barrier, inc=1, device_id=place, device_id_type=MESH)

        if exists is True:
            signal()
        else:
            pl.when(exists)(signal)

    arrivals = sum(1 for _, _, exists in peers if exists is True)
    for _, _, exists in peers:
        if exists is not True:
            arrivals = arrivals + exists.astype(jnp.int32)
    pl.semaphore_wait(barrier, arrivals)


def others(axis, count):
    me = lax.axis_index(axis)
    return [(axis, lax.rem(me + shift, count), True) for shift in range(1, count)]


class Line:
    def __init__(self, pieces):
        self.chips = pieces // 2
        self.me = lax.axis_index("ctx")
        self.chip, self.core = self.me // 2, lax.rem(self.me, 2)
        self.sibling = self.me + 1 - 2 * self.core
        self.right, self.left = self.me + 2, self.me - 2
        self.has_right, self.has_left = self.chip < self.chips - 1, self.chip > 0

    def peers(self):
        return [
            ("ctx", self.sibling, True),
            ("ctx", self.right, self.has_right),
            ("ctx", self.left, self.has_left),
        ]


def gather_scratch(pieces, parts):
    chips = pieces // 2
    return [DMA((chips, 2, parts))] * 2 + [DMA((chips, parts))] * 4


class Gather:
    def __init__(self, line, parts, rows, out_ref, sems):
        self.line, self.parts, self.rows, self.out_ref = line, parts, rows, out_ref
        self.size = rows // parts
        self.sib_send, self.sib_recv, self.r_send, self.r_recv, self.l_send, self.l_recv = sems

    def at(self, position, part):
        start = pl.multiple_of(position * self.rows + part * self.size, self.size)
        return self.out_ref.at[pl.ds(start, self.size)]

    def to_sibling(self, source, hop, side, part, position):
        return remote(
            source,
            self.at(position, part),
            self.sib_send.at[hop, side, part],
            self.sib_recv.at[hop, side, part],
            "ctx",
            self.line.sibling,
        )

    def to_right(self, source, hop, part, position):
        return remote(
            source,
            self.at(position, part),
            self.r_send.at[hop, part],
            self.r_recv.at[hop, part],
            "ctx",
            self.line.right,
        )

    def to_left(self, source, hop, part, position):
        return remote(
            source,
            self.at(position, part),
            self.l_send.at[hop, part],
            self.l_recv.at[hop, part],
            "ctx",
            self.line.left,
        )

    def start(self, x_ref):
        line = self.line
        for part in range(self.parts):
            piece = x_ref.at[pl.ds(part * self.size, self.size)]

            @pl.when(line.has_right)
            def _():
                self.to_right(piece, 0, part, line.me).start()

            @pl.when(line.has_left)
            def _():
                self.to_left(piece, 0, part, line.me).start()

            self.to_sibling(piece, 0, 0, part, line.me).start()

    def forward(self, hop):
        line = self.line
        for part in range(self.parts):
            from_left, from_right = line.me - 2 * hop, line.me + 2 * hop

            @pl.when(line.chip - hop >= 0)
            def _():
                piece = self.at(from_left, part)
                self.to_right(piece, hop - 1, part, from_left).wait_recv()

                @pl.when(line.has_right)
                def _():
                    self.to_right(piece, hop, part, from_left).start()

                self.to_sibling(piece, hop, 0, part, from_left).start()

            @pl.when(line.chip + hop < line.chips)
            def _():
                piece = self.at(from_right, part)
                self.to_left(piece, hop - 1, part, from_right).wait_recv()

                @pl.when(line.has_left)
                def _():
                    self.to_left(piece, hop, part, from_right).start()

                self.to_sibling(piece, hop, 1, part, from_right).start()

    def legs(self, hop):
        line = self.line
        return [
            (
                side,
                (line.chip - hop >= 0) if side == 0 else (line.chip + hop < line.chips),
                (line.me - 2 * hop) if side == 0 else (line.me + 2 * hop),
            )
            for side in range(1 if hop == 0 else 2)
        ]

    def arrive(self, hop):
        for side, there, position in self.legs(hop):
            for part in range(self.parts):

                @pl.when(there)
                def _():
                    self.to_sibling(
                        self.at(position, part), hop, side, part, position
                    ).wait_recv()

    def finish(self):
        line = self.line
        for hop in range(line.chips):
            for side, there, position in self.legs(hop):
                for part in range(self.parts):

                    @pl.when(there)
                    def _():
                        piece = self.at(position, part)
                        self.to_sibling(piece, hop, side, part, position).wait_send()
                        if side == 0:

                            @pl.when(line.has_right)
                            def _():
                                self.to_right(piece, hop, part, position).wait_send()

                        if side == 1 or hop == 0:

                            @pl.when(line.has_left)
                            def _():
                                self.to_left(piece, hop, part, position).wait_send()

    def complete(self):
        for hop in range(self.line.chips):
            self.arrive(hop)
        self.finish()


def scatter_scratch(pieces, rows, width):
    chips = pieces // 2
    slots = pltpu.VMEM((chips, rows, width), low)
    return [slots] * 3 + [pltpu.VMEM((chips + 1, rows, width), low)] + [DMA((chips,))] * 6


class Scatter:
    def __init__(self, line, rows, scratch):
        self.line, self.rows = line, rows
        (
            self.own,
            self.give,
            self.sib,
            self.arrived,
            self.sib_send,
            self.sib_recv,
            self.r_send,
            self.r_recv,
            self.l_send,
            self.l_recv,
        ) = scratch

    def clear(self):
        line = self.line

        @pl.when(jnp.logical_not(line.has_left))
        def _():
            self.arrived[line.chip] = jnp.zeros(self.arrived.shape[1:], low)

        @pl.when(jnp.logical_not(line.has_right))
        def _():
            self.arrived[line.chips] = jnp.zeros(self.arrived.shape[1:], low)

    def there(self, far, side):
        line = self.line
        return (line.chip + far < line.chips) if side == 0 else (line.chip - far >= 0)

    def target(self, far, side):
        return self.line.chip + far if side == 0 else self.line.chip - far

    def exchange(self, target):
        return remote(
            self.give.at[target],
            self.sib.at[target],
            self.sib_send.at[target],
            self.sib_recv.at[target],
            "ctx",
            self.line.sibling,
        )

    def send(self, target, side):
        if side == 0:
            return remote(
                self.own.at[target],
                self.arrived.at[target],
                self.r_send.at[target],
                self.r_recv.at[target],
                "ctx",
                self.line.right,
            )
        chips, chip = self.line.chips, self.line.chip
        return remote(
            self.own.at[target],
            self.arrived.at[jnp.where(target == chip - 1, chips, target)],
            self.l_send.at[target],
            self.l_recv.at[target],
            "ctx",
            self.line.left,
        )

    def order(self):
        return [
            (far, side)
            for far in range(self.line.chips - 1, -1, -1)
            for side in range(2 if far else 1)
        ]

    def fill(self, least, most, block):
        line = self.line

        def step(target, unused):
            far = jnp.abs(target - line.chip)

            @pl.when(jnp.logical_and(far >= least, far <= most))
            def _():
                def store(columns, value):
                    first, second = value[: self.rows], value[self.rows :]
                    mine = line.core == 0
                    self.own[target, :, columns] = jnp.where(mine, first, second).astype(low)
                    self.give[target, :, columns] = jnp.where(mine, second, first).astype(low)

                block(target, store)
                self.exchange(target).start()

            return unused

        lax.fori_loop(0, line.chips, step, 0)

    def push(self, far, side):
        line = self.line
        behind = line.has_left if side == 0 else line.has_right

        @pl.when(self.there(far, side))
        def _():
            target = self.target(far, side)
            self.exchange(target).wait_recv()

            def add(across):
                self.own[target, across, :] = (
                    self.own[target, across, :].astype(full) + self.sib[target, across, :].astype(full)
                ).astype(low)

            def add_all(across):
                self.own[target, across, :] = (
                    self.own[target, across, :].astype(full)
                    + self.sib[target, across, :].astype(full)
                    + self.arrived[target, across, :].astype(full)
                ).astype(low)

            if far == line.chips - 1:
                by_rows(self.rows, add)
            else:

                @pl.when(behind)
                def _():
                    self.send(target, side).wait_recv()
                    by_rows(self.rows, add_all)

                @pl.when(jnp.logical_not(behind))
                def _():
                    by_rows(self.rows, add)

            self.send(target, side).start()

    def total(self, total_ref):
        line = self.line
        chip = line.chip
        self.exchange(chip).wait_recv()

        @pl.when(line.has_left)
        def _():
            self.send(chip, 0).wait_recv()

        @pl.when(line.has_right)
        def _():
            self.send(chip, 1).wait_recv()

        def add(across):
            total = self.own[chip, across, :].astype(full) + self.sib[chip, across, :].astype(full)
            total = total + jnp.where(
                line.has_left, self.arrived[chip, across, :].astype(full), 0.0
            )
            total_ref[across, :] = total + jnp.where(
                line.has_right, self.arrived[line.chips, across, :].astype(full), 0.0
            )

        by_rows(self.rows, add)

    def finish(self):
        for far, side in self.order():

            @pl.when(self.there(far, side))
            def _():
                target = self.target(far, side)
                self.exchange(target).wait_send()
                if far > 0:
                    self.send(target, side).wait_send()


def blocks_nn(left_ref, right_ref, rows, tile=512):
    def block(target, store):
        start = pl.multiple_of(target * 2 * rows, 2 * rows)
        left_side = left_ref[pl.ds(start, 2 * rows), :]

        def step(index, unused):
            columns = pl.ds(pl.multiple_of(index * tile, tile), tile)
            store(columns, product(left_side, right_ref[:, columns]))
            return unused

        lax.fori_loop(0, right_ref.shape[1] // tile, step, 0)

    return block


def blocks_nt(left_ref, right_ref, rows, tile=512):
    def block(target, store):
        start = pl.multiple_of(target * 2 * rows, 2 * rows)
        left_side = left_ref[pl.ds(start, 2 * rows), :]

        def step(index, unused):
            columns = pl.ds(pl.multiple_of(index * tile, tile), tile)
            store(columns, product_nt(left_side, right_ref[columns, :]))
            return unused

        lax.fori_loop(0, right_ref.shape[0] // tile, step, 0)

    return block


class LineSwap:
    def __init__(self, line, send_of, recv_of, s_sem, r_sem):
        self.line, self.send_of, self.recv_of = line, send_of, recv_of
        self.s_sem, self.r_sem = s_sem, r_sem

    def copy(self, far, side, core):
        line = self.line
        if far == 0:
            peer, slot = line.sibling, self.r_sem.at[0, 0, 0]
        else:
            peer = (line.chip + (far if side == 0 else -far)) * 2 + core
            slot = self.r_sem.at[far, side, line.core]
        return remote(
            self.send_of(peer), self.recv_of(line.me), self.s_sem.at[far, side, core], slot, "ctx", peer
        )

    def legs(self, far):
        line = self.line
        if far == 0:
            return [(0, 0, True, True)]
        return [
            (
                side,
                core,
                (line.chip + far < line.chips) if side == 0 else (line.chip - far >= 0),
                (line.chip - far >= 0) if side == 0 else (line.chip + far < line.chips),
            )
            for side in range(2)
            for core in range(2)
        ]

    def start(self):
        for far in range(self.line.chips):
            for side, core, sends, _ in self.legs(far):
                if far == 0:
                    self.copy(far, side, core).start()
                else:

                    @pl.when(sends)
                    def _():
                        self.copy(far, side, core).start()

    def receive(self, far, then):
        line = self.line
        for side, core, _, comes in self.legs(far):
            if far == 0:
                source, slot = line.sibling, self.r_sem.at[0, 0, 0]
            else:
                source = (line.chip + (-far if side == 0 else far)) * 2 + core
                slot = self.r_sem.at[far, side, core]

            def wait():
                remote(
                    self.recv_of(source),
                    self.recv_of(source),
                    self.s_sem.at[far, side, core],
                    slot,
                    "ctx",
                    source,
                ).wait_recv()
                then(source)

            if far == 0:
                wait()
            else:
                pl.when(comes)(wait)

    def again(self, far, then):
        line = self.line
        for side, core, _, comes in self.legs(far):
            if far == 0:
                then(line.sibling)
            else:
                source = (line.chip + (-far if side == 0 else far)) * 2 + core

                @pl.when(comes)
                def _():
                    then(source)

    def finish(self):
        for far in range(self.line.chips):
            for side, core, sends, _ in self.legs(far):
                if far == 0:
                    self.copy(far, side, core).wait_send()
                else:

                    @pl.when(sends)
                    def _():
                        self.copy(far, side, core).wait_send()


def swap_scratch(pieces):
    return [DMA((pieces // 2, 2, 2))] * 2


class Share:
    def __init__(self, groups, place, s_sem, r_sem, relays=True):
        self.groups, self.place, self.s_sem, self.r_sem = groups, place, s_sem, r_sem
        self.group = lax.axis_index("seq")
        self.square = groups == 4 and relays
        self.across = self.group + 1 - 2 * lax.rem(self.group, 2)
        self.along = lax.rem(self.group + 2, groups)
        self.corner = groups - 1 - self.group

    def copy(self, source, slot, peer, origin, target):
        return remote(
            origin, target, self.s_sem.at[source, slot], self.r_sem.at[source, slot], "seq", peer
        )

    def half(self, index, source, which):
        ref = self.place(index, source)
        rows = ref.shape[0] // 2
        return ref.at[pl.ds(which * rows, rows)]

    def first(self, source, origin=None):
        target = self.place(self.group, source)
        origin = target if origin is None else origin
        if self.square:
            peers = [(1, self.across), (2, self.along)]
        else:
            peers = [
                (shift, lax.rem(self.group + shift, self.groups)) for shift in range(1, self.groups)
            ]
        return [self.copy(source, slot, peer, origin, target) for slot, peer in peers]

    def second(self, source):
        one, two = self.half(self.across, source, 0), self.half(self.along, source, 1)
        return [
            self.copy(source, 3, self.along, one, one),
            self.copy(source, 0, self.across, two, two),
        ]

    def send(self, source, origin=None):
        for copy in self.first(source, origin):
            copy.start()

    def relay(self, source):
        if not self.square:
            return
        for slot, index, copy in zip((1, 2), (self.across, self.along), self.second(source)):
            block = self.place(index, source)
            self.copy(source, slot, index, block, block).wait_recv()
            copy.start()

    def finish(self, sources):
        for source in range(sources):
            if self.square:
                for slot, which in ((3, 0), (0, 1)):
                    half = self.half(self.corner, source, which)
                    self.copy(source, slot, self.corner, half, half).wait_recv()
                for copy in self.second(source):
                    copy.wait_send()
            else:
                for shift in range(1, self.groups):
                    index = lax.rem(self.group + self.groups - shift, self.groups)
                    block = self.place(index, source)
                    self.copy(source, shift, index, block, block).wait_recv()
            for copy in self.first(source):
                copy.wait_send()


class Fold:
    def __init__(self, groups, term_ref, inbox, s_sem, r_sem):
        self.groups, self.term, self.inbox = groups, term_ref, inbox
        self.s_sem, self.r_sem = s_sem, r_sem
        self.group = lax.axis_index("seq")
        self.order = [lax.rem(self.group + shift, groups) for shift in range(1, groups)] + [
            self.group
        ]

    def copy(self, job):
        return remote(
            self.term.at[self.order[job]],
            self.inbox.at[job],
            self.s_sem.at[job],
            self.r_sem.at[job],
            "seq",
            self.order[job],
        )

    def ready(self, job):
        if job < self.groups - 1:
            self.copy(job).start()

    def arrive(self):
        for job in range(self.groups - 1):
            self.copy(job).wait_recv()

    def sum(self, across, own=None):
        total = (self.term[self.group, across, :] if own is None else own[across, :]).astype(full)
        for job in range(self.groups - 1):
            total = total + self.inbox[job, across, :].astype(full)
        return total

    def finish(self):
        for job in range(self.groups - 1):
            self.copy(job).wait_send()


class Spread:
    def __init__(self, groups, pieces):
        group, me = lax.axis_index("seq"), lax.axis_index("ctx")
        flat = group * pieces + me
        self.use = (lax.rem(flat, groups), flat // groups)
        held = me * groups + group
        self.rest = (held // pieces, lax.rem(held, pieces))
        self.moves = jnp.logical_or(self.use[0] != group, self.use[1] != me)

    def peers(self):
        return [(None, self.use, self.moves), (None, self.rest, self.moves)]

    def copy(self, source, target, send, receive, back):
        place = self.rest if back else self.use
        return pltpu.make_async_remote_copy(
            src_ref=source,
            dst_ref=target,
            send_sem=send,
            recv_sem=receive,
            device_id={"seq": place[0], "ctx": place[1]},
            device_id_type=MESH,
        )


def lanes(start, size):
    return pl.ds(pl.multiple_of(start, 128), size)


def turn(values, cosine, sine):
    half = values.shape[0] // 2
    first, second = values[:half], values[half:]
    return jnp.concatenate(
        [first * cosine - second * sine, second * cosine + first * sine], axis=0
    )


def turn_back(values, cosine, sine):
    half = values.shape[0] // 2
    first, second = values[:half], values[half:]
    return jnp.concatenate(
        [first * cosine + second * sine, second * cosine - first * sine], axis=0
    )


def column(gains, start):
    return jnp.broadcast_to(gains[:, pl.ds(start, HD)], (HD, HD)).T[:, 0:1]


def inverse_rms(values):
    return lax.rsqrt(jnp.mean(values * values, axis=0, keepdims=True) + epsilon)


def kept(first_key, keys, first_query, queries, prefix):
    key = first_key + lax.broadcasted_iota(jnp.int32, (keys, queries), 0)
    query = first_query + lax.broadcasted_iota(jnp.int32, (keys, queries), 1)
    return key <= jnp.maximum(query, prefix - 1)


def query_blocks(length, body):
    tile = min(256, length // 2)
    half = length // 2

    def early(index, unused):
        body(index * tile, tile, half)
        return unused

    def late(index, unused):
        body(half + index * tile, tile, length)
        return unused

    lax.fori_loop(0, half // tile, early, 0)
    lax.fori_loop(0, half // tile, late, 0)


def forward_kernel(
    shape,
    hidden,
    gains_ref,
    query_weight,
    key_weight,
    value_weight,
    gate_weight_t,
    out_weight,
    cosine,
    sine,
    prefix_ref,
    out_grad,
    gate_weight,
    up_weight,
    normed,
    attn_low,
    gains_out,
    out_low,
    raw_t,
    gate_t,
    q_ref,
    qt_ref,
    k_ref,
    kt_ref,
    v_ref,
    att_t,
    lse_ref,
    gated_t,
    middle,
    normed_two,
    og_all,
    ff_low,
    raw,
    hidden_all,
    blocks,
    out_block,
    gains_row,
    gains_all,
    corner,
    vt_ref,
    gated,
    ff_blocks,
    own_attn,
    own_out,
    out_s,
    out_r,
    ff_sem,
    og_sem,
    ga_s,
    ga_r,
    gs_s,
    gs_r,
    at_s,
    at_r,
    as_s,
    as_r,
    os_s,
    os_r,
    fs_s,
    fs_r,
    fh_s,
    fh_r,
    *sems,
):
    pieces, groups, heads, kv_heads, ff_block = shape
    rows_sems, og_sems, scatter_refs = sems[:6], sems[6:12], sems[12:]
    line = Line(pieces)
    me, group = line.me, lax.axis_index("seq")
    rows, model = hidden.shape
    length = pieces * rows
    weight_rows = out_weight.shape[0]
    q_width, kv_width = heads * HD, kv_heads * HD
    copies = max(1, pieces // KV)
    spread = Spread(groups, pieces)
    greet(others("ctx", pieces) + others("seq", groups) + spread.peers())
    gain_count = gains_ref.shape[1]
    gains_row[...] = jnp.zeros(gains_row.shape, full)
    gains_row[0:1, pl.ds(0, gain_count)] = gains_ref[...].astype(low).astype(full)
    gains_all[group, me] = gains_row[...]
    gain_swap = LineSwap(
        line, lambda peer: gains_row, lambda source: gains_all.at[group, source], ga_s, ga_r
    )
    gain_swap.start()

    blocks[:, :, pl.ds(q_width + 2 * kv_width, HD)] = jnp.zeros((pieces, weight_rows, HD), low)
    corner[...] = jnp.zeros(corner.shape, full)
    corner[pl.ds(0, gate_weight_t.shape[0]), pl.ds(0, weight_rows)] = gate_weight_t[...]
    gate_rows = corner[...].T
    for piece in range(pieces):
        blocks[piece, :, pl.ds(0, q_width)] = query_weight[
            :, pl.ds(piece * q_width, q_width)
        ].astype(low)
        start = piece // copies * kv_width
        blocks[piece, :, pl.ds(q_width, kv_width)] = key_weight[:, pl.ds(start, kv_width)].astype(low)
        blocks[piece, :, pl.ds(q_width + kv_width, kv_width)] = value_weight[
            :, pl.ds(start, kv_width)
        ].astype(low)
        blocks[piece, :, pl.ds(q_width + 2 * kv_width, heads)] = gate_rows[
            :weight_rows, piece * heads : (piece + 1) * heads
        ].astype(low)

    def place(index, source):
        start = pl.multiple_of((index * pieces + source) * weight_rows, weight_rows)
        return attn_low.at[pl.ds(start, weight_rows)]

    attn_swap = LineSwap(
        line, lambda peer: blocks.at[peer], lambda source: place(group, source), at_s, at_r
    )
    attn_swap.start()
    share = Share(groups, place, as_s, as_r, False)
    share.send(me, blocks.at[me])
    attn_own = pltpu.make_async_copy(blocks.at[me], place(group, me), own_attn)
    attn_own.start()
    gather = Gather(line, 2, rows, hidden_all, rows_sems)
    gather.start(hidden)
    hidden_all[pl.ds(pl.multiple_of(me * rows, rows), rows), :] = hidden[...]
    out_block[...] = out_weight[...].astype(low)

    def out_place(index):
        return out_low.at[pl.ds(pl.multiple_of(index * weight_rows, weight_rows), weight_rows)]

    out_move = spread.copy(out_block, out_place(spread.use[0]), out_s, out_r, False)
    out_stay = pltpu.make_async_copy(out_block, out_place(group), own_out)

    @pl.when(spread.moves)
    def _():
        out_move.start()

    @pl.when(jnp.logical_not(spread.moves))
    def _():
        out_stay.start()

    def to_groups(shift):
        peer = lax.rem(group + shift, groups)
        return remote(
            gains_all.at[group], gains_all.at[group], gs_s.at[shift], gs_r.at[shift], "seq", peer
        )

    def from_groups(shift):
        peer = lax.rem(group + groups - shift, groups)
        return remote(
            gains_all.at[peer], gains_all.at[peer], gs_s.at[shift], gs_r.at[shift], "seq", peer
        )

    attn_swap.receive(0, share.send)
    for far in range(line.chips):
        gain_swap.receive(far, lambda source: None)
    for shift in range(1, groups):
        to_groups(shift).start()
    if line.chips > 1:
        attn_swap.receive(1, share.send)

    def chip_rows(chip):
        return chip * 2 * rows

    def both(far, body):
        if far == 0:
            body(chip_rows(line.chip))
            return

        @pl.when(line.chip - far >= 0)
        def _():
            body(chip_rows(line.chip - far))

        @pl.when(line.chip + far < line.chips)
        def _():
            body(chip_rows(line.chip + far))

    def normalise(start):
        def some(part):
            across = pl.ds(pl.multiple_of(start + part.start, part.size), part.size)
            values = hidden_all[across, :].astype(full)
            inverse = lax.rsqrt(jnp.mean(values * values, axis=-1, keepdims=True) + epsilon)
            normed[across, :] = (values * inverse * gains_out[0:1, pl.ds(0, model)]).astype(low)

        by_rows(2 * rows, some)

    def project(least, most):
        def step(chip, unused):
            far = jnp.abs(chip - line.chip)

            @pl.when(jnp.logical_and(far >= least, far <= most))
            def _():
                across = pl.ds(pl.multiple_of(chip * 2 * rows, 2 * rows), 2 * rows)
                raw[across, :] = product(normed[across, :], attn_low[...])

            return unused

        lax.fori_loop(0, line.chips, step, 0)

    for far in range(2, line.chips):
        attn_swap.receive(far, share.send)
    out_share = Share(groups, lambda index, source: out_place(index), os_s, os_r)

    @pl.when(spread.moves)
    def _():
        spread.copy(out_place(group), out_place(group), out_s, out_r, False).wait_recv()

    @pl.when(jnp.logical_not(spread.moves))
    def _():
        out_stay.wait()

    out_share.send(0)
    for shift in range(1, groups):
        from_groups(shift).wait_recv()
    for index in range(groups * pieces):
        gains_out[0:1, pl.ds(index * gain_count, gain_count)] = gains_all[
            index // pieces, index % pieces, 0:1, pl.ds(0, gain_count)
        ]
    own_width = groups * ff_block

    def prepare(across):
        for half, weight_ref in enumerate((gate_weight, up_weight)):
            for index in range(groups):
                for piece in range(pieces):
                    start = (index * pieces + piece) * ff_block
                    ff_blocks[piece, across, pl.ds(half * own_width + index * ff_block, ff_block)] = (
                        weight_ref[across, pl.ds(start, ff_block)].astype(low)
                    )

    by_rows(gate_weight.shape[0], prepare, 16)
    for hop in range(1, line.chips - 1):
        gather.forward(hop)
        gather.arrive(hop - 1)
        both(hop - 1, normalise)
    ff_swap = LineSwap(
        line, lambda peer: ff_blocks.at[peer], lambda source: ff_low.at[group, source], fs_s, fs_r
    )
    ff_swap.start()
    ff_share = Share(groups, lambda index, source: ff_low.at[index, source], fh_s, fh_r, False)
    ff_share.send(me, ff_blocks.at[me])
    ff_own = pltpu.make_async_copy(ff_blocks.at[me], ff_low.at[group, me], ff_sem)
    ff_own.start()
    gather.arrive(line.chips - 2)
    both(line.chips - 2, normalise)
    attn_own.wait()
    out_share.relay(0)
    share.finish(pieces)
    project(0, line.chips - 2)
    gather.forward(line.chips - 1)
    gather.arrive(line.chips - 1)
    both(line.chips - 1, normalise)
    project(line.chips - 1, line.chips - 1)
    og_gather = Gather(line, 2, rows, og_all, og_sems)
    og_gather.start(out_grad)
    start = pl.multiple_of(me * rows, rows)
    og_own = pltpu.make_async_copy(out_grad, og_all.at[pl.ds(start, rows)], og_sem)
    og_own.start()
    prefix = prefix_ref[0, 0]
    query_gain, key_gain = column(gains_out, 2 * model), column(gains_out, 2 * model + HD)
    scale = HD ** (-0.5)
    for head in range(heads + kv_heads):
        part = pl.ds(head * HD, HD)
        values = raw[:, part].T
        raw_t[part, :] = values
        gain = query_gain if head < heads else key_gain
        turned = turn(values * inverse_rms(values) * gain, cosine[...], sine[...])
        if head < heads:
            qt_ref[part, :] = turned.astype(low)
            q_ref[:, part] = turned.T.astype(low)
        else:
            part = pl.ds((head - heads) * HD, HD)
            kt_ref[part, :] = turned.astype(low)
            k_ref[:, part] = turned.T.astype(low)
    for head in range(kv_heads):
        part = pl.ds(head * HD, HD)
        values = raw[:, pl.ds((heads + kv_heads + head) * HD, HD)]
        v_ref[:, part] = values.astype(low)
        vt_ref[part, :] = values.T.astype(low)
    gate_t[...] = raw[:, pl.ds((heads + 2 * kv_heads) * HD, HD)].T[: gate_t.shape[0]]
    ff_swap.receive(0, ff_share.send)
    for head in range(heads):
        part = pl.ds(head * HD, HD)
        kv_part = pl.ds(head * kv_heads // heads * HD, HD)

        def block(first, tile, keys):
            columns = lanes(first, tile)
            scores = product(k_ref[pl.ds(0, keys), kv_part], qt_ref[part, columns]) * scale
            scores = jnp.where(kept(0, keys, first, tile, prefix), scores, negative)
            top = jnp.max(scores, axis=0, keepdims=True)
            expanded = jnp.exp(scores - top)
            total = jnp.sum(expanded, axis=0, keepdims=True)
            lse_ref[head : head + 1, columns] = top + jnp.log(total)
            att_t[part, columns] = (
                product(vt_ref[kv_part, pl.ds(0, keys)], expanded.astype(low)) / total
            )

        query_blocks(length, block)
        scaled = att_t[part, :] * jax.nn.sigmoid(gate_t[head : head + 1, :])
        gated_t[part, :] = scaled.astype(low)
        gated[:, part] = scaled.T.astype(low)
        if head == 0 and line.chips > 1:
            ff_swap.receive(1, ff_share.send)

    out_share.finish(1)
    scatter = Scatter(line, rows, scatter_refs)
    scatter.clear()
    block = blocks_nn(gated, out_low, rows)
    last = line.chips - 1
    scatter.fill(last, last, block)
    for far, side in scatter.order():
        if far == last:
            scatter.push(far, side)
    scatter.fill(0, last - 1, block)
    for far in range(2, line.chips):
        ff_swap.receive(far, ff_share.send)
    for hop in range(1, line.chips):
        og_gather.forward(hop)
        for far, side in scatter.order():
            if far == last - hop and far > 0:
                scatter.push(far, side)
    scatter.total(middle)

    def normalise_two(across):
        values = hidden[across, :].astype(full) + middle[across, :]
        middle[across, :] = values
        inverse = lax.rsqrt(jnp.mean(values * values, axis=-1, keepdims=True) + epsilon)
        normed_two[across, :] = (values * inverse * gains_out[:, pl.ds(model, model)]).astype(low)

    by_rows(rows, normalise_two)
    og_own.wait()
    ff_own.wait()
    og_gather.complete()
    scatter.finish()
    ff_swap.finish()
    ff_share.finish(pieces)
    gather.finish()
    gain_swap.finish()
    attn_swap.finish()
    for shift in range(1, groups):
        to_groups(shift).wait_send()

    @pl.when(spread.moves)
    def _():
        out_move.wait_send()


def forward(hidden, norm_gains, weights, tables, prefix, out_grad, ff_weights, shape, number):
    pieces, groups, heads, kv_heads, ff_block = shape
    rows, model = hidden.shape
    length = pieces * rows
    weight_rows = weights[0].shape[0]
    gains = norm_gains.shape[0]
    padded = -(-gains // 128) * 128
    q_width, kv_width = heads * HD, kv_heads * HD
    width = (heads + 2 * kv_heads + 1) * HD
    ff_shape = (pieces, weight_rows, 2 * groups * ff_block)
    struct, vmem = jax.ShapeDtypeStruct, pltpu.VMEM
    return pl.pallas_call(
        functools.partial(forward_kernel, shape),
        out_shape=(
            struct((length, model), low),
            struct((model, width), low),
            struct((1, groups * pieces * gains), full),
            struct((groups * weight_rows, model), low),
            struct((q_width + kv_width, length), full),
            struct((8, length), full),
            struct((length, q_width), low),
            struct((q_width, length), low),
            struct((length, kv_width), low),
            struct((kv_width, length), low),
            struct((length, kv_width), low),
            struct((q_width, length), full),
            struct((8, length), full),
            struct((q_width, length), low),
            struct((rows, model), full),
            struct((rows, model), low),
            struct((length, model), low),
            struct((groups,) + ff_shape, low),
        ),
        in_specs=[IN_VMEM] * 9 + [pl.BlockSpec(memory_space=pltpu.SMEM)] + [IN_VMEM] * 3,
        out_specs=(IN_VMEM,) * 16 + (ANY, ANY),
        scratch_shapes=[
            vmem((length, width), full),
            vmem((length, model), low),
            vmem((pieces, weight_rows, width), low),
            vmem((weight_rows, model), low),
            vmem((8, padded), full),
            vmem((groups, pieces, 8, padded), full),
            vmem((HD, HD), full),
            vmem((kv_width, length), low),
            vmem((length, q_width), low),
            vmem(ff_shape, low),
        ]
        + [DMA] * 6
        + swap_scratch(pieces)
        + [DMA((groups,))] * 2
        + swap_scratch(pieces)
        + [DMA((pieces, groups))] * 2
        + [DMA((1, groups))] * 2
        + swap_scratch(pieces)
        + [DMA((pieces, groups))] * 2
        + gather_scratch(pieces, 2) * 2
        + scatter_scratch(pieces, rows, model),
        compiler_params=pltpu.CompilerParams(
            collective_id=number, has_side_effects=True, vmem_limit_bytes=67043328
        ),
        name=f"forward_{number}",
    )(
        hidden, norm_gains.reshape(1, gains), *weights, *tables, prefix, out_grad, *ff_weights,
    )


def attend_back_kernel(
    shape,
    grad_branch,
    out_low,
    raw_t,
    gate_t,
    q_ref,
    qt_ref,
    k_ref,
    kt_ref,
    v_ref,
    att_t,
    lse_ref,
    gated_t,
    cosine,
    sine,
    gains,
    prefix_ref,
    normed,
    attn_low,
    hidden,
    grad_middle,
    swiglu_gain_grad,
    ff_share,
    down_term,
    hidden_grad,
    gains_grad,
    query_grad,
    key_grad,
    value_grad,
    head_grad,
    gate_grad,
    up_grad,
    out_grad,
    down_grad,
    down_in,
    down_mine,
    down_sem,
    ff_sem,
    corner,
    out_term,
    out_in,
    out_send,
    gg_t,
    ga_t,
    ga,
    gqt,
    dk,
    dv,
    grad_t,
    grad,
    total_ref,
    ff_recv,
    normed_part,
    part_sem,
    term,
    term_in,
    attn_send,
    attn_recv,
    gains_vector,
    gain_give,
    gain_sib,
    gain_row,
    gain_last,
    ffs_s,
    ffs_r,
    at_s,
    at_r,
    gc_s,
    gc_r,
    ts_s,
    ts_r,
    gs_s,
    gs_r,
    ot_s,
    ot_r,
    om_s,
    om_r,
    de_s,
    de_r,
    dl_s,
    dl_r,
    *scatter_refs,
):
    pieces, groups, heads, kv_heads, ff_block = shape
    line = Line(pieces)
    me, group = line.me, lax.axis_index("seq")
    length, rows = grad_branch.shape[0], hidden.shape[0]
    width, model = attn_low.shape[1], attn_low.shape[0]
    weight_rows = ff_share.shape[1]
    q_width, kv_width = heads * HD, kv_heads * HD
    spread = Spread(groups, pieces)
    greet(others("ctx", pieces) + others("seq", groups) + spread.peers())
    share = model // groups
    fold = Fold(groups, term, term_in, ts_s, ts_r)
    out_fold = Fold(groups, out_term, out_in, ot_s, ot_r)

    def load(job):
        index = fold.order[job]
        return pltpu.make_async_copy(
            normed.at[:, lanes(index * share, share)], normed_part.at[job % 2], part_sem.at[job % 2]
        )

    load(0).start()
    down_rows = down_in.shape[1]
    half = down_rows // 32 * 16
    early, late = pl.ds(0, half), pl.ds(half, down_rows - half)
    down_early = Fold(groups, down_term.at[:, early], down_in.at[:, early], de_s, de_r)
    down_late = Fold(groups, down_term.at[:, late], down_in.at[:, late], dl_s, dl_r)
    for job in range(groups):
        down_early.ready(job)
    down_own = pltpu.make_async_copy(down_term.at[group], down_mine, down_sem)
    down_own.start()
    ff_own = pltpu.make_async_copy(ff_share.at[me], ff_recv.at[me], ff_sem)
    ff_own.start()
    ff_swap = LineSwap(
        line, lambda peer: ff_share.at[peer], lambda source: ff_recv.at[source], ffs_s, ffs_r
    )
    ff_swap.start()

    prefix = prefix_ref[0, 0]
    query_gain, key_gain = column(gains, 2 * model), column(gains, 2 * model + HD)
    scale = HD ** (-0.5)

    def branch(index, unused):
        columns = lanes(index * 256, 256)
        gg_t[:, columns] = product_nt(out_low[...], grad_branch[columns, :])
        return unused

    lax.fori_loop(0, length // 256, branch, 0)

    def out_grads(index, unused):
        columns = lanes(index * 256, 256)
        value = product(gated_t[...], grad_branch[:, columns]).astype(low)
        for place in range(groups):
            out_term[place, :, columns] = value[place * weight_rows : (place + 1) * weight_rows]
        return unused

    lax.fori_loop(0, model // 256, out_grads, 0)

    for job in range(groups):
        out_fold.ready(job)
    dk[...] = jnp.zeros(dk.shape, full)
    dv[...] = jnp.zeros(dv.shape, full)
    gate_rows = []
    for head in range(heads):
        part = pl.ds(head * HD, HD)
        kv_part = pl.ds(head * kv_heads // heads * HD, HD)
        sigmoid = jax.nn.sigmoid(gate_t[head : head + 1, :])
        grads = gg_t[part, :]
        rounded = (grads * sigmoid).astype(low)
        ga_t[...] = rounded
        ga[...] = rounded.astype(full).T.astype(low)
        gate_rows.append(
            jnp.sum(grads * att_t[part, :], axis=0, keepdims=True) * sigmoid * (1.0 - sigmoid)
        )

        def block(first, tile, keys):
            columns, across = lanes(first, tile), pl.ds(0, keys)
            scores = product(k_ref[across, kv_part], qt_ref[part, columns]) * scale
            chance = jnp.where(
                kept(0, keys, first, tile, prefix),
                jnp.exp(scores - lse_ref[head : head + 1, columns]),
                0.0,
            )
            taken = ga_t[:, columns]
            delta = jnp.sum(taken.astype(full) * att_t[part, columns], axis=0, keepdims=True)
            change = product(v_ref[across, kv_part], taken)
            score_grad = (chance * (change - delta)).astype(low)
            gqt[part, columns] = product(kt_ref[kv_part, across], score_grad) * scale
            dk[across, kv_part] += product(score_grad, q_ref[columns, part])
            dv[across, kv_part] += product(chance.astype(low), ga[columns, :])

        query_blocks(length, block)

    gain_columns = [jnp.zeros((HD, 1), full), jnp.zeros((HD, 1), full)]
    for head in range(heads + kv_heads):
        part = pl.ds(head * HD, HD)
        if head < heads:
            turned = gqt[part, :]
            gain = query_gain
        else:
            turned = dk[:, pl.ds((head - heads) * HD, HD)].T * scale
            gain = key_gain
        grads = turn_back(turned, cosine[...], sine[...])
        values = raw_t[part, :]
        inverse = inverse_rms(values)
        kind = 0 if head < heads else 1
        gain_columns[kind] = gain_columns[kind] + jnp.sum(
            grads * values * inverse, axis=1, keepdims=True
        )
        scaled = grads * gain
        result = inverse * scaled - values * (
            inverse * inverse * inverse * jnp.mean(scaled * values, axis=0, keepdims=True)
        )
        grad_t[part, :] = result.astype(low)
        grad[:, part] = result.T.astype(low)
    for head in range(kv_heads):
        part = pl.ds((heads + kv_heads + head) * HD, HD)
        values = dv[:, pl.ds(head * HD, HD)]
        grad[:, part] = values.astype(low)
        grad_t[part, :] = values.T.astype(low)
    part = pl.ds((heads + 2 * kv_heads) * HD, HD)
    gate_block = jnp.concatenate(
        gate_rows + [jnp.zeros((HD - heads, length), full)], axis=0
    )
    grad_t[part, :] = gate_block.astype(low)
    grad[:, part] = gate_block.T.astype(low)

    scatter = Scatter(line, rows, scatter_refs)
    scatter.clear()
    block = blocks_nt(grad, attn_low, rows)
    last = line.chips - 1

    def fills(far):
        scatter.fill(far, far, block)

    def pushes(far):
        for distance, side in scatter.order():
            if distance == far and far > 0:
                scatter.push(far, side)

    def weight_grad(job):
        index = fold.order[job]
        load(job).wait()
        if job + 1 < groups:
            load(job + 1).start()

        def step(tile, unused):
            start = index * share + tile * 128
            value = product(grad_t[...], normed_part[job % 2, :, lanes(tile * 128, 128)])
            turned = value.T
            term[index, pl.ds(pl.multiple_of(tile * 128, 128), 128), :] = turned.astype(low)
            weighted = jnp.sum(
                turned * attn_low[pl.ds(pl.multiple_of(start, 128), 128), :].astype(full),
                axis=1,
                keepdims=True,
            )
            wide = jnp.broadcast_to(weighted, (128, 128)).T
            gains_vector[:, lanes(start, 128)] = wide[0:1, :] / gains[:, lanes(start, 128)]
            return unused

        lax.fori_loop(0, share // 128, step, 0)
        fold.ready(job)

    weight_grad(0)
    fills(last)
    pushes(last)
    for job in range(1, groups):
        weight_grad(job)
        if job <= last:
            fills(last - job)
    for far in range(last - groups, -1, -1):
        fills(far)

    for job in range(groups):
        down_late.ready(job)

    gain_count = gains_grad.shape[1]
    gains_vector[:, pl.ds(model, model)] = swiglu_gain_grad[...]
    for kind in range(2):
        wide = jnp.broadcast_to(gain_columns[kind], (HD, HD)).T
        gains_vector[:, pl.ds(2 * model + kind * HD, HD)] = wide[0:1, :]
    gain_give[...] = jnp.zeros(gain_give.shape, full)
    for index in range(groups * pieces):
        gain_give[index % pieces, index // pieces, 0:1, pl.ds(0, gain_count)] = gains_vector[
            :, pl.ds(index * gain_count, gain_count)
        ]
    gain_swap = LineSwap(
        line, lambda peer: gain_give.at[peer], lambda source: gain_sib.at[source], gc_s, gc_r
    )
    gain_swap.start()
    gain_sib[me] = gain_give[me]
    pushes(last - 1)

    out_fold.arrive()

    def total_out(across):
        out_send[across, :] = out_fold.sum(across).astype(low)

    by_rows(weight_rows, total_out, 16)
    out_move = spread.copy(out_send, out_grad, om_s, om_r, True)

    @pl.when(spread.moves)
    def _():
        out_move.start()

    @pl.when(jnp.logical_not(spread.moves))
    def _():
        out_grad[...] = out_send[...]

    for far in range(line.chips):
        gain_swap.receive(far, lambda source: None)
    gain_row[...] = jnp.sum(gain_sib[...], axis=0)

    def gain_to(shift):
        peer = lax.rem(group + shift, groups)
        return remote(
            gain_row.at[peer], gain_last.at[shift], gs_s.at[shift], gs_r.at[shift], "seq", peer
        )

    for shift in range(1, groups):
        gain_to(shift).start()
    gain_last[0] = gain_row[group]

    for far in range(line.chips):
        ff_swap.receive(far, lambda source: None)
    ff_own.wait()
    own_width = groups * ff_block

    def restore(across):
        for part, grad_ref in enumerate((gate_grad, up_grad)):
            for index in range(groups):
                for piece in range(pieces):
                    start = (index * pieces + piece) * ff_block
                    grad_ref[across, pl.ds(start, ff_block)] = ff_recv[
                        piece, across, pl.ds(part * own_width + index * ff_block, ff_block)
                    ]

    by_rows(weight_rows, restore, 16)

    for far in range(last - 2, 0, -1):
        pushes(far)

    fold.arrive()

    def total_term(piece, unused):
        across = pl.ds(pl.multiple_of(piece * weight_rows, weight_rows), weight_rows)
        attn_send[piece] = fold.sum(across).astype(low)
        return unused

    lax.fori_loop(0, pieces, total_term, 0)
    attn_swap = LineSwap(
        line, lambda peer: attn_send.at[peer], lambda source: attn_recv.at[source], at_s, at_r
    )
    attn_swap.start()

    scatter.total(total_ref)

    def rest(across):
        values = hidden[across, :].astype(full)
        inverse = lax.rsqrt(jnp.mean(values * values, axis=-1, keepdims=True) + epsilon)
        scaled = total_ref[across, :] * gains[:, pl.ds(0, model)]
        hidden_grad[across, :] = (
            grad_middle[across, :]
            + inverse * scaled
            - values
            * (inverse * inverse * inverse * jnp.mean(scaled * values, axis=-1, keepdims=True))
        ).astype(low)

    by_rows(rows, rest)
    down_early.arrive()
    down_late.arrive()
    down_own.wait()
    whole_fold = Fold(groups, down_term, down_in, de_s, de_r)

    def total_down(across):
        down_grad[across, :] = whole_fold.sum(across, down_mine).astype(low)

    by_rows(down_grad.shape[0], total_down, 16)
    for shift in range(1, groups):
        peer = lax.rem(group + groups - shift, groups)
        remote(
            gain_row.at[peer], gain_last.at[shift], gs_s.at[shift], gs_r.at[shift], "seq", peer
        ).wait_recv()
    gains_grad[...] = jnp.sum(gain_last[...], axis=0)[0:1, pl.ds(0, gain_count)]

    for far in range(line.chips):
        attn_swap.receive(far, lambda source: None)
    attn_recv[me] = attn_send[me]
    copies = max(1, pieces // KV)
    corner[...] = jnp.zeros(corner.shape, full)
    for piece in range(pieces):
        query_grad[:, pl.ds(piece * q_width, q_width)] = attn_recv[piece, :, pl.ds(0, q_width)]
        corner[pl.ds(0, weight_rows), pl.ds(piece * heads, heads)] = attn_recv[
            piece, :, pl.ds(q_width + 2 * kv_width, heads)
        ].astype(full)
    head_grad[...] = corner[...].T[: head_grad.shape[0], :weight_rows]
    for place in range(pieces // copies):
        for kind, grad_ref in enumerate((key_grad, value_grad)):
            columns = pl.ds(q_width + kind * kv_width, kv_width)
            summed = attn_recv[place * copies, :, columns].astype(full)
            for copy in range(1, copies):
                summed = summed + attn_recv[place * copies + copy, :, columns].astype(full)
            grad_ref[:, pl.ds(place * kv_width, kv_width)] = summed

    @pl.when(spread.moves)
    def _():
        spread.copy(out_grad, out_grad, om_s, om_r, True).wait_recv()
        out_move.wait_send()

    scatter.finish()
    ff_swap.finish()
    attn_swap.finish()
    gain_swap.finish()
    for shift in range(1, groups):
        gain_to(shift).wait_send()
    fold.finish()
    out_fold.finish()
    down_early.finish()
    down_late.finish()


def attend_back(
    grad_branch, out_low, saved, gated_t, tables, gains, prefix, normed, attn_low, hidden, grad_middle,
    swiglu_gain_grad, ff_share, down_term, gain_count, shape, number,
):
    pieces, groups, heads, kv_heads, ff_block = shape
    length, (rows, model) = grad_branch.shape[0], hidden.shape
    width = attn_low.shape[1]
    weight_rows = ff_share.shape[1]
    q_width, kv_width = heads * HD, kv_heads * HD
    struct, vmem = jax.ShapeDtypeStruct, pltpu.VMEM
    padded = -(-gain_count // 128) * 128
    return pl.pallas_call(
        functools.partial(attend_back_kernel, shape),
        out_shape=(
            struct((rows, model), low),
            struct((1, gain_count), full),
            struct((weight_rows, H * HD), low),
            struct((weight_rows, KV * HD), full),
            struct((weight_rows, KV * HD), full),
            struct((H, weight_rows), full),
            struct((weight_rows, pieces * groups * ff_block), low),
            struct((weight_rows, pieces * groups * ff_block), low),
            struct((weight_rows, model), low),
            struct(down_term.shape[1:], low),
        ),
        in_specs=[IN_VMEM] * 15 + [pl.BlockSpec(memory_space=pltpu.SMEM), ANY] + [IN_VMEM] * 4 + [ANY, ANY],
        out_specs=(IN_VMEM,) * 10,
        scratch_shapes=[
            vmem((groups - 1,) + down_term.shape[1:], low),
            vmem(down_term.shape[1:], low),
            DMA,
            DMA,
            vmem((HD, HD), full),
            vmem((groups, weight_rows, model), low),
            vmem((groups - 1, weight_rows, model), low),
            vmem((weight_rows, model), low),
            vmem((q_width, length), full),
            vmem((HD, length), low),
            vmem((length, HD), low),
            vmem((q_width, length), full),
            vmem((length, kv_width), full),
            vmem((length, kv_width), full),
            vmem((width, length), low),
            vmem((length, width), low),
            vmem((rows, model), full),
            vmem(ff_share.shape, low),
            vmem((2, length, model // groups), low),
            DMA((2,)),
            vmem((groups, model // groups, width), low),
            vmem((groups - 1, model // groups, width), low),
            vmem((pieces, weight_rows, width), low),
            vmem((pieces, weight_rows, width), low),
            vmem((1, 2 * model + 2 * HD), full),
            vmem((pieces, groups, 8, padded), full),
            vmem((pieces, groups, 8, padded), full),
            vmem((groups, 8, padded), full),
            vmem((groups, 8, padded), full),
        ]
        + swap_scratch(pieces) * 3
        + [DMA((groups,))] * 6
        + [DMA] * 2
        + [DMA((groups,))] * 4
        + scatter_scratch(pieces, rows, model),
        compiler_params=pltpu.CompilerParams(
            collective_id=number, has_side_effects=True, vmem_limit_bytes=67043328
        ),
        name=f"attend_back_{number}",
    )(
        grad_branch, out_low, *saved, gated_t, *tables, gains, prefix, normed, attn_low, hidden, grad_middle,
        swiglu_gain_grad, ff_share, down_term,
    )


def feed_kernel(
    shape,
    normed_two,
    ff_low,
    down_weight,
    og_all,
    n2_all,
    hidden_ff,
    grad_pre,
    down_low,
    down_block,
    before,
    share_s,
    share_r,
    *gather_sems,
):
    pieces, groups = shape[:2]
    line = Line(pieces)
    rows, length = normed_two.shape[0], og_all.shape[0]
    own_width = ff_low.shape[1] // 2
    tile = own_width // 3 if own_width % 384 == 0 else 128
    greet(line.peers() + others("seq", groups))
    group = lax.axis_index("seq")
    block_rows = down_weight.shape[0]

    def place(index, source):
        start = pl.multiple_of(index * block_rows, block_rows)
        return down_low.at[pl.ds(start, block_rows)]

    gather = Gather(line, 2, rows, n2_all, gather_sems)
    gather.start(normed_two)
    n2_all[pl.ds(pl.multiple_of(line.me * rows, rows), rows), :] = normed_two[...]

    def narrow(across):
        down_block[across, :] = down_weight[across, :].astype(low)

    by_rows(block_rows, narrow, 16)
    share = Share(groups, place, share_s, share_r)
    share.send(0, down_block)
    down_low[pl.ds(pl.multiple_of(group * block_rows, block_rows), block_rows), :] = down_block[...]

    def chip_rows(chip):
        across = pl.ds(pl.multiple_of(chip * 2 * rows, 2 * rows), 2 * rows)

        def step(index, unused):
            start = index * tile
            first, second = lanes(start, tile), lanes(own_width + start, tile)
            before[across, first] = product(n2_all[across, :], ff_low[:, first])
            before[across, second] = product(n2_all[across, :], ff_low[:, second])
            return unused

        lax.fori_loop(0, own_width // tile, step, 0)

    def swiglu(least, most):
        def rows_of(chip, unused):
            far = jnp.abs(chip - line.chip)
            across = pl.ds(pl.multiple_of(chip * 2 * rows, 2 * rows), 2 * rows)

            def step(column, unused):
                first, second = lanes(column * tile, tile), lanes(own_width + column * tile, tile)
                grads = product_nt(og_all[across, :], down_low[lanes(column * tile, tile), :])
                gate, up = before[across, first], before[across, second]
                sigmoid = jax.nn.sigmoid(gate)
                silu = gate * sigmoid
                hidden_ff[across, first] = (silu * up).astype(low)
                grad_pre[across, first] = (
                    grads * up * (sigmoid * (1.0 + gate * (1.0 - sigmoid)))
                ).astype(low)
                grad_pre[across, second] = (grads * silu).astype(low)
                return unused

            @pl.when(jnp.logical_and(far >= least, far <= most))
            def _():
                lax.fori_loop(0, own_width // tile, step, 0)

            return unused

        lax.fori_loop(0, line.chips, rows_of, 0)

    def compute(far):
        gather.arrive(far)
        if far == 0:
            chip_rows(line.chip)
            return

        @pl.when(line.chip - far >= 0)
        def _():
            chip_rows(line.chip - far)

        @pl.when(line.chip + far < line.chips)
        def _():
            chip_rows(line.chip + far)

    for hop in range(1, line.chips - 1):
        gather.forward(hop)
        compute(hop - 1)
        if hop == 1:
            share.relay(0)
    if line.chips > 1:
        compute(line.chips - 2)
        share.finish(1)
        swiglu(0, line.chips - 2)
        gather.forward(line.chips - 1)
    compute(line.chips - 1)
    swiglu(line.chips - 1, line.chips - 1)
    gather.finish()


def feed(normed_two, ff_low, down_weight, og_all, shape, number):
    pieces, groups = shape[:2]
    length, model = og_all.shape
    own_width = ff_low.shape[1] // 2
    struct = jax.ShapeDtypeStruct
    return pl.pallas_call(
        functools.partial(feed_kernel, shape),
        out_shape=(
            struct((length, model), low),
            struct((length, own_width), low),
            struct((length, 2 * own_width), low),
            struct((own_width, model), low),
        ),
        in_specs=[IN_VMEM] * 4,
        out_specs=(IN_VMEM,) * 4,
        scratch_shapes=[
            pltpu.VMEM(down_weight.shape, low),
            pltpu.VMEM((length, 2 * own_width), full),
            DMA((1, groups)),
            DMA((1, groups)),
        ]
        + gather_scratch(pieces, 2),
        compiler_params=pltpu.CompilerParams(
            collective_id=number, has_side_effects=True, vmem_limit_bytes=60 << 20
        ),
        name=f"feed_{number}",
    )(normed_two, ff_low, down_weight, og_all)


def feed_back_kernel(
    shape,
    grad_pre,
    ff_low,
    hidden_ff,
    down_low,
    og_all,
    n2_all,
    middle,
    out_grad,
    gains,
    gb_all,
    grad_middle,
    gain_grad,
    hidden_out,
    ff_share,
    down_term,
    total_ref,
    branch,
    n2_part,
    term,
    term_in,
    part_sem,
    own_sem,
    ts_s,
    ts_r,
    *sems,
):
    pieces, groups = shape[:2]
    buffers, sems = sems[:2], sems[2:]
    gather_sems, sems = sems[:6], sems[6:]
    line = Line(pieces)
    me, group = line.me, lax.axis_index("seq")
    length, rows, model = og_all.shape[0], middle.shape[0], og_all.shape[1]
    weight_rows = ff_share.shape[1]
    greet(line.peers() + others("seq", groups))
    half = len(sems) // 2
    inner = Scatter(line, rows, buffers + sems[:half])
    outer = Scatter(line, rows, buffers + sems[half:])
    inner.clear()
    outer.clear()
    block = blocks_nt(grad_pre, ff_low, rows)
    last = line.chips - 1

    def fills(scatter, far, block):
        scatter.fill(far, far, block)

    def pushes(scatter, far):
        for distance, side in scatter.order():
            if distance == far and far > 0:
                scatter.push(far, side)

    share = model // groups

    fold = Fold(groups, term, term_in, ts_s, ts_r)

    def load(job):
        index = fold.order[job]
        return pltpu.make_async_copy(
            n2_all.at[:, lanes(index * share, share)], n2_part.at[job % 2], part_sem.at[job % 2]
        )

    def ff_grad(job, index):
        load(job).wait()
        if job + 1 < groups:
            load(job + 1).start()

        def step(tile, unused):
            value = product_tn(n2_part[job % 2, :, lanes(tile * 128, 128)], grad_pre[...])
            term[index, pl.ds(pl.multiple_of(tile * 128, 128), 128), :] = value.astype(low)
            return unused

        lax.fori_loop(0, share // 128, step, 0)

    jobs = list(range(groups))

    def some_grads(count):
        for _ in range(min(count, len(jobs))):
            job = jobs.pop(0)
            ff_grad(job, fold.order[job])
            fold.ready(job)

    load(0).start()
    fills(inner, last, block)
    pushes(inner, last)
    fills(inner, last - 1, block)
    some_grads(1)
    each = -(-(groups - 1) // max(1, last - 1))
    for hop in range(1, line.chips):
        pushes(inner, last - hop)
        if hop < last:
            fills(inner, last - 1 - hop, block)
        some_grads(each)
    some_grads(groups)

    down_rows = down_term.shape[1]
    piece_rows = math.gcd(down_rows, 128)

    def down_grads(index, unused):
        value = product_tn(hidden_ff[:, lanes(index * 128, 128)], og_all[...]).astype(low)
        for part in range(128 // piece_rows):
            row = index * 128 + part * piece_rows
            down_term[row // down_rows, pl.ds(pl.multiple_of(lax.rem(row, down_rows), piece_rows), piece_rows), :] = (
                value[part * piece_rows : (part + 1) * piece_rows]
            )
        return unused

    lax.fori_loop(0, down_low.shape[0] // 128, down_grads, 0)
    inner.total(total_ref)
    inner.finish()
    gain_grad[...] = jnp.zeros(gain_grad.shape, full)

    def rest(across):
        values, grads = middle[across, :], total_ref[across, :]
        inverse = lax.rsqrt(jnp.mean(values * values, axis=-1, keepdims=True) + epsilon)
        gain_grad[...] += jnp.sum(grads * values * inverse, axis=0, keepdims=True)
        scaled = grads * gains[:, pl.ds(model, model)]
        result = (
            out_grad[across, :].astype(full)
            + inverse * scaled
            - values
            * (inverse * inverse * inverse * jnp.mean(scaled * values, axis=-1, keepdims=True))
        )
        grad_middle[across, :] = result
        branch[across, :] = result.astype(low)

    by_rows(rows, rest)

    gather = Gather(line, 2, rows, gb_all, gather_sems)
    gather.start(branch)
    start = pl.multiple_of(me * rows, rows)
    own = pltpu.make_async_copy(branch, gb_all.at[pl.ds(start, rows)], own_sem)
    own.start()
    block = blocks_nn(hidden_ff, down_low, rows)
    fills(outer, last, block)
    pushes(outer, last)
    fills(outer, last - 1, block)
    for hop in range(1, line.chips):
        gather.forward(hop)
        pushes(outer, last - hop)
        if hop < last:
            fills(outer, last - 1 - hop, block)
    fold.arrive()

    def total_term(piece, unused):
        across = pl.ds(pl.multiple_of(piece * weight_rows, weight_rows), weight_rows)
        ff_share[piece] = fold.sum(across).astype(low)
        return unused

    lax.fori_loop(0, pieces, total_term, 0)
    outer.total(total_ref)

    def output(across):
        hidden_out[across, :] = (middle[across, :] + total_ref[across, :]).astype(low)

    by_rows(rows, output)
    own.wait()
    for hop in range(line.chips):
        gather.arrive(hop)
    gather.finish()
    outer.finish()
    fold.finish()


def feed_back(
    grad_pre, ff_low, hidden_ff, down_low, og_all, n2_all, middle, out_grad, gains, shape, number
):
    pieces, groups = shape[:2]
    length, (rows, model) = og_all.shape[0], middle.shape
    own_width, width = hidden_ff.shape[1], grad_pre.shape[1]
    weight_rows = model // (groups * pieces)
    struct, vmem = jax.ShapeDtypeStruct, pltpu.VMEM
    scatter = scatter_scratch(pieces, rows, model)
    return pl.pallas_call(
        functools.partial(feed_back_kernel, shape),
        out_shape=(
            struct((length, model), low),
            struct((rows, model), full),
            struct((1, model), full),
            struct((rows, model), low),
            struct((pieces, weight_rows, width), low),
            struct((groups, own_width // groups, model), low),
        ),
        in_specs=[IN_VMEM] * 5 + [ANY] + [IN_VMEM] * 3,
        out_specs=(ANY,) + (IN_VMEM,) * 5,
        scratch_shapes=[
            vmem((rows, model), full),
            vmem((rows, model), low),
            vmem((2, length, model // groups), low),
            vmem((groups, model // groups, width), low),
            vmem((groups - 1, model // groups, width), low),
            DMA((2,)),
            DMA,
            DMA((groups,)),
            DMA((groups,)),
        ]
        + scatter[:2]
        + gather_scratch(pieces, 2)
        + scatter[2:] * 2,
        compiler_params=pltpu.CompilerParams(
            collective_id=number, has_side_effects=True, vmem_limit_bytes=63 << 20
        ),
        name=f"feed_back_{number}",
    )(grad_pre, ff_low, hidden_ff, down_low, og_all, n2_all, middle, out_grad, gains)


def widen_kernel(*refs):
    for source, target in zip(refs[: len(refs) // 2], refs[len(refs) // 2 :]):
        target[...] = source[...].astype(target.dtype)


def widen(arrays, kinds):
    steps = math.gcd(*(array.shape[0] for array in arrays[:-2])) // 16
    specs = [
        pl.BlockSpec((array.shape[0] // steps, array.shape[1]), lambda step: (step, 0))
        for array in arrays[:-2]
    ] + [pl.BlockSpec(array.shape, lambda step: (0, 0)) for array in arrays[-2:]]
    return pl.pallas_call(
        widen_kernel,
        grid=(steps,),
        out_shape=[
            jax.ShapeDtypeStruct(array.shape, kind) for array, kind in zip(arrays, kinds)
        ],
        in_specs=specs,
        out_specs=specs,
        name="widen",
    )(*arrays)


def on_device(
    hidden_in,
    out_grad,
    prefix_len,
    norm_gains,
    query_weight,
    key_weight,
    value_weight,
    head_gate_weight,
    out_weight,
    gate_weight,
    up_weight,
    down_weight,
):
    row_count, model = hidden_in.shape
    groups = lax.axis_size("seq")
    pieces = lax.axis_size("ctx")
    length = row_count * pieces
    weight_rows = query_weight.shape[0]
    heads = H // pieces
    kv_heads = max(1, KV // pieces)
    ff_block = down_weight.shape[0]
    ff_own = ff_block * groups
    gain_count = norm_gains.shape[0]
    shape = (pieces, groups, heads, kv_heads, ff_block)
    inverse = rope_base ** (-jnp.arange(HD // 2, dtype=full) * 2.0 / HD)
    angles = inverse[:, None] * jnp.arange(length, dtype=jnp.int32).astype(full)[None, :]
    tables = (jnp.cos(angles), jnp.sin(angles))
    prefix = prefix_len.reshape(1, 1)

    (
        normed, attn_low, gains_full, out_low, *saved, gated_t, middle, normed_two, out_grad_all, ff_low
    ) = forward(
        hidden_in,
        norm_gains,
        (query_weight, key_weight, value_weight, head_gate_weight.T, out_weight),
        tables,
        prefix,
        out_grad,
        (gate_weight, up_weight),
        shape,
        0,
    )
    ff_low = ff_low.reshape(model, 2 * ff_own)
    n2_all, hidden_ff, grad_pre, down_low = feed(
        normed_two, ff_low, down_weight, out_grad_all, shape, 2
    )
    grad_branch, grad_middle, swiglu_gain_grad, hidden_out, ff_share, down_term = feed_back(
        grad_pre, ff_low, hidden_ff, down_low, out_grad_all, n2_all, middle, out_grad, gains_full, shape, 3
    )
    hidden_grad, gains_share, query_share, key_share, value_share, head_share, gate_share, up_share, output_share, down_share = (
        attend_back(
            grad_branch,
            out_low,
            saved,
            gated_t,
            tables,
            gains_full,
            prefix,
            normed,
            attn_low,
            hidden_in,
            grad_middle,
            swiglu_gain_grad,
            ff_share,
            down_term,
            gain_count,
            shape,
            4,
        )
    )
    (
        hidden_out,
        hidden_grad,
        query_share,
        key_share,
        value_share,
        output_share,
        gate_share,
        up_share,
        down_share,
        head_share,
        gains_share,
    ) = widen(
        (
            hidden_out,
            hidden_grad,
            query_share,
            key_share,
            value_share,
            output_share,
            gate_share,
            up_share,
            down_share,
            head_share,
            gains_share,
        ),
        (low, low) + (full,) * 9,
    )
    return (
        hidden_out,
        hidden_grad,
        gains_share.reshape(gain_count),
        query_share,
        key_share,
        value_share,
        head_share.T,
        output_share,
        gate_share,
        up_share,
        down_share,
    )


def solution(mesh):
    rows = P(("seq", "ctx"), None)
    return jax.shard_map(
        on_device,
        mesh=mesh,
        in_specs=(rows, rows, P("seq"), P(("seq", "ctx"))) + (rows,) * 8,
        out_specs=(rows, rows, P(("seq", "ctx"))) + (rows,) * 8,
        check_vma=False,
    )
```

```python
import functools
import math

import jax
import jax.numpy as jnp
from jax import lax
from jax.experimental import pallas as pl
from jax.experimental.pallas import tpu as pltpu
from jax.sharding import PartitionSpec as P

H = 16
KV = 8
HD = 128


epsilon = 1e-06
rope_base = 1000000.0
negative = -1e30
low = jnp.bfloat16
full = jnp.float32
MESH = pl.DeviceIdType.MESH
ANY = pl.BlockSpec(memory_space=pl.ANY)
IN_VMEM = pl.BlockSpec(memory_space=pltpu.VMEM)
DMA = pltpu.SemaphoreType.DMA


def product(left_side, right_side):
    return jnp.dot(left_side, right_side, preferred_element_type=full)


def product_nt(left_side, right_side):
    return lax.dot_general(
        left_side, right_side, (((1,), (1,)), ((), ())), preferred_element_type=full
    )


def product_tn(left_side, right_side):
    return lax.dot_general(
        left_side, right_side, (((0,), (0,)), ((), ())), preferred_element_type=full
    )


def by_rows(rows, body, tile=32):
    tile = min(tile, rows)

    def step(index, unused):
        body(pl.ds(pl.multiple_of(index * tile, tile), tile))
        return unused

    lax.fori_loop(0, rows // tile, step, 0)


def remote(source, target, send, receive, axis, peer):
    return pltpu.make_async_remote_copy(
        src_ref=source,
        dst_ref=target,
        send_sem=send,
        recv_sem=receive,
        device_id={axis: peer},
        device_id_type=MESH,
    )


def greet(peers):
    barrier = pltpu.get_barrier_semaphore()
    for axis, peer, exists in peers:
        place = {"seq": peer[0], "ctx": peer[1]} if axis is None else {axis: peer}

        def signal():
            pl.semaphore_signal(barrier, inc=1, device_id=place, device_id_type=MESH)

        if exists is True:
            signal()
        else:
            pl.when(exists)(signal)

    arrivals = sum(1 for _, _, exists in peers if exists is True)
    for _, _, exists in peers:
        if exists is not True:
            arrivals = arrivals + exists.astype(jnp.int32)
    pl.semaphore_wait(barrier, arrivals)


def others(axis, count):
    me = lax.axis_index(axis)
    return [(axis, lax.rem(me + shift, count), True) for shift in range(1, count)]


class Line:
    def __init__(self, pieces):
        self.chips = pieces // 2
        self.me = lax.axis_index("ctx")
        self.chip, self.core = self.me // 2, lax.rem(self.me, 2)
        self.sibling = self.me + 1 - 2 * self.core
        self.right, self.left = self.me + 2, self.me - 2
        self.has_right, self.has_left = self.chip < self.chips - 1, self.chip > 0

    def peers(self):
        return [
            ("ctx", self.sibling, True),
            ("ctx", self.right, self.has_right),
            ("ctx", self.left, self.has_left),
        ]


def gather_scratch(pieces, parts):
    chips = pieces // 2
    return [DMA((chips, 2, parts))] * 2 + [DMA((chips, parts))] * 4


class Gather:
    def __init__(self, line, parts, rows, out_ref, sems):
        self.line, self.parts, self.rows, self.out_ref = line, parts, rows, out_ref
        self.size = rows // parts
        self.sib_send, self.sib_recv, self.r_send, self.r_recv, self.l_send, self.l_recv = sems

    def at(self, position, part):
        start = pl.multiple_of(position * self.rows + part * self.size, self.size)
        return self.out_ref.at[pl.ds(start, self.size)]

    def to_sibling(self, source, hop, side, part, position):
        return remote(
            source,
            self.at(position, part),
            self.sib_send.at[hop, side, part],
            self.sib_recv.at[hop, side, part],
            "ctx",
            self.line.sibling,
        )

    def to_right(self, source, hop, part, position):
        return remote(
            source,
            self.at(position, part),
            self.r_send.at[hop, part],
            self.r_recv.at[hop, part],
            "ctx",
            self.line.right,
        )

    def to_left(self, source, hop, part, position):
        return remote(
            source,
            self.at(position, part),
            self.l_send.at[hop, part],
            self.l_recv.at[hop, part],
            "ctx",
            self.line.left,
        )

    def start(self, x_ref):
        line = self.line
        for part in range(self.parts):
            piece = x_ref.at[pl.ds(part * self.size, self.size)]

            @pl.when(line.has_right)
            def _():
                self.to_right(piece, 0, part, line.me).start()

            @pl.when(line.has_left)
            def _():
                self.to_left(piece, 0, part, line.me).start()

            self.to_sibling(piece, 0, 0, part, line.me).start()

    def forward(self, hop):
        line = self.line
        for part in range(self.parts):
            from_left, from_right = line.me - 2 * hop, line.me + 2 * hop

            @pl.when(line.chip - hop >= 0)
            def _():
                piece = self.at(from_left, part)
                self.to_right(piece, hop - 1, part, from_left).wait_recv()

                @pl.when(line.has_right)
                def _():
                    self.to_right(piece, hop, part, from_left).start()

                self.to_sibling(piece, hop, 0, part, from_left).start()

            @pl.when(line.chip + hop < line.chips)
            def _():
                piece = self.at(from_right, part)
                self.to_left(piece, hop - 1, part, from_right).wait_recv()

                @pl.when(line.has_left)
                def _():
                    self.to_left(piece, hop, part, from_right).start()

                self.to_sibling(piece, hop, 1, part, from_right).start()

    def legs(self, hop):
        line = self.line
        return [
            (
                side,
                (line.chip - hop >= 0) if side == 0 else (line.chip + hop < line.chips),
                (line.me - 2 * hop) if side == 0 else (line.me + 2 * hop),
            )
            for side in range(1 if hop == 0 else 2)
        ]

    def arrive(self, hop):
        for side, there, position in self.legs(hop):
            for part in range(self.parts):

                @pl.when(there)
                def _():
                    self.to_sibling(
                        self.at(position, part), hop, side, part, position
                    ).wait_recv()

    def finish(self):
        line = self.line
        for hop in range(line.chips):
            for side, there, position in self.legs(hop):
                for part in range(self.parts):

                    @pl.when(there)
                    def _():
                        piece = self.at(position, part)
                        self.to_sibling(piece, hop, side, part, position).wait_send()
                        if side == 0:

                            @pl.when(line.has_right)
                            def _():
                                self.to_right(piece, hop, part, position).wait_send()

                        if side == 1 or hop == 0:

                            @pl.when(line.has_left)
                            def _():
                                self.to_left(piece, hop, part, position).wait_send()

    def complete(self):
        for hop in range(self.line.chips):
            self.arrive(hop)
        self.finish()


def scatter_scratch(pieces, rows, width):
    chips = pieces // 2
    slots = pltpu.VMEM((chips, rows, width), low)
    return [slots] * 3 + [pltpu.VMEM((chips + 1, rows, width), low)] + [DMA((chips,))] * 2 + [DMA((chips, 2))] * 4


class Scatter:
    def __init__(self, line, rows, scratch):
        self.line, self.rows = line, rows
        (
            self.own,
            self.give,
            self.sib,
            self.arrived,
            self.sib_send,
            self.sib_recv,
            self.r_send,
            self.r_recv,
            self.l_send,
            self.l_recv,
        ) = scratch

    def clear(self):
        line = self.line

        @pl.when(jnp.logical_not(line.has_left))
        def _():
            self.arrived[line.chip] = jnp.zeros(self.arrived.shape[1:], low)

        @pl.when(jnp.logical_not(line.has_right))
        def _():
            self.arrived[line.chips] = jnp.zeros(self.arrived.shape[1:], low)

    def there(self, far, side):
        line = self.line
        return (line.chip + far < line.chips) if side == 0 else (line.chip - far >= 0)

    def target(self, far, side):
        return self.line.chip + far if side == 0 else self.line.chip - far

    def exchange(self, target):
        return remote(
            self.give.at[target],
            self.sib.at[target],
            self.sib_send.at[target],
            self.sib_recv.at[target],
            "ctx",
            self.line.sibling,
        )

    def part(self, which):
        return pl.ds(which * (self.rows // 2), self.rows // 2)

    def send(self, target, side, which):
        part = self.part(which)
        if side == 0:
            return remote(
                self.own.at[target, part],
                self.arrived.at[target, part],
                self.r_send.at[target, which],
                self.r_recv.at[target, which],
                "ctx",
                self.line.right,
            )
        chips, chip = self.line.chips, self.line.chip
        return remote(
            self.own.at[target, part],
            self.arrived.at[jnp.where(target == chip - 1, chips, target), part],
            self.l_send.at[target, which],
            self.l_recv.at[target, which],
            "ctx",
            self.line.left,
        )

    def order(self):
        return [
            (far, side)
            for far in range(self.line.chips - 1, -1, -1)
            for side in range(2 if far else 1)
        ]

    def fill(self, least, most, block):
        line = self.line

        def step(target, unused):
            far = jnp.abs(target - line.chip)

            @pl.when(jnp.logical_and(far >= least, far <= most))
            def _():
                def store(columns, value):
                    first, second = value[: self.rows], value[self.rows :]
                    mine = line.core == 0
                    self.own[target, :, columns] = jnp.where(mine, first, second).astype(low)
                    self.give[target, :, columns] = jnp.where(mine, second, first).astype(low)

                block(target, store)
                self.exchange(target).start()

            return unused

        lax.fori_loop(0, line.chips, step, 0)

    def push(self, far, side):
        line = self.line
        behind = line.has_left if side == 0 else line.has_right

        @pl.when(self.there(far, side))
        def _():
            target = self.target(far, side)
            self.exchange(target).wait_recv()

            for which in range(2):
                first = which * (self.rows // 2)

                def add(part):
                    across = pl.ds(pl.multiple_of(first + part.start, part.size), part.size)
                    self.own[target, across, :] = (
                        self.own[target, across, :].astype(full)
                        + self.sib[target, across, :].astype(full)
                    ).astype(low)

                def add_all(part):
                    across = pl.ds(pl.multiple_of(first + part.start, part.size), part.size)
                    self.own[target, across, :] = (
                        self.own[target, across, :].astype(full)
                        + self.sib[target, across, :].astype(full)
                        + self.arrived[target, across, :].astype(full)
                    ).astype(low)

                if far == line.chips - 1:
                    by_rows(self.rows // 2, add)
                else:

                    @pl.when(behind)
                    def _():
                        self.send(target, side, which).wait_recv()
                        by_rows(self.rows // 2, add_all)

                    @pl.when(jnp.logical_not(behind))
                    def _():
                        by_rows(self.rows // 2, add)

                self.send(target, side, which).start()

    def total(self, total_ref):
        line = self.line
        chip = line.chip
        self.exchange(chip).wait_recv()

        @pl.when(line.has_left)
        def _():
            for which in range(2):
                self.send(chip, 0, which).wait_recv()

        @pl.when(line.has_right)
        def _():
            for which in range(2):
                self.send(chip, 1, which).wait_recv()

        def add(across):
            total = self.own[chip, across, :].astype(full) + self.sib[chip, across, :].astype(full)
            total = total + jnp.where(
                line.has_left, self.arrived[chip, across, :].astype(full), 0.0
            )
            total_ref[across, :] = total + jnp.where(
                line.has_right, self.arrived[line.chips, across, :].astype(full), 0.0
            )

        by_rows(self.rows, add)

    def finish(self):
        for far, side in self.order():

            @pl.when(self.there(far, side))
            def _():
                target = self.target(far, side)
                self.exchange(target).wait_send()
                if far > 0:
                    for which in range(2):
                        self.send(target, side, which).wait_send()


def blocks_nn(left_ref, right_ref, rows, tile=512):
    def block(target, store):
        start = pl.multiple_of(target * 2 * rows, 2 * rows)
        left_side = left_ref[pl.ds(start, 2 * rows), :]

        def step(index, unused):
            columns = pl.ds(pl.multiple_of(index * tile, tile), tile)
            store(columns, product(left_side, right_ref[:, columns]))
            return unused

        lax.fori_loop(0, right_ref.shape[1] // tile, step, 0)

    return block


def blocks_nt(left_ref, right_ref, rows, tile=512):
    def block(target, store):
        start = pl.multiple_of(target * 2 * rows, 2 * rows)
        left_side = left_ref[pl.ds(start, 2 * rows), :]

        def step(index, unused):
            columns = pl.ds(pl.multiple_of(index * tile, tile), tile)
            store(columns, product_nt(left_side, right_ref[columns, :]))
            return unused

        lax.fori_loop(0, right_ref.shape[0] // tile, step, 0)

    return block


class LineSwap:
    def __init__(self, line, send_of, recv_of, s_sem, r_sem):
        self.line, self.send_of, self.recv_of = line, send_of, recv_of
        self.s_sem, self.r_sem = s_sem, r_sem

    def copy(self, far, side, core):
        line = self.line
        if far == 0:
            peer, slot = line.sibling, self.r_sem.at[0, 0, 0]
        else:
            peer = (line.chip + (far if side == 0 else -far)) * 2 + core
            slot = self.r_sem.at[far, side, line.core]
        return remote(
            self.send_of(peer), self.recv_of(line.me), self.s_sem.at[far, side, core], slot, "ctx", peer
        )

    def legs(self, far):
        line = self.line
        if far == 0:
            return [(0, 0, True, True)]
        return [
            (
                side,
                core,
                (line.chip + far < line.chips) if side == 0 else (line.chip - far >= 0),
                (line.chip - far >= 0) if side == 0 else (line.chip + far < line.chips),
            )
            for side in range(2)
            for core in range(2)
        ]

    def start(self):
        for far in range(self.line.chips):
            for side, core, sends, _ in self.legs(far):
                if far == 0:
                    self.copy(far, side, core).start()
                else:

                    @pl.when(sends)
                    def _():
                        self.copy(far, side, core).start()

    def receive(self, far, then):
        line = self.line
        for side, core, _, comes in self.legs(far):
            if far == 0:
                source, slot = line.sibling, self.r_sem.at[0, 0, 0]
            else:
                source = (line.chip + (-far if side == 0 else far)) * 2 + core
                slot = self.r_sem.at[far, side, core]

            def wait():
                remote(
                    self.recv_of(source),
                    self.recv_of(source),
                    self.s_sem.at[far, side, core],
                    slot,
                    "ctx",
                    source,
                ).wait_recv()
                then(source)

            if far == 0:
                wait()
            else:
                pl.when(comes)(wait)

    def again(self, far, then):
        line = self.line
        for side, core, _, comes in self.legs(far):
            if far == 0:
                then(line.sibling)
            else:
                source = (line.chip + (-far if side == 0 else far)) * 2 + core

                @pl.when(comes)
                def _():
                    then(source)

    def finish(self):
        for far in range(self.line.chips):
            for side, core, sends, _ in self.legs(far):
                if far == 0:
                    self.copy(far, side, core).wait_send()
                else:

                    @pl.when(sends)
                    def _():
                        self.copy(far, side, core).wait_send()


def swap_scratch(pieces):
    return [DMA((pieces // 2, 2, 2))] * 2


class Share:
    def __init__(self, groups, place, s_sem, r_sem, relays=True):
        self.groups, self.place, self.s_sem, self.r_sem = groups, place, s_sem, r_sem
        self.group = lax.axis_index("seq")
        self.square = groups == 4 and relays
        self.across = self.group + 1 - 2 * lax.rem(self.group, 2)
        self.along = lax.rem(self.group + 2, groups)
        self.corner = groups - 1 - self.group

    def copy(self, source, slot, peer, origin, target):
        return remote(
            origin, target, self.s_sem.at[source, slot], self.r_sem.at[source, slot], "seq", peer
        )

    def half(self, index, source, which):
        ref = self.place(index, source)
        rows = ref.shape[0] // 2
        return ref.at[pl.ds(which * rows, rows)]

    def first(self, source, origin=None):
        target = self.place(self.group, source)
        origin = target if origin is None else origin
        if self.square:
            peers = [(1, self.across), (2, self.along)]
        else:
            peers = [
                (shift, lax.rem(self.group + shift, self.groups)) for shift in range(1, self.groups)
            ]
        return [self.copy(source, slot, peer, origin, target) for slot, peer in peers]

    def second(self, source):
        one, two = self.half(self.across, source, 0), self.half(self.along, source, 1)
        return [
            self.copy(source, 3, self.along, one, one),
            self.copy(source, 0, self.across, two, two),
        ]

    def send(self, source, origin=None):
        for copy in self.first(source, origin):
            copy.start()

    def relay(self, source):
        if not self.square:
            return
        for slot, index, copy in zip((1, 2), (self.across, self.along), self.second(source)):
            block = self.place(index, source)
            self.copy(source, slot, index, block, block).wait_recv()
            copy.start()

    def finish(self, sources):
        for source in range(sources):
            if self.square:
                for slot, which in ((3, 0), (0, 1)):
                    half = self.half(self.corner, source, which)
                    self.copy(source, slot, self.corner, half, half).wait_recv()
                for copy in self.second(source):
                    copy.wait_send()
            else:
                for shift in range(1, self.groups):
                    index = lax.rem(self.group + self.groups - shift, self.groups)
                    block = self.place(index, source)
                    self.copy(source, shift, index, block, block).wait_recv()
            for copy in self.first(source):
                copy.wait_send()


class Fold:
    def __init__(self, groups, term_ref, inbox, s_sem, r_sem):
        self.groups, self.term, self.inbox = groups, term_ref, inbox
        self.s_sem, self.r_sem = s_sem, r_sem
        self.group = lax.axis_index("seq")
        self.order = [lax.rem(self.group + shift, groups) for shift in range(1, groups)] + [
            self.group
        ]

    def copy(self, job):
        return remote(
            self.term.at[self.order[job]],
            self.inbox.at[job],
            self.s_sem.at[job],
            self.r_sem.at[job],
            "seq",
            self.order[job],
        )

    def ready(self, job):
        if job < self.groups - 1:
            self.copy(job).start()

    def arrive(self):
        for job in range(self.groups - 1):
            self.copy(job).wait_recv()

    def sum(self, across, own=None):
        total = (self.term[self.group, across, :] if own is None else own[across, :]).astype(full)
        for job in range(self.groups - 1):
            total = total + self.inbox[job, across, :].astype(full)
        return total

    def finish(self):
        for job in range(self.groups - 1):
            self.copy(job).wait_send()


class Spread:
    def __init__(self, groups, pieces):
        group, me = lax.axis_index("seq"), lax.axis_index("ctx")
        flat = group * pieces + me
        self.use = (lax.rem(flat, groups), flat // groups)
        held = me * groups + group
        self.rest = (held // pieces, lax.rem(held, pieces))
        self.moves = jnp.logical_or(self.use[0] != group, self.use[1] != me)

    def peers(self):
        return [(None, self.use, self.moves), (None, self.rest, self.moves)]

    def copy(self, source, target, send, receive, back):
        place = self.rest if back else self.use
        return pltpu.make_async_remote_copy(
            src_ref=source,
            dst_ref=target,
            send_sem=send,
            recv_sem=receive,
            device_id={"seq": place[0], "ctx": place[1]},
            device_id_type=MESH,
        )


def lanes(start, size):
    return pl.ds(pl.multiple_of(start, 128), size)


def turn(values, cosine, sine):
    half = values.shape[0] // 2
    first, second = values[:half], values[half:]
    return jnp.concatenate(
        [first * cosine - second * sine, second * cosine + first * sine], axis=0
    )


def turn_back(values, cosine, sine):
    half = values.shape[0] // 2
    first, second = values[:half], values[half:]
    return jnp.concatenate(
        [first * cosine + second * sine, second * cosine - first * sine], axis=0
    )


def column(gains, start):
    return jnp.broadcast_to(gains[:, pl.ds(start, HD)], (HD, HD)).T[:, 0:1]


def inverse_rms(values):
    return lax.rsqrt(jnp.mean(values * values, axis=0, keepdims=True) + epsilon)


def kept(first_key, keys, first_query, queries, prefix):
    key = first_key + lax.broadcasted_iota(jnp.int32, (keys, queries), 0)
    query = first_query + lax.broadcasted_iota(jnp.int32, (keys, queries), 1)
    return key <= jnp.maximum(query, prefix - 1)


def query_blocks(length, body):
    tile = min(256, length // 2)
    half = length // 2

    def early(index, unused):
        body(index * tile, tile, half)
        return unused

    def late(index, unused):
        body(half + index * tile, tile, length)
        return unused

    lax.fori_loop(0, half // tile, early, 0)
    lax.fori_loop(0, half // tile, late, 0)


def forward_kernel(
    shape,
    hidden,
    gains_ref,
    query_weight,
    key_weight,
    value_weight,
    gate_weight_t,
    out_weight,
    cosine,
    sine,
    prefix_ref,
    out_grad,
    gate_weight,
    up_weight,
    normed,
    attn_low,
    gains_out,
    out_low,
    raw_t,
    gate_t,
    q_ref,
    qt_ref,
    k_ref,
    kt_ref,
    v_ref,
    att_t,
    lse_ref,
    gated_t,
    middle,
    normed_two,
    og_all,
    ff_low,
    raw,
    hidden_all,
    blocks,
    out_block,
    gains_row,
    gains_all,
    corner,
    vt_ref,
    gated,
    ff_blocks,
    own_attn,
    own_out,
    out_s,
    out_r,
    ff_sem,
    og_sem,
    ga_s,
    ga_r,
    gs_s,
    gs_r,
    at_s,
    at_r,
    as_s,
    as_r,
    os_s,
    os_r,
    fs_s,
    fs_r,
    fh_s,
    fh_r,
    *sems,
):
    pieces, groups, heads, kv_heads, ff_block = shape
    rows_sems, og_sems, scatter_refs = sems[:6], sems[6:12], sems[12:]
    line = Line(pieces)
    me, group = line.me, lax.axis_index("seq")
    rows, model = hidden.shape
    length = pieces * rows
    weight_rows = out_weight.shape[0]
    q_width, kv_width = heads * HD, kv_heads * HD
    copies = max(1, pieces // KV)
    spread = Spread(groups, pieces)
    greet(others("ctx", pieces) + others("seq", groups) + spread.peers())
    gain_count = gains_ref.shape[1]
    gains_row[...] = jnp.zeros(gains_row.shape, full)
    gains_row[0:1, pl.ds(0, gain_count)] = gains_ref[...].astype(low).astype(full)
    gains_all[group, me] = gains_row[...]
    gain_swap = LineSwap(
        line, lambda peer: gains_row, lambda source: gains_all.at[group, source], ga_s, ga_r
    )
    gain_swap.start()

    blocks[:, :, pl.ds(q_width + 2 * kv_width, HD)] = jnp.zeros((pieces, weight_rows, HD), low)
    corner[...] = jnp.zeros(corner.shape, full)
    corner[pl.ds(0, gate_weight_t.shape[0]), pl.ds(0, weight_rows)] = gate_weight_t[...]
    gate_rows = corner[...].T
    for piece in range(pieces):
        blocks[piece, :, pl.ds(0, q_width)] = query_weight[
            :, pl.ds(piece * q_width, q_width)
        ].astype(low)
        start = piece // copies * kv_width
        blocks[piece, :, pl.ds(q_width, kv_width)] = key_weight[:, pl.ds(start, kv_width)].astype(low)
        blocks[piece, :, pl.ds(q_width + kv_width, kv_width)] = value_weight[
            :, pl.ds(start, kv_width)
        ].astype(low)
        blocks[piece, :, pl.ds(q_width + 2 * kv_width, heads)] = gate_rows[
            :weight_rows, piece * heads : (piece + 1) * heads
        ].astype(low)

    def place(index, source):
        start = pl.multiple_of((index * pieces + source) * weight_rows, weight_rows)
        return attn_low.at[pl.ds(start, weight_rows)]

    attn_swap = LineSwap(
        line, lambda peer: blocks.at[peer], lambda source: place(group, source), at_s, at_r
    )
    attn_swap.start()
    share = Share(groups, place, as_s, as_r, False)
    share.send(me, blocks.at[me])
    attn_own = pltpu.make_async_copy(blocks.at[me], place(group, me), own_attn)
    attn_own.start()
    gather = Gather(line, 2, rows, hidden_all, rows_sems)
    gather.start(hidden)
    hidden_all[pl.ds(pl.multiple_of(me * rows, rows), rows), :] = hidden[...]
    out_block[...] = out_weight[...].astype(low)

    def out_place(index):
        return out_low.at[pl.ds(pl.multiple_of(index * weight_rows, weight_rows), weight_rows)]

    out_move = spread.copy(out_block, out_place(spread.use[0]), out_s, out_r, False)
    out_stay = pltpu.make_async_copy(out_block, out_place(group), own_out)

    @pl.when(spread.moves)
    def _():
        out_move.start()

    @pl.when(jnp.logical_not(spread.moves))
    def _():
        out_stay.start()

    def to_groups(shift):
        peer = lax.rem(group + shift, groups)
        return remote(
            gains_all.at[group], gains_all.at[group], gs_s.at[shift], gs_r.at[shift], "seq", peer
        )

    def from_groups(shift):
        peer = lax.rem(group + groups - shift, groups)
        return remote(
            gains_all.at[peer], gains_all.at[peer], gs_s.at[shift], gs_r.at[shift], "seq", peer
        )

    attn_swap.receive(0, share.send)
    for far in range(line.chips):
        gain_swap.receive(far, lambda source: None)
    for shift in range(1, groups):
        to_groups(shift).start()
    if line.chips > 1:
        attn_swap.receive(1, share.send)

    def chip_rows(chip):
        return chip * 2 * rows

    def both(far, body):
        if far == 0:
            body(chip_rows(line.chip))
            return

        @pl.when(line.chip - far >= 0)
        def _():
            body(chip_rows(line.chip - far))

        @pl.when(line.chip + far < line.chips)
        def _():
            body(chip_rows(line.chip + far))

    def normalise(start):
        def some(part):
            across = pl.ds(pl.multiple_of(start + part.start, part.size), part.size)
            values = hidden_all[across, :].astype(full)
            inverse = lax.rsqrt(jnp.mean(values * values, axis=-1, keepdims=True) + epsilon)
            normed[across, :] = (values * inverse * gains_out[0:1, pl.ds(0, model)]).astype(low)

        by_rows(2 * rows, some)

    def project(least, most):
        def step(chip, unused):
            far = jnp.abs(chip - line.chip)

            @pl.when(jnp.logical_and(far >= least, far <= most))
            def _():
                across = pl.ds(pl.multiple_of(chip * 2 * rows, 2 * rows), 2 * rows)
                raw[across, :] = product(normed[across, :], attn_low[...])

            return unused

        lax.fori_loop(0, line.chips, step, 0)

    for far in range(2, line.chips):
        attn_swap.receive(far, share.send)
    out_share = Share(groups, lambda index, source: out_place(index), os_s, os_r)

    @pl.when(spread.moves)
    def _():
        spread.copy(out_place(group), out_place(group), out_s, out_r, False).wait_recv()

    @pl.when(jnp.logical_not(spread.moves))
    def _():
        out_stay.wait()

    out_share.send(0)
    for shift in range(1, groups):
        from_groups(shift).wait_recv()
    for index in range(groups * pieces):
        gains_out[0:1, pl.ds(index * gain_count, gain_count)] = gains_all[
            index // pieces, index % pieces, 0:1, pl.ds(0, gain_count)
        ]
    own_width = groups * ff_block

    def prepare(across):
        for half, weight_ref in enumerate((gate_weight, up_weight)):
            for index in range(groups):
                for piece in range(pieces):
                    start = (index * pieces + piece) * ff_block
                    ff_blocks[piece, across, pl.ds(half * own_width + index * ff_block, ff_block)] = (
                        weight_ref[across, pl.ds(start, ff_block)].astype(low)
                    )

    by_rows(gate_weight.shape[0], prepare, 16)
    for hop in range(1, line.chips - 1):
        gather.forward(hop)
        gather.arrive(hop - 1)
        both(hop - 1, normalise)
    ff_swap = LineSwap(
        line, lambda peer: ff_blocks.at[peer], lambda source: ff_low.at[group, source], fs_s, fs_r
    )
    ff_swap.start()
    ff_share = Share(groups, lambda index, source: ff_low.at[index, source], fh_s, fh_r, False)
    ff_share.send(me, ff_blocks.at[me])
    ff_own = pltpu.make_async_copy(ff_blocks.at[me], ff_low.at[group, me], ff_sem)
    ff_own.start()
    gather.arrive(line.chips - 2)
    both(line.chips - 2, normalise)
    attn_own.wait()
    out_share.relay(0)
    share.finish(pieces)
    project(0, line.chips - 2)
    gather.forward(line.chips - 1)
    gather.arrive(line.chips - 1)
    both(line.chips - 1, normalise)
    project(line.chips - 1, line.chips - 1)
    og_gather = Gather(line, 2, rows, og_all, og_sems)
    og_gather.start(out_grad)
    start = pl.multiple_of(me * rows, rows)
    og_own = pltpu.make_async_copy(out_grad, og_all.at[pl.ds(start, rows)], og_sem)
    og_own.start()
    prefix = prefix_ref[0, 0]
    query_gain, key_gain = column(gains_out, 2 * model), column(gains_out, 2 * model + HD)
    scale = HD ** (-0.5)
    for head in range(heads + kv_heads):
        part = pl.ds(head * HD, HD)
        values = raw[:, part].T
        raw_t[part, :] = values
        gain = query_gain if head < heads else key_gain
        turned = turn(values * inverse_rms(values) * gain, cosine[...], sine[...])
        if head < heads:
            qt_ref[part, :] = turned.astype(low)
            q_ref[:, part] = turned.T.astype(low)
        else:
            part = pl.ds((head - heads) * HD, HD)
            kt_ref[part, :] = turned.astype(low)
            k_ref[:, part] = turned.T.astype(low)
    for head in range(kv_heads):
        part = pl.ds(head * HD, HD)
        values = raw[:, pl.ds((heads + kv_heads + head) * HD, HD)]
        v_ref[:, part] = values.astype(low)
        vt_ref[part, :] = values.T.astype(low)
    gate_t[...] = raw[:, pl.ds((heads + 2 * kv_heads) * HD, HD)].T[: gate_t.shape[0]]
    ff_swap.receive(0, ff_share.send)
    for head in range(heads):
        part = pl.ds(head * HD, HD)
        kv_part = pl.ds(head * kv_heads // heads * HD, HD)

        def block(first, tile, keys):
            columns = lanes(first, tile)
            scores = product(k_ref[pl.ds(0, keys), kv_part], qt_ref[part, columns]) * scale
            scores = jnp.where(kept(0, keys, first, tile, prefix), scores, negative)
            top = jnp.max(scores, axis=0, keepdims=True)
            expanded = jnp.exp(scores - top)
            total = jnp.sum(expanded, axis=0, keepdims=True)
            lse_ref[head : head + 1, columns] = top + jnp.log(total)
            att_t[part, columns] = (
                product(vt_ref[kv_part, pl.ds(0, keys)], expanded.astype(low)) / total
            )

        query_blocks(length, block)
        scaled = att_t[part, :] * jax.nn.sigmoid(gate_t[head : head + 1, :])
        gated_t[part, :] = scaled.astype(low)
        gated[:, part] = scaled.T.astype(low)
        if head == 0 and line.chips > 1:
            ff_swap.receive(1, ff_share.send)

    out_share.finish(1)
    scatter = Scatter(line, rows, scatter_refs)
    scatter.clear()
    block = blocks_nn(gated, out_low, rows)
    last = line.chips - 1
    scatter.fill(last, last, block)
    for far, side in scatter.order():
        if far == last:
            scatter.push(far, side)
    scatter.fill(0, last - 1, block)
    for far in range(2, line.chips):
        ff_swap.receive(far, ff_share.send)
    for hop in range(1, line.chips):
        og_gather.forward(hop)
        for far, side in scatter.order():
            if far == last - hop and far > 0:
                scatter.push(far, side)
    scatter.total(middle)

    def normalise_two(across):
        values = hidden[across, :].astype(full) + middle[across, :]
        middle[across, :] = values
        inverse = lax.rsqrt(jnp.mean(values * values, axis=-1, keepdims=True) + epsilon)
        normed_two[across, :] = (values * inverse * gains_out[:, pl.ds(model, model)]).astype(low)

    by_rows(rows, normalise_two)
    og_own.wait()
    ff_own.wait()
    og_gather.complete()
    scatter.finish()
    ff_swap.finish()
    ff_share.finish(pieces)
    gather.finish()
    gain_swap.finish()
    attn_swap.finish()
    for shift in range(1, groups):
        to_groups(shift).wait_send()

    @pl.when(spread.moves)
    def _():
        out_move.wait_send()


def forward(hidden, norm_gains, weights, tables, prefix, out_grad, ff_weights, shape, number):
    pieces, groups, heads, kv_heads, ff_block = shape
    rows, model = hidden.shape
    length = pieces * rows
    weight_rows = weights[0].shape[0]
    gains = norm_gains.shape[0]
    padded = -(-gains // 128) * 128
    q_width, kv_width = heads * HD, kv_heads * HD
    width = (heads + 2 * kv_heads + 1) * HD
    ff_shape = (pieces, weight_rows, 2 * groups * ff_block)
    struct, vmem = jax.ShapeDtypeStruct, pltpu.VMEM
    return pl.pallas_call(
        functools.partial(forward_kernel, shape),
        out_shape=(
            struct((length, model), low),
            struct((model, width), low),
            struct((1, groups * pieces * gains), full),
            struct((groups * weight_rows, model), low),
            struct((q_width + kv_width, length), full),
            struct((8, length), full),
            struct((length, q_width), low),
            struct((q_width, length), low),
            struct((length, kv_width), low),
            struct((kv_width, length), low),
            struct((length, kv_width), low),
            struct((q_width, length), full),
            struct((8, length), full),
            struct((q_width, length), low),
            struct((rows, model), full),
            struct((rows, model), low),
            struct((length, model), low),
            struct((groups,) + ff_shape, low),
        ),
        in_specs=[IN_VMEM] * 9 + [pl.BlockSpec(memory_space=pltpu.SMEM)] + [IN_VMEM] * 3,
        out_specs=(IN_VMEM,) * 16 + (ANY, ANY),
        scratch_shapes=[
            vmem((length, width), full),
            vmem((length, model), low),
            vmem((pieces, weight_rows, width), low),
            vmem((weight_rows, model), low),
            vmem((8, padded), full),
            vmem((groups, pieces, 8, padded), full),
            vmem((HD, HD), full),
            vmem((kv_width, length), low),
            vmem((length, q_width), low),
            vmem(ff_shape, low),
        ]
        + [DMA] * 6
        + swap_scratch(pieces)
        + [DMA((groups,))] * 2
        + swap_scratch(pieces)
        + [DMA((pieces, groups))] * 2
        + [DMA((1, groups))] * 2
        + swap_scratch(pieces)
        + [DMA((pieces, groups))] * 2
        + gather_scratch(pieces, 2) * 2
        + scatter_scratch(pieces, rows, model),
        compiler_params=pltpu.CompilerParams(
            collective_id=number, has_side_effects=True, vmem_limit_bytes=67043328
        ),
        name=f"forward_{number}",
    )(
        hidden, norm_gains.reshape(1, gains), *weights, *tables, prefix, out_grad, *ff_weights,
    )


def attend_back_kernel(
    shape,
    grad_branch,
    out_low,
    raw_t,
    gate_t,
    q_ref,
    qt_ref,
    k_ref,
    kt_ref,
    v_ref,
    att_t,
    lse_ref,
    gated_t,
    cosine,
    sine,
    gains,
    prefix_ref,
    normed,
    attn_low,
    hidden,
    grad_middle,
    swiglu_gain_grad,
    ff_share,
    down_term,
    hidden_grad,
    gains_grad,
    query_grad,
    key_grad,
    value_grad,
    head_grad,
    gate_grad,
    up_grad,
    out_grad,
    down_grad,
    down_in,
    down_mine,
    down_sem,
    ff_sem,
    corner,
    out_term,
    out_in,
    out_send,
    gg_t,
    ga_t,
    ga,
    gqt,
    dk,
    dv,
    grad_t,
    grad,
    total_ref,
    ff_recv,
    normed_part,
    part_sem,
    term,
    term_in,
    attn_send,
    attn_recv,
    gains_vector,
    gain_give,
    gain_sib,
    gain_row,
    gain_last,
    ffs_s,
    ffs_r,
    at_s,
    at_r,
    gc_s,
    gc_r,
    ts_s,
    ts_r,
    gs_s,
    gs_r,
    ot_s,
    ot_r,
    om_s,
    om_r,
    de_s,
    de_r,
    dl_s,
    dl_r,
    *scatter_refs,
):
    pieces, groups, heads, kv_heads, ff_block = shape
    line = Line(pieces)
    me, group = line.me, lax.axis_index("seq")
    length, rows = grad_branch.shape[0], hidden.shape[0]
    width, model = attn_low.shape[1], attn_low.shape[0]
    weight_rows = ff_share.shape[1]
    q_width, kv_width = heads * HD, kv_heads * HD
    spread = Spread(groups, pieces)
    greet(others("ctx", pieces) + others("seq", groups) + spread.peers())
    share = model // groups
    fold = Fold(groups, term, term_in, ts_s, ts_r)
    out_fold = Fold(groups, out_term, out_in, ot_s, ot_r)

    def load(job):
        index = fold.order[job]
        return pltpu.make_async_copy(
            normed.at[:, lanes(index * share, share)], normed_part.at[job % 2], part_sem.at[job % 2]
        )

    load(0).start()
    down_rows = down_in.shape[1]
    half = down_rows // 32 * 16
    early, late = pl.ds(0, half), pl.ds(half, down_rows - half)
    down_early = Fold(groups, down_term.at[:, early], down_in.at[:, early], de_s, de_r)
    down_late = Fold(groups, down_term.at[:, late], down_in.at[:, late], dl_s, dl_r)
    for job in range(groups):
        down_early.ready(job)
    down_own = pltpu.make_async_copy(down_term.at[group], down_mine, down_sem)
    down_own.start()
    ff_own = pltpu.make_async_copy(ff_share.at[me], ff_recv.at[me], ff_sem)
    ff_own.start()
    ff_swap = LineSwap(
        line, lambda peer: ff_share.at[peer], lambda source: ff_recv.at[source], ffs_s, ffs_r
    )
    ff_swap.start()

    prefix = prefix_ref[0, 0]
    query_gain, key_gain = column(gains, 2 * model), column(gains, 2 * model + HD)
    scale = HD ** (-0.5)

    def branch(index, unused):
        columns = lanes(index * 256, 256)
        gg_t[:, columns] = product_nt(out_low[...], grad_branch[columns, :])
        return unused

    lax.fori_loop(0, length // 256, branch, 0)

    def out_grads(index, unused):
        columns = lanes(index * 256, 256)
        value = product(gated_t[...], grad_branch[:, columns]).astype(low)
        for place in range(groups):
            out_term[place, :, columns] = value[place * weight_rows : (place + 1) * weight_rows]
        return unused

    lax.fori_loop(0, model // 256, out_grads, 0)

    for job in range(groups):
        out_fold.ready(job)
    dk[...] = jnp.zeros(dk.shape, full)
    dv[...] = jnp.zeros(dv.shape, full)
    gate_rows = []
    for head in range(heads):
        part = pl.ds(head * HD, HD)
        kv_part = pl.ds(head * kv_heads // heads * HD, HD)
        sigmoid = jax.nn.sigmoid(gate_t[head : head + 1, :])
        grads = gg_t[part, :]
        rounded = (grads * sigmoid).astype(low)
        ga_t[...] = rounded
        ga[...] = rounded.astype(full).T.astype(low)
        gate_rows.append(
            jnp.sum(grads * att_t[part, :], axis=0, keepdims=True) * sigmoid * (1.0 - sigmoid)
        )

        def block(first, tile, keys):
            columns, across = lanes(first, tile), pl.ds(0, keys)
            scores = product(k_ref[across, kv_part], qt_ref[part, columns]) * scale
            chance = jnp.where(
                kept(0, keys, first, tile, prefix),
                jnp.exp(scores - lse_ref[head : head + 1, columns]),
                0.0,
            )
            taken = ga_t[:, columns]
            delta = jnp.sum(taken.astype(full) * att_t[part, columns], axis=0, keepdims=True)
            change = product(v_ref[across, kv_part], taken)
            score_grad = (chance * (change - delta)).astype(low)
            gqt[part, columns] = product(kt_ref[kv_part, across], score_grad) * scale
            dk[across, kv_part] += product(score_grad, q_ref[columns, part])
            dv[across, kv_part] += product(chance.astype(low), ga[columns, :])

        query_blocks(length, block)

    gain_columns = [jnp.zeros((HD, 1), full), jnp.zeros((HD, 1), full)]
    for head in range(heads + kv_heads):
        part = pl.ds(head * HD, HD)
        if head < heads:
            turned = gqt[part, :]
            gain = query_gain
        else:
            turned = dk[:, pl.ds((head - heads) * HD, HD)].T * scale
            gain = key_gain
        grads = turn_back(turned, cosine[...], sine[...])
        values = raw_t[part, :]
        inverse = inverse_rms(values)
        kind = 0 if head < heads else 1
        gain_columns[kind] = gain_columns[kind] + jnp.sum(
            grads * values * inverse, axis=1, keepdims=True
        )
        scaled = grads * gain
        result = inverse * scaled - values * (
            inverse * inverse * inverse * jnp.mean(scaled * values, axis=0, keepdims=True)
        )
        grad_t[part, :] = result.astype(low)
        grad[:, part] = result.T.astype(low)
    for head in range(kv_heads):
        part = pl.ds((heads + kv_heads + head) * HD, HD)
        values = dv[:, pl.ds(head * HD, HD)]
        grad[:, part] = values.astype(low)
        grad_t[part, :] = values.T.astype(low)
    part = pl.ds((heads + 2 * kv_heads) * HD, HD)
    gate_block = jnp.concatenate(
        gate_rows + [jnp.zeros((HD - heads, length), full)], axis=0
    )
    grad_t[part, :] = gate_block.astype(low)
    grad[:, part] = gate_block.T.astype(low)

    scatter = Scatter(line, rows, scatter_refs)
    scatter.clear()
    block = blocks_nt(grad, attn_low, rows)
    last = line.chips - 1

    def fills(far):
        scatter.fill(far, far, block)

    def pushes(far):
        for distance, side in scatter.order():
            if distance == far and far > 0:
                scatter.push(far, side)

    def weight_grad(job):
        index = fold.order[job]
        load(job).wait()
        if job + 1 < groups:
            load(job + 1).start()

        def step(tile, unused):
            start = index * share + tile * 128
            value = product(grad_t[...], normed_part[job % 2, :, lanes(tile * 128, 128)])
            turned = value.T
            term[index, pl.ds(pl.multiple_of(tile * 128, 128), 128), :] = turned.astype(low)
            weighted = jnp.sum(
                turned * attn_low[pl.ds(pl.multiple_of(start, 128), 128), :].astype(full),
                axis=1,
                keepdims=True,
            )
            wide = jnp.broadcast_to(weighted, (128, 128)).T
            gains_vector[:, lanes(start, 128)] = wide[0:1, :] / gains[:, lanes(start, 128)]
            return unused

        lax.fori_loop(0, share // 128, step, 0)
        fold.ready(job)

    weight_grad(0)
    fills(last)
    pushes(last)
    for job in range(1, groups):
        weight_grad(job)
        if job <= last:
            fills(last - job)
    for far in range(last - groups, -1, -1):
        fills(far)

    for job in range(groups):
        down_late.ready(job)

    gain_count = gains_grad.shape[1]
    gains_vector[:, pl.ds(model, model)] = swiglu_gain_grad[...]
    for kind in range(2):
        wide = jnp.broadcast_to(gain_columns[kind], (HD, HD)).T
        gains_vector[:, pl.ds(2 * model + kind * HD, HD)] = wide[0:1, :]
    gain_give[...] = jnp.zeros(gain_give.shape, full)
    for index in range(groups * pieces):
        gain_give[index % pieces, index // pieces, 0:1, pl.ds(0, gain_count)] = gains_vector[
            :, pl.ds(index * gain_count, gain_count)
        ]
    gain_swap = LineSwap(
        line, lambda peer: gain_give.at[peer], lambda source: gain_sib.at[source], gc_s, gc_r
    )
    gain_swap.start()
    gain_sib[me] = gain_give[me]
    pushes(last - 1)

    out_fold.arrive()

    def total_out(across):
        out_send[across, :] = out_fold.sum(across).astype(low)

    by_rows(weight_rows, total_out, 16)
    out_move = spread.copy(out_send, out_grad, om_s, om_r, True)

    @pl.when(spread.moves)
    def _():
        out_move.start()

    @pl.when(jnp.logical_not(spread.moves))
    def _():
        out_grad[...] = out_send[...]

    for far in range(line.chips):
        gain_swap.receive(far, lambda source: None)
    gain_row[...] = jnp.sum(gain_sib[...], axis=0)

    def gain_to(shift):
        peer = lax.rem(group + shift, groups)
        return remote(
            gain_row.at[peer], gain_last.at[shift], gs_s.at[shift], gs_r.at[shift], "seq", peer
        )

    for shift in range(1, groups):
        gain_to(shift).start()
    gain_last[0] = gain_row[group]

    for far in range(line.chips):
        ff_swap.receive(far, lambda source: None)
    ff_own.wait()
    own_width = groups * ff_block

    def restore(across):
        for part, grad_ref in enumerate((gate_grad, up_grad)):
            for index in range(groups):
                for piece in range(pieces):
                    start = (index * pieces + piece) * ff_block
                    grad_ref[across, pl.ds(start, ff_block)] = ff_recv[
                        piece, across, pl.ds(part * own_width + index * ff_block, ff_block)
                    ]

    by_rows(weight_rows, restore, 16)

    for far in range(last - 2, 0, -1):
        pushes(far)

    fold.arrive()

    def total_term(piece, unused):
        across = pl.ds(pl.multiple_of(piece * weight_rows, weight_rows), weight_rows)
        attn_send[piece] = fold.sum(across).astype(low)
        return unused

    lax.fori_loop(0, pieces, total_term, 0)
    attn_swap = LineSwap(
        line, lambda peer: attn_send.at[peer], lambda source: attn_recv.at[source], at_s, at_r
    )
    attn_swap.start()

    scatter.total(total_ref)

    def rest(across):
        values = hidden[across, :].astype(full)
        inverse = lax.rsqrt(jnp.mean(values * values, axis=-1, keepdims=True) + epsilon)
        scaled = total_ref[across, :] * gains[:, pl.ds(0, model)]
        hidden_grad[across, :] = (
            grad_middle[across, :]
            + inverse * scaled
            - values
            * (inverse * inverse * inverse * jnp.mean(scaled * values, axis=-1, keepdims=True))
        ).astype(low)

    by_rows(rows, rest)
    down_early.arrive()
    down_late.arrive()
    down_own.wait()
    whole_fold = Fold(groups, down_term, down_in, de_s, de_r)

    def total_down(across):
        down_grad[across, :] = whole_fold.sum(across, down_mine).astype(low)

    by_rows(down_grad.shape[0], total_down, 16)
    for shift in range(1, groups):
        peer = lax.rem(group + groups - shift, groups)
        remote(
            gain_row.at[peer], gain_last.at[shift], gs_s.at[shift], gs_r.at[shift], "seq", peer
        ).wait_recv()
    gains_grad[...] = jnp.sum(gain_last[...], axis=0)[0:1, pl.ds(0, gain_count)]

    for far in range(line.chips):
        attn_swap.receive(far, lambda source: None)
    attn_recv[me] = attn_send[me]
    copies = max(1, pieces // KV)
    corner[...] = jnp.zeros(corner.shape, full)
    for piece in range(pieces):
        query_grad[:, pl.ds(piece * q_width, q_width)] = attn_recv[piece, :, pl.ds(0, q_width)]
        corner[pl.ds(0, weight_rows), pl.ds(piece * heads, heads)] = attn_recv[
            piece, :, pl.ds(q_width + 2 * kv_width, heads)
        ].astype(full)
    head_grad[...] = corner[...].T[: head_grad.shape[0], :weight_rows]
    for place in range(pieces // copies):
        for kind, grad_ref in enumerate((key_grad, value_grad)):
            columns = pl.ds(q_width + kind * kv_width, kv_width)
            summed = attn_recv[place * copies, :, columns].astype(full)
            for copy in range(1, copies):
                summed = summed + attn_recv[place * copies + copy, :, columns].astype(full)
            grad_ref[:, pl.ds(place * kv_width, kv_width)] = summed

    @pl.when(spread.moves)
    def _():
        spread.copy(out_grad, out_grad, om_s, om_r, True).wait_recv()
        out_move.wait_send()

    scatter.finish()
    ff_swap.finish()
    attn_swap.finish()
    gain_swap.finish()
    for shift in range(1, groups):
        gain_to(shift).wait_send()
    fold.finish()
    out_fold.finish()
    down_early.finish()
    down_late.finish()


def attend_back(
    grad_branch, out_low, saved, gated_t, tables, gains, prefix, normed, attn_low, hidden, grad_middle,
    swiglu_gain_grad, ff_share, down_term, gain_count, shape, number,
):
    pieces, groups, heads, kv_heads, ff_block = shape
    length, (rows, model) = grad_branch.shape[0], hidden.shape
    width = attn_low.shape[1]
    weight_rows = ff_share.shape[1]
    q_width, kv_width = heads * HD, kv_heads * HD
    struct, vmem = jax.ShapeDtypeStruct, pltpu.VMEM
    padded = -(-gain_count // 128) * 128
    return pl.pallas_call(
        functools.partial(attend_back_kernel, shape),
        out_shape=(
            struct((rows, model), low),
            struct((1, gain_count), full),
            struct((weight_rows, H * HD), low),
            struct((weight_rows, KV * HD), full),
            struct((weight_rows, KV * HD), full),
            struct((H, weight_rows), full),
            struct((weight_rows, pieces * groups * ff_block), low),
            struct((weight_rows, pieces * groups * ff_block), low),
            struct((weight_rows, model), low),
            struct(down_term.shape[1:], low),
        ),
        in_specs=[IN_VMEM] * 15 + [pl.BlockSpec(memory_space=pltpu.SMEM), ANY] + [IN_VMEM] * 4 + [ANY, ANY],
        out_specs=(IN_VMEM,) * 10,
        scratch_shapes=[
            vmem((groups - 1,) + down_term.shape[1:], low),
            vmem(down_term.shape[1:], low),
            DMA,
            DMA,
            vmem((HD, HD), full),
            vmem((groups, weight_rows, model), low),
            vmem((groups - 1, weight_rows, model), low),
            vmem((weight_rows, model), low),
            vmem((q_width, length), full),
            vmem((HD, length), low),
            vmem((length, HD), low),
            vmem((q_width, length), full),
            vmem((length, kv_width), full),
            vmem((length, kv_width), full),
            vmem((width, length), low),
            vmem((length, width), low),
            vmem((rows, model), full),
            vmem(ff_share.shape, low),
            vmem((2, length, model // groups), low),
            DMA((2,)),
            vmem((groups, model // groups, width), low),
            vmem((groups - 1, model // groups, width), low),
            vmem((pieces, weight_rows, width), low),
            vmem((pieces, weight_rows, width), low),
            vmem((1, 2 * model + 2 * HD), full),
            vmem((pieces, groups, 8, padded), full),
            vmem((pieces, groups, 8, padded), full),
            vmem((groups, 8, padded), full),
            vmem((groups, 8, padded), full),
        ]
        + swap_scratch(pieces) * 3
        + [DMA((groups,))] * 6
        + [DMA] * 2
        + [DMA((groups,))] * 4
        + scatter_scratch(pieces, rows, model),
        compiler_params=pltpu.CompilerParams(
            collective_id=number, has_side_effects=True, vmem_limit_bytes=67043328
        ),
        name=f"attend_back_{number}",
    )(
        grad_branch, out_low, *saved, gated_t, *tables, gains, prefix, normed, attn_low, hidden, grad_middle,
        swiglu_gain_grad, ff_share, down_term,
    )


def feed_kernel(
    shape,
    normed_two,
    ff_low,
    down_weight,
    og_all,
    n2_all,
    hidden_ff,
    grad_pre,
    down_low,
    down_block,
    before,
    share_s,
    share_r,
    *gather_sems,
):
    pieces, groups = shape[:2]
    line = Line(pieces)
    rows, length = normed_two.shape[0], og_all.shape[0]
    own_width = ff_low.shape[1] // 2
    tile = own_width // 3 if own_width % 384 == 0 else 128
    greet(line.peers() + others("seq", groups))
    group = lax.axis_index("seq")
    block_rows = down_weight.shape[0]

    def place(index, source):
        start = pl.multiple_of(index * block_rows, block_rows)
        return down_low.at[pl.ds(start, block_rows)]

    gather = Gather(line, 2, rows, n2_all, gather_sems)
    gather.start(normed_two)
    n2_all[pl.ds(pl.multiple_of(line.me * rows, rows), rows), :] = normed_two[...]

    def narrow(across):
        down_block[across, :] = down_weight[across, :].astype(low)

    by_rows(block_rows, narrow, 16)
    share = Share(groups, place, share_s, share_r)
    share.send(0, down_block)
    down_low[pl.ds(pl.multiple_of(group * block_rows, block_rows), block_rows), :] = down_block[...]

    def chip_rows(chip):
        across = pl.ds(pl.multiple_of(chip * 2 * rows, 2 * rows), 2 * rows)

        def step(index, unused):
            start = index * tile
            first, second = lanes(start, tile), lanes(own_width + start, tile)
            before[across, first] = product(n2_all[across, :], ff_low[:, first])
            before[across, second] = product(n2_all[across, :], ff_low[:, second])
            return unused

        lax.fori_loop(0, own_width // tile, step, 0)

    def swiglu(least, most):
        def rows_of(chip, unused):
            far = jnp.abs(chip - line.chip)
            across = pl.ds(pl.multiple_of(chip * 2 * rows, 2 * rows), 2 * rows)

            def step(column, unused):
                first, second = lanes(column * tile, tile), lanes(own_width + column * tile, tile)
                grads = product_nt(og_all[across, :], down_low[lanes(column * tile, tile), :])
                gate, up = before[across, first], before[across, second]
                sigmoid = jax.nn.sigmoid(gate)
                silu = gate * sigmoid
                hidden_ff[across, first] = (silu * up).astype(low)
                grad_pre[across, first] = (
                    grads * up * (sigmoid * (1.0 + gate * (1.0 - sigmoid)))
                ).astype(low)
                grad_pre[across, second] = (grads * silu).astype(low)
                return unused

            @pl.when(jnp.logical_and(far >= least, far <= most))
            def _():
                lax.fori_loop(0, own_width // tile, step, 0)

            return unused

        lax.fori_loop(0, line.chips, rows_of, 0)

    def compute(far):
        gather.arrive(far)
        if far == 0:
            chip_rows(line.chip)
            return

        @pl.when(line.chip - far >= 0)
        def _():
            chip_rows(line.chip - far)

        @pl.when(line.chip + far < line.chips)
        def _():
            chip_rows(line.chip + far)

    for hop in range(1, line.chips - 1):
        gather.forward(hop)
        compute(hop - 1)
        if hop == 1:
            share.relay(0)
    if line.chips > 1:
        compute(line.chips - 2)
        share.finish(1)
        swiglu(0, line.chips - 2)
        gather.forward(line.chips - 1)
    compute(line.chips - 1)
    swiglu(line.chips - 1, line.chips - 1)
    gather.finish()


def feed(normed_two, ff_low, down_weight, og_all, shape, number):
    pieces, groups = shape[:2]
    length, model = og_all.shape
    own_width = ff_low.shape[1] // 2
    struct = jax.ShapeDtypeStruct
    return pl.pallas_call(
        functools.partial(feed_kernel, shape),
        out_shape=(
            struct((length, model), low),
            struct((length, own_width), low),
            struct((length, 2 * own_width), low),
            struct((own_width, model), low),
        ),
        in_specs=[IN_VMEM] * 4,
        out_specs=(IN_VMEM,) * 4,
        scratch_shapes=[
            pltpu.VMEM(down_weight.shape, low),
            pltpu.VMEM((length, 2 * own_width), full),
            DMA((1, groups)),
            DMA((1, groups)),
        ]
        + gather_scratch(pieces, 2),
        compiler_params=pltpu.CompilerParams(
            collective_id=number, has_side_effects=True, vmem_limit_bytes=60 << 20
        ),
        name=f"feed_{number}",
    )(normed_two, ff_low, down_weight, og_all)


def feed_back_kernel(
    shape,
    grad_pre,
    ff_low,
    hidden_ff,
    down_low,
    og_all,
    n2_all,
    middle,
    out_grad,
    gains,
    gb_all,
    grad_middle,
    gain_grad,
    hidden_out,
    ff_share,
    down_term,
    total_ref,
    branch,
    n2_part,
    term,
    term_in,
    part_sem,
    own_sem,
    ts_s,
    ts_r,
    *sems,
):
    pieces, groups = shape[:2]
    buffers, sems = sems[:2], sems[2:]
    gather_sems, sems = sems[:6], sems[6:]
    line = Line(pieces)
    me, group = line.me, lax.axis_index("seq")
    length, rows, model = og_all.shape[0], middle.shape[0], og_all.shape[1]
    weight_rows = ff_share.shape[1]
    greet(line.peers() + others("seq", groups))
    half = len(sems) // 2
    inner = Scatter(line, rows, buffers + sems[:half])
    outer = Scatter(line, rows, buffers + sems[half:])
    inner.clear()
    outer.clear()
    block = blocks_nt(grad_pre, ff_low, rows)
    last = line.chips - 1

    def fills(scatter, far, block):
        scatter.fill(far, far, block)

    def pushes(scatter, far):
        for distance, side in scatter.order():
            if distance == far and far > 0:
                scatter.push(far, side)

    share = model // groups

    fold = Fold(groups, term, term_in, ts_s, ts_r)

    def load(job):
        index = fold.order[job]
        return pltpu.make_async_copy(
            n2_all.at[:, lanes(index * share, share)], n2_part.at[job % 2], part_sem.at[job % 2]
        )

    def ff_grad(job, index):
        load(job).wait()
        if job + 1 < groups:
            load(job + 1).start()

        def step(tile, unused):
            value = product_tn(n2_part[job % 2, :, lanes(tile * 128, 128)], grad_pre[...])
            term[index, pl.ds(pl.multiple_of(tile * 128, 128), 128), :] = value.astype(low)
            return unused

        lax.fori_loop(0, share // 128, step, 0)

    jobs = list(range(groups))

    def some_grads(count):
        for _ in range(min(count, len(jobs))):
            job = jobs.pop(0)
            ff_grad(job, fold.order[job])
            fold.ready(job)

    load(0).start()
    fills(inner, last, block)
    pushes(inner, last)
    fills(inner, last - 1, block)
    some_grads(1)
    each = -(-(groups - 1) // max(1, last - 1))
    for hop in range(1, line.chips):
        pushes(inner, last - hop)
        if hop < last:
            fills(inner, last - 1 - hop, block)
        some_grads(each)
    some_grads(groups)

    down_rows = down_term.shape[1]
    piece_rows = math.gcd(down_rows, 128)

    def down_grads(index, unused):
        value = product_tn(hidden_ff[:, lanes(index * 128, 128)], og_all[...]).astype(low)
        for part in range(128 // piece_rows):
            row = index * 128 + part * piece_rows
            down_term[row // down_rows, pl.ds(pl.multiple_of(lax.rem(row, down_rows), piece_rows), piece_rows), :] = (
                value[part * piece_rows : (part + 1) * piece_rows]
            )
        return unused

    lax.fori_loop(0, down_low.shape[0] // 128, down_grads, 0)
    inner.total(total_ref)
    inner.finish()
    gain_grad[...] = jnp.zeros(gain_grad.shape, full)

    def rest(across):
        values, grads = middle[across, :], total_ref[across, :]
        inverse = lax.rsqrt(jnp.mean(values * values, axis=-1, keepdims=True) + epsilon)
        gain_grad[...] += jnp.sum(grads * values * inverse, axis=0, keepdims=True)
        scaled = grads * gains[:, pl.ds(model, model)]
        result = (
            out_grad[across, :].astype(full)
            + inverse * scaled
            - values
            * (inverse * inverse * inverse * jnp.mean(scaled * values, axis=-1, keepdims=True))
        )
        grad_middle[across, :] = result
        branch[across, :] = result.astype(low)

    by_rows(rows, rest)

    gather = Gather(line, 2, rows, gb_all, gather_sems)
    gather.start(branch)
    start = pl.multiple_of(me * rows, rows)
    own = pltpu.make_async_copy(branch, gb_all.at[pl.ds(start, rows)], own_sem)
    own.start()
    block = blocks_nn(hidden_ff, down_low, rows)
    fills(outer, last, block)
    pushes(outer, last)
    fills(outer, last - 1, block)
    for hop in range(1, line.chips):
        gather.forward(hop)
        pushes(outer, last - hop)
        if hop < last:
            fills(outer, last - 1 - hop, block)
    fold.arrive()

    def total_term(piece, unused):
        across = pl.ds(pl.multiple_of(piece * weight_rows, weight_rows), weight_rows)
        ff_share[piece] = fold.sum(across).astype(low)
        return unused

    lax.fori_loop(0, pieces, total_term, 0)
    outer.total(total_ref)

    def output(across):
        hidden_out[across, :] = (middle[across, :] + total_ref[across, :]).astype(low)

    by_rows(rows, output)
    own.wait()
    for hop in range(line.chips):
        gather.arrive(hop)
    gather.finish()
    outer.finish()
    fold.finish()


def feed_back(
    grad_pre, ff_low, hidden_ff, down_low, og_all, n2_all, middle, out_grad, gains, shape, number
):
    pieces, groups = shape[:2]
    length, (rows, model) = og_all.shape[0], middle.shape
    own_width, width = hidden_ff.shape[1], grad_pre.shape[1]
    weight_rows = model // (groups * pieces)
    struct, vmem = jax.ShapeDtypeStruct, pltpu.VMEM
    scatter = scatter_scratch(pieces, rows, model)
    return pl.pallas_call(
        functools.partial(feed_back_kernel, shape),
        out_shape=(
            struct((length, model), low),
            struct((rows, model), full),
            struct((1, model), full),
            struct((rows, model), low),
            struct((pieces, weight_rows, width), low),
            struct((groups, own_width // groups, model), low),
        ),
        in_specs=[IN_VMEM] * 5 + [ANY] + [IN_VMEM] * 3,
        out_specs=(ANY,) + (IN_VMEM,) * 5,
        scratch_shapes=[
            vmem((rows, model), full),
            vmem((rows, model), low),
            vmem((2, length, model // groups), low),
            vmem((groups, model // groups, width), low),
            vmem((groups - 1, model // groups, width), low),
            DMA((2,)),
            DMA,
            DMA((groups,)),
            DMA((groups,)),
        ]
        + scatter[:2]
        + gather_scratch(pieces, 2)
        + scatter[2:] * 2,
        compiler_params=pltpu.CompilerParams(
            collective_id=number, has_side_effects=True, vmem_limit_bytes=63 << 20
        ),
        name=f"feed_back_{number}",
    )(grad_pre, ff_low, hidden_ff, down_low, og_all, n2_all, middle, out_grad, gains)


def widen_kernel(*refs):
    for source, target in zip(refs[: len(refs) // 2], refs[len(refs) // 2 :]):
        target[...] = source[...].astype(target.dtype)


def widen(arrays, kinds):
    steps = math.gcd(*(array.shape[0] for array in arrays[:-2])) // 16
    specs = [
        pl.BlockSpec((array.shape[0] // steps, array.shape[1]), lambda step: (step, 0))
        for array in arrays[:-2]
    ] + [pl.BlockSpec(array.shape, lambda step: (0, 0)) for array in arrays[-2:]]
    return pl.pallas_call(
        widen_kernel,
        grid=(steps,),
        out_shape=[
            jax.ShapeDtypeStruct(array.shape, kind) for array, kind in zip(arrays, kinds)
        ],
        in_specs=specs,
        out_specs=specs,
        name="widen",
    )(*arrays)


def on_device(
    hidden_in,
    out_grad,
    prefix_len,
    norm_gains,
    query_weight,
    key_weight,
    value_weight,
    head_gate_weight,
    out_weight,
    gate_weight,
    up_weight,
    down_weight,
):
    row_count, model = hidden_in.shape
    groups = lax.axis_size("seq")
    pieces = lax.axis_size("ctx")
    length = row_count * pieces
    weight_rows = query_weight.shape[0]
    heads = H // pieces
    kv_heads = max(1, KV // pieces)
    ff_block = down_weight.shape[0]
    ff_own = ff_block * groups
    gain_count = norm_gains.shape[0]
    shape = (pieces, groups, heads, kv_heads, ff_block)
    inverse = rope_base ** (-jnp.arange(HD // 2, dtype=full) * 2.0 / HD)
    angles = inverse[:, None] * jnp.arange(length, dtype=jnp.int32).astype(full)[None, :]
    tables = (jnp.cos(angles), jnp.sin(angles))
    prefix = prefix_len.reshape(1, 1)

    (
        normed, attn_low, gains_full, out_low, *saved, gated_t, middle, normed_two, out_grad_all, ff_low
    ) = forward(
        hidden_in,
        norm_gains,
        (query_weight, key_weight, value_weight, head_gate_weight.T, out_weight),
        tables,
        prefix,
        out_grad,
        (gate_weight, up_weight),
        shape,
        0,
    )
    ff_low = ff_low.reshape(model, 2 * ff_own)
    n2_all, hidden_ff, grad_pre, down_low = feed(
        normed_two, ff_low, down_weight, out_grad_all, shape, 2
    )
    grad_branch, grad_middle, swiglu_gain_grad, hidden_out, ff_share, down_term = feed_back(
        grad_pre, ff_low, hidden_ff, down_low, out_grad_all, n2_all, middle, out_grad, gains_full, shape, 3
    )
    hidden_grad, gains_share, query_share, key_share, value_share, head_share, gate_share, up_share, output_share, down_share = (
        attend_back(
            grad_branch,
            out_low,
            saved,
            gated_t,
            tables,
            gains_full,
            prefix,
            normed,
            attn_low,
            hidden_in,
            grad_middle,
            swiglu_gain_grad,
            ff_share,
            down_term,
            gain_count,
            shape,
            4,
        )
    )
    (
        hidden_out,
        hidden_grad,
        query_share,
        key_share,
        value_share,
        output_share,
        gate_share,
        up_share,
        down_share,
        head_share,
        gains_share,
    ) = widen(
        (
            hidden_out,
            hidden_grad,
            query_share,
            key_share,
            value_share,
            output_share,
            gate_share,
            up_share,
            down_share,
            head_share,
            gains_share,
        ),
        (low, low) + (full,) * 9,
    )
    return (
        hidden_out,
        hidden_grad,
        gains_share.reshape(gain_count),
        query_share,
        key_share,
        value_share,
        head_share.T,
        output_share,
        gate_share,
        up_share,
        down_share,
    )


def solution(mesh):
    rows = P(("seq", "ctx"), None)
    return jax.shard_map(
        on_device,
        mesh=mesh,
        in_specs=(rows, rows, P("seq"), P(("seq", "ctx"))) + (rows,) * 8,
        out_specs=(rows, rows, P(("seq", "ctx"))) + (rows,) * 8,
        check_vma=False,
    )
```

```python
import functools
import math

import jax
import jax.numpy as jnp
from jax import lax
from jax.experimental import pallas as pl
from jax.experimental.pallas import tpu as pltpu
from jax.sharding import PartitionSpec as P

H = 16
KV = 8
HD = 128


epsilon = 1e-06
rope_base = 1000000.0
negative = -1e30
low = jnp.bfloat16
full = jnp.float32
MESH = pl.DeviceIdType.MESH
ANY = pl.BlockSpec(memory_space=pl.ANY)
IN_VMEM = pl.BlockSpec(memory_space=pltpu.VMEM)
DMA = pltpu.SemaphoreType.DMA


def product(left_side, right_side):
    return jnp.dot(left_side, right_side, preferred_element_type=full)


def product_nt(left_side, right_side):
    return lax.dot_general(
        left_side, right_side, (((1,), (1,)), ((), ())), preferred_element_type=full
    )


def product_tn(left_side, right_side):
    return lax.dot_general(
        left_side, right_side, (((0,), (0,)), ((), ())), preferred_element_type=full
    )


def by_rows(rows, body, tile=32):
    tile = min(tile, rows)

    def step(index, unused):
        body(pl.ds(pl.multiple_of(index * tile, tile), tile))
        return unused

    lax.fori_loop(0, rows // tile, step, 0)


def remote(source, target, send, receive, axis, peer):
    return pltpu.make_async_remote_copy(
        src_ref=source,
        dst_ref=target,
        send_sem=send,
        recv_sem=receive,
        device_id={axis: peer},
        device_id_type=MESH,
    )


def greet(peers):
    barrier = pltpu.get_barrier_semaphore()
    for axis, peer, exists in peers:
        place = {"seq": peer[0], "ctx": peer[1]} if axis is None else {axis: peer}

        def signal():
            pl.semaphore_signal(barrier, inc=1, device_id=place, device_id_type=MESH)

        if exists is True:
            signal()
        else:
            pl.when(exists)(signal)

    arrivals = sum(1 for _, _, exists in peers if exists is True)
    for _, _, exists in peers:
        if exists is not True:
            arrivals = arrivals + exists.astype(jnp.int32)
    pl.semaphore_wait(barrier, arrivals)


def others(axis, count):
    me = lax.axis_index(axis)
    return [(axis, lax.rem(me + shift, count), True) for shift in range(1, count)]


class Line:
    def __init__(self, pieces):
        self.chips = pieces // 2
        self.me = lax.axis_index("ctx")
        self.chip, self.core = self.me // 2, lax.rem(self.me, 2)
        self.sibling = self.me + 1 - 2 * self.core
        self.right, self.left = self.me + 2, self.me - 2
        self.has_right, self.has_left = self.chip < self.chips - 1, self.chip > 0

    def peers(self):
        return [
            ("ctx", self.sibling, True),
            ("ctx", self.right, self.has_right),
            ("ctx", self.left, self.has_left),
        ]


def gather_scratch(pieces, parts):
    chips = pieces // 2
    return [DMA((chips, 2, parts))] * 2 + [DMA((chips, parts))] * 4


class Gather:
    def __init__(self, line, parts, rows, out_ref, sems):
        self.line, self.parts, self.rows, self.out_ref = line, parts, rows, out_ref
        self.size = rows // parts
        self.sib_send, self.sib_recv, self.r_send, self.r_recv, self.l_send, self.l_recv = sems

    def at(self, position, part):
        start = pl.multiple_of(position * self.rows + part * self.size, self.size)
        return self.out_ref.at[pl.ds(start, self.size)]

    def to_sibling(self, source, hop, side, part, position):
        return remote(
            source,
            self.at(position, part),
            self.sib_send.at[hop, side, part],
            self.sib_recv.at[hop, side, part],
            "ctx",
            self.line.sibling,
        )

    def to_right(self, source, hop, part, position):
        return remote(
            source,
            self.at(position, part),
            self.r_send.at[hop, part],
            self.r_recv.at[hop, part],
            "ctx",
            self.line.right,
        )

    def to_left(self, source, hop, part, position):
        return remote(
            source,
            self.at(position, part),
            self.l_send.at[hop, part],
            self.l_recv.at[hop, part],
            "ctx",
            self.line.left,
        )

    def start(self, x_ref):
        line = self.line
        for part in range(self.parts):
            piece = x_ref.at[pl.ds(part * self.size, self.size)]

            @pl.when(line.has_right)
            def _():
                self.to_right(piece, 0, part, line.me).start()

            @pl.when(line.has_left)
            def _():
                self.to_left(piece, 0, part, line.me).start()

            self.to_sibling(piece, 0, 0, part, line.me).start()

    def forward(self, hop):
        line = self.line
        for part in range(self.parts):
            from_left, from_right = line.me - 2 * hop, line.me + 2 * hop

            @pl.when(line.chip - hop >= 0)
            def _():
                piece = self.at(from_left, part)
                self.to_right(piece, hop - 1, part, from_left).wait_recv()

                @pl.when(line.has_right)
                def _():
                    self.to_right(piece, hop, part, from_left).start()

                self.to_sibling(piece, hop, 0, part, from_left).start()

            @pl.when(line.chip + hop < line.chips)
            def _():
                piece = self.at(from_right, part)
                self.to_left(piece, hop - 1, part, from_right).wait_recv()

                @pl.when(line.has_left)
                def _():
                    self.to_left(piece, hop, part, from_right).start()

                self.to_sibling(piece, hop, 1, part, from_right).start()

    def legs(self, hop):
        line = self.line
        return [
            (
                side,
                (line.chip - hop >= 0) if side == 0 else (line.chip + hop < line.chips),
                (line.me - 2 * hop) if side == 0 else (line.me + 2 * hop),
            )
            for side in range(1 if hop == 0 else 2)
        ]

    def arrive(self, hop):
        for side, there, position in self.legs(hop):
            for part in range(self.parts):

                @pl.when(there)
                def _():
                    self.to_sibling(
                        self.at(position, part), hop, side, part, position
                    ).wait_recv()

    def finish(self):
        line = self.line
        for hop in range(line.chips):
            for side, there, position in self.legs(hop):
                for part in range(self.parts):

                    @pl.when(there)
                    def _():
                        piece = self.at(position, part)
                        self.to_sibling(piece, hop, side, part, position).wait_send()
                        if side == 0:

                            @pl.when(line.has_right)
                            def _():
                                self.to_right(piece, hop, part, position).wait_send()

                        if side == 1 or hop == 0:

                            @pl.when(line.has_left)
                            def _():
                                self.to_left(piece, hop, part, position).wait_send()

    def complete(self):
        for hop in range(self.line.chips):
            self.arrive(hop)
        self.finish()


def scatter_scratch(pieces, rows, width):
    chips = pieces // 2
    slots = pltpu.VMEM((chips, rows, width), low)
    return [slots] * 3 + [pltpu.VMEM((chips + 1, rows, width), low)] + [DMA((chips,))] * 2 + [DMA((chips, 2))] * 4


class Scatter:
    def __init__(self, line, rows, scratch):
        self.line, self.rows = line, rows
        (
            self.own,
            self.give,
            self.sib,
            self.arrived,
            self.sib_send,
            self.sib_recv,
            self.r_send,
            self.r_recv,
            self.l_send,
            self.l_recv,
        ) = scratch

    def clear(self):
        line = self.line

        @pl.when(jnp.logical_not(line.has_left))
        def _():
            self.arrived[line.chip] = jnp.zeros(self.arrived.shape[1:], low)

        @pl.when(jnp.logical_not(line.has_right))
        def _():
            self.arrived[line.chips] = jnp.zeros(self.arrived.shape[1:], low)

    def there(self, far, side):
        line = self.line
        return (line.chip + far < line.chips) if side == 0 else (line.chip - far >= 0)

    def target(self, far, side):
        return self.line.chip + far if side == 0 else self.line.chip - far

    def exchange(self, target):
        return remote(
            self.give.at[target],
            self.sib.at[target],
            self.sib_send.at[target],
            self.sib_recv.at[target],
            "ctx",
            self.line.sibling,
        )

    def part(self, which):
        return pl.ds(which * (self.rows // 2), self.rows // 2)

    def send(self, target, side, which):
        part = self.part(which)
        if side == 0:
            return remote(
                self.own.at[target, part],
                self.arrived.at[target, part],
                self.r_send.at[target, which],
                self.r_recv.at[target, which],
                "ctx",
                self.line.right,
            )
        chips, chip = self.line.chips, self.line.chip
        return remote(
            self.own.at[target, part],
            self.arrived.at[jnp.where(target == chip - 1, chips, target), part],
            self.l_send.at[target, which],
            self.l_recv.at[target, which],
            "ctx",
            self.line.left,
        )

    def order(self):
        return [
            (far, side)
            for far in range(self.line.chips - 1, -1, -1)
            for side in range(2 if far else 1)
        ]

    def fill(self, least, most, block):
        line = self.line

        def step(target, unused):
            far = jnp.abs(target - line.chip)

            @pl.when(jnp.logical_and(far >= least, far <= most))
            def _():
                def store(columns, value):
                    first, second = value[: self.rows], value[self.rows :]
                    mine = line.core == 0
                    self.own[target, :, columns] = jnp.where(mine, first, second).astype(low)
                    self.give[target, :, columns] = jnp.where(mine, second, first).astype(low)

                block(target, store)
                self.exchange(target).start()

            return unused

        lax.fori_loop(0, line.chips, step, 0)

    def push(self, far, side):
        line = self.line
        behind = line.has_left if side == 0 else line.has_right

        @pl.when(self.there(far, side))
        def _():
            target = self.target(far, side)
            self.exchange(target).wait_recv()

            for which in range(2):
                first = which * (self.rows // 2)

                def add(part):
                    across = pl.ds(pl.multiple_of(first + part.start, part.size), part.size)
                    self.own[target, across, :] = (
                        self.own[target, across, :].astype(full)
                        + self.sib[target, across, :].astype(full)
                    ).astype(low)

                def add_all(part):
                    across = pl.ds(pl.multiple_of(first + part.start, part.size), part.size)
                    self.own[target, across, :] = (
                        self.own[target, across, :].astype(full)
                        + self.sib[target, across, :].astype(full)
                        + self.arrived[target, across, :].astype(full)
                    ).astype(low)

                if far == line.chips - 1:
                    by_rows(self.rows // 2, add)
                else:

                    @pl.when(behind)
                    def _():
                        self.send(target, side, which).wait_recv()
                        by_rows(self.rows // 2, add_all)

                    @pl.when(jnp.logical_not(behind))
                    def _():
                        by_rows(self.rows // 2, add)

                self.send(target, side, which).start()

    def total(self, total_ref):
        line = self.line
        chip = line.chip
        self.exchange(chip).wait_recv()

        @pl.when(line.has_left)
        def _():
            for which in range(2):
                self.send(chip, 0, which).wait_recv()

        @pl.when(line.has_right)
        def _():
            for which in range(2):
                self.send(chip, 1, which).wait_recv()

        def add(across):
            total = self.own[chip, across, :].astype(full) + self.sib[chip, across, :].astype(full)
            total = total + jnp.where(
                line.has_left, self.arrived[chip, across, :].astype(full), 0.0
            )
            total_ref[across, :] = total + jnp.where(
                line.has_right, self.arrived[line.chips, across, :].astype(full), 0.0
            )

        by_rows(self.rows, add)

    def finish(self):
        for far, side in self.order():

            @pl.when(self.there(far, side))
            def _():
                target = self.target(far, side)
                self.exchange(target).wait_send()
                if far > 0:
                    for which in range(2):
                        self.send(target, side, which).wait_send()


def blocks_nn(left_ref, right_ref, rows, tile=512):
    def block(target, store):
        start = pl.multiple_of(target * 2 * rows, 2 * rows)
        left_side = left_ref[pl.ds(start, 2 * rows), :]

        def step(index, unused):
            columns = pl.ds(pl.multiple_of(index * tile, tile), tile)
            store(columns, product(left_side, right_ref[:, columns]))
            return unused

        lax.fori_loop(0, right_ref.shape[1] // tile, step, 0)

    return block


def blocks_nt(left_ref, right_ref, rows, tile=512):
    def block(target, store):
        start = pl.multiple_of(target * 2 * rows, 2 * rows)
        left_side = left_ref[pl.ds(start, 2 * rows), :]

        def step(index, unused):
            columns = pl.ds(pl.multiple_of(index * tile, tile), tile)
            store(columns, product_nt(left_side, right_ref[columns, :]))
            return unused

        lax.fori_loop(0, right_ref.shape[0] // tile, step, 0)

    return block


class LineSwap:
    def __init__(self, line, send_of, recv_of, s_sem, r_sem):
        self.line, self.send_of, self.recv_of = line, send_of, recv_of
        self.s_sem, self.r_sem = s_sem, r_sem

    def copy(self, far, side, core):
        line = self.line
        if far == 0:
            peer, slot = line.sibling, self.r_sem.at[0, 0, 0]
        else:
            peer = (line.chip + (far if side == 0 else -far)) * 2 + core
            slot = self.r_sem.at[far, side, line.core]
        return remote(
            self.send_of(peer), self.recv_of(line.me), self.s_sem.at[far, side, core], slot, "ctx", peer
        )

    def legs(self, far):
        line = self.line
        if far == 0:
            return [(0, 0, True, True)]
        return [
            (
                side,
                core,
                (line.chip + far < line.chips) if side == 0 else (line.chip - far >= 0),
                (line.chip - far >= 0) if side == 0 else (line.chip + far < line.chips),
            )
            for side in range(2)
            for core in range(2)
        ]

    def start(self):
        for far in range(self.line.chips):
            for side, core, sends, _ in self.legs(far):
                if far == 0:
                    self.copy(far, side, core).start()
                else:

                    @pl.when(sends)
                    def _():
                        self.copy(far, side, core).start()

    def receive(self, far, then):
        line = self.line
        for side, core, _, comes in self.legs(far):
            if far == 0:
                source, slot = line.sibling, self.r_sem.at[0, 0, 0]
            else:
                source = (line.chip + (-far if side == 0 else far)) * 2 + core
                slot = self.r_sem.at[far, side, core]

            def wait():
                remote(
                    self.recv_of(source),
                    self.recv_of(source),
                    self.s_sem.at[far, side, core],
                    slot,
                    "ctx",
                    source,
                ).wait_recv()
                then(source)

            if far == 0:
                wait()
            else:
                pl.when(comes)(wait)

    def again(self, far, then):
        line = self.line
        for side, core, _, comes in self.legs(far):
            if far == 0:
                then(line.sibling)
            else:
                source = (line.chip + (-far if side == 0 else far)) * 2 + core

                @pl.when(comes)
                def _():
                    then(source)

    def finish(self):
        for far in range(self.line.chips):
            for side, core, sends, _ in self.legs(far):
                if far == 0:
                    self.copy(far, side, core).wait_send()
                else:

                    @pl.when(sends)
                    def _():
                        self.copy(far, side, core).wait_send()


def swap_scratch(pieces):
    return [DMA((pieces // 2, 2, 2))] * 2


class Share:
    def __init__(self, groups, place, s_sem, r_sem, relays=True):
        self.groups, self.place, self.s_sem, self.r_sem = groups, place, s_sem, r_sem
        self.group = lax.axis_index("seq")
        self.square = groups == 4 and relays
        self.across = self.group + 1 - 2 * lax.rem(self.group, 2)
        self.along = lax.rem(self.group + 2, groups)
        self.corner = groups - 1 - self.group

    def copy(self, source, slot, peer, origin, target):
        return remote(
            origin, target, self.s_sem.at[source, slot], self.r_sem.at[source, slot], "seq", peer
        )

    def half(self, index, source, which):
        ref = self.place(index, source)
        rows = ref.shape[0] // 2
        return ref.at[pl.ds(which * rows, rows)]

    def first(self, source, origin=None):
        target = self.place(self.group, source)
        origin = target if origin is None else origin
        if self.square:
            peers = [(1, self.across), (2, self.along)]
        else:
            peers = [
                (shift, lax.rem(self.group + shift, self.groups)) for shift in range(1, self.groups)
            ]
        return [self.copy(source, slot, peer, origin, target) for slot, peer in peers]

    def second(self, source):
        one, two = self.half(self.across, source, 0), self.half(self.along, source, 1)
        return [
            self.copy(source, 3, self.along, one, one),
            self.copy(source, 0, self.across, two, two),
        ]

    def send(self, source, origin=None):
        for copy in self.first(source, origin):
            copy.start()

    def relay(self, source):
        if not self.square:
            return
        for slot, index, copy in zip((1, 2), (self.across, self.along), self.second(source)):
            block = self.place(index, source)
            self.copy(source, slot, index, block, block).wait_recv()
            copy.start()

    def finish(self, sources):
        for source in range(sources):
            if self.square:
                for slot, which in ((3, 0), (0, 1)):
                    half = self.half(self.corner, source, which)
                    self.copy(source, slot, self.corner, half, half).wait_recv()
                for copy in self.second(source):
                    copy.wait_send()
            else:
                for shift in range(1, self.groups):
                    index = lax.rem(self.group + self.groups - shift, self.groups)
                    block = self.place(index, source)
                    self.copy(source, shift, index, block, block).wait_recv()
            for copy in self.first(source):
                copy.wait_send()


class Fold:
    def __init__(self, groups, term_ref, inbox, s_sem, r_sem):
        self.groups, self.term, self.inbox = groups, term_ref, inbox
        self.s_sem, self.r_sem = s_sem, r_sem
        self.group = lax.axis_index("seq")
        self.order = [lax.rem(self.group + shift, groups) for shift in range(1, groups)] + [
            self.group
        ]

    def copy(self, job):
        return remote(
            self.term.at[self.order[job]],
            self.inbox.at[job],
            self.s_sem.at[job],
            self.r_sem.at[job],
            "seq",
            self.order[job],
        )

    def ready(self, job):
        if job < self.groups - 1:
            self.copy(job).start()

    def arrive(self):
        for job in range(self.groups - 1):
            self.copy(job).wait_recv()

    def sum(self, across, own=None):
        total = (self.term[self.group, across, :] if own is None else own[across, :]).astype(full)
        for job in range(self.groups - 1):
            total = total + self.inbox[job, across, :].astype(full)
        return total

    def finish(self):
        for job in range(self.groups - 1):
            self.copy(job).wait_send()


class Spread:
    def __init__(self, groups, pieces):
        group, me = lax.axis_index("seq"), lax.axis_index("ctx")
        flat = group * pieces + me
        self.use = (lax.rem(flat, groups), flat // groups)
        held = me * groups + group
        self.rest = (held // pieces, lax.rem(held, pieces))
        self.moves = jnp.logical_or(self.use[0] != group, self.use[1] != me)

    def peers(self):
        return [(None, self.use, self.moves), (None, self.rest, self.moves)]

    def copy(self, source, target, send, receive, back):
        place = self.rest if back else self.use
        return pltpu.make_async_remote_copy(
            src_ref=source,
            dst_ref=target,
            send_sem=send,
            recv_sem=receive,
            device_id={"seq": place[0], "ctx": place[1]},
            device_id_type=MESH,
        )


def lanes(start, size):
    return pl.ds(pl.multiple_of(start, 128), size)


def turn(values, cosine, sine):
    half = values.shape[0] // 2
    first, second = values[:half], values[half:]
    return jnp.concatenate(
        [first * cosine - second * sine, second * cosine + first * sine], axis=0
    )


def turn_back(values, cosine, sine):
    half = values.shape[0] // 2
    first, second = values[:half], values[half:]
    return jnp.concatenate(
        [first * cosine + second * sine, second * cosine - first * sine], axis=0
    )


def column(gains, start):
    return jnp.broadcast_to(gains[:, pl.ds(start, HD)], (HD, HD)).T[:, 0:1]


def inverse_rms(values):
    return lax.rsqrt(jnp.mean(values * values, axis=0, keepdims=True) + epsilon)


def kept(first_key, keys, first_query, queries, prefix):
    key = first_key + lax.broadcasted_iota(jnp.int32, (keys, queries), 0)
    query = first_query + lax.broadcasted_iota(jnp.int32, (keys, queries), 1)
    return key <= jnp.maximum(query, prefix - 1)


def query_blocks(length, body):
    tile = min(256, length // 2)
    half = length // 2

    def early(index, unused):
        body(index * tile, tile, half)
        return unused

    def late(index, unused):
        body(half + index * tile, tile, length)
        return unused

    lax.fori_loop(0, half // tile, early, 0)
    lax.fori_loop(0, half // tile, late, 0)


def forward_kernel(
    shape,
    hidden,
    gains_ref,
    query_weight,
    key_weight,
    value_weight,
    gate_weight_t,
    out_weight,
    cosine,
    sine,
    prefix_ref,
    out_grad,
    gate_weight,
    up_weight,
    normed,
    attn_low,
    gains_out,
    out_low,
    raw_t,
    gate_t,
    q_ref,
    qt_ref,
    k_ref,
    kt_ref,
    v_ref,
    att_t,
    lse_ref,
    gated_t,
    middle,
    normed_two,
    og_all,
    ff_low,
    raw,
    hidden_all,
    blocks,
    out_block,
    gains_row,
    gains_all,
    corner,
    vt_ref,
    gated,
    ff_blocks,
    own_attn,
    own_out,
    out_s,
    out_r,
    ff_sem,
    og_sem,
    ga_s,
    ga_r,
    gs_s,
    gs_r,
    at_s,
    at_r,
    as_s,
    as_r,
    os_s,
    os_r,
    fs_s,
    fs_r,
    fh_s,
    fh_r,
    *sems,
):
    pieces, groups, heads, kv_heads, ff_block = shape
    rows_sems, og_sems, scatter_refs = sems[:6], sems[6:12], sems[12:]
    line = Line(pieces)
    me, group = line.me, lax.axis_index("seq")
    rows, model = hidden.shape
    length = pieces * rows
    weight_rows = out_weight.shape[0]
    q_width, kv_width = heads * HD, kv_heads * HD
    copies = max(1, pieces // KV)
    spread = Spread(groups, pieces)
    greet(others("ctx", pieces) + others("seq", groups) + spread.peers())
    gain_count = gains_ref.shape[1]
    gains_row[...] = jnp.zeros(gains_row.shape, full)
    gains_row[0:1, pl.ds(0, gain_count)] = gains_ref[...].astype(low).astype(full)
    gains_all[group, me] = gains_row[...]
    gain_swap = LineSwap(
        line, lambda peer: gains_row, lambda source: gains_all.at[group, source], ga_s, ga_r
    )
    gain_swap.start()

    blocks[:, :, pl.ds(q_width + 2 * kv_width, HD)] = jnp.zeros((pieces, weight_rows, HD), low)
    corner[...] = jnp.zeros(corner.shape, full)
    corner[pl.ds(0, gate_weight_t.shape[0]), pl.ds(0, weight_rows)] = gate_weight_t[...]
    gate_rows = corner[...].T
    for piece in range(pieces):
        blocks[piece, :, pl.ds(0, q_width)] = query_weight[
            :, pl.ds(piece * q_width, q_width)
        ].astype(low)
        start = piece // copies * kv_width
        blocks[piece, :, pl.ds(q_width, kv_width)] = key_weight[:, pl.ds(start, kv_width)].astype(low)
        blocks[piece, :, pl.ds(q_width + kv_width, kv_width)] = value_weight[
            :, pl.ds(start, kv_width)
        ].astype(low)
        blocks[piece, :, pl.ds(q_width + 2 * kv_width, heads)] = gate_rows[
            :weight_rows, piece * heads : (piece + 1) * heads
        ].astype(low)

    def place(index, source):
        start = pl.multiple_of((index * pieces + source) * weight_rows, weight_rows)
        return attn_low.at[pl.ds(start, weight_rows)]

    attn_swap = LineSwap(
        line, lambda peer: blocks.at[peer], lambda source: place(group, source), at_s, at_r
    )
    attn_swap.start()
    share = Share(groups, place, as_s, as_r, False)
    share.send(me, blocks.at[me])
    attn_own = pltpu.make_async_copy(blocks.at[me], place(group, me), own_attn)
    attn_own.start()
    gather = Gather(line, 2, rows, hidden_all, rows_sems)
    gather.start(hidden)
    hidden_all[pl.ds(pl.multiple_of(me * rows, rows), rows), :] = hidden[...]
    out_block[...] = out_weight[...].astype(low)

    def out_place(index):
        return out_low.at[pl.ds(pl.multiple_of(index * weight_rows, weight_rows), weight_rows)]

    out_move = spread.copy(out_block, out_place(spread.use[0]), out_s, out_r, False)
    out_stay = pltpu.make_async_copy(out_block, out_place(group), own_out)

    @pl.when(spread.moves)
    def _():
        out_move.start()

    @pl.when(jnp.logical_not(spread.moves))
    def _():
        out_stay.start()

    def to_groups(shift):
        peer = lax.rem(group + shift, groups)
        return remote(
            gains_all.at[group], gains_all.at[group], gs_s.at[shift], gs_r.at[shift], "seq", peer
        )

    def from_groups(shift):
        peer = lax.rem(group + groups - shift, groups)
        return remote(
            gains_all.at[peer], gains_all.at[peer], gs_s.at[shift], gs_r.at[shift], "seq", peer
        )

    attn_swap.receive(0, share.send)
    for far in range(line.chips):
        gain_swap.receive(far, lambda source: None)
    for shift in range(1, groups):
        to_groups(shift).start()
    if line.chips > 1:
        attn_swap.receive(1, share.send)

    def chip_rows(chip):
        return chip * 2 * rows

    def both(far, body):
        if far == 0:
            body(chip_rows(line.chip))
            return

        @pl.when(line.chip - far >= 0)
        def _():
            body(chip_rows(line.chip - far))

        @pl.when(line.chip + far < line.chips)
        def _():
            body(chip_rows(line.chip + far))

    def normalise(start):
        def some(part):
            across = pl.ds(pl.multiple_of(start + part.start, part.size), part.size)
            values = hidden_all[across, :].astype(full)
            inverse = lax.rsqrt(jnp.mean(values * values, axis=-1, keepdims=True) + epsilon)
            normed[across, :] = (values * inverse * gains_out[0:1, pl.ds(0, model)]).astype(low)

        by_rows(2 * rows, some)

    def project(least, most):
        def step(chip, unused):
            far = jnp.abs(chip - line.chip)

            @pl.when(jnp.logical_and(far >= least, far <= most))
            def _():
                across = pl.ds(pl.multiple_of(chip * 2 * rows, 2 * rows), 2 * rows)
                raw[across, :] = product(normed[across, :], attn_low[...])

            return unused

        lax.fori_loop(0, line.chips, step, 0)

    for far in range(2, line.chips):
        attn_swap.receive(far, share.send)
    out_share = Share(groups, lambda index, source: out_place(index), os_s, os_r)

    @pl.when(spread.moves)
    def _():
        spread.copy(out_place(group), out_place(group), out_s, out_r, False).wait_recv()

    @pl.when(jnp.logical_not(spread.moves))
    def _():
        out_stay.wait()

    out_share.send(0)
    for shift in range(1, groups):
        from_groups(shift).wait_recv()
    for index in range(groups * pieces):
        gains_out[0:1, pl.ds(index * gain_count, gain_count)] = gains_all[
            index // pieces, index % pieces, 0:1, pl.ds(0, gain_count)
        ]
    own_width = groups * ff_block

    def prepare(across):
        for half, weight_ref in enumerate((gate_weight, up_weight)):
            for index in range(groups):
                for piece in range(pieces):
                    start = (index * pieces + piece) * ff_block
                    ff_blocks[piece, across, pl.ds(half * own_width + index * ff_block, ff_block)] = (
                        weight_ref[across, pl.ds(start, ff_block)].astype(low)
                    )

    by_rows(gate_weight.shape[0], prepare, 16)
    for hop in range(1, line.chips - 1):
        gather.forward(hop)
        gather.arrive(hop - 1)
        both(hop - 1, normalise)
    ff_swap = LineSwap(
        line, lambda peer: ff_blocks.at[peer], lambda source: ff_low.at[group, source], fs_s, fs_r
    )
    ff_swap.start()
    ff_share = Share(groups, lambda index, source: ff_low.at[index, source], fh_s, fh_r, False)
    ff_share.send(me, ff_blocks.at[me])
    ff_own = pltpu.make_async_copy(ff_blocks.at[me], ff_low.at[group, me], ff_sem)
    ff_own.start()
    gather.arrive(line.chips - 2)
    both(line.chips - 2, normalise)
    attn_own.wait()
    out_share.relay(0)
    share.finish(pieces)
    project(0, line.chips - 2)
    gather.forward(line.chips - 1)
    gather.arrive(line.chips - 1)
    both(line.chips - 1, normalise)
    project(line.chips - 1, line.chips - 1)
    og_gather = Gather(line, 2, rows, og_all, og_sems)
    og_gather.start(out_grad)
    start = pl.multiple_of(me * rows, rows)
    og_own = pltpu.make_async_copy(out_grad, og_all.at[pl.ds(start, rows)], og_sem)
    og_own.start()
    prefix = prefix_ref[0, 0]
    query_gain, key_gain = column(gains_out, 2 * model), column(gains_out, 2 * model + HD)
    scale = HD ** (-0.5)
    for head in range(heads + kv_heads):
        part = pl.ds(head * HD, HD)
        values = raw[:, part].T
        raw_t[part, :] = values
        gain = query_gain if head < heads else key_gain
        turned = turn(values * inverse_rms(values) * gain, cosine[...], sine[...])
        if head < heads:
            qt_ref[part, :] = turned.astype(low)
            q_ref[:, part] = turned.T.astype(low)
        else:
            part = pl.ds((head - heads) * HD, HD)
            kt_ref[part, :] = turned.astype(low)
            k_ref[:, part] = turned.T.astype(low)
    for head in range(kv_heads):
        part = pl.ds(head * HD, HD)
        values = raw[:, pl.ds((heads + kv_heads + head) * HD, HD)]
        v_ref[:, part] = values.astype(low)
        vt_ref[part, :] = values.T.astype(low)
    gate_t[...] = raw[:, pl.ds((heads + 2 * kv_heads) * HD, HD)].T[: gate_t.shape[0]]
    ff_swap.receive(0, ff_share.send)
    for head in range(heads):
        part = pl.ds(head * HD, HD)
        kv_part = pl.ds(head * kv_heads // heads * HD, HD)

        def block(first, tile, keys):
            columns = lanes(first, tile)
            scores = product(k_ref[pl.ds(0, keys), kv_part], qt_ref[part, columns]) * scale
            scores = jnp.where(kept(0, keys, first, tile, prefix), scores, negative)
            top = jnp.max(scores, axis=0, keepdims=True)
            expanded = jnp.exp(scores - top)
            total = jnp.sum(expanded, axis=0, keepdims=True)
            lse_ref[head : head + 1, columns] = top + jnp.log(total)
            att_t[part, columns] = (
                product(vt_ref[kv_part, pl.ds(0, keys)], expanded.astype(low)) / total
            )

        query_blocks(length, block)
        scaled = att_t[part, :] * jax.nn.sigmoid(gate_t[head : head + 1, :])
        gated_t[part, :] = scaled.astype(low)
        gated[:, part] = scaled.T.astype(low)
        if head == 0 and line.chips > 1:
            ff_swap.receive(1, ff_share.send)

    out_share.finish(1)
    scatter = Scatter(line, rows, scatter_refs)
    scatter.clear()
    block = blocks_nn(gated, out_low, rows)
    last = line.chips - 1
    scatter.fill(last, last, block)
    for far, side in scatter.order():
        if far == last:
            scatter.push(far, side)
    scatter.fill(0, last - 1, block)
    if line.chips > 2:
        ff_swap.receive(2, ff_share.send)
    for hop in range(1, line.chips):
        og_gather.forward(hop)
        for far, side in scatter.order():
            if far == last - hop and far > 0:
                scatter.push(far, side)
        if hop == 1:
            for far in range(3, line.chips):
                ff_swap.receive(far, ff_share.send)
    scatter.total(middle)

    def normalise_two(across):
        values = hidden[across, :].astype(full) + middle[across, :]
        middle[across, :] = values
        inverse = lax.rsqrt(jnp.mean(values * values, axis=-1, keepdims=True) + epsilon)
        normed_two[across, :] = (values * inverse * gains_out[:, pl.ds(model, model)]).astype(low)

    by_rows(rows, normalise_two)
    og_own.wait()
    ff_own.wait()
    og_gather.complete()
    scatter.finish()
    ff_swap.finish()
    ff_share.finish(pieces)
    gather.finish()
    gain_swap.finish()
    attn_swap.finish()
    for shift in range(1, groups):
        to_groups(shift).wait_send()

    @pl.when(spread.moves)
    def _():
        out_move.wait_send()


def forward(hidden, norm_gains, weights, tables, prefix, out_grad, ff_weights, shape, number):
    pieces, groups, heads, kv_heads, ff_block = shape
    rows, model = hidden.shape
    length = pieces * rows
    weight_rows = weights[0].shape[0]
    gains = norm_gains.shape[0]
    padded = -(-gains // 128) * 128
    q_width, kv_width = heads * HD, kv_heads * HD
    width = (heads + 2 * kv_heads + 1) * HD
    ff_shape = (pieces, weight_rows, 2 * groups * ff_block)
    struct, vmem = jax.ShapeDtypeStruct, pltpu.VMEM
    return pl.pallas_call(
        functools.partial(forward_kernel, shape),
        out_shape=(
            struct((length, model), low),
            struct((model, width), low),
            struct((1, groups * pieces * gains), full),
            struct((groups * weight_rows, model), low),
            struct((q_width + kv_width, length), full),
            struct((8, length), full),
            struct((length, q_width), low),
            struct((q_width, length), low),
            struct((length, kv_width), low),
            struct((kv_width, length), low),
            struct((length, kv_width), low),
            struct((q_width, length), full),
            struct((8, length), full),
            struct((q_width, length), low),
            struct((rows, model), full),
            struct((rows, model), low),
            struct((length, model), low),
            struct((groups,) + ff_shape, low),
        ),
        in_specs=[IN_VMEM] * 9 + [pl.BlockSpec(memory_space=pltpu.SMEM)] + [IN_VMEM] * 3,
        out_specs=(IN_VMEM,) * 16 + (ANY, ANY),
        scratch_shapes=[
            vmem((length, width), full),
            vmem((length, model), low),
            vmem((pieces, weight_rows, width), low),
            vmem((weight_rows, model), low),
            vmem((8, padded), full),
            vmem((groups, pieces, 8, padded), full),
            vmem((HD, HD), full),
            vmem((kv_width, length), low),
            vmem((length, q_width), low),
            vmem(ff_shape, low),
        ]
        + [DMA] * 6
        + swap_scratch(pieces)
        + [DMA((groups,))] * 2
        + swap_scratch(pieces)
        + [DMA((pieces, groups))] * 2
        + [DMA((1, groups))] * 2
        + swap_scratch(pieces)
        + [DMA((pieces, groups))] * 2
        + gather_scratch(pieces, 2) * 2
        + scatter_scratch(pieces, rows, model),
        compiler_params=pltpu.CompilerParams(
            collective_id=number, has_side_effects=True, vmem_limit_bytes=67043328
        ),
        name=f"forward_{number}",
    )(
        hidden, norm_gains.reshape(1, gains), *weights, *tables, prefix, out_grad, *ff_weights,
    )


def attend_back_kernel(
    shape,
    grad_branch,
    out_low,
    raw_t,
    gate_t,
    q_ref,
    qt_ref,
    k_ref,
    kt_ref,
    v_ref,
    att_t,
    lse_ref,
    gated_t,
    cosine,
    sine,
    gains,
    prefix_ref,
    normed,
    attn_low,
    hidden,
    grad_middle,
    swiglu_gain_grad,
    ff_share,
    down_term,
    hidden_grad,
    gains_grad,
    query_grad,
    key_grad,
    value_grad,
    head_grad,
    gate_grad,
    up_grad,
    out_grad,
    down_grad,
    down_in,
    down_mine,
    down_sem,
    ff_sem,
    corner,
    out_term,
    out_in,
    out_send,
    gg_t,
    ga_t,
    ga,
    gqt,
    dk,
    dv,
    grad_t,
    grad,
    total_ref,
    ff_recv,
    normed_part,
    part_sem,
    term,
    term_in,
    attn_send,
    attn_recv,
    gains_vector,
    gain_give,
    gain_sib,
    gain_row,
    gain_last,
    ffs_s,
    ffs_r,
    at_s,
    at_r,
    gc_s,
    gc_r,
    ts_s,
    ts_r,
    gs_s,
    gs_r,
    ot_s,
    ot_r,
    om_s,
    om_r,
    de_s,
    de_r,
    dl_s,
    dl_r,
    *scatter_refs,
):
    pieces, groups, heads, kv_heads, ff_block = shape
    line = Line(pieces)
    me, group = line.me, lax.axis_index("seq")
    length, rows = grad_branch.shape[0], hidden.shape[0]
    width, model = attn_low.shape[1], attn_low.shape[0]
    weight_rows = ff_share.shape[1]
    q_width, kv_width = heads * HD, kv_heads * HD
    spread = Spread(groups, pieces)
    greet(others("ctx", pieces) + others("seq", groups) + spread.peers())
    share = model // groups
    fold = Fold(groups, term, term_in, ts_s, ts_r)
    out_fold = Fold(groups, out_term, out_in, ot_s, ot_r)

    def load(job):
        index = fold.order[job]
        return pltpu.make_async_copy(
            normed.at[:, lanes(index * share, share)], normed_part.at[job % 2], part_sem.at[job % 2]
        )

    load(0).start()
    down_rows = down_in.shape[1]
    half = down_rows // 32 * 16
    early, late = pl.ds(0, half), pl.ds(half, down_rows - half)
    down_early = Fold(groups, down_term.at[:, early], down_in.at[:, early], de_s, de_r)
    down_late = Fold(groups, down_term.at[:, late], down_in.at[:, late], dl_s, dl_r)
    for job in range(groups):
        down_early.ready(job)
    down_own = pltpu.make_async_copy(down_term.at[group], down_mine, down_sem)
    down_own.start()
    ff_own = pltpu.make_async_copy(ff_share.at[me], ff_recv.at[me], ff_sem)
    ff_own.start()
    ff_swap = LineSwap(
        line, lambda peer: ff_share.at[peer], lambda source: ff_recv.at[source], ffs_s, ffs_r
    )
    ff_swap.start()

    prefix = prefix_ref[0, 0]
    query_gain, key_gain = column(gains, 2 * model), column(gains, 2 * model + HD)
    scale = HD ** (-0.5)

    def branch(index, unused):
        columns = lanes(index * 256, 256)
        gg_t[:, columns] = product_nt(out_low[...], grad_branch[columns, :])
        return unused

    lax.fori_loop(0, length // 256, branch, 0)

    def out_grads(index, unused):
        columns = lanes(index * 256, 256)
        value = product(gated_t[...], grad_branch[:, columns]).astype(low)
        for place in range(groups):
            out_term[place, :, columns] = value[place * weight_rows : (place + 1) * weight_rows]
        return unused

    lax.fori_loop(0, model // 256, out_grads, 0)

    for job in range(groups):
        out_fold.ready(job)
    dk[...] = jnp.zeros(dk.shape, full)
    dv[...] = jnp.zeros(dv.shape, full)
    gate_rows = []
    for head in range(heads):
        part = pl.ds(head * HD, HD)
        kv_part = pl.ds(head * kv_heads // heads * HD, HD)
        sigmoid = jax.nn.sigmoid(gate_t[head : head + 1, :])
        grads = gg_t[part, :]
        rounded = (grads * sigmoid).astype(low)
        ga_t[...] = rounded
        ga[...] = rounded.astype(full).T.astype(low)
        gate_rows.append(
            jnp.sum(grads * att_t[part, :], axis=0, keepdims=True) * sigmoid * (1.0 - sigmoid)
        )

        def block(first, tile, keys):
            columns, across = lanes(first, tile), pl.ds(0, keys)
            scores = product(k_ref[across, kv_part], qt_ref[part, columns]) * scale
            chance = jnp.where(
                kept(0, keys, first, tile, prefix),
                jnp.exp(scores - lse_ref[head : head + 1, columns]),
                0.0,
            )
            taken = ga_t[:, columns]
            delta = jnp.sum(taken.astype(full) * att_t[part, columns], axis=0, keepdims=True)
            change = product(v_ref[across, kv_part], taken)
            score_grad = (chance * (change - delta)).astype(low)
            gqt[part, columns] = product(kt_ref[kv_part, across], score_grad) * scale
            dk[across, kv_part] += product(score_grad, q_ref[columns, part])
            dv[across, kv_part] += product(chance.astype(low), ga[columns, :])

        query_blocks(length, block)

    gain_columns = [jnp.zeros((HD, 1), full), jnp.zeros((HD, 1), full)]
    for head in range(heads + kv_heads):
        part = pl.ds(head * HD, HD)
        if head < heads:
            turned = gqt[part, :]
            gain = query_gain
        else:
            turned = dk[:, pl.ds((head - heads) * HD, HD)].T * scale
            gain = key_gain
        grads = turn_back(turned, cosine[...], sine[...])
        values = raw_t[part, :]
        inverse = inverse_rms(values)
        kind = 0 if head < heads else 1
        gain_columns[kind] = gain_columns[kind] + jnp.sum(
            grads * values * inverse, axis=1, keepdims=True
        )
        scaled = grads * gain
        result = inverse * scaled - values * (
            inverse * inverse * inverse * jnp.mean(scaled * values, axis=0, keepdims=True)
        )
        grad_t[part, :] = result.astype(low)
        grad[:, part] = result.T.astype(low)
    for head in range(kv_heads):
        part = pl.ds((heads + kv_heads + head) * HD, HD)
        values = dv[:, pl.ds(head * HD, HD)]
        grad[:, part] = values.astype(low)
        grad_t[part, :] = values.T.astype(low)
    part = pl.ds((heads + 2 * kv_heads) * HD, HD)
    gate_block = jnp.concatenate(
        gate_rows + [jnp.zeros((HD - heads, length), full)], axis=0
    )
    grad_t[part, :] = gate_block.astype(low)
    grad[:, part] = gate_block.T.astype(low)

    scatter = Scatter(line, rows, scatter_refs)
    scatter.clear()
    block = blocks_nt(grad, attn_low, rows)
    last = line.chips - 1

    def fills(far):
        scatter.fill(far, far, block)

    def pushes(far):
        for distance, side in scatter.order():
            if distance == far and far > 0:
                scatter.push(far, side)

    def weight_grad(job):
        index = fold.order[job]
        load(job).wait()
        if job + 1 < groups:
            load(job + 1).start()

        def step(tile, unused):
            start = index * share + tile * 128
            value = product(grad_t[...], normed_part[job % 2, :, lanes(tile * 128, 128)])
            turned = value.T
            term[index, pl.ds(pl.multiple_of(tile * 128, 128), 128), :] = turned.astype(low)
            weighted = jnp.sum(
                turned * attn_low[pl.ds(pl.multiple_of(start, 128), 128), :].astype(full),
                axis=1,
                keepdims=True,
            )
            wide = jnp.broadcast_to(weighted, (128, 128)).T
            gains_vector[:, lanes(start, 128)] = wide[0:1, :] / gains[:, lanes(start, 128)]
            return unused

        lax.fori_loop(0, share // 128, step, 0)
        fold.ready(job)

    fills(last)
    pushes(last)
    weight_grad(0)
    for job in range(1, groups):
        weight_grad(job)
        if job <= last:
            fills(last - job)
    for far in range(last - groups, -1, -1):
        fills(far)

    for job in range(groups):
        down_late.ready(job)

    gain_count = gains_grad.shape[1]
    gains_vector[:, pl.ds(model, model)] = swiglu_gain_grad[...]
    for kind in range(2):
        wide = jnp.broadcast_to(gain_columns[kind], (HD, HD)).T
        gains_vector[:, pl.ds(2 * model + kind * HD, HD)] = wide[0:1, :]
    gain_give[...] = jnp.zeros(gain_give.shape, full)
    for index in range(groups * pieces):
        gain_give[index % pieces, index // pieces, 0:1, pl.ds(0, gain_count)] = gains_vector[
            :, pl.ds(index * gain_count, gain_count)
        ]
    gain_swap = LineSwap(
        line, lambda peer: gain_give.at[peer], lambda source: gain_sib.at[source], gc_s, gc_r
    )
    gain_swap.start()
    gain_sib[me] = gain_give[me]
    pushes(last - 1)

    out_fold.arrive()

    def total_out(across):
        out_send[across, :] = out_fold.sum(across).astype(low)

    by_rows(weight_rows, total_out, 16)
    out_move = spread.copy(out_send, out_grad, om_s, om_r, True)

    @pl.when(spread.moves)
    def _():
        out_move.start()

    @pl.when(jnp.logical_not(spread.moves))
    def _():
        out_grad[...] = out_send[...]

    for far in range(line.chips):
        gain_swap.receive(far, lambda source: None)
    gain_row[...] = jnp.sum(gain_sib[...], axis=0)

    def gain_to(shift):
        peer = lax.rem(group + shift, groups)
        return remote(
            gain_row.at[peer], gain_last.at[shift], gs_s.at[shift], gs_r.at[shift], "seq", peer
        )

    for shift in range(1, groups):
        gain_to(shift).start()
    gain_last[0] = gain_row[group]

    for far in range(line.chips):
        ff_swap.receive(far, lambda source: None)
    ff_own.wait()
    own_width = groups * ff_block

    def restore(across):
        for part, grad_ref in enumerate((gate_grad, up_grad)):
            for index in range(groups):
                for piece in range(pieces):
                    start = (index * pieces + piece) * ff_block
                    grad_ref[across, pl.ds(start, ff_block)] = ff_recv[
                        piece, across, pl.ds(part * own_width + index * ff_block, ff_block)
                    ]

    by_rows(weight_rows, restore, 16)

    for far in range(last - 2, 0, -1):
        pushes(far)

    fold.arrive()

    def total_term(piece, unused):
        across = pl.ds(pl.multiple_of(piece * weight_rows, weight_rows), weight_rows)
        attn_send[piece] = fold.sum(across).astype(low)
        return unused

    lax.fori_loop(0, pieces, total_term, 0)
    attn_swap = LineSwap(
        line, lambda peer: attn_send.at[peer], lambda source: attn_recv.at[source], at_s, at_r
    )
    attn_swap.start()

    scatter.total(total_ref)

    def rest(across):
        values = hidden[across, :].astype(full)
        inverse = lax.rsqrt(jnp.mean(values * values, axis=-1, keepdims=True) + epsilon)
        scaled = total_ref[across, :] * gains[:, pl.ds(0, model)]
        hidden_grad[across, :] = (
            grad_middle[across, :]
            + inverse * scaled
            - values
            * (inverse * inverse * inverse * jnp.mean(scaled * values, axis=-1, keepdims=True))
        ).astype(low)

    by_rows(rows, rest)
    down_early.arrive()
    down_late.arrive()
    down_own.wait()
    whole_fold = Fold(groups, down_term, down_in, de_s, de_r)

    def total_down(across):
        down_grad[across, :] = whole_fold.sum(across, down_mine).astype(low)

    by_rows(down_grad.shape[0], total_down, 16)
    for shift in range(1, groups):
        peer = lax.rem(group + groups - shift, groups)
        remote(
            gain_row.at[peer], gain_last.at[shift], gs_s.at[shift], gs_r.at[shift], "seq", peer
        ).wait_recv()
    gains_grad[...] = jnp.sum(gain_last[...], axis=0)[0:1, pl.ds(0, gain_count)]

    for far in range(line.chips):
        attn_swap.receive(far, lambda source: None)
    attn_recv[me] = attn_send[me]
    copies = max(1, pieces // KV)
    corner[...] = jnp.zeros(corner.shape, full)
    for piece in range(pieces):
        query_grad[:, pl.ds(piece * q_width, q_width)] = attn_recv[piece, :, pl.ds(0, q_width)]
        corner[pl.ds(0, weight_rows), pl.ds(piece * heads, heads)] = attn_recv[
            piece, :, pl.ds(q_width + 2 * kv_width, heads)
        ].astype(full)
    head_grad[...] = corner[...].T[: head_grad.shape[0], :weight_rows]
    for place in range(pieces // copies):
        for kind, grad_ref in enumerate((key_grad, value_grad)):
            columns = pl.ds(q_width + kind * kv_width, kv_width)
            summed = attn_recv[place * copies, :, columns].astype(full)
            for copy in range(1, copies):
                summed = summed + attn_recv[place * copies + copy, :, columns].astype(full)
            grad_ref[:, pl.ds(place * kv_width, kv_width)] = summed

    @pl.when(spread.moves)
    def _():
        spread.copy(out_grad, out_grad, om_s, om_r, True).wait_recv()
        out_move.wait_send()

    scatter.finish()
    ff_swap.finish()
    attn_swap.finish()
    gain_swap.finish()
    for shift in range(1, groups):
        gain_to(shift).wait_send()
    fold.finish()
    out_fold.finish()
    down_early.finish()
    down_late.finish()


def attend_back(
    grad_branch, out_low, saved, gated_t, tables, gains, prefix, normed, attn_low, hidden, grad_middle,
    swiglu_gain_grad, ff_share, down_term, gain_count, shape, number,
):
    pieces, groups, heads, kv_heads, ff_block = shape
    length, (rows, model) = grad_branch.shape[0], hidden.shape
    width = attn_low.shape[1]
    weight_rows = ff_share.shape[1]
    q_width, kv_width = heads * HD, kv_heads * HD
    struct, vmem = jax.ShapeDtypeStruct, pltpu.VMEM
    padded = -(-gain_count // 128) * 128
    return pl.pallas_call(
        functools.partial(attend_back_kernel, shape),
        out_shape=(
            struct((rows, model), low),
            struct((1, gain_count), full),
            struct((weight_rows, H * HD), low),
            struct((weight_rows, KV * HD), full),
            struct((weight_rows, KV * HD), full),
            struct((H, weight_rows), full),
            struct((weight_rows, pieces * groups * ff_block), low),
            struct((weight_rows, pieces * groups * ff_block), low),
            struct((weight_rows, model), low),
            struct(down_term.shape[1:], low),
        ),
        in_specs=[IN_VMEM] * 15 + [pl.BlockSpec(memory_space=pltpu.SMEM), ANY] + [IN_VMEM] * 4 + [ANY, ANY],
        out_specs=(IN_VMEM,) * 10,
        scratch_shapes=[
            vmem((groups - 1,) + down_term.shape[1:], low),
            vmem(down_term.shape[1:], low),
            DMA,
            DMA,
            vmem((HD, HD), full),
            vmem((groups, weight_rows, model), low),
            vmem((groups - 1, weight_rows, model), low),
            vmem((weight_rows, model), low),
            vmem((q_width, length), full),
            vmem((HD, length), low),
            vmem((length, HD), low),
            vmem((q_width, length), full),
            vmem((length, kv_width), full),
            vmem((length, kv_width), full),
            vmem((width, length), low),
            vmem((length, width), low),
            vmem((rows, model), full),
            vmem(ff_share.shape, low),
            vmem((2, length, model // groups), low),
            DMA((2,)),
            vmem((groups, model // groups, width), low),
            vmem((groups - 1, model // groups, width), low),
            vmem((pieces, weight_rows, width), low),
            vmem((pieces, weight_rows, width), low),
            vmem((1, 2 * model + 2 * HD), full),
            vmem((pieces, groups, 8, padded), full),
            vmem((pieces, groups, 8, padded), full),
            vmem((groups, 8, padded), full),
            vmem((groups, 8, padded), full),
        ]
        + swap_scratch(pieces) * 3
        + [DMA((groups,))] * 6
        + [DMA] * 2
        + [DMA((groups,))] * 4
        + scatter_scratch(pieces, rows, model),
        compiler_params=pltpu.CompilerParams(
            collective_id=number, has_side_effects=True, vmem_limit_bytes=67043328
        ),
        name=f"attend_back_{number}",
    )(
        grad_branch, out_low, *saved, gated_t, *tables, gains, prefix, normed, attn_low, hidden, grad_middle,
        swiglu_gain_grad, ff_share, down_term,
    )


def feed_kernel(
    shape,
    normed_two,
    ff_low,
    down_weight,
    og_all,
    n2_all,
    hidden_ff,
    grad_pre,
    down_low,
    down_block,
    before,
    share_s,
    share_r,
    *gather_sems,
):
    pieces, groups = shape[:2]
    line = Line(pieces)
    rows, length = normed_two.shape[0], og_all.shape[0]
    own_width = ff_low.shape[1] // 2
    tile = own_width // 3 if own_width % 384 == 0 else 128
    greet(line.peers() + others("seq", groups))
    group = lax.axis_index("seq")
    block_rows = down_weight.shape[0]

    def place(index, source):
        start = pl.multiple_of(index * block_rows, block_rows)
        return down_low.at[pl.ds(start, block_rows)]

    gather = Gather(line, 2, rows, n2_all, gather_sems)
    gather.start(normed_two)
    n2_all[pl.ds(pl.multiple_of(line.me * rows, rows), rows), :] = normed_two[...]

    def narrow(across):
        down_block[across, :] = down_weight[across, :].astype(low)

    by_rows(block_rows, narrow, 16)
    share = Share(groups, place, share_s, share_r)
    share.send(0, down_block)
    down_low[pl.ds(pl.multiple_of(group * block_rows, block_rows), block_rows), :] = down_block[...]

    def chip_rows(chip):
        across = pl.ds(pl.multiple_of(chip * 2 * rows, 2 * rows), 2 * rows)

        def step(index, unused):
            start = index * tile
            first, second = lanes(start, tile), lanes(own_width + start, tile)
            before[across, first] = product(n2_all[across, :], ff_low[:, first])
            before[across, second] = product(n2_all[across, :], ff_low[:, second])
            return unused

        lax.fori_loop(0, own_width // tile, step, 0)

    def swiglu(least, most):
        def rows_of(chip, unused):
            far = jnp.abs(chip - line.chip)
            across = pl.ds(pl.multiple_of(chip * 2 * rows, 2 * rows), 2 * rows)

            def step(column, unused):
                first, second = lanes(column * tile, tile), lanes(own_width + column * tile, tile)
                grads = product_nt(og_all[across, :], down_low[lanes(column * tile, tile), :])
                gate, up = before[across, first], before[across, second]
                sigmoid = jax.nn.sigmoid(gate)
                silu = gate * sigmoid
                hidden_ff[across, first] = (silu * up).astype(low)
                grad_pre[across, first] = (
                    grads * up * (sigmoid * (1.0 + gate * (1.0 - sigmoid)))
                ).astype(low)
                grad_pre[across, second] = (grads * silu).astype(low)
                return unused

            @pl.when(jnp.logical_and(far >= least, far <= most))
            def _():
                lax.fori_loop(0, own_width // tile, step, 0)

            return unused

        lax.fori_loop(0, line.chips, rows_of, 0)

    def compute(far):
        gather.arrive(far)
        if far == 0:
            chip_rows(line.chip)
            return

        @pl.when(line.chip - far >= 0)
        def _():
            chip_rows(line.chip - far)

        @pl.when(line.chip + far < line.chips)
        def _():
            chip_rows(line.chip + far)

    for hop in range(1, line.chips - 1):
        gather.forward(hop)
        compute(hop - 1)
        if hop == 1:
            share.relay(0)
    if line.chips > 1:
        compute(line.chips - 2)
        share.finish(1)
        swiglu(0, line.chips - 2)
        gather.forward(line.chips - 1)
    compute(line.chips - 1)
    swiglu(line.chips - 1, line.chips - 1)
    gather.finish()


def feed(normed_two, ff_low, down_weight, og_all, shape, number):
    pieces, groups = shape[:2]
    length, model = og_all.shape
    own_width = ff_low.shape[1] // 2
    struct = jax.ShapeDtypeStruct
    return pl.pallas_call(
        functools.partial(feed_kernel, shape),
        out_shape=(
            struct((length, model), low),
            struct((length, own_width), low),
            struct((length, 2 * own_width), low),
            struct((own_width, model), low),
        ),
        in_specs=[IN_VMEM] * 4,
        out_specs=(IN_VMEM,) * 4,
        scratch_shapes=[
            pltpu.VMEM(down_weight.shape, low),
            pltpu.VMEM((length, 2 * own_width), full),
            DMA((1, groups)),
            DMA((1, groups)),
        ]
        + gather_scratch(pieces, 2),
        compiler_params=pltpu.CompilerParams(
            collective_id=number, has_side_effects=True, vmem_limit_bytes=60 << 20
        ),
        name=f"feed_{number}",
    )(normed_two, ff_low, down_weight, og_all)


def feed_back_kernel(
    shape,
    grad_pre,
    ff_low,
    hidden_ff,
    down_low,
    og_all,
    n2_all,
    middle,
    out_grad,
    gains,
    gb_all,
    grad_middle,
    gain_grad,
    hidden_out,
    ff_share,
    down_term,
    total_ref,
    branch,
    n2_part,
    term,
    term_in,
    part_sem,
    own_sem,
    ts_s,
    ts_r,
    *sems,
):
    pieces, groups = shape[:2]
    buffers, sems = sems[:2], sems[2:]
    gather_sems, sems = sems[:6], sems[6:]
    line = Line(pieces)
    me, group = line.me, lax.axis_index("seq")
    length, rows, model = og_all.shape[0], middle.shape[0], og_all.shape[1]
    weight_rows = ff_share.shape[1]
    greet(line.peers() + others("seq", groups))
    half = len(sems) // 2
    inner = Scatter(line, rows, buffers + sems[:half])
    outer = Scatter(line, rows, buffers + sems[half:])
    inner.clear()
    outer.clear()
    block = blocks_nt(grad_pre, ff_low, rows)
    last = line.chips - 1

    def fills(scatter, far, block):
        scatter.fill(far, far, block)

    def pushes(scatter, far):
        for distance, side in scatter.order():
            if distance == far and far > 0:
                scatter.push(far, side)

    share = model // groups

    fold = Fold(groups, term, term_in, ts_s, ts_r)

    def load(job):
        index = fold.order[job]
        return pltpu.make_async_copy(
            n2_all.at[:, lanes(index * share, share)], n2_part.at[job % 2], part_sem.at[job % 2]
        )

    def ff_grad(job, index):
        load(job).wait()
        if job + 1 < groups:
            load(job + 1).start()

        def step(tile, unused):
            value = product_tn(n2_part[job % 2, :, lanes(tile * 128, 128)], grad_pre[...])
            term[index, pl.ds(pl.multiple_of(tile * 128, 128), 128), :] = value.astype(low)
            return unused

        lax.fori_loop(0, share // 128, step, 0)

    jobs = list(range(groups))

    def some_grads(count):
        for _ in range(min(count, len(jobs))):
            job = jobs.pop(0)
            ff_grad(job, fold.order[job])
            fold.ready(job)

    load(0).start()
    fills(inner, last, block)
    pushes(inner, last)
    fills(inner, last - 1, block)
    some_grads(1)
    each = -(-(groups - 1) // max(1, last - 1))
    for hop in range(1, line.chips):
        pushes(inner, last - hop)
        if hop < last:
            fills(inner, last - 1 - hop, block)
        some_grads(each)
    some_grads(groups)

    down_rows = down_term.shape[1]
    piece_rows = math.gcd(down_rows, 128)

    def down_grads(index, unused):
        value = product_tn(hidden_ff[:, lanes(index * 128, 128)], og_all[...]).astype(low)
        for part in range(128 // piece_rows):
            row = index * 128 + part * piece_rows
            down_term[row // down_rows, pl.ds(pl.multiple_of(lax.rem(row, down_rows), piece_rows), piece_rows), :] = (
                value[part * piece_rows : (part + 1) * piece_rows]
            )
        return unused

    lax.fori_loop(0, down_low.shape[0] // 128, down_grads, 0)
    inner.total(total_ref)
    inner.finish()
    gain_grad[...] = jnp.zeros(gain_grad.shape, full)

    def rest(across):
        values, grads = middle[across, :], total_ref[across, :]
        inverse = lax.rsqrt(jnp.mean(values * values, axis=-1, keepdims=True) + epsilon)
        gain_grad[...] += jnp.sum(grads * values * inverse, axis=0, keepdims=True)
        scaled = grads * gains[:, pl.ds(model, model)]
        result = (
            out_grad[across, :].astype(full)
            + inverse * scaled
            - values
            * (inverse * inverse * inverse * jnp.mean(scaled * values, axis=-1, keepdims=True))
        )
        grad_middle[across, :] = result
        branch[across, :] = result.astype(low)

    by_rows(rows, rest)

    gather = Gather(line, 2, rows, gb_all, gather_sems)
    gather.start(branch)
    start = pl.multiple_of(me * rows, rows)
    own = pltpu.make_async_copy(branch, gb_all.at[pl.ds(start, rows)], own_sem)
    own.start()
    block = blocks_nn(hidden_ff, down_low, rows)
    fills(outer, last, block)
    pushes(outer, last)
    fills(outer, last - 1, block)
    for hop in range(1, line.chips):
        gather.forward(hop)
        pushes(outer, last - hop)
        if hop < last:
            fills(outer, last - 1 - hop, block)
    fold.arrive()

    def total_term(piece, unused):
        across = pl.ds(pl.multiple_of(piece * weight_rows, weight_rows), weight_rows)
        ff_share[piece] = fold.sum(across).astype(low)
        return unused

    lax.fori_loop(0, pieces, total_term, 0)
    outer.total(total_ref)

    def output(across):
        hidden_out[across, :] = (middle[across, :] + total_ref[across, :]).astype(low)

    by_rows(rows, output)
    own.wait()
    for hop in range(line.chips):
        gather.arrive(hop)
    gather.finish()
    outer.finish()
    fold.finish()


def feed_back(
    grad_pre, ff_low, hidden_ff, down_low, og_all, n2_all, middle, out_grad, gains, shape, number
):
    pieces, groups = shape[:2]
    length, (rows, model) = og_all.shape[0], middle.shape
    own_width, width = hidden_ff.shape[1], grad_pre.shape[1]
    weight_rows = model // (groups * pieces)
    struct, vmem = jax.ShapeDtypeStruct, pltpu.VMEM
    scatter = scatter_scratch(pieces, rows, model)
    return pl.pallas_call(
        functools.partial(feed_back_kernel, shape),
        out_shape=(
            struct((length, model), low),
            struct((rows, model), full),
            struct((1, model), full),
            struct((rows, model), low),
            struct((pieces, weight_rows, width), low),
            struct((groups, own_width // groups, model), low),
        ),
        in_specs=[IN_VMEM] * 5 + [ANY] + [IN_VMEM] * 3,
        out_specs=(ANY,) + (IN_VMEM,) * 5,
        scratch_shapes=[
            vmem((rows, model), full),
            vmem((rows, model), low),
            vmem((2, length, model // groups), low),
            vmem((groups, model // groups, width), low),
            vmem((groups - 1, model // groups, width), low),
            DMA((2,)),
            DMA,
            DMA((groups,)),
            DMA((groups,)),
        ]
        + scatter[:2]
        + gather_scratch(pieces, 2)
        + scatter[2:] * 2,
        compiler_params=pltpu.CompilerParams(
            collective_id=number, has_side_effects=True, vmem_limit_bytes=63 << 20
        ),
        name=f"feed_back_{number}",
    )(grad_pre, ff_low, hidden_ff, down_low, og_all, n2_all, middle, out_grad, gains)


def widen_kernel(*refs):
    for source, target in zip(refs[: len(refs) // 2], refs[len(refs) // 2 :]):
        target[...] = source[...].astype(target.dtype)


def widen(arrays, kinds):
    steps = math.gcd(*(array.shape[0] for array in arrays[:-2])) // 16
    specs = [
        pl.BlockSpec((array.shape[0] // steps, array.shape[1]), lambda step: (step, 0))
        for array in arrays[:-2]
    ] + [pl.BlockSpec(array.shape, lambda step: (0, 0)) for array in arrays[-2:]]
    return pl.pallas_call(
        widen_kernel,
        grid=(steps,),
        out_shape=[
            jax.ShapeDtypeStruct(array.shape, kind) for array, kind in zip(arrays, kinds)
        ],
        in_specs=specs,
        out_specs=specs,
        name="widen",
    )(*arrays)


def on_device(
    hidden_in,
    out_grad,
    prefix_len,
    norm_gains,
    query_weight,
    key_weight,
    value_weight,
    head_gate_weight,
    out_weight,
    gate_weight,
    up_weight,
    down_weight,
):
    row_count, model = hidden_in.shape
    groups = lax.axis_size("seq")
    pieces = lax.axis_size("ctx")
    length = row_count * pieces
    weight_rows = query_weight.shape[0]
    heads = H // pieces
    kv_heads = max(1, KV // pieces)
    ff_block = down_weight.shape[0]
    ff_own = ff_block * groups
    gain_count = norm_gains.shape[0]
    shape = (pieces, groups, heads, kv_heads, ff_block)
    inverse = rope_base ** (-jnp.arange(HD // 2, dtype=full) * 2.0 / HD)
    angles = inverse[:, None] * jnp.arange(length, dtype=jnp.int32).astype(full)[None, :]
    tables = (jnp.cos(angles), jnp.sin(angles))
    prefix = prefix_len.reshape(1, 1)

    (
        normed, attn_low, gains_full, out_low, *saved, gated_t, middle, normed_two, out_grad_all, ff_low
    ) = forward(
        hidden_in,
        norm_gains,
        (query_weight, key_weight, value_weight, head_gate_weight.T, out_weight),
        tables,
        prefix,
        out_grad,
        (gate_weight, up_weight),
        shape,
        0,
    )
    ff_low = ff_low.reshape(model, 2 * ff_own)
    n2_all, hidden_ff, grad_pre, down_low = feed(
        normed_two, ff_low, down_weight, out_grad_all, shape, 2
    )
    grad_branch, grad_middle, swiglu_gain_grad, hidden_out, ff_share, down_term = feed_back(
        grad_pre, ff_low, hidden_ff, down_low, out_grad_all, n2_all, middle, out_grad, gains_full, shape, 3
    )
    hidden_grad, gains_share, query_share, key_share, value_share, head_share, gate_share, up_share, output_share, down_share = (
        attend_back(
            grad_branch,
            out_low,
            saved,
            gated_t,
            tables,
            gains_full,
            prefix,
            normed,
            attn_low,
            hidden_in,
            grad_middle,
            swiglu_gain_grad,
            ff_share,
            down_term,
            gain_count,
            shape,
            4,
        )
    )
    (
        hidden_out,
        hidden_grad,
        query_share,
        key_share,
        value_share,
        output_share,
        gate_share,
        up_share,
        down_share,
        head_share,
        gains_share,
    ) = widen(
        (
            hidden_out,
            hidden_grad,
            query_share,
            key_share,
            value_share,
            output_share,
            gate_share,
            up_share,
            down_share,
            head_share,
            gains_share,
        ),
        (low, low) + (full,) * 9,
    )
    return (
        hidden_out,
        hidden_grad,
        gains_share.reshape(gain_count),
        query_share,
        key_share,
        value_share,
        head_share.T,
        output_share,
        gate_share,
        up_share,
        down_share,
    )


def solution(mesh):
    rows = P(("seq", "ctx"), None)
    return jax.shard_map(
        on_device,
        mesh=mesh,
        in_specs=(rows, rows, P("seq"), P(("seq", "ctx"))) + (rows,) * 8,
        out_specs=(rows, rows, P(("seq", "ctx"))) + (rows,) * 8,
        check_vma=False,
    )
```
